32 devices in a mesh: dp: 4 (over z), row: 2 (over core), col: 4 (over y, x).
Axes of the slice: x: 2, y: 2, z: 4, core: 2. Of those that a mesh axis runs over, the one named last changes fastest.
Arguments:
- tokens: bfloat16 [8192, 2048], P(('dp', 'row'), 'col'), may hold values from -6 to 6
- lengths: int32 [4], P('dp'), may hold values from 1024 to 2048, as said below
- attn_gain: float32 [2048], P('col'), may hold values from 0.5 to 1.5
- w_query: bfloat16 [2048, 2048], P('col', 'row'), may hold values from -16 to 16
- w_key: bfloat16 [2048, 512], P('col', 'row'), may hold values from -0.125 to 0.125
- w_value: bfloat16 [2048, 512], P('col', 'row'), may hold values from -0.125 to 0.125
- w_out: bfloat16 [2048, 2048], P('row', 'col'), may hold values from -1 to 1
- mlp_gain: float32 [2048], P('col'), may hold values from 0.5 to 1.5
- w_gate: bfloat16 [2048, 8192], P('col', 'row'), may hold values from -0.125 to 0.125
- w_up: bfloat16 [2048, 8192], P('col', 'row'), may hold values from -0.125 to 0.125
- w_down: bfloat16 [8192, 2048], P('row', 'col'), may hold values from -0.0625 to 0.0625
- cotangent: bfloat16 [8192, 2048], P(('dp', 'row'), 'col'), may hold values from -6 to 6
Outputs:
- output: bfloat16 [8192, 2048], P(('dp', 'row'), 'col')
- input_grad: float32 [8192, 2048], P(('dp', 'row'), 'col')
- grad_attn_gain: float32 [2048], P('col')
- grad_query: float32 [2048, 2048], P('col', 'row')
- grad_key: float32 [2048, 512], P('col', 'row')
- grad_value: float32 [2048, 512], P('col', 'row')
- grad_out: float32 [2048, 2048], P('row', 'col')
- grad_mlp_gain: float32 [2048], P('col')
- grad_gate: float32 [2048, 8192], P('col', 'row')
- grad_up: float32 [2048, 8192], P('col', 'row')
- grad_down: float32 [8192, 2048], P('row', 'col')
- head_max: float32 [32], P(('row', 'col'))
- clipped_query: bfloat16 [2048, 2048], P('col', 'row')
- clipped_key: bfloat16 [2048, 512], P('col', 'row')
The draws below stay inside these ranges and needn't reach their ends.
Inputs may be any that keep to these rules, and one draw needn't show every extreme that they name: `lengths`: each slot's valid tokens come first; some slot is full in every draw.
All inputs are finite; a program needn't handle non-finite values.
Results may differ from the reference program's by a relative error of at most 0.014.
The reference program's roundings to bfloat16 on the way count: a program that leaves them out, or rounds other values in their place, can miss the bound.
Values may be sent and summed in bfloat16 or wider, within the bound.
A program may use at most 384 MiB of HBM per device.

```python
import math
import jax
import jax.numpy as jnp
from jax import lax

D = 2048
HQ = 32
KV = 8
HD = 64
FF = 8192
SEQ_LEN = 2048
SEQ_DP = 1
SEQS = 4
TOKENS = 8192
N_DP = 4


def draw_lengths(key, part):
    lengths_key, spot_key = jax.random.split(jax.random.fold_in(key, 11))
    drawn_len = jax.random.randint(lengths_key, (SEQS,), SEQ_LEN // 2, SEQ_LEN + 1)
    spot_index = jax.random.randint(spot_key, (), 0, SEQS)
    return jnp.where(jnp.arange(SEQS) == spot_index, SEQ_LEN, drawn_len).astype(jnp.int32)


def draw_w_query(key, part):
    base_key, scale_key = jax.random.split(jax.random.fold_in(key, 23))
    head_scale = jnp.exp(jax.random.uniform(scale_key, (HQ,), jnp.float32, 0.0, math.log(3.0)))
    base_draw = jnp.clip(jax.random.normal(base_key, (D, HQ * HD), jnp.float32), -5.0, 5.0)
    scaled = base_draw * D ** (-0.5) * jnp.repeat(head_scale, HD)[None, :]
    return scaled.astype(jnp.bfloat16)


def steps_of(rng, shape, cuts, least, high):
    factor_of = 1.0
    for dim, blocks in cuts:
        heights = jax.random.uniform(jax.random.fold_in(jax.random.fold_in(rng, 6), dim), (blocks,), jnp.float32, least / len(cuts), high / len(cuts))
        factor_of = factor_of * jnp.repeat(jnp.exp(heights), shape[dim] // blocks).reshape((-1,) + (1,) * (len(shape) - 1 - dim))
    return factor_of


def centred(key, dims, scale, most, cuts=(), kind=jnp.bfloat16):
    entries = jax.random.normal(key, dims, jnp.float32) * scale
    if len(cuts) > 0:
        entries = steps_of(key, dims, cuts, -0.22, 0.18) * entries
    return jnp.clip(entries, min=-most, max=most).astype(kind)


def setup_inputs(seed: int = 0) -> dict:
    streams_of = jax.random.split(jax.random.key(seed), 13)
    return {
        "tokens": centred(streams_of[0], (TOKENS, D), 1.0, 6.0, ((0, 8), (1, 4))),
        "lengths": draw_lengths(jax.random.fold_in(streams_of[12], 71), 0),
        "attn_gain": jnp.clip(1.0 + 0.1 * jax.random.normal(streams_of[2], (D,), jnp.float32), 0.5, 1.5),
        "w_query": draw_w_query(jax.random.fold_in(streams_of[12], 71), 0),
        "w_key": centred(streams_of[4], (D, KV * HD), D ** -0.5, 0.125, ((0, 4), (1, 2))),
        "w_value": centred(streams_of[5], (D, KV * HD), D ** -0.5, 0.125, ((0, 4), (1, 2))),
        "w_out": centred(streams_of[6], (HQ * HD, D), (HQ * HD // 64) ** -0.5, 1.0, ((0, 2), (1, 4))),
        "mlp_gain": jnp.clip(1.0 + 0.1 * jax.random.normal(streams_of[7], (D,), jnp.float32), 0.5, 1.5),
        "w_gate": centred(streams_of[8], (D, FF), D ** -0.5, 0.125, ((0, 4), (1, 2))),
        "w_up": centred(streams_of[9], (D, FF), D ** -0.5, 0.125, ((0, 4), (1, 2))),
        "w_down": centred(streams_of[10], (FF, D), FF ** -0.5, 0.0625, ((0, 2), (1, 4))),
        "cotangent": centred(streams_of[11], (TOKENS, D), 1.0, 6.0, ((0, 8), (1, 4))),
    }


EPSILON = 1e-05
NEG_FILL = -1e+30
CLIP_LEVEL = 5.0
ROPE_BASE = 500000.0
PRECISE = lax.Precision.HIGHEST

@jax.custom_vjp
def low(v):
    return lax.optimization_barrier(v.astype(jnp.bfloat16)).astype(jnp.float32)

@jax.custom_vjp
def low_back(v):
    return v

def low_keep(v):
    return (low(v), None)

def low_pass(kept, grad):
    return (grad,)

def back_keep(v):
    return (v, None)

def back_low(kept, grad):
    return (low(grad),)
low.defvjp(low_keep, low_pass)
low_back.defvjp(back_keep, back_low)

def rope_tables(seq_span, head_width):
    position = jnp.arange(seq_span, dtype=jnp.float32)
    frequency = ROPE_BASE ** (-jnp.arange(head_width // 2, dtype=jnp.float32) * (2.0 / head_width))
    angle = position[:, None] * frequency[None, :]
    return (jnp.cos(angle), jnp.sin(angle))

def rotate(values_in, cos_table, sin_table, turn_sign):
    half_width = values_in.shape[-1] // 2
    first_half = values_in[..., :half_width]
    second_half = values_in[..., half_width:]
    cos_wide = cos_table[:, None, :]
    sin_wide = sin_table[:, None, :] * turn_sign
    return jnp.concatenate([first_half * cos_wide - second_half * sin_wide, second_half * cos_wide + first_half * sin_wide], axis=-1)

def rms_normalize(values_in, gain_in):
    return values_in * lax.rsqrt(lax.optimization_barrier(jnp.mean(values_in * values_in, axis=1, keepdims=True)) + EPSILON) * gain_in

def attend_seq(seq_parts):
    query_seq, keys_seq, values_seq, seq_length = seq_parts
    group_size = HQ // KV
    position = jnp.arange(SEQ_LEN, dtype=jnp.int32)
    allowed = (position[None, :] <= position[:, None]) & (position[None, :] < seq_length)
    live_pairs = allowed & (position[:, None] < seq_length)

    def one_head(head_parts):
        query_head, keys_head, values_head = head_parts
        scores = low_back(jnp.einsum('qgd,kd->gqk', query_head, keys_head, precision=PRECISE) * HD ** (-0.5))
        masked = jnp.where(allowed[None], scores, NEG_FILL)
        row_top = lax.optimization_barrier(jnp.max(masked, axis=-1, keepdims=True))
        exponent = jnp.exp(masked - row_top)
        soft_weights = exponent / lax.optimization_barrier(jnp.sum(exponent, axis=-1, keepdims=True))
        mixed_out = jnp.einsum('gqk,kd->qgd', low(soft_weights), values_head, precision=PRECISE)
        head_peak = lax.optimization_barrier(jnp.max(jnp.where(live_pairs[None], scores, NEG_FILL), axis=(1, 2)))
        return (mixed_out, head_peak)
    query_groups = query_seq.reshape(SEQ_LEN, KV, group_size, HD).transpose(1, 0, 2, 3)
    mixed_out, head_peak = lax.map(jax.checkpoint(one_head), (query_groups, keys_seq.transpose(1, 0, 2), values_seq.transpose(1, 0, 2)))
    return (mixed_out.transpose(1, 0, 2, 3).reshape(SEQ_LEN, HQ * HD), head_peak.reshape(HQ))

def block_layer(resid_in, param_set, lens_group, cos_table, sin_table):
    gain_attn, query_w, key_w, value_w, out_w, gain_mlp, gate_w, up_w, down_w = param_set
    normed_attn = low(rms_normalize(resid_in, gain_attn))
    query_raw = low_back(jnp.dot(normed_attn, query_w, precision=PRECISE))
    key_raw = low_back(jnp.dot(normed_attn, key_w, precision=PRECISE))
    value_low = low(low_back(jnp.dot(normed_attn, value_w, precision=PRECISE)))
    query_rot = low(rotate(query_raw.reshape(SEQ_DP, SEQ_LEN, HQ, HD), cos_table, sin_table, 1.0))
    key_rot = low(rotate(key_raw.reshape(SEQ_DP, SEQ_LEN, KV, HD), cos_table, sin_table, 1.0))
    value_seqs = value_low.reshape(SEQ_DP, SEQ_LEN, KV, HD)
    mixed_out, seq_peaks = lax.map(jax.checkpoint(attend_seq), (query_rot, key_rot, value_seqs, lens_group))
    mixed_out = low(low_back(mixed_out.reshape(SEQ_DP * SEQ_LEN, HQ * HD)))
    resid_mid = resid_in + low_back(jnp.dot(mixed_out, out_w, precision=PRECISE))
    normed_mlp = low(rms_normalize(resid_mid, gain_mlp))
    gate_value = low_back(jnp.dot(normed_mlp, gate_w, precision=PRECISE))
    up_value = low_back(jnp.dot(normed_mlp, up_w, precision=PRECISE))
    hidden = low(jax.nn.silu(gate_value) * up_value)
    layer_out = resid_mid + low_back(jnp.dot(hidden, down_w, precision=PRECISE))
    return (layer_out, lax.optimization_barrier(jnp.max(seq_peaks, axis=0)))

def reference(tokens, lengths, attn_gain, w_query, w_key, w_value, w_out, mlp_gain, w_gate, w_up, w_down, cotangent):
    params = tuple((item.astype(jnp.float32) for item in (attn_gain, w_query, w_key, w_value, w_out, mlp_gain, w_gate, w_up, w_down)))
    cos_table, sin_table = rope_tables(SEQ_LEN, HD)
    group_tokens = SEQ_DP * SEQ_LEN
    inputs = tokens.astype(jnp.float32).reshape(N_DP, group_tokens, D)
    cot_groups = cotangent.astype(jnp.float32).reshape(N_DP, group_tokens, D)
    group_lengths = lengths.reshape(N_DP, SEQ_DP)
    token_place = jnp.arange(group_tokens, dtype=jnp.int32)

    def group_step(running, group_parts):
        totals, peak_top = running
        group_in, cot_group, lens_group = group_parts
        valid_rows = (token_place % SEQ_LEN < lens_group[token_place // SEQ_LEN]).astype(jnp.float32)

        def forward(resid_arg, param_arg):
            return block_layer(resid_arg, param_arg, lens_group, cos_table, sin_table)
        layer_out, pullback, peaks = jax.vjp(forward, group_in, params, has_aux=True)
        grad_in, grad_params = pullback(cot_group * valid_rows[:, None])
        totals = jax.tree.map(lambda first_sum, second_sum: first_sum + second_sum, totals, grad_params)
        return ((totals, jnp.maximum(peak_top, peaks)), (layer_out.astype(jnp.bfloat16), grad_in))
    zero_grads = jax.tree.map(jnp.zeros_like, params)
    start_peak = jnp.full((HQ,), NEG_FILL, jnp.float32)
    (totals, peaks), (outs, grad_ins) = lax.scan(group_step, (zero_grads, start_peak), (inputs, cot_groups, group_lengths))
    clip_factor = CLIP_LEVEL / jnp.maximum(peaks, CLIP_LEVEL)
    query_scale = jnp.repeat(jnp.sqrt(clip_factor), HD)
    key_scale = jnp.repeat(jnp.sqrt(lax.optimization_barrier(jnp.min(clip_factor.reshape(KV, HQ // KV), axis=1))), HD)
    clipped_query = (params[1] * query_scale[None, :]).astype(jnp.bfloat16)
    clipped_key = (params[2] * key_scale[None, :]).astype(jnp.bfloat16)
    return (outs.reshape(TOKENS, D), grad_ins.reshape(TOKENS, D), totals[0], totals[1], totals[2], totals[3], totals[4], totals[5], totals[6], totals[7], totals[8], peaks, clipped_query, clipped_key)
```

```python
import functools

import jax
import jax.numpy as jnp
from jax import lax
from jax.experimental import pallas as pl
from jax.experimental.pallas import tpu as pltpu
from jax.sharding import PartitionSpec as P

D = 2048
HQ = 32
KV = 8
HD = 64
SEQ_LEN = 2048

EPSILON = 1e-05
NEG_FILL = -1e30
CLIP_LEVEL = 5.0
ROPE_BASE = 500000.0

BF = jnp.bfloat16
F32 = jnp.float32
LANES = 128
QB = 512
FWD_KB = 512
BWD_KB = 512


def contract(left, right, left_dim, right_dim):
    return lax.dot_general(
        left, right, (((left_dim,), (right_dim,)), ((), ())), preferred_element_type=F32
    )


def swap(values, axis, step):
    count = lax.axis_size(axis)
    return lax.ppermute(values, axis, [(i, i ^ step) for i in range(count)])


def gather_cols(values):
    parts = [values] + [swap(values, "col", s) for s in range(1, lax.axis_size("col"))]
    return jnp.concatenate(parts, axis=1)


def gather_rows(values):
    return jnp.concatenate([values, swap(values, "row", 1)], axis=0)


def reduce_tokens(partial, width):
    half_rows = partial.shape[0] // 2
    other = swap(partial[half_rows:].astype(BF), "row", 1)
    half = partial[:half_rows].astype(F32) + other.astype(F32)
    total = half[:, :width]
    for s in range(1, lax.axis_size("col")):
        block = half[:, s * width : (s + 1) * width].astype(BF)
        total = total + swap(block, "col", s).astype(F32)
    return total


def group_sum(values):
    count = lax.axis_size("dp")
    if count == 1:
        return values
    place = lax.axis_index("dp")
    mid = count // 2
    halves = values.reshape((2, values.shape[0] // 2) + values.shape[1:])
    total = halves.astype(F32)
    for t in range(mid - 1):
        moves = [(t, t + 1), (count - 1 - t, count - 2 - t)]
        total = total + lax.ppermute(total.astype(BF), "dp", moves).astype(F32)
    is_left = place == mid - 1
    across = [(mid - 1, mid), (mid, mid - 1)]
    given = jnp.where(is_left, total[1], total[0]).astype(BF)
    kept = jnp.where(is_left, total[0], total[1])
    own = (kept + lax.ppermute(given, "dp", across).astype(F32)).astype(BF)
    other = lax.ppermute(own, "dp", across)
    whole = jnp.stack([jnp.where(is_left, own, other), jnp.where(is_left, other, own)])
    for t in range(mid - 1):
        moves = [(mid - 1 - t, mid - 2 - t), (mid + t, mid + 1 + t)]
        moved = lax.ppermute(whole, "dp", moves)
        takes = (place == mid - 2 - t) | (place == mid + 1 + t)
        whole = jnp.where(takes, moved, whole)
    return whole.reshape(values.shape)


def attn_forward_kernel(
    info_ref, q_ref, k_ref, v_ref, mixed_ref, wide_ref, lse_ref, peak_ref, score_ref, sum_ref
):
    heads = q_ref.shape[1] // HD
    span = k_ref.shape[0]
    rows = heads * QB
    length = info_ref[0]
    half = info_ref[1]
    step = pl.program_id(0)
    first = step * QB
    key_tiles = span // FWD_KB
    q = jnp.concatenate([q_ref[:, h * HD : (h + 1) * HD] for h in range(heads)], axis=0)
    tiles = jnp.minimum(pl.cdiv(first + QB, FWD_KB), pl.cdiv(length, FWD_KB))
    plain = jnp.minimum(first // FWD_KB, length // FWD_KB)

    def tile_of(ref, tile):
        stored = lax.rem(tile + half * (key_tiles // 2), key_tiles)
        return ref[pl.ds(pl.multiple_of(stored * FWD_KB, FWD_KB), FWD_KB), :]

    def fold(values, running, op):
        for t in range(FWD_KB // LANES):
            running = op(running, values[:, t * LANES : (t + 1) * LANES])
        return running

    def scores_of(tile):
        return contract(q, tile_of(k_ref, tile), 1, 1) * HD**-0.5

    def plain_scores(tile, top):
        scores = scores_of(tile)
        score_ref[tile] = scores
        return fold(scores, top, jnp.maximum)

    def masked_scores(tile, top):
        place = first + lax.broadcasted_iota(jnp.int32, (QB, FWD_KB), 0)
        key_place = tile * FWD_KB + lax.broadcasted_iota(jnp.int32, (QB, FWD_KB), 1)
        allowed = (key_place <= place) & (key_place < length)
        scores = scores_of(tile).reshape(heads, QB, FWD_KB)
        scores = jnp.where(allowed[None], scores, NEG_FILL).reshape(rows, FWD_KB)
        score_ref[tile] = scores
        return fold(scores, top, jnp.maximum)

    top = jnp.full((rows, LANES), NEG_FILL, F32)
    top = lax.fori_loop(0, plain, plain_scores, top)
    top = lax.fori_loop(plain, tiles, masked_scores, top)
    top = jnp.max(top, axis=1, keepdims=True)
    live = first + lax.broadcasted_iota(jnp.int32, (QB, 1), 0) < length
    peak = jnp.max(jnp.where(live[None], top.reshape(heads, QB, 1), NEG_FILL), axis=1)

    @pl.when(step == 0)
    def _():
        peak_ref[...] = jnp.full_like(peak_ref, NEG_FILL)

    peak_ref[...] = jnp.maximum(peak_ref[...], jnp.broadcast_to(peak, peak_ref.shape))
    sum_ref[...] = jnp.zeros_like(sum_ref)

    def weigh(tile, total):
        weights = jnp.exp(score_ref[tile] - top)
        sum_ref[...] += contract(weights.astype(BF), tile_of(v_ref, tile), 1, 0)
        return fold(weights, total, jnp.add)

    total = lax.fori_loop(0, tiles, weigh, jnp.zeros((rows, LANES), F32))
    total = jnp.sum(total, axis=1, keepdims=True)
    mixed = sum_ref[...] / total
    log_total = jnp.broadcast_to(top + jnp.log(total), (rows, LANES))
    lse_ref[0] = log_total.T[0:1, :]
    for h in range(heads):
        part = mixed[h * QB : (h + 1) * QB]
        mixed_ref[:, h * HD : (h + 1) * HD] = part.astype(BF)
        wide_ref[:, h * HD : (h + 1) * HD] = part


def attn_forward(info, q, k, v):
    span, width = q.shape
    heads = width // HD
    steps = span // QB

    def stored(i, info_ref):
        return (lax.rem(i + info_ref[1] * (steps // 2), steps), 0)

    whole = pl.BlockSpec((span, HD), lambda i, info_ref: (0, 0))
    pairs = heads * span * span // 2
    return pl.pallas_call(
        attn_forward_kernel,
        grid_spec=pltpu.PrefetchScalarGridSpec(
            num_scalar_prefetch=1,
            grid=(steps,),
            in_specs=[pl.BlockSpec((QB, width), stored), whole, whole],
            out_specs=[
                pl.BlockSpec((QB, width), stored),
                pl.BlockSpec((QB, width), stored),
                pl.BlockSpec((1, 1, heads * QB), lambda i, info_ref: (i, 0, 0)),
                pl.BlockSpec((heads, LANES), lambda i, info_ref: (0, 0)),
            ],
            scratch_shapes=[
                pltpu.VMEM((span // FWD_KB, heads * QB, FWD_KB), F32),
                pltpu.VMEM((heads * QB, HD), F32),
            ],
        ),
        out_shape=[
            jax.ShapeDtypeStruct((span, width), BF),
            jax.ShapeDtypeStruct((span, width), F32),
            jax.ShapeDtypeStruct((steps, 1, heads * QB), F32),
            jax.ShapeDtypeStruct((heads, LANES), F32),
        ],
        compiler_params=pltpu.CompilerParams(vmem_limit_bytes=40 * 2**20),
        cost_estimate=pl.CostEstimate(
            flops=40 * pairs * HD // 4, transcendentals=pairs, bytes_accessed=8 * span * width
        ),
        name="attn_forward",
    )(info, q, k, v)


def turn_back(values, cos_ref, sin_ref):
    half = HD // 2
    swapped = jnp.concatenate([values[:, half:], -values[:, :half]], axis=1)
    return values * cos_ref[...] + swapped * sin_ref[...]


def attn_backward_kernel(
    info_ref, q_ref, k_ref, v_ref, cot_ref, wide_ref, lse_ref, cosq_ref, sinq_ref, cosk_ref, sink_ref,
    dq_ref, dk_ref, dv_ref, dq_sum, dk_sum, dv_sum,
):
    heads = q_ref.shape[1] // HD
    span = k_ref.shape[0]
    rows = heads * QB
    length = info_ref[0]
    half = info_ref[1]
    step = pl.program_id(0)
    first = step * QB
    key_tiles = span // BWD_KB

    @pl.when(step == 0)
    def _():
        dk_sum[...] = jnp.zeros_like(dk_sum)
        dv_sum[...] = jnp.zeros_like(dv_sum)

    dq_sum[...] = jnp.zeros_like(dq_sum)

    @pl.when(first < length)
    def _():
        pieces = [slice(h * HD, (h + 1) * HD) for h in range(heads)]
        q = jnp.concatenate([q_ref[:, s] for s in pieces], axis=0)
        cot = jnp.concatenate([cot_ref[:, s] for s in pieces], axis=0)
        wide = jnp.concatenate([wide_ref[:, s] for s in pieces], axis=0)
        log_total = lse_ref[0]
        inner = jnp.sum(wide * cot.astype(F32), axis=1, keepdims=True)
        inner = jnp.broadcast_to(inner, (rows, LANES)).T[0:1, :]

        def tile_step(tile, masked):
            stored = lax.rem(tile + half * (key_tiles // 2), key_tiles)
            keys = pl.ds(pl.multiple_of(stored * BWD_KB, BWD_KB), BWD_KB)
            k_tile = k_ref[keys, :]
            v_tile = v_ref[keys, :]
            scores = contract(k_tile, q, 1, 1) * HD**-0.5 - log_total
            if masked:
                key_place = tile * BWD_KB + lax.broadcasted_iota(jnp.int32, (BWD_KB, rows), 0)
                place = first + lax.rem(lax.broadcasted_iota(jnp.int32, (BWD_KB, rows), 1), QB)
                scores = jnp.where((key_place <= place) & (key_place < length), scores, NEG_FILL)
            weights = jnp.exp(scores)
            prob_cot = contract(v_tile, cot, 1, 1)
            score_cot = (weights * (prob_cot - inner)).astype(BF)
            dv_sum[keys, :] += contract(weights.astype(BF), cot, 1, 0)
            dk_sum[keys, :] += contract(score_cot, q, 1, 0) * HD**-0.5
            dq_sum[...] += contract(score_cot, k_tile, 0, 0) * HD**-0.5

        @pl.loop(0, first // BWD_KB)
        def _(tile):
            tile_step(tile, False)

        @pl.loop(first // BWD_KB, pl.cdiv(first + QB, BWD_KB))
        def _(tile):
            tile_step(tile, True)

    for h in range(heads):
        part = turn_back(dq_sum[h * QB : (h + 1) * QB, :], cosq_ref, sinq_ref)
        dq_ref[:, h * HD : (h + 1) * HD] = part.astype(dq_ref.dtype)

    @pl.when(step == pl.num_programs(0) - 1)
    def _():
        dk_ref[...] = turn_back(dk_sum[...], cosk_ref, sink_ref).astype(dk_ref.dtype)
        dv_ref[...] = dv_sum[...].astype(dv_ref.dtype)


def attn_backward(info, q, k, v, cot, wide, lse, cos, sin, kv_type):
    span, width = q.shape
    heads = width // HD
    steps = span // QB

    def stored(i, info_ref):
        return (lax.rem(i + info_ref[1] * (steps // 2), steps), 0)

    whole = pl.BlockSpec((span, HD), lambda i, info_ref: (0, 0))
    mine = pl.BlockSpec((QB, width), stored)
    turn = pl.BlockSpec((QB, HD), stored)
    pairs = heads * span * span // 2
    return pl.pallas_call(
        attn_backward_kernel,
        grid_spec=pltpu.PrefetchScalarGridSpec(
            num_scalar_prefetch=1,
            grid=(steps,),
            in_specs=[
                mine, whole, whole, mine, mine,
                pl.BlockSpec((1, 1, heads * QB), lambda i, info_ref: (i, 0, 0)),
                turn, turn, whole, whole,
            ],
            out_specs=[mine, whole, whole],
            scratch_shapes=[
                pltpu.VMEM((heads * QB, HD), F32),
                pltpu.VMEM((span, HD), F32),
                pltpu.VMEM((span, HD), F32),
            ],
        ),
        out_shape=[
            jax.ShapeDtypeStruct((span, width), BF),
            jax.ShapeDtypeStruct((span, HD), kv_type),
            jax.ShapeDtypeStruct((span, HD), kv_type),
        ],
        compiler_params=pltpu.CompilerParams(vmem_limit_bytes=40 * 2**20),
        cost_estimate=pl.CostEstimate(
            flops=60 * pairs * HD // 4, transcendentals=pairs, bytes_accessed=12 * span * width
        ),
        name="attn_backward",
    )(info, q, k, v, cot, wide, lse, cos, sin, cos, sin)


def on_device(
    tokens, lengths, attn_gain, w_query, w_key, w_value, w_out, mlp_gain, w_gate, w_up, w_down, cotangent
):
    row_devices = lax.axis_size("row")
    col_devices = lax.axis_size("col")
    row = lax.axis_index("row")
    col = lax.axis_index("col")
    tok, width = tokens.shape
    span = tok * row_devices
    group = HQ // KV
    heads_row = HQ // row_devices
    heads = heads_row // col_devices
    head_width = heads * HD
    keyval_row = KV // row_devices
    units = w_gate.shape[1] // col_devices
    steps = range(1, col_devices)
    length = lengths[0]
    info = jnp.stack([length, row]).astype(jnp.int32)

    place = lax.rem(jnp.arange(span, dtype=jnp.int32) + row * tok, span)
    frequency = ROPE_BASE ** (-jnp.arange(HD // 2, dtype=F32) * (2.0 / HD))
    angle = place.astype(F32)[:, None] * frequency[None, :]
    cos = jnp.tile(jnp.cos(angle), (1, 2))
    sin = jnp.tile(jnp.sin(angle), (1, 2))

    tokens_full = gather_rows(gather_cols(tokens))

    def head_weights(owner):
        key_head = owner * heads // group
        return jnp.concatenate(
            [
                lax.dynamic_slice_in_dim(w_query, owner * head_width, head_width, 1),
                lax.dynamic_slice_in_dim(w_key, key_head * HD, HD, 1),
                lax.dynamic_slice_in_dim(w_value, key_head * HD, HD, 1),
            ],
            axis=1,
        )

    w_heads = jnp.concatenate(
        [head_weights(col)] + [swap(head_weights(col ^ s), "col", s) for s in steps], axis=0
    )
    gains = gather_cols(jnp.stack([attn_gain, mlp_gain]))
    gain_a, gain_m = gains[0], gains[1]
    turned = w_heads[:, : head_width + HD].reshape(D, heads + 1, 2, HD // 2)
    turned = jnp.concatenate([-turned[:, :, 1], turned[:, :, 0]], axis=2)
    turned = turned.reshape(D, head_width + HD)

    resid_in = tokens_full.astype(F32)
    scale_a = lax.rsqrt(jnp.mean(resid_in * resid_in, axis=1) + EPSILON)
    normed_attn = (resid_in * scale_a[:, None] * gain_a).astype(BF)
    raw = jnp.dot(normed_attn, w_heads, preferred_element_type=F32)
    raw_turned = jnp.dot(normed_attn, turned, preferred_element_type=F32)
    rotated = (
        raw[:, : head_width + HD] * jnp.tile(cos, (1, heads + 1))
        + raw_turned * jnp.tile(sin, (1, heads + 1))
    ).astype(BF)
    query = rotated[:, :head_width]
    key = rotated[:, head_width:]
    value = raw[:, head_width + HD :].astype(BF)

    mixed, mixed_wide, log_total, peak = attn_forward(info, query, key, value)

    mixed_row = gather_cols(mixed)
    mixed_other = swap(mixed_row, "row", 1)
    mixed_other = jnp.concatenate([mixed_other[tok:], mixed_other[:tok]], axis=0)
    mixed_full = jnp.concatenate([mixed_row, mixed_other], axis=1)
    w_out_row = gather_cols(w_out)
    w_out_row = jnp.concatenate(
        [
            lax.dynamic_slice_in_dim(w_out_row, (col ^ s) * head_width, head_width, 0)
            for s in range(col_devices)
        ],
        axis=0,
    )
    w_out_full = gather_rows(w_out_row)
    resid_mid = resid_in + jnp.dot(mixed_full, w_out_full, preferred_element_type=F32)
    scale_m = lax.rsqrt(jnp.mean(resid_mid * resid_mid, axis=1) + EPSILON)
    normed_mlp = (resid_mid * scale_m[:, None] * gain_m).astype(BF)

    def unit_columns(weight):
        return jnp.concatenate(
            [
                swap(lax.dynamic_slice_in_dim(weight, (col ^ s) * units, units, 1), "col", s)
                if s
                else lax.dynamic_slice_in_dim(weight, col * units, units, 1)
                for s in range(col_devices)
            ],
            axis=0,
        )

    w_gate_units = unit_columns(w_gate)
    w_up_units = unit_columns(w_up)
    w_down_units = jnp.concatenate(
        [
            swap(lax.dynamic_slice_in_dim(w_down, (col ^ s) * units, units, 0), "col", s)
            if s
            else lax.dynamic_slice_in_dim(w_down, col * units, units, 0)
            for s in range(col_devices)
        ],
        axis=1,
    )
    gate = jnp.dot(normed_mlp, w_gate_units, preferred_element_type=F32)
    up = jnp.dot(normed_mlp, w_up_units, preferred_element_type=F32)
    gate_sigmoid = jax.nn.sigmoid(gate)
    hidden = (gate * gate_sigmoid * up).astype(BF)
    down_part = jnp.dot(hidden, w_down_units, preferred_element_type=F32)
    output = (resid_mid[:tok, :width] + reduce_tokens(down_part, width)).astype(BF)

    valid = (row * tok + jnp.arange(tok, dtype=jnp.int32) < length).astype(BF)
    out_low = gather_rows(gather_cols(cotangent * valid[:, None]))
    grad_down = contract(hidden, out_low, 0, 0)
    hidden_cot = contract(out_low, w_down_units, 1, 1)
    gate_cot = (
        hidden_cot * up * gate_sigmoid * (1.0 + gate * (1.0 - gate_sigmoid))
    ).astype(BF)
    up_cot = (hidden_cot * gate * gate_sigmoid).astype(BF)
    grad_gate = contract(normed_mlp, gate_cot, 0, 0)
    grad_up = contract(normed_mlp, up_cot, 0, 0)
    mlp_part = contract(gate_cot, w_gate_units, 1, 1) + contract(up_cot, w_up_units, 1, 1)
    mlp_cot = reduce_tokens(mlp_part, width).astype(BF)
    mlp_cot = gather_rows(gather_cols(mlp_cot)).astype(F32)
    width_dot_m = jnp.sum(mlp_cot * gain_m * resid_mid, axis=1)
    mid_cot = (
        out_low.astype(F32)
        + mlp_cot * gain_m * scale_m[:, None]
        - resid_mid * (scale_m**3 * width_dot_m / D)[:, None]
    )
    mid_low = mid_cot.astype(BF)
    gain_m_part = jnp.sum(
        mlp_cot[:tok, :width] * resid_mid[:tok, :width] * scale_m[:tok, None], axis=0
    )

    grad_out = contract(mixed, mid_low, 0, 0)
    mixed_cot = contract(mid_low, w_out_full[:head_width], 1, 1).astype(BF)
    shared_key = heads < group
    query_cot, key_cot, value_cot = attn_backward(
        info, query, key, value, mixed_cot, mixed_wide, log_total, cos, sin, F32 if shared_key else BF
    )
    if shared_key:
        sharers = group // heads
        for bit in range(sharers.bit_length() - 1):
            key_cot = key_cot + swap(key_cot, "col", 1 << bit)
            value_cot = value_cot + swap(value_cot, "col", 1 << bit)
        key_cot, value_cot = key_cot.astype(BF), value_cot.astype(BF)
    heads_cot = jnp.concatenate([query_cot, key_cot, value_cot], axis=1)
    grad_heads = contract(normed_attn, heads_cot, 0, 0)
    if shared_key:
        own_part = [head_width, HD, HD]
        leader = (col % sharers == 0).astype(BF)
        alone = jnp.concatenate([query_cot, key_cot * leader, value_cot * leader], axis=1)
    else:
        alone = heads_cot
    attn_part = contract(alone, w_heads, 1, 1)
    dot_part = jnp.sum(attn_part * gain_a * resid_in, axis=1)
    width_dot_a = dot_part[:tok] + swap(dot_part[tok:], "row", 1)
    step = 1
    while step < col_devices:
        width_dot_a = width_dot_a + swap(width_dot_a, "col", step)
        step *= 2
    attn_cot = reduce_tokens(attn_part, width)
    own_in = resid_in[:tok, :width]
    input_grad = (
        mid_cot[:tok, :width]
        + attn_cot * attn_gain * scale_a[:tok, None]
        - own_in * (scale_a[:tok] ** 3 * width_dot_a / D)[:, None]
    )
    gain_a_part = jnp.sum(attn_cot * own_in * scale_a[:tok, None], axis=0)

    gain_sums = jnp.stack([gain_a_part, gain_m_part])
    gain_sums = gain_sums + swap(gain_sums, "row", 1)
    step = 1
    while step < lax.axis_size("dp"):
        gain_sums = gain_sums + swap(gain_sums, "dp", step)
        step *= 2
    step = 1
    while step < lax.axis_size("dp"):
        peak = jnp.maximum(peak, swap(peak, "dp", step))
        step *= 2
    own_peaks = peak[:, 0]
    slots = jnp.arange(col_devices)[:, None]
    row_peaks = jnp.where(slots == col, own_peaks[None, :], NEG_FILL)
    step = 1
    while step < col_devices:
        row_peaks = jnp.maximum(row_peaks, swap(row_peaks, "col", step))
        step *= 2
    row_peaks = row_peaks.reshape(heads_row)
    clip_factor = CLIP_LEVEL / jnp.maximum(row_peaks, CLIP_LEVEL)
    query_scale = jnp.repeat(jnp.sqrt(clip_factor), HD)
    key_scale = jnp.repeat(jnp.sqrt(jnp.min(clip_factor.reshape(keyval_row, group), axis=1)), HD)
    clipped_query = (w_query.astype(F32) * query_scale[None, :]).astype(BF)
    clipped_key = (w_key.astype(F32) * key_scale[None, :]).astype(BF)

    def own_blocks(grad, dim):
        blocks = []
        for s in range(col_devices):
            block = lax.slice_in_dim(grad, s * width, (s + 1) * width, axis=dim).astype(BF)
            block = group_sum(block)
            blocks.append(swap(block, "col", s) if s else block)
        return blocks

    def placed(blocks, dim, sizes):
        shape = list(blocks[0].shape)
        shape[dim] = sizes * col_devices
        out = jnp.zeros(shape, F32)
        for s, block in enumerate(blocks):
            out = lax.dynamic_update_slice_in_dim(out, block.astype(F32), (col ^ s) * sizes, dim)
        return out

    out_down = placed(own_blocks(grad_down, 1), 0, units)
    out_gate = placed(own_blocks(grad_gate, 0), 1, units)
    out_up = placed(own_blocks(grad_up, 0), 1, units)
    out_out = placed(own_blocks(grad_out, 1), 0, head_width)
    head_blocks = own_blocks(grad_heads, 0)
    out_query = placed([b[:, :head_width] for b in head_blocks], 1, head_width)
    out_key = jnp.zeros(w_key.shape, F32)
    out_value = jnp.zeros(w_value.shape, F32)
    for s, block in enumerate(head_blocks):
        start = ((col ^ s) * heads // group) * HD
        out_key = lax.dynamic_update_slice_in_dim(
            out_key, block[:, head_width : head_width + HD].astype(F32), start, 1
        )
        out_value = lax.dynamic_update_slice_in_dim(
            out_value, block[:, head_width + HD :].astype(F32), start, 1
        )
    return (
        output,
        input_grad,
        gain_sums[0],
        out_query,
        out_key,
        out_value,
        out_out,
        gain_sums[1],
        out_gate,
        out_up,
        out_down,
        own_peaks,
        clipped_query,
        clipped_key,
    )


def solution(mesh):
    in_specs = (
        P(("dp", "row"), "col"),
        P("dp"),
        P("col"),
        P("col", "row"),
        P("col", "row"),
        P("col", "row"),
        P("row", "col"),
        P("col"),
        P("col", "row"),
        P("col", "row"),
        P("row", "col"),
        P(("dp", "row"), "col"),
    )
    out_specs = (
        P(("dp", "row"), "col"),
        P(("dp", "row"), "col"),
        P("col"),
        P("col", "row"),
        P("col", "row"),
        P("col", "row"),
        P("row", "col"),
        P("col"),
        P("col", "row"),
        P("col", "row"),
        P("row", "col"),
        P(("row", "col")),
        P("col", "row"),
        P("col", "row"),
    )
    return jax.shard_map(
        on_device, mesh=mesh, in_specs=in_specs, out_specs=out_specs, check_vma=False
    )
```

```python
import functools

import jax
import jax.numpy as jnp
from jax import lax
from jax.experimental import pallas as pl
from jax.experimental.pallas import tpu as pltpu
from jax.sharding import PartitionSpec as P

D = 2048
HQ = 32
KV = 8
HD = 64
SEQ_LEN = 2048

EPSILON = 1e-05
NEG_FILL = -1e30
CLIP_LEVEL = 5.0
ROPE_BASE = 500000.0

BF = jnp.bfloat16
F32 = jnp.float32
LANES = 128
QB = 512
FWD_KB = 512
BWD_KB = 512
MESH = pl.DeviceIdType.MESH
ANY = pl.BlockSpec(memory_space=pl.ANY)
NCH = 4
CR, CC = 256, 512
HR = CR // 2
OFFS = (0, 2, 4, 6)
MIB = 2**20


def contract(left, right, left_dim, right_dim):
    return lax.dot_general(
        left, right, (((left_dim,), (right_dim,)), ((), ())), preferred_element_type=F32
    )


def swap(values, axis, step):
    count = lax.axis_size(axis)
    return lax.ppermute(values, axis, [(i, i ^ step) for i in range(count)])


def flip(index, bit):
    return index + bit - 2 * bit * lax.rem(index // bit, 2)

def remote(src, dst, send, recv, **where):
    return pltpu.make_async_remote_copy(src_ref=src, dst_ref=dst, send_sem=send, recv_sem=recv, device_id=where, device_id_type=MESH)

def greet(targets):
    barrier = pltpu.get_barrier_semaphore()
    for t in targets:
        pl.semaphore_signal(barrier, inc=1, device_id=t, device_id_type=MESH)
    pl.semaphore_wait(barrier, len(targets))

NCH = 4

def plane_peers():
    row = lax.axis_index("row"); col = lax.axis_index("col")
    return {"col": flip(col, 1)}, {"col": flip(col, 2)}, {"row": 1 - row}

def gather_body(src, out, place, sems, near_x, near_y, mate):
    col = lax.axis_index("col")
    at_x, at_y = near_x["col"], near_y["col"]
    own_send, relay_send, mate_send, recv, mate_recv = sems
    half = NCH // 2
    copies = []
    order_x = list(range(NCH)); order_y = order_x[half:] + order_x[:half]
    for jx, jy in zip(order_x, order_y):
        cx = remote(src(jx), place(out, 0, 1, jx, at_x), own_send.at[0, jx], recv.at[0, jx], **near_x)
        cy = remote(src(jy), place(out, 0, 2, jy, at_y), own_send.at[1, jy], recv.at[1, jy], **near_y)
        cx.start(); cy.start(); copies += [cx, cy]
    for j in range(NCH):
        cm = remote(src(j), place(out, 1, 0, j, col), mate_send.at[0, j], mate_recv.at[0, j], **mate)
        cm.start(); copies.append(cm)
    def arrived(s, j):
        pltpu.make_async_copy(place(out, 0, s, j, col), place(out, 0, s, j, col), recv.at[s - 1, j]).wait()
    def to_mate(s, j):
        cm = remote(place(out, 0, s, j, col), place(out, 1, s, j, col), mate_send.at[s, j], mate_recv.at[s, j], **mate)
        cm.start(); copies.append(cm)
    for i in range(NCH):
        jx, jy = order_x[i], order_y[i]
        arrived(1, jx)
        if jx < half:
            c = remote(place(out, 0, 1, jx, col), place(out, 0, 3, jx, at_y), relay_send.at[jx], recv.at[2, jx], **near_y)
            c.start(); copies.append(c)
        to_mate(1, jx)
        arrived(2, jy)
        if jy >= half:
            c = remote(place(out, 0, 2, jy, col), place(out, 0, 3, jy, at_x), relay_send.at[jy], recv.at[2, jy], **near_x)
            c.start(); copies.append(c)
        to_mate(2, jy)
    for i in range(half):
        for j in (i, half + i):
            arrived(3, j); to_mate(3, j)
    return copies

def gather_finish(out, place, copies, mate_recv):
    col = lax.axis_index("col")
    for s in range(4):
        for j in range(NCH):
            pltpu.make_async_copy(place(out, 1, s, j, col), place(out, 1, s, j, col), mate_recv.at[s, j]).wait()
    for c in copies:
        c.wait_send()

GATHER_SEMS = lambda: [pltpu.SemaphoreType.DMA((2, NCH)), pltpu.SemaphoreType.DMA((NCH,)), pltpu.SemaphoreType.DMA((4, NCH)),
                 pltpu.SemaphoreType.DMA((3, NCH)), pltpu.SemaphoreType.DMA((4, NCH))]

def gather_tokens_kernel(x_ref, out_ref, stage, stage_sem, *sems):
    near_x, near_y, mate = plane_peers()
    tok, width = x_ref.shape
    rows = tok // NCH
    def place(out, half, s, j, who):
        return out.at[pl.ds(half * tok + j * rows, rows), pl.ds(s * width, width)]
    load = pltpu.make_async_copy(x_ref, stage, stage_sem.at[0]); load.start()
    greet([near_x, near_y, mate])
    copies = gather_body(lambda j: x_ref.at[pl.ds(j * rows, rows), :], out_ref, place, sems, near_x, near_y, mate)
    load.wait()
    keep = pltpu.make_async_copy(stage, out_ref.at[pl.ds(0, tok), pl.ds(0, width)], stage_sem.at[1]); keep.start()
    gather_finish(out_ref, place, copies, sems[4])
    keep.wait()

def gather_tokens(x, cid):
    tok, width = x.shape
    return pl.pallas_call(gather_tokens_kernel, in_specs=[ANY], out_specs=ANY,
        out_shape=jax.ShapeDtypeStruct((2 * tok, 4 * width), x.dtype),
        scratch_shapes=[pltpu.VMEM((tok, width), x.dtype), pltpu.SemaphoreType.DMA((2,))] + GATHER_SEMS(),
        compiler_params=pltpu.CompilerParams(collective_id=cid, has_side_effects=True),
        name="gather_tokens")(x)

def gather_heads_kernel(x_ref, out_ref, stage, stage_sem, *sems):
    near_x, near_y, mate = plane_peers()
    span, width = x_ref.shape
    rows = span // NCH
    def place(out, half, s, j, who):
        start = j * rows if half == 0 else ((j + NCH // 2) % NCH) * rows
        return out.at[pl.ds(start, rows), pl.ds(pl.multiple_of((half * 4 + xor(who, s)) * width, LANES), width)]
    load = pltpu.make_async_copy(x_ref, stage, stage_sem.at[0]); load.start()
    greet([near_x, near_y, mate])
    copies = gather_body(lambda j: x_ref.at[pl.ds(j * rows, rows), :], out_ref, place, sems, near_x, near_y, mate)
    load.wait()
    keep = pltpu.make_async_copy(stage, out_ref.at[:, pl.ds(pl.multiple_of(lax.axis_index("col") * width, LANES), width)], stage_sem.at[1]); keep.start()
    gather_finish(out_ref, place, copies, sems[4])
    keep.wait()

def gather_heads(x, cid):
    span, width = x.shape
    return pl.pallas_call(gather_heads_kernel, in_specs=[ANY], out_specs=ANY,
        out_shape=jax.ShapeDtypeStruct((span, 8 * width), x.dtype),
        scratch_shapes=[pltpu.VMEM((span, width), x.dtype), pltpu.SemaphoreType.DMA((2,))] + GATHER_SEMS(),
        compiler_params=pltpu.CompilerParams(collective_id=cid, has_side_effects=True),
        name="gather_heads")(x)

def reduce_steps(part_ref, own, given, sent, got_one, got_two, sems, near_x, near_y, mate, emit):
    load, mate_send, mate_recv, one_send, one_recv, two_send, two_recv = sems
    tok, full = own.shape
    width = full // 4
    h = tok // 2
    rows = [pl.ds(0, h), pl.ds(h, h)]
    other = [pl.ds(tok, h), pl.ds(tok + h, h)]
    copies = []
    for a in range(2):
        c = remote(part_ref.at[other[a], :], given.at[rows[a], :], mate_send.at[a], mate_recv.at[a], **mate)
        c.start(); copies.append(c)
        l = pltpu.make_async_copy(part_ref.at[rows[a], :], own.at[rows[a], :], load.at[a]); l.start()
    first = [near_x, near_y]; second = [near_y, near_x]
    goes = [1, 2];
    for a in range(2):
        pltpu.make_async_copy(part_ref.at[rows[a], :], own.at[rows[a], :], load.at[a]).wait()
        pltpu.make_async_copy(given.at[rows[a], :], given.at[rows[a], :], mate_recv.at[a]).wait()
        for i, s in enumerate((goes[a], 3)):
            cols = pl.ds(s * width, width)
            sent[a, i] = (own[rows[a], cols].astype(F32) + given[rows[a], cols].astype(F32)).astype(BF)
        c = remote(sent.at[a, pl.ds(0, 2)], got_one.at[a], one_send.at[a], one_recv.at[a], **first[a])
        c.start(); copies.append(c)
    for a in range(2):
        pltpu.make_async_copy(got_one.at[a], got_one.at[a], one_recv.at[a]).wait()
        s = 3 - goes[a]
        cols = pl.ds(s * width, width)
        sent[a, 2] = (own[rows[a], cols].astype(F32) + given[rows[a], cols].astype(F32) + got_one[a, 1].astype(F32)).astype(BF)
        c = remote(sent.at[a, 2], got_two.at[a], two_send.at[a], two_recv.at[a], **second[a])
        c.start(); copies.append(c)
    for a in range(2):
        cols = pl.ds(0, width)
        total = own[rows[a], cols].astype(F32) + given[rows[a], cols].astype(F32) + got_one[a, 0].astype(F32)
        pltpu.make_async_copy(got_two.at[a], got_two.at[a], two_recv.at[a]).wait()
        emit(a, total + got_two[a].astype(F32))
    return copies

def REDUCE_SCRATCH(tok, full):
    w = full // 4; h = tok // 2
    return [pltpu.VMEM((tok, full), BF), pltpu.VMEM((tok, full), BF), pltpu.VMEM((2, 3, h, w), BF), pltpu.VMEM((2, 2, h, w), BF), pltpu.VMEM((2, h, w), BF)]
REDUCE_SEMS = lambda: [pltpu.SemaphoreType.DMA((2,))] * 7

def reduce_kernel(part_ref, out_ref, own, given, sent, got_one, got_two, *sems):
    near_x, near_y, mate = plane_peers()
    greet([near_x, near_y, mate])
    h = own.shape[0] // 2
    def emit(a, v): out_ref[pl.ds(a * h, h), :] = v.astype(out_ref.dtype)
    copies = reduce_steps(part_ref, own, given, sent, got_one, got_two, sems, near_x, near_y, mate, emit)
    for c in copies: c.wait_send()

def reduce_scatter(part, cid, dtype=F32):
    span, full = part.shape; tok = span // 2; w = full // 4
    return pl.pallas_call(reduce_kernel, in_specs=[ANY], out_specs=pl.BlockSpec(memory_space=pltpu.VMEM),
        out_shape=jax.ShapeDtypeStruct((tok, w), dtype),
        scratch_shapes=REDUCE_SCRATCH(tok, full) + REDUCE_SEMS(),
        compiler_params=pltpu.CompilerParams(collective_id=cid, has_side_effects=True, vmem_limit_bytes=40*2**20),
        name="reduce_scatter")(part)

def all_reduce_kernel(part_ref, out_ref, own, given, sent, got_one, got_two, mine, keep_sem, *sems):
    near_x, near_y, mate = plane_peers()
    greet([near_x, near_y, mate])
    tok, width = mine.shape; h = tok // 2
    def emit(a, v): mine[pl.ds(a * h, h), :] = v.astype(BF)
    copies = reduce_steps(part_ref, own, given, sent, got_one, got_two, sems[:7], near_x, near_y, mate, emit)
    rows = tok // NCH
    def place(out, half, s, j, who):
        return out.at[pl.ds(half * tok + j * rows, rows), pl.ds(s * width, width)]
    keep = pltpu.make_async_copy(mine, out_ref.at[pl.ds(0, tok), pl.ds(0, width)], keep_sem.at[0]); keep.start()
    more = gather_body(lambda j: mine.at[pl.ds(j * rows, rows), :], out_ref, place, sems[7:], near_x, near_y, mate)
    gather_finish(out_ref, place, more, sems[11])
    keep.wait()
    for c in copies: c.wait_send()

def all_reduce(part, cid):
    span, full = part.shape; tok = span // 2; w = full // 4
    return pl.pallas_call(all_reduce_kernel, in_specs=[ANY], out_specs=ANY,
        out_shape=jax.ShapeDtypeStruct((span, full), BF),
        scratch_shapes=REDUCE_SCRATCH(tok, full) + [pltpu.VMEM((tok, w), BF), pltpu.SemaphoreType.DMA((1,))] + REDUCE_SEMS() + GATHER_SEMS(),
        compiler_params=pltpu.CompilerParams(collective_id=cid, has_side_effects=True, vmem_limit_bytes=40*2**20),
        name="all_reduce")(part)


def first_gather_kernel(
    x_ref, wq_ref, wkv_ref, gain_ref, out_ref, wq_out, wkv_out, gain_out,
    stage, wq_stage, wkv_stage, gain_stage, stage_sem, small_send, small_recv, *sems,
):
    near_x, near_y, mate = plane_peers()
    col = lax.axis_index("col")
    tok, width = x_ref.shape
    rows = tok // NCH
    wide = wq_ref.shape[1] // 4
    thin = wkv_ref.shape[1] // 4

    def place(out, half, s, j, who):
        return out.at[pl.ds(half * tok + j * rows, rows), pl.ds(s * width, width)]

    def share(ref, owner, size):
        return ref.at[:, pl.ds(pl.multiple_of(owner * size, LANES), size)]

    loads = [
        pltpu.make_async_copy(x_ref, stage, stage_sem.at[0]),
        pltpu.make_async_copy(share(wq_ref, col, wide), wq_stage, stage_sem.at[1]),
        pltpu.make_async_copy(share(wkv_ref, col, thin), wkv_stage, stage_sem.at[2]),
        pltpu.make_async_copy(gain_ref, gain_stage, stage_sem.at[3]),
    ]
    for c in loads:
        c.start()
    greet([near_x, near_y, {"col": 3 - col}, mate])
    smalls = []
    for s, peer in ((1, near_x), (2, near_y), (3, {"col": 3 - col})):
        owner = peer["col"]
        lines = pl.ds(s * width, width)
        smalls += [
            remote(share(wq_ref, owner, wide), wq_out.at[lines, :], small_send.at[0, s], small_recv.at[0, s], **peer),
            remote(share(wkv_ref, owner, thin), wkv_out.at[lines, :], small_send.at[1, s], small_recv.at[1, s], **peer),
            remote(gain_ref, gain_out.at[:, lines], small_send.at[2, s], small_recv.at[2, s], **peer),
        ]
    for c in smalls:
        c.start()
    copies = gather_body(
        lambda j: x_ref.at[pl.ds(j * rows, rows), :], out_ref, place, sems, near_x, near_y, mate
    )
    lines = pl.ds(0, width)
    keeps = [
        pltpu.make_async_copy(stage, out_ref.at[pl.ds(0, tok), lines], stage_sem.at[4]),
        pltpu.make_async_copy(wq_stage, wq_out.at[lines, :], stage_sem.at[5]),
        pltpu.make_async_copy(wkv_stage, wkv_out.at[lines, :], stage_sem.at[6]),
        pltpu.make_async_copy(gain_stage, gain_out.at[:, lines], stage_sem.at[7]),
    ]
    for load, keep in zip(loads, keeps):
        load.wait()
        keep.start()
    gather_finish(out_ref, place, copies, sems[4])
    for c in smalls:
        c.wait()
    for c in keeps:
        c.wait()


def first_gather(x, wq, wkv, gains, cid):
    tok, width = x.shape
    wide, thin = wq.shape[1] // 4, wkv.shape[1] // 4
    return pl.pallas_call(
        first_gather_kernel,
        in_specs=[ANY] * 4,
        out_specs=[ANY] * 4,
        out_shape=[
            jax.ShapeDtypeStruct((2 * tok, 4 * width), BF),
            jax.ShapeDtypeStruct((4 * width, wide), BF),
            jax.ShapeDtypeStruct((4 * width, thin), BF),
            jax.ShapeDtypeStruct((8, 4 * width), F32),
        ],
        scratch_shapes=[
            pltpu.VMEM((tok, width), BF),
            pltpu.VMEM((width, wide), BF),
            pltpu.VMEM((width, thin), BF),
            pltpu.VMEM((8, width), F32),
            pltpu.SemaphoreType.DMA((8,)),
            pltpu.SemaphoreType.DMA((3, 4)),
            pltpu.SemaphoreType.DMA((3, 4)),
        ]
        + GATHER_SEMS(),
        compiler_params=pltpu.CompilerParams(collective_id=cid, has_side_effects=True),
        name="first_gather",
    )(x, wq, wkv, gains)


def grad_plan(kind, shape):
    rows, cols = shape
    if kind == "columns":
        w = rows // 4
        across = cols // CC
        return (w // CR) * across, (lambda s, k: (s * w + (k // across) * CR, (k % across) * CC)), (w, 4 * cols), (
            lambda c, k: ((k // across) * CR, c * cols + (k % across) * CC))
    if kind == "rows":
        w = cols // 4
        return rows // CR, (lambda s, k: (k * CR, s * w)), (4 * rows, w), (lambda c, k: (c * rows + k * CR, 0))
    w = rows // 4
    return w // CR, (lambda s, k: (s * w + k * CR, 0)), (rows, cols), (lambda c, k: (c * w + k * CR, 0))

def group_sum_kernel(kinds, n_in, *refs):
    ins = refs[:n_in]; outs = refs[n_in:2 * n_in]
    (own, land, mids, tops, load, in_send, in_recv, mid_send, mid_recv, top_send, top_recv, out_send, out_recv,
     far_send, far_recv, near) = refs[2 * n_in:]
    plans = [grad_plan(k, r.shape) for k, r in zip(kinds, ins)]
    counts = [4 * p[0] for p in plans]
    begins = [sum(counts[:i]) for i in range(n_in)]
    total = sum(counts)
    z = lax.axis_index("dp"); col = lax.axis_index("col")
    is_mid = (z == 1) | (z == 2)
    is_left = z < 2
    inward = {"dp": jnp.where(is_left, z + 1, z - 1)}
    outward = {"dp": jnp.where(is_left, z - 1, z + 1)}
    kept = jnp.where(is_left, 0, 1)
    for m in range(n_in):
        per, where_in = plans[m][0], plans[m][1]
        def start_load(j, c, m=m, per=per, where_in=where_in):
            r, q = where_in(j // per, lax.rem(j, per))
            pltpu.make_async_copy(ins[m].at[pl.ds(pl.multiple_of(r, CR), CR), pl.ds(pl.multiple_of(q, CC), CC)],
                                  own.at[begins[m] + j], load.at[begins[m] + j]).start()
            return c
        lax.fori_loop(0, counts[m], start_load, 0)
    barrier = pltpu.get_barrier_semaphore()
    pl.semaphore_signal(barrier, inc=1, device_id=inward, device_id_type=MESH)
    @pl.when(is_mid)
    def _():
        pl.semaphore_signal(barrier, inc=1, device_id=outward, device_id_type=MESH)
    for s in range(1, 4):
        pl.semaphore_signal(barrier, inc=1, device_id={"col": xor(col, s)}, device_id_type=MESH)
    @pl.when(is_mid)
    def _():
        pl.semaphore_wait(barrier, 5)
    @pl.when(jnp.logical_not(is_mid))
    def _():
        pl.semaphore_wait(barrier, 4)

    def done(ref, sem):
        pltpu.make_async_copy(ref, ref, sem).wait()

    def spread(j, half, src):
        for m in range(n_in):
            per, _, _, where_out = plans[m]
            @pl.when((j >= begins[m]) & (j < begins[m] + counts[m]))
            def _(m=m, per=per, where_out=where_out):
                i = j - begins[m]
                s = i // per
                r, q = where_out(col, lax.rem(i, per))
                dst = outs[m].at[pl.ds(pl.multiple_of(r + half * HR, HR), HR), pl.ds(pl.multiple_of(q, CC), CC)]
                @pl.when(s == 0)
                def _():
                    pltpu.make_async_copy(src, dst, near.at[m]).start()
                @pl.when(s > 0)
                def _():
                    owner = lax.rem(lax.rem(col, 2) + lax.rem(s, 2), 2) + 2 * lax.rem(col // 2 + s // 2, 2)
                    remote(src, dst, far_send.at[m], far_recv.at[m], col=owner).start()

    def inbound(j):
        pltpu.make_async_copy(own.at[j], own.at[j], load.at[j]).wait()
        @pl.when(is_mid)
        def _():
            done(land.at[j], in_recv.at[j])
            own[j] = (own[j].astype(F32) + land[j].astype(F32)).astype(BF)
            remote(own.at[j, pl.ds((1 - kept) * HR, HR)], mids.at[j], mid_send.at[j], mid_recv.at[j], **inward).start()
        @pl.when(jnp.logical_not(is_mid))
        def _():
            remote(own.at[j], land.at[j], in_send.at[j], in_recv.at[j], **inward).start()

    def middle(j):
        @pl.when(is_mid)
        def _():
            done(mids.at[j], mid_recv.at[j])
            rows = pl.ds(pl.multiple_of(kept * HR, HR), HR)
            own[j, rows] = (own[j, rows].astype(F32) + mids[j].astype(F32)).astype(BF)
            remote(own.at[j, rows], tops.at[j], top_send.at[j], top_recv.at[j], **inward).start()
            remote(own.at[j, rows], land.at[j, rows], out_send.at[j, kept], out_recv.at[j, kept], **outward).start()
            spread(j, kept, own.at[j, rows])

    def finish(j):
        @pl.when(is_mid)
        def _():
            done(tops.at[j], top_recv.at[j])
            rows = pl.ds(pl.multiple_of((1 - kept) * HR, HR), HR)
            remote(tops.at[j], land.at[j, rows], out_send.at[j, 1 - kept], out_recv.at[j, 1 - kept], **outward).start()
            spread(j, 1 - kept, tops.at[j])

    def outbound(j):
        @pl.when(jnp.logical_not(is_mid))
        def _():
            for half in range(2):
                rows = pl.ds(half * HR, HR)
                done(land.at[j, rows], out_recv.at[j, half])
                spread(j, half, land.at[j, rows])

    def tick(t, c):
        for off, stage in zip(OFFS, (inbound, middle, finish, outbound)):
            @pl.when((t >= off) & (t < total + off))
            def _(): stage(t - off)
        return c
    lax.fori_loop(0, total + OFFS[3], tick, 0)

    def drain(j, c):
        @pl.when(is_mid)
        def _():
            done(mids.at[j], mid_send.at[j])
            done(tops.at[j], top_send.at[j])
            for half in range(2):
                done(mids.at[j], out_send.at[j, half])
        @pl.when(jnp.logical_not(is_mid))
        def _():
            done(own.at[j], in_send.at[j])
        return c
    lax.fori_loop(0, total, drain, 0)
    for m in range(n_in):
        r, q = outs[m].shape
        most = outs[m].at[pl.ds(0, 3 * r // 4)]
        some = outs[m].at[pl.ds(0, r // 4)]
        done(most, far_send.at[m]); done(most, far_recv.at[m])
        done(some, near.at[m])

def xor(c, s):
    return lax.rem(lax.rem(c, 2) + s % 2, 2) + 2 * lax.rem(c // 2 + s // 2, 2)

def group_sum(grads, kinds, cid):
    plans = [grad_plan(k, g.shape) for k, g in zip(kinds, grads)]
    total = sum(4 * p[0] for p in plans)
    n = len(grads)
    D = pltpu.SemaphoreType.DMA
    return pl.pallas_call(
        functools.partial(group_sum_kernel, kinds, n),
        in_specs=[ANY] * n, out_specs=[ANY] * n,
        out_shape=[jax.ShapeDtypeStruct(p[2], BF) for p in plans],
        scratch_shapes=[pltpu.VMEM((total, CR, CC), BF), pltpu.VMEM((total, CR, CC), BF),
            pltpu.VMEM((total, HR, CC), BF), pltpu.VMEM((total, HR, CC), BF)]
            + [D((total,))] * 7 + [D((total, 2))] * 2 + [D((n,))] * 3,
        compiler_params=pltpu.CompilerParams(collective_id=cid, has_side_effects=True, vmem_limit_bytes=60*2**20),
        name="group_sum")(*grads)


def by_distance(stacked, dim):
    count = lax.axis_size("col")
    order = lax.axis_index("col") ^ jnp.arange(count)
    blocks = jnp.take(stacked, order, axis=0)
    return jnp.concatenate([blocks[i] for i in range(count)], axis=dim)


def plain_gather(x):
    cols = by_distance(lax.all_gather(x, "col"), 1)
    return jnp.concatenate([cols, swap(cols, "row", 1)], axis=0)


def plain_gather_heads(x):
    mine = lax.all_gather(x, "col", axis=1, tiled=True)
    half = x.shape[0] // 2
    other = swap(mine, "row", 1)
    other = jnp.concatenate([other[half:], other[:half]], axis=0)
    return jnp.concatenate([mine, other], axis=1)


def plain_reduce(part):
    span, full = part.shape
    count = lax.axis_size("col")
    width = full // count
    half = part[: span // 2].astype(F32) + swap(part[span // 2 :], "row", 1).astype(F32)
    order = lax.axis_index("col") ^ jnp.arange(count)
    blocks = jnp.stack([half[:, s * width : (s + 1) * width] for s in range(count)])
    return lax.psum_scatter(jnp.take(blocks, order, axis=0), "col", tiled=False)


def exchange(packs, dim):
    if kernels_fit():
        return jnp.concatenate([p if s == 0 else swap(p, "col", s) for s, p in enumerate(packs)], axis=dim)
    order = lax.axis_index("col") ^ jnp.arange(len(packs))
    sent = jnp.take(jnp.stack(packs), order, axis=0)
    return by_distance(lax.all_to_all(sent, "col", 0, 0, tiled=True), dim)


def plain_group_sum(grads, kinds):
    outs = []
    count = lax.axis_size("col")
    order = lax.axis_index("col") ^ jnp.arange(count)
    for grad, kind in zip(grads, kinds):
        grad = lax.psum(grad.astype(F32), "dp").astype(BF)
        dim = 1 if kind == "rows" else 0
        blocks = jnp.stack(jnp.split(grad, count, axis=dim))
        blocks = lax.all_to_all(jnp.take(blocks, order, axis=0), "col", 0, 0, tiled=True)
        out_dim = 1 if kind == "columns" else 0
        outs.append(jnp.concatenate([blocks[i] for i in range(count)], axis=out_dim))
    return outs


def kernels_fit():
    return lax.axis_size("col") == 4 and lax.axis_size("dp") == 4 and lax.axis_size("row") == 2


def gather_plane(x, cid):
    return gather_tokens(x, cid) if kernels_fit() else plain_gather(x)


def attn_forward_kernel(
    info_ref, q_ref, k_ref, v_ref, mixed_ref, wide_ref, lse_ref, peak_ref, score_ref, sum_ref
):
    heads = q_ref.shape[1] // HD
    span = k_ref.shape[0]
    rows = heads * QB
    length = info_ref[0]
    half = info_ref[1]
    step = pl.program_id(0)
    first = step * QB
    key_tiles = span // FWD_KB
    q = jnp.concatenate([q_ref[:, h * HD : (h + 1) * HD] for h in range(heads)], axis=0)
    tiles = jnp.minimum(pl.cdiv(first + QB, FWD_KB), pl.cdiv(length, FWD_KB))
    plain = jnp.minimum(first // FWD_KB, length // FWD_KB)

    def tile_of(ref, tile):
        stored = lax.rem(tile + half * (key_tiles // 2), key_tiles)
        return ref[pl.ds(pl.multiple_of(stored * FWD_KB, FWD_KB), FWD_KB), :]

    def fold(values, running, op):
        for t in range(FWD_KB // LANES):
            running = op(running, values[:, t * LANES : (t + 1) * LANES])
        return running

    def scores_of(tile):
        return contract(q, tile_of(k_ref, tile), 1, 1) * HD**-0.5

    def plain_scores(tile, top):
        scores = scores_of(tile)
        score_ref[tile] = scores
        return fold(scores, top, jnp.maximum)

    def masked_scores(tile, top):
        place = first + lax.broadcasted_iota(jnp.int32, (QB, FWD_KB), 0)
        key_place = tile * FWD_KB + lax.broadcasted_iota(jnp.int32, (QB, FWD_KB), 1)
        allowed = (key_place <= place) & (key_place < length)
        scores = scores_of(tile).reshape(heads, QB, FWD_KB)
        scores = jnp.where(allowed[None], scores, NEG_FILL).reshape(rows, FWD_KB)
        score_ref[tile] = scores
        return fold(scores, top, jnp.maximum)

    top = jnp.full((rows, LANES), NEG_FILL, F32)
    top = lax.fori_loop(0, plain, plain_scores, top)
    top = lax.fori_loop(plain, tiles, masked_scores, top)
    top = jnp.max(top, axis=1, keepdims=True)
    live = first + lax.broadcasted_iota(jnp.int32, (QB, 1), 0) < length
    peak = jnp.max(jnp.where(live[None], top.reshape(heads, QB, 1), NEG_FILL), axis=1)

    @pl.when(step == 0)
    def _():
        peak_ref[...] = jnp.full_like(peak_ref, NEG_FILL)

    peak_ref[...] = jnp.maximum(peak_ref[...], jnp.broadcast_to(peak, peak_ref.shape))
    sum_ref[...] = jnp.zeros_like(sum_ref)

    def weigh(tile, total):
        weights = jnp.exp(score_ref[tile] - top)
        sum_ref[...] += contract(weights.astype(BF), tile_of(v_ref, tile), 1, 0)
        return fold(weights, total, jnp.add)

    total = lax.fori_loop(0, tiles, weigh, jnp.zeros((rows, LANES), F32))
    total = jnp.sum(total, axis=1, keepdims=True)
    mixed = sum_ref[...] / total
    log_total = jnp.broadcast_to(top + jnp.log(total), (rows, LANES))
    lse_ref[0] = log_total.T[0:1, :]
    for h in range(heads):
        part = mixed[h * QB : (h + 1) * QB]
        mixed_ref[:, h * HD : (h + 1) * HD] = part.astype(BF)
        wide_ref[:, h * HD : (h + 1) * HD] = part


def attn_forward(info, q, k, v):
    span, width = q.shape
    heads = width // HD
    steps = span // QB

    def stored(i, info_ref):
        return (lax.rem(i + info_ref[1] * (steps // 2), steps), 0)

    whole = pl.BlockSpec((span, HD), lambda i, info_ref: (0, 0))
    pairs = heads * span * span // 2
    return pl.pallas_call(
        attn_forward_kernel,
        grid_spec=pltpu.PrefetchScalarGridSpec(
            num_scalar_prefetch=1,
            grid=(steps,),
            in_specs=[pl.BlockSpec((QB, width), stored), whole, whole],
            out_specs=[
                pl.BlockSpec((QB, width), stored),
                pl.BlockSpec((QB, width), stored),
                pl.BlockSpec((1, 1, heads * QB), lambda i, info_ref: (i, 0, 0)),
                pl.BlockSpec((heads, LANES), lambda i, info_ref: (0, 0)),
            ],
            scratch_shapes=[
                pltpu.VMEM((span // FWD_KB, heads * QB, FWD_KB), F32),
                pltpu.VMEM((heads * QB, HD), F32),
            ],
        ),
        out_shape=[
            jax.ShapeDtypeStruct((span, width), BF),
            jax.ShapeDtypeStruct((span, width), F32),
            jax.ShapeDtypeStruct((steps, 1, heads * QB), F32),
            jax.ShapeDtypeStruct((heads, LANES), F32),
        ],
        compiler_params=pltpu.CompilerParams(vmem_limit_bytes=40 * 2**20),
        cost_estimate=pl.CostEstimate(
            flops=40 * pairs * HD // 4, transcendentals=pairs, bytes_accessed=8 * span * width
        ),
        name="attn_forward",
    )(info, q, k, v)


def turn_back(values, cos_ref, sin_ref):
    half = HD // 2
    swapped = jnp.concatenate([values[:, half:], -values[:, :half]], axis=1)
    return values * cos_ref[...] + swapped * sin_ref[...]


def attn_backward_kernel(
    info_ref, q_ref, k_ref, v_ref, cot_ref, wide_ref, lse_ref, cosq_ref, sinq_ref, cosk_ref, sink_ref,
    dq_ref, dk_ref, dv_ref, dq_sum, dk_sum, dv_sum,
):
    heads = q_ref.shape[1] // HD
    span = k_ref.shape[0]
    rows = heads * QB
    length = info_ref[0]
    half = info_ref[1]
    step = pl.program_id(0)
    first = step * QB
    key_tiles = span // BWD_KB

    @pl.when(step == 0)
    def _():
        dk_sum[...] = jnp.zeros_like(dk_sum)
        dv_sum[...] = jnp.zeros_like(dv_sum)

    dq_sum[...] = jnp.zeros_like(dq_sum)

    @pl.when(first < length)
    def _():
        pieces = [slice(h * HD, (h + 1) * HD) for h in range(heads)]
        q = jnp.concatenate([q_ref[:, s] for s in pieces], axis=0)
        cot = jnp.concatenate([cot_ref[:, s] for s in pieces], axis=0)
        wide = jnp.concatenate([wide_ref[:, s] for s in pieces], axis=0)
        log_total = lse_ref[0]
        inner = jnp.sum(wide * cot.astype(F32), axis=1, keepdims=True)
        inner = jnp.broadcast_to(inner, (rows, LANES)).T[0:1, :]

        def tile_step(tile, masked):
            stored = lax.rem(tile + half * (key_tiles // 2), key_tiles)
            keys = pl.ds(pl.multiple_of(stored * BWD_KB, BWD_KB), BWD_KB)
            k_tile = k_ref[keys, :]
            v_tile = v_ref[keys, :]
            scores = contract(k_tile, q, 1, 1) * HD**-0.5 - log_total
            if masked:
                key_place = tile * BWD_KB + lax.broadcasted_iota(jnp.int32, (BWD_KB, rows), 0)
                place = first + lax.rem(lax.broadcasted_iota(jnp.int32, (BWD_KB, rows), 1), QB)
                scores = jnp.where((key_place <= place) & (key_place < length), scores, NEG_FILL)
            weights = jnp.exp(scores)
            prob_cot = contract(v_tile, cot, 1, 1)
            score_cot = (weights * (prob_cot - inner)).astype(BF)
            dv_sum[keys, :] += contract(weights.astype(BF), cot, 1, 0)
            dk_sum[keys, :] += contract(score_cot, q, 1, 0) * HD**-0.5
            dq_sum[...] += contract(score_cot, k_tile, 0, 0) * HD**-0.5

        @pl.loop(0, first // BWD_KB)
        def _(tile):
            tile_step(tile, False)

        @pl.loop(first // BWD_KB, pl.cdiv(first + QB, BWD_KB))
        def _(tile):
            tile_step(tile, True)

    for h in range(heads):
        part = turn_back(dq_sum[h * QB : (h + 1) * QB, :], cosq_ref, sinq_ref)
        dq_ref[:, h * HD : (h + 1) * HD] = part.astype(dq_ref.dtype)

    @pl.when(step == pl.num_programs(0) - 1)
    def _():
        dk_ref[...] = turn_back(dk_sum[...], cosk_ref, sink_ref).astype(dk_ref.dtype)
        dv_ref[...] = dv_sum[...].astype(dv_ref.dtype)


def attn_backward(info, q, k, v, cot, wide, lse, cos, sin, kv_type):
    span, width = q.shape
    heads = width // HD
    steps = span // QB

    def stored(i, info_ref):
        return (lax.rem(i + info_ref[1] * (steps // 2), steps), 0)

    whole = pl.BlockSpec((span, HD), lambda i, info_ref: (0, 0))
    mine = pl.BlockSpec((QB, width), stored)
    turn = pl.BlockSpec((QB, HD), stored)
    pairs = heads * span * span // 2
    return pl.pallas_call(
        attn_backward_kernel,
        grid_spec=pltpu.PrefetchScalarGridSpec(
            num_scalar_prefetch=1,
            grid=(steps,),
            in_specs=[
                mine, whole, whole, mine, mine,
                pl.BlockSpec((1, 1, heads * QB), lambda i, info_ref: (i, 0, 0)),
                turn, turn, whole, whole,
            ],
            out_specs=[mine, whole, whole],
            scratch_shapes=[
                pltpu.VMEM((heads * QB, HD), F32),
                pltpu.VMEM((span, HD), F32),
                pltpu.VMEM((span, HD), F32),
            ],
        ),
        out_shape=[
            jax.ShapeDtypeStruct((span, width), BF),
            jax.ShapeDtypeStruct((span, HD), kv_type),
            jax.ShapeDtypeStruct((span, HD), kv_type),
        ],
        compiler_params=pltpu.CompilerParams(vmem_limit_bytes=40 * 2**20),
        cost_estimate=pl.CostEstimate(
            flops=60 * pairs * HD // 4, transcendentals=pairs, bytes_accessed=12 * span * width
        ),
        name="attn_backward",
    )(info, q, k, v, cot, wide, lse, cos, sin, cos, sin)


def head_kernel(x_ref, gain_ref, wq_ref, wkv_ref, cos_ref, sin_ref, normed_ref, q_ref, k_ref, v_ref, scale_ref):
    x = x_ref[...].astype(F32)
    scale = lax.rsqrt(jnp.mean(x * x, axis=1, keepdims=True) + EPSILON)
    scale_ref[...] = jnp.broadcast_to(scale, scale_ref.shape)
    normed = (x * scale * gain_ref[0:1, :]).astype(BF)
    normed_ref[...] = normed

    def turned(raw):
        pieces = []
        half = HD // 2
        for h in range(raw.shape[1] // HD):
            pieces += [-raw[:, h * HD + half : (h + 1) * HD], raw[:, h * HD : h * HD + half]]
        pieces = jnp.concatenate(pieces, axis=1)
        count = raw.shape[1] // HD
        cos = jnp.concatenate([cos_ref[...]] * count, axis=1)
        sin = jnp.concatenate([sin_ref[...]] * count, axis=1)
        return (raw * cos + pieces * sin).astype(BF)

    q_ref[...] = turned(contract(normed, wq_ref[...], 1, 0))
    keyval = contract(normed, wkv_ref[...], 1, 0)
    k_ref[...] = turned(keyval[:, :HD])
    v_ref[...] = keyval[:, HD:].astype(BF)


def project_heads(tokens_full, gains, wq, wkv, cos, sin):
    span, full = tokens_full.shape
    width = wq.shape[1]
    block = 512
    line = lambda n: pl.BlockSpec((block, n), lambda i: (i, 0))
    whole = lambda a: pl.BlockSpec(a.shape, lambda i: (0, 0))
    return pl.pallas_call(
        head_kernel,
        grid=(span // block,),
        in_specs=[line(full), whole(gains), whole(wq), whole(wkv), line(HD), line(HD)],
        out_specs=[line(full), line(width), line(HD), line(HD), line(LANES)],
        out_shape=[
            jax.ShapeDtypeStruct((span, full), BF),
            jax.ShapeDtypeStruct((span, width), BF),
            jax.ShapeDtypeStruct((span, HD), BF),
            jax.ShapeDtypeStruct((span, HD), BF),
            jax.ShapeDtypeStruct((span, LANES), F32),
        ],
        compiler_params=pltpu.CompilerParams(vmem_limit_bytes=48 * MIB),
        cost_estimate=pl.CostEstimate(
            flops=2 * span * full * (width + LANES), transcendentals=0, bytes_accessed=5 * span * full
        ),
        name="project_heads",
    )(tokens_full, gains, wq, wkv, cos, sin)


def project_out_kernel(mixed_ref, w_ref, x_ref, gain_ref, resid_ref, normed_ref):
    resid = x_ref[...].astype(F32) + contract(mixed_ref[...], w_ref[...], 1, 0)
    resid_ref[...] = resid
    scale = lax.rsqrt(jnp.mean(resid * resid, axis=1, keepdims=True) + EPSILON)
    normed_ref[...] = (resid * scale * gain_ref[1:2, :]).astype(BF)


def project_out(mixed_full, w_out_full, tokens_full, gains):
    span, full = tokens_full.shape
    block = 256
    line = pl.BlockSpec((block, full), lambda i: (i, 0))
    return pl.pallas_call(
        project_out_kernel,
        grid=(span // block,),
        in_specs=[
            pl.BlockSpec((block, mixed_full.shape[1]), lambda i: (i, 0)),
            pl.BlockSpec(w_out_full.shape, lambda i: (0, 0), pipeline_mode=pl.Buffered(1)),
            line,
            pl.BlockSpec(gains.shape, lambda i: (0, 0)),
        ],
        out_specs=[line, line],
        out_shape=[jax.ShapeDtypeStruct((span, full), F32), jax.ShapeDtypeStruct((span, full), BF)],
        compiler_params=pltpu.CompilerParams(vmem_limit_bytes=48 * MIB),
        cost_estimate=pl.CostEstimate(
            flops=2 * span * full * full, transcendentals=0, bytes_accessed=12 * span * full
        ),
        name="project_out",
    )(mixed_full, w_out_full, tokens_full, gains)


def middle_kernel(
    cot_ref, resid_ref, low_ref, gain_ref, w_ref, mixed_ref,
    mixed_cot_ref, own_ref, grad_ref, gain_part_ref, total_ref,
):
    step = pl.program_id(0)
    last = pl.num_programs(0) - 1
    width = own_ref.shape[1]
    cot = cot_ref[...].astype(F32)
    resid = resid_ref[...]
    scale = lax.rsqrt(jnp.mean(resid * resid, axis=1, keepdims=True) + EPSILON)
    weighed = cot * gain_ref[1:2, :]
    inner = jnp.sum(weighed * resid, axis=1, keepdims=True)
    mid = low_ref[...].astype(F32) + weighed * scale - resid * (scale * scale * scale * inner / D)
    low = mid.astype(BF)
    mixed_cot_ref[...] = contract(low, w_ref[...], 1, 1).astype(BF)

    @pl.when(step == 0)
    def _():
        total_ref[...] = jnp.zeros_like(total_ref)
        gain_part_ref[...] = jnp.zeros_like(gain_part_ref)

    total_ref[...] += contract(mixed_ref[...], low, 0, 0)

    @pl.when(step <= last // 2)
    def _():
        own_ref[...] = mid[:, :width]
        part = jnp.sum((cot * resid * scale)[:, :width], axis=0, keepdims=True)
        gain_part_ref[...] += jnp.broadcast_to(part, gain_part_ref.shape)

    @pl.when(step == last)
    def _():
        grad_ref[...] = total_ref[...].astype(BF)


def middle(mlp_cot, resid_mid, out_low, gains, w_mine, mixed, width):
    span, full = resid_mid.shape
    heads_width = mixed.shape[1]
    block = 256
    steps = span // block
    line = pl.BlockSpec((block, full), lambda i: (i, 0))
    thin = pl.BlockSpec((block, heads_width), lambda i: (i, 0))
    return pl.pallas_call(
        middle_kernel,
        grid=(steps,),
        in_specs=[
            line, line, line,
            pl.BlockSpec(gains.shape, lambda i: (0, 0)),
            pl.BlockSpec(w_mine.shape, lambda i: (0, 0)),
            thin,
        ],
        out_specs=[
            thin,
            pl.BlockSpec((block, width), lambda i: (jnp.minimum(i, steps // 2 - 1), 0)),
            pl.BlockSpec((heads_width, full), lambda i: (0, 0)),
            pl.BlockSpec((8, width), lambda i: (0, 0)),
        ],
        out_shape=[
            jax.ShapeDtypeStruct((span, heads_width), BF),
            jax.ShapeDtypeStruct((span // 2, width), F32),
            jax.ShapeDtypeStruct((heads_width, full), BF),
            jax.ShapeDtypeStruct((8, width), F32),
        ],
        scratch_shapes=[pltpu.VMEM((heads_width, full), F32)],
        compiler_params=pltpu.CompilerParams(vmem_limit_bytes=48 * MIB),
        cost_estimate=pl.CostEstimate(
            flops=4 * span * full * heads_width, transcendentals=0, bytes_accessed=8 * span * full
        ),
        name="middle",
    )(mlp_cot, resid_mid, out_low, gains, w_mine, mixed)


def head_back_kernel(
    info_ref, qc_ref, kc_ref, vc_ref, wq_ref, wkv_ref, normed_ref, x_ref, gain_ref,
    part_ref, dot_ref, grad_ref, total_ref,
):
    step = pl.program_id(0)
    wide = qc_ref.shape[1]
    keyval = jnp.concatenate([kc_ref[...], vc_ref[...]], axis=1)
    counted = keyval * info_ref[2].astype(BF)
    part = contract(qc_ref[...], wq_ref[...], 1, 1) + contract(counted, wkv_ref[...], 1, 1)
    part_ref[...] = part.astype(BF)
    inner = jnp.sum(part * gain_ref[0:1, :] * x_ref[...].astype(F32), axis=1, keepdims=True)
    dot_ref[0] = jnp.broadcast_to(inner, (inner.shape[0], LANES)).T[0:1, :]

    @pl.when(step == 0)
    def _():
        total_ref[...] = jnp.zeros_like(total_ref)

    total_ref[:, :wide] += contract(normed_ref[...], qc_ref[...], 0, 0)
    total_ref[:, wide:] += contract(normed_ref[...], keyval, 0, 0)

    @pl.when(step == pl.num_programs(0) - 1)
    def _():
        used = wide + 2 * HD
        grad_ref[:, :used] = total_ref[...].astype(BF)
        grad_ref[:, used:] = jnp.zeros((grad_ref.shape[0], grad_ref.shape[1] - used), BF)


def head_back(info, query_cot, key_cot, value_cot, wq, wkv, normed, tokens_full, gains):
    span, full = normed.shape
    wide = query_cot.shape[1]
    block = 512
    steps = span // block
    line = lambda n: pl.BlockSpec((block, n), lambda i, info_ref: (i, 0))
    whole = lambda shape: pl.BlockSpec(shape, lambda i, info_ref: (0, 0))
    grad_width = max(CC, wide + 2 * HD)
    return pl.pallas_call(
        head_back_kernel,
        grid_spec=pltpu.PrefetchScalarGridSpec(
            num_scalar_prefetch=1,
            grid=(steps,),
            in_specs=[
                line(wide), line(HD), line(HD), whole(wq.shape), whole(wkv.shape), line(full), line(full),
                whole(gains.shape),
            ],
            out_specs=[
                line(full),
                pl.BlockSpec((1, 1, block), lambda i, info_ref: (i, 0, 0)),
                whole((full, grad_width)),
            ],
            scratch_shapes=[pltpu.VMEM((full, wide + 2 * HD), F32)],
        ),
        out_shape=[
            jax.ShapeDtypeStruct((span, full), BF),
            jax.ShapeDtypeStruct((steps, 1, block), F32),
            jax.ShapeDtypeStruct((full, grad_width), BF),
        ],
        compiler_params=pltpu.CompilerParams(vmem_limit_bytes=48 * MIB),
        cost_estimate=pl.CostEstimate(
            flops=4 * span * full * (wide + LANES), transcendentals=0, bytes_accessed=6 * span * full
        ),
        name="head_back",
    )(info, query_cot, key_cot, value_cot, wq, wkv, normed, tokens_full, gains)


def on_device(
    tokens, lengths, attn_gain, w_query, w_key, w_value, w_out, mlp_gain, w_gate, w_up, w_down, cotangent
):
    row_devices = lax.axis_size("row")
    col_devices = lax.axis_size("col")
    row = lax.axis_index("row")
    col = lax.axis_index("col")
    fit = kernels_fit()
    tok, width = tokens.shape
    span = tok * row_devices
    group = HQ // KV
    heads_row = HQ // row_devices
    heads = heads_row // col_devices
    head_width = heads * HD
    keyval_row = KV // row_devices
    units = w_gate.shape[1] // col_devices
    length = lengths[0]
    shared_key = heads < group
    sharers = max(1, group // heads)
    leader = (col % sharers == 0).astype(jnp.int32)
    info = jnp.stack([length, row, leader]).astype(jnp.int32)

    keyval = []
    for owner in range(col_devices):
        first = owner * heads // group * HD
        keyval += [w_key[:, first : first + HD], w_value[:, first : first + HD]]
    keyval = jnp.concatenate(keyval, axis=1)
    gains = jnp.concatenate([attn_gain[None], mlp_gain[None], jnp.zeros((6, width), F32)], axis=0)

    if fit:
        tokens_full, wq, wkv, gains = first_gather(tokens, w_query, keyval, gains, 1)
    else:
        tokens_full = plain_gather(tokens)
        wq = exchange(
            [lax.dynamic_slice_in_dim(w_query, (col ^ s) * head_width, head_width, 1) for s in range(col_devices)], 0
        )
        wkv = exchange([lax.dynamic_slice_in_dim(keyval, (col ^ s) * LANES, LANES, 1) for s in range(col_devices)], 0)
        gains = by_distance(lax.all_gather(gains, "col"), 1)
    w_gate, w_up, w_down, w_out_mine, cotangent, tokens_full = lax.optimization_barrier(
        (w_gate, w_up, w_down, w_out, cotangent, tokens_full)
    )
    place = lax.rem(jnp.arange(span, dtype=jnp.int32) + row * tok, span)
    frequency = ROPE_BASE ** (-jnp.arange(HD // 2, dtype=F32) * (2.0 / HD))
    angle = place.astype(F32)[:, None] * frequency[None, :]
    cos = jnp.tile(jnp.cos(angle), (1, 2))
    sin = jnp.tile(jnp.sin(angle), (1, 2))

    normed_attn, query, key, value, scale_a = project_heads(tokens_full, gains, wq, wkv, cos, sin)
    mixed, mixed_wide, log_total, peak = attn_forward(info, query, key, value)

    def slow_gather(x):
        if not fit:
            return plain_gather(x)
        cols = jnp.concatenate([x] + [swap(x, "col", s) for s in range(1, 4)], axis=1)
        return jnp.concatenate([cols, swap(cols, "row", 1)], axis=0)

    w_out_full = slow_gather(w_out_mine)
    mixed_full = gather_heads(mixed, 2) if fit else plain_gather_heads(mixed)
    resid_mid, normed_mlp = project_out(mixed_full, w_out_full, tokens_full, gains)

    def unit_slices(weight, dim):
        return [lax.dynamic_slice_in_dim(weight, (col ^ s) * units, units, dim) for s in range(col_devices)]

    w_gate_units = exchange(unit_slices(w_gate, 1), 0)
    w_up_units = exchange(unit_slices(w_up, 1), 0)
    w_down_units = exchange(unit_slices(w_down, 0), 1)
    gate = jnp.dot(normed_mlp, w_gate_units, preferred_element_type=F32)
    up = jnp.dot(normed_mlp, w_up_units, preferred_element_type=F32)
    gate_sigmoid = jax.nn.sigmoid(gate)
    hidden = (gate * gate_sigmoid * up).astype(BF)

    valid = (row * tok + jnp.arange(tok, dtype=jnp.int32) < length).astype(BF)
    out_low = slow_gather(cotangent * valid[:, None])
    grad_down = contract(hidden, out_low, 0, 0).astype(BF)
    hidden_cot = contract(out_low, w_down_units, 1, 1)
    gate_cot = (
        hidden_cot * up * gate_sigmoid * (1.0 + gate * (1.0 - gate_sigmoid))
    ).astype(BF)
    up_cot = (hidden_cot * gate * gate_sigmoid).astype(BF)
    mlp_part = (contract(gate_cot, w_gate_units, 1, 1) + contract(up_cot, w_up_units, 1, 1)).astype(BF)
    grad_gate = contract(normed_mlp, gate_cot, 0, 0).astype(BF)
    grad_up = contract(normed_mlp, up_cot, 0, 0).astype(BF)
    mlp_cot = all_reduce(mlp_part, 3) if fit else plain_gather(plain_reduce(mlp_part).astype(BF))

    w_mine = lax.dynamic_slice_in_dim(w_out_full, col * head_width, head_width, 0)
    mixed_cot, mid_cot, grad_out, gain_m_part = middle(
        mlp_cot, resid_mid, out_low, gains, w_mine, mixed, width
    )
    query_cot, key_cot, value_cot = attn_backward(
        info, query, key, value, mixed_cot, mixed_wide, log_total, cos, sin, F32 if shared_key else BF
    )
    if shared_key:
        for bit in range(sharers.bit_length() - 1):
            key_cot = key_cot + swap(key_cot, "col", 1 << bit)
            value_cot = value_cot + swap(value_cot, "col", 1 << bit)
        key_cot, value_cot = key_cot.astype(BF), value_cot.astype(BF)
    attn_part, dot_part, grad_heads = head_back(
        info, query_cot, key_cot, value_cot, wq, wkv, normed_attn, tokens_full, gains
    )
    dot_part = dot_part.reshape(span)
    width_dot = dot_part[:tok] + swap(dot_part[tok:], "row", 1)
    step = 1
    while step < col_devices:
        width_dot = width_dot + swap(width_dot, "col", step)
        step *= 2
    attn_cot = reduce_scatter(attn_part, 4) if fit else plain_reduce(attn_part)
    down_part = jnp.dot(hidden, w_down_units, preferred_element_type=F32).astype(BF)
    down_sum = reduce_scatter(down_part, 5) if fit else plain_reduce(down_part)
    output = (resid_mid[:tok, :width] + down_sum).astype(BF)
    own_in = tokens.astype(F32)
    scale_own = scale_a[:tok, :1]
    input_grad = (
        mid_cot
        + attn_cot * attn_gain * scale_own
        - own_in * (scale_own * scale_own * scale_own * width_dot[:, None] / D)
    )
    gain_a_part = jnp.sum(attn_cot * own_in * scale_own, axis=0)

    grads = [grad_gate, grad_up, grad_down, grad_out, grad_heads]
    kinds = ["columns", "columns", "rows", "rows", "stack"]
    if fit:
        sums = group_sum(grads, kinds, 6)
    else:
        sums = plain_group_sum(grads, kinds)
    out_gate, out_up, out_down, out_out, out_heads = [g.astype(F32) for g in sums]
    out_heads = out_heads.reshape(col_devices, width, out_heads.shape[1])
    out_query = jnp.concatenate([out_heads[i, :, :head_width] for i in range(col_devices)], axis=1)
    leaders = range(0, col_devices, sharers)
    out_key = jnp.concatenate([out_heads[i, :, head_width : head_width + HD] for i in leaders], axis=1)
    out_value = jnp.concatenate(
        [out_heads[i, :, head_width + HD : head_width + 2 * HD] for i in leaders], axis=1
    )

    gain_sums = jnp.stack([gain_a_part, gain_m_part[0]])
    gain_sums = gain_sums + swap(gain_sums, "row", 1)
    step = 1
    while step < lax.axis_size("dp"):
        gain_sums = gain_sums + swap(gain_sums, "dp", step)
        step *= 2
    step = 1
    while step < lax.axis_size("dp"):
        peak = jnp.maximum(peak, swap(peak, "dp", step))
        step *= 2
    own_peaks = peak[:, 0]
    slots = jnp.arange(col_devices)[:, None]
    row_peaks = jnp.where(slots == col, own_peaks[None, :], NEG_FILL)
    step = 1
    while step < col_devices:
        row_peaks = jnp.maximum(row_peaks, swap(row_peaks, "col", step))
        step *= 2
    row_peaks = row_peaks.reshape(heads_row)
    clip_factor = CLIP_LEVEL / jnp.maximum(row_peaks, CLIP_LEVEL)
    query_scale = jnp.repeat(jnp.sqrt(clip_factor), HD)
    key_scale = jnp.repeat(jnp.sqrt(jnp.min(clip_factor.reshape(keyval_row, group), axis=1)), HD)
    clipped_query = (w_query.astype(F32) * query_scale[None, :]).astype(BF)
    clipped_key = (w_key.astype(F32) * key_scale[None, :]).astype(BF)
    return (
        output,
        input_grad,
        gain_sums[0],
        out_query,
        out_key,
        out_value,
        out_out,
        gain_sums[1],
        out_gate,
        out_up,
        out_down,
        own_peaks,
        clipped_query,
        clipped_key,
    )


def solution(mesh):
    in_specs = (
        P(("dp", "row"), "col"),
        P("dp"),
        P("col"),
        P("col", "row"),
        P("col", "row"),
        P("col", "row"),
        P("row", "col"),
        P("col"),
        P("col", "row"),
        P("col", "row"),
        P("row", "col"),
        P(("dp", "row"), "col"),
    )
    out_specs = (
        P(("dp", "row"), "col"),
        P(("dp", "row"), "col"),
        P("col"),
        P("col", "row"),
        P("col", "row"),
        P("col", "row"),
        P("row", "col"),
        P("col"),
        P("col", "row"),
        P("col", "row"),
        P("row", "col"),
        P(("row", "col")),
        P("col", "row"),
        P("col", "row"),
    )
    return jax.shard_map(
        on_device, mesh=mesh, in_specs=in_specs, out_specs=out_specs, check_vma=False
    )
```

```python
import functools

import jax
import jax.numpy as jnp
from jax import lax
from jax.experimental import pallas as pl
from jax.experimental.pallas import tpu as pltpu
from jax.sharding import PartitionSpec as P

D = 2048
HQ = 32
KV = 8
HD = 64
SEQ_LEN = 2048

EPSILON = 1e-05
NEG_FILL = -1e30
CLIP_LEVEL = 5.0
ROPE_BASE = 500000.0

BF = jnp.bfloat16
F32 = jnp.float32
LANES = 128
QB = 512
FWD_KB = 512
BWD_KB = 512
MESH = pl.DeviceIdType.MESH
ANY = pl.BlockSpec(memory_space=pl.ANY)
NCH = 4
CR, CC = 256, 512
HR = CR // 2
OFFS = (0, 2, 4, 6)
RING = 12
MIB = 2**20
VMEM_ALL = 63 * MIB


def contract(left, right, left_dim, right_dim):
    return lax.dot_general(
        left, right, (((left_dim,), (right_dim,)), ((), ())), preferred_element_type=F32
    )


def swap(values, axis, step):
    count = lax.axis_size(axis)
    return lax.ppermute(values, axis, [(i, i ^ step) for i in range(count)])


def flip(index, bit):
    return index + bit - 2 * bit * lax.rem(index // bit, 2)


def xor(index, step):
    return lax.rem(lax.rem(index, 2) + step % 2, 2) + 2 * lax.rem(index // 2 + step // 2, 2)


def remote(src, dst, send, recv, **where):
    return pltpu.make_async_remote_copy(
        src_ref=src, dst_ref=dst, send_sem=send, recv_sem=recv, device_id=where, device_id_type=MESH
    )


def done(ref, sem):
    pltpu.make_async_copy(ref, ref, sem).wait()


def greet(targets):
    barrier = pltpu.get_barrier_semaphore()
    for target in targets:
        pl.semaphore_signal(barrier, inc=1, device_id=target, device_id_type=MESH)
    pl.semaphore_wait(barrier, len(targets))


def plane_peers():
    row = lax.axis_index("row")
    col = lax.axis_index("col")
    return {"col": flip(col, 1)}, {"col": flip(col, 2)}, {"row": 1 - row}


def token_place(tok, width):
    rows = tok // NCH

    def place(ref, half, s, j, who):
        return ref.at[pl.ds(half * tok + j * rows, rows), pl.ds(s * width, width)]

    return place


def head_place(span, width):
    rows = span // NCH

    def place(ref, half, s, j, who):
        start = j * rows if half == 0 else ((j + NCH // 2) % NCH) * rows
        return ref.at[pl.ds(start, rows), pl.ds(pl.multiple_of((half * 4 + xor(who, s)) * width, LANES), width)]

    return place


class Gather:
    SEMS = 6

    def __init__(self, src, out, place, stage, sems):
        self.src, self.out, self.place, self.stage = src, out, place, stage
        self.own_send, self.relay_send, self.mate_send, self.recv, self.mate_recv, self.local = sems
        self.col = lax.axis_index("col")
        self.near = plane_peers()

    @staticmethod
    def sems():
        shapes = [(2, NCH), (NCH,), (4, NCH), (3, NCH), (4, NCH), (2,)]
        return [pltpu.SemaphoreType.DMA(s) for s in shapes]

    def chunk(self, j):
        rows = self.src.shape[0] // NCH
        return self.src.at[pl.ds(j * rows, rows), :]

    def here(self, half, s, j):
        return self.place(self.out, half, s, j, self.col)

    def own(self, axis, j):
        peer = self.near[axis]
        dst = self.place(self.out, 0, axis + 1, j, peer["col"])
        return remote(self.chunk(j), dst, self.own_send.at[axis, j], self.recv.at[axis, j], **peer)

    def relay(self, axis, j):
        peer = self.near[1 - axis]
        dst = self.place(self.out, 0, 3, j, peer["col"])
        return remote(self.here(0, axis + 1, j), dst, self.relay_send.at[j], self.recv.at[2, j], **peer)

    def mate(self, s, j):
        src = self.chunk(j) if s == 0 else self.here(0, s, j)
        dst = self.place(self.out, 1, s, j, self.col)
        return remote(src, dst, self.mate_send.at[s, j], self.mate_recv.at[s, j], **self.near[2])

    def load(self):
        return pltpu.make_async_copy(self.src, self.stage, self.local.at[0])

    def keep(self, j):
        rows = self.src.shape[0] // NCH
        whole = self.stage if self.stage is not None else self.src
        return pltpu.make_async_copy(whole.at[pl.ds(j * rows, rows), :], self.here(0, 0, j), self.local.at[1])

    def begin(self):
        half = NCH // 2
        if self.stage is not None:
            self.load().start()
        for i in range(NCH):
            self.own(0, i).start()
            self.own(1, (i + half) % NCH).start()
        for j in range(NCH):
            self.mate(0, j).start()

    def arrived(self, s, j):
        done(self.here(0, s, j), self.recv.at[s - 1, j])

    def first(self):
        half = NCH // 2
        for i in range(half):
            self.arrived(1, i)
            self.relay(0, i).start()
            self.mate(1, i).start()
            self.arrived(2, half + i)
            self.relay(1, half + i).start()
            self.mate(2, half + i).start()

    def second(self):
        half = NCH // 2
        if self.stage is not None:
            self.load().wait()
        for j in range(NCH):
            self.keep(j).start()
        for i in range(half):
            self.arrived(1, half + i)
            self.mate(1, half + i).start()
            self.arrived(2, i)
            self.mate(2, i).start()
        for i in range(half):
            for j in (i, half + i):
                self.arrived(3, j)
                self.mate(3, j).start()

    def finish(self):
        half = NCH // 2
        for s in range(4):
            for j in range(NCH):
                done(self.here(1, s, j), self.mate_recv.at[s, j])
                self.mate(s, j).wait_send()
        for j in range(NCH):
            self.own(0, j).wait_send()
            self.own(1, j).wait_send()
            self.relay(0 if j < half else 1, j).wait_send()
        whole = self.stage if self.stage is not None else self.src
        done(whole, self.local.at[1])


def gather_kernel(place_of, x_ref, out_ref, stage, *sems):
    near_x, near_y, mate = plane_peers()
    greet([near_x, near_y, mate])
    gather = Gather(x_ref, out_ref, place_of(*x_ref.shape), stage, sems)
    gather.begin()
    gather.first()
    gather.second()
    gather.finish()


def gather_call(x, shape, place_of, cid, name):
    return pl.pallas_call(
        functools.partial(gather_kernel, place_of),
        in_specs=[ANY],
        out_specs=ANY,
        out_shape=jax.ShapeDtypeStruct(shape, x.dtype),
        scratch_shapes=[pltpu.VMEM(x.shape, x.dtype)] + Gather.sems(),
        compiler_params=pltpu.CompilerParams(collective_id=cid, has_side_effects=True),
        name=name,
    )(x)


def gather_tokens(x, cid):
    tok, width = x.shape
    return gather_call(x, (2 * tok, 4 * width), token_place, cid, "gather_tokens")


def gather_heads(x, cid):
    span, width = x.shape
    return gather_call(x, (span, 8 * width), head_place, cid, "gather_heads")


class Reduce:
    def __init__(self, part, scratch, sems):
        self.part = part
        self.own, self.given, self.sent, self.got_one, self.got_two = scratch
        self.loads, self.mate_send, self.mate_recv, self.one_send, self.one_recv, self.two_send, self.two_recv = sems
        self.near = plane_peers()
        self.h = self.own.shape[0] // 2
        self.width = self.own.shape[1] // 4

    @staticmethod
    def scratch(tok, full):
        h, w = tok // 2, full // 4
        shapes = [(tok, full), (tok, full), (2, 3, h, w), (2, 2, h, w), (2, h, w)]
        return [pltpu.VMEM(s, BF) for s in shapes]

    @staticmethod
    def sems():
        return [pltpu.SemaphoreType.DMA((2,))] * 7

    def lines(self, a):
        return pl.ds(a * self.h, self.h)

    def give(self, a):
        src = self.part.at[pl.ds((2 + a) * self.h, self.h), :]
        return remote(src, self.given.at[self.lines(a), :], self.mate_send.at[a], self.mate_recv.at[a], **self.near[2])

    def load(self, a):
        return pltpu.make_async_copy(self.part.at[self.lines(a), :], self.own.at[self.lines(a), :], self.loads.at[a])

    def one(self, a):
        src = self.sent.at[a, pl.ds(0, 2)]
        return remote(src, self.got_one.at[a], self.one_send.at[a], self.one_recv.at[a], **self.near[a])

    def two(self, a):
        return remote(self.sent.at[a, 2], self.got_two.at[a], self.two_send.at[a], self.two_recv.at[a], **self.near[1 - a])

    def pair(self, a, s):
        cols = pl.ds(s * self.width, self.width)
        rows = self.lines(a)
        return self.own[rows, cols].astype(F32) + self.given[rows, cols].astype(F32)

    def begin(self):
        for a in range(2):
            self.give(a).start()
            self.load(a).start()

    def first(self, a):
        self.load(a).wait()
        done(self.given.at[self.lines(a), :], self.mate_recv.at[a])
        for i, s in enumerate((a + 1, 3)):
            self.sent[a, i] = self.pair(a, s).astype(BF)
        self.one(a).start()

    def second(self, a):
        done(self.got_one.at[a], self.one_recv.at[a])
        self.sent[a, 2] = (self.pair(a, 2 - a) + self.got_one[a, 1].astype(F32)).astype(BF)
        self.two(a).start()

    def total(self, a):
        done(self.got_two.at[a], self.two_recv.at[a])
        return self.pair(a, 0) + self.got_one[a, 0].astype(F32) + self.got_two[a].astype(F32)

    def finish(self):
        for a in range(2):
            self.give(a).wait_send()
            self.one(a).wait_send()
            self.two(a).wait_send()


def first_gather_kernel(
    x_ref, wq_ref, wkv_ref, gain_ref, out_ref, wq_out, wkv_out, gain_out,
    stage, wq_stage, wkv_stage, gain_stage, stage_sem, small_send, small_recv, *sems,
):
    near_x, near_y, mate = plane_peers()
    col = lax.axis_index("col")
    tok, width = x_ref.shape
    wide = wq_ref.shape[1] // 4
    thin = wkv_ref.shape[1] // 4

    def share(ref, owner, size):
        return ref.at[:, pl.ds(pl.multiple_of(owner * size, LANES), size)]

    loads = [
        pltpu.make_async_copy(share(wq_ref, col, wide), wq_stage, stage_sem.at[0]),
        pltpu.make_async_copy(share(wkv_ref, col, thin), wkv_stage, stage_sem.at[1]),
        pltpu.make_async_copy(gain_ref, gain_stage, stage_sem.at[2]),
    ]
    for c in loads:
        c.start()
    greet([near_x, near_y, {"col": 3 - col}, mate])
    smalls = []
    for s, peer in ((1, near_x), (2, near_y), (3, {"col": 3 - col})):
        owner = peer["col"]
        lines = pl.ds(s * width, width)
        smalls += [
            remote(share(wq_ref, owner, wide), wq_out.at[lines, :], small_send.at[0, s], small_recv.at[0, s], **peer),
            remote(share(wkv_ref, owner, thin), wkv_out.at[lines, :], small_send.at[1, s], small_recv.at[1, s], **peer),
            remote(gain_ref, gain_out.at[:, lines], small_send.at[2, s], small_recv.at[2, s], **peer),
        ]
    gather = Gather(x_ref, out_ref, token_place(tok, width), stage, sems)
    gather.begin()
    for c in smalls:
        c.start()
    lines = pl.ds(0, width)
    keeps = [
        pltpu.make_async_copy(wq_stage, wq_out.at[lines, :], stage_sem.at[3]),
        pltpu.make_async_copy(wkv_stage, wkv_out.at[lines, :], stage_sem.at[4]),
        pltpu.make_async_copy(gain_stage, gain_out.at[:, lines], stage_sem.at[5]),
    ]
    for load, keep in zip(loads, keeps):
        load.wait()
        keep.start()
    gather.first()
    gather.second()
    gather.finish()
    for c in smalls:
        c.wait()
    for c in keeps:
        c.wait()


def first_gather(x, wq, wkv, gains, cid):
    tok, width = x.shape
    wide, thin = wq.shape[1] // 4, wkv.shape[1] // 4
    return pl.pallas_call(
        first_gather_kernel,
        in_specs=[ANY] * 4,
        out_specs=[ANY] * 4,
        out_shape=[
            jax.ShapeDtypeStruct((2 * tok, 4 * width), BF),
            jax.ShapeDtypeStruct((4 * width, wide), BF),
            jax.ShapeDtypeStruct((4 * width, thin), BF),
            jax.ShapeDtypeStruct((8, 4 * width), F32),
        ],
        scratch_shapes=[
            pltpu.VMEM((tok, width), BF),
            pltpu.VMEM((width, wide), BF),
            pltpu.VMEM((width, thin), BF),
            pltpu.VMEM((8, width), F32),
            pltpu.SemaphoreType.DMA((6,)),
            pltpu.SemaphoreType.DMA((3, 4)),
            pltpu.SemaphoreType.DMA((3, 4)),
        ]
        + Gather.sems(),
        compiler_params=pltpu.CompilerParams(collective_id=cid, has_side_effects=True),
        name="first_gather",
    )(x, wq, wkv, gains)


def grad_plan(kind, shape):
    rows, cols = shape
    if kind == "columns":
        w = rows // 4
        across = cols // CC
        return (
            (w // CR) * across,
            lambda s, k: (s * w + (k // across) * CR, lax.rem(k, across) * CC),
            (w, 4 * cols),
            lambda c, k: ((k // across) * CR, c * cols + lax.rem(k, across) * CC),
        )
    if kind == "rows":
        w = cols // 4
        return rows // CR, lambda s, k: (k * CR, s * w), (4 * rows, w), lambda c, k: (c * rows + k * CR, 0)
    w = rows // 4
    return w // CR, lambda s, k: (s * w + k * CR, 0), (rows, cols), lambda c, k: (c * w + k * CR, 0)


class GroupSum:
    def __init__(self, kinds, ins, outs, refs):
        (self.own, self.land, self.mids, self.tops, self.loads, self.in_send, self.in_recv, self.mid_send,
         self.mid_recv, self.top_send, self.top_recv, self.out_send, self.out_recv, self.far_send, self.far_recv) = refs
        self.ins, self.outs = ins, outs
        self.plans = [grad_plan(k, r.shape) for k, r in zip(kinds, ins)]
        self.counts = [4 * p[0] for p in self.plans]
        self.begins = [sum(self.counts[:i]) for i in range(len(ins))]
        self.total = sum(self.counts)
        z = lax.axis_index("dp")
        self.col = lax.axis_index("col")
        self.is_mid = (z == 1) | (z == 2)
        self.is_end = jnp.logical_not(self.is_mid)
        left = z < 2
        self.inward = {"dp": jnp.where(left, z + 1, z - 1)}
        self.outward = {"dp": jnp.where(left, z - 1, z + 1)}
        self.kept = jnp.where(left, 0, 1)

    @staticmethod
    def scratch(kinds):
        dma = pltpu.SemaphoreType.DMA
        return (
            [pltpu.VMEM((RING, CR, CC), BF)] * 2
            + [pltpu.VMEM((RING, HR, CC), BF)] * 2
            + [dma((RING,))] * 7
            + [dma((RING, 2))] * 3
            + [dma((len(kinds),))]
        )

    def greet(self, others):
        barrier = pltpu.get_barrier_semaphore()
        targets = [self.inward] + others
        for target in targets:
            pl.semaphore_signal(barrier, inc=1, device_id=target, device_id_type=MESH)

        @pl.when(self.is_mid)
        def _():
            pl.semaphore_signal(barrier, inc=1, device_id=self.outward, device_id_type=MESH)
            pl.semaphore_wait(barrier, len(targets) + 1)

        @pl.when(self.is_end)
        def _():
            pl.semaphore_wait(barrier, len(targets))

    def rows(self, half):
        return pl.ds(pl.multiple_of(half * HR, HR), HR)

    def load(self, j):
        slot = lax.rem(j, RING)
        for m, (per, place, _, _) in enumerate(self.plans):

            @pl.when((j >= self.begins[m]) & (j < self.begins[m] + self.counts[m]))
            def _(m=m, per=per, place=place):
                i = j - self.begins[m]
                r, q = place(i // per, lax.rem(i, per))
                src = self.ins[m].at[pl.ds(pl.multiple_of(r, CR), CR), pl.ds(pl.multiple_of(q, CC), CC)]
                pltpu.make_async_copy(src, self.own.at[slot], self.loads.at[slot]).start()

    def spread(self, j, half, src):
        slot = lax.rem(j, RING)
        for m, (per, _, _, place) in enumerate(self.plans):

            @pl.when((j >= self.begins[m]) & (j < self.begins[m] + self.counts[m]))
            def _(m=m, per=per, place=place):
                i = j - self.begins[m]
                s = i // per
                r, q = place(self.col, lax.rem(i, per))
                dst = self.outs[m].at[
                    pl.ds(pl.multiple_of(r + half * HR, HR), HR), pl.ds(pl.multiple_of(q, CC), CC)
                ]

                @pl.when(s == 0)
                def _():
                    pltpu.make_async_copy(src, dst, self.far_send.at[slot, half]).start()

                @pl.when(s > 0)
                def _():
                    owner = lax.rem(lax.rem(self.col, 2) + lax.rem(s, 2), 2) + 2 * lax.rem(self.col // 2 + s // 2, 2)
                    remote(src, dst, self.far_send.at[slot, half], self.far_recv.at[m], col=owner).start()

    def reclaim(self, j):
        slot = lax.rem(j, RING)
        for half in range(2):
            done(self.mids.at[slot], self.far_send.at[slot, half])

        @pl.when(self.is_mid)
        def _():
            done(self.mids.at[slot], self.mid_send.at[slot])
            done(self.mids.at[slot], self.top_send.at[slot])
            for half in range(2):
                done(self.mids.at[slot], self.out_send.at[slot, half])

        @pl.when(self.is_end)
        def _():
            done(self.own.at[slot], self.in_send.at[slot])

    def inbound(self, j):
        slot = lax.rem(j, RING)
        done(self.own.at[slot], self.loads.at[slot])

        @pl.when(self.is_mid)
        def _():
            done(self.land.at[slot], self.in_recv.at[slot])
            self.own[slot] = (self.own[slot].astype(F32) + self.land[slot].astype(F32)).astype(BF)
            src = self.own.at[slot, self.rows(1 - self.kept)]
            remote(src, self.mids.at[slot], self.mid_send.at[slot], self.mid_recv.at[slot], **self.inward).start()

        @pl.when(self.is_end)
        def _():
            remote(
                self.own.at[slot], self.land.at[slot], self.in_send.at[slot], self.in_recv.at[slot], **self.inward
            ).start()

    def middle(self, j):
        slot = lax.rem(j, RING)

        @pl.when(self.is_mid)
        def _():
            done(self.mids.at[slot], self.mid_recv.at[slot])
            rows = self.rows(self.kept)
            self.own[slot, rows] = (self.own[slot, rows].astype(F32) + self.mids[slot].astype(F32)).astype(BF)
            src = self.own.at[slot, rows]
            remote(src, self.tops.at[slot], self.top_send.at[slot], self.top_recv.at[slot], **self.inward).start()
            remote(
                src, self.land.at[slot, rows], self.out_send.at[slot, self.kept], self.out_recv.at[slot, self.kept],
                **self.outward,
            ).start()
            self.spread(j, self.kept, src)

    def settle(self, j):
        slot = lax.rem(j, RING)

        @pl.when(self.is_mid)
        def _():
            done(self.tops.at[slot], self.top_recv.at[slot])
            half = 1 - self.kept
            src = self.tops.at[slot]
            remote(
                src, self.land.at[slot, self.rows(half)], self.out_send.at[slot, half], self.out_recv.at[slot, half],
                **self.outward,
            ).start()
            self.spread(j, half, src)

    def outbound(self, j):
        slot = lax.rem(j, RING)

        @pl.when(self.is_end)
        def _():
            for half in range(2):
                src = self.land.at[slot, pl.ds(half * HR, HR)]
                done(src, self.out_recv.at[slot, half])
                self.spread(j, half, src)

    def tick(self, t):
        ahead = t + 1

        @pl.when(ahead < self.total)
        def _():
            @pl.when(ahead >= RING)
            def _():
                self.reclaim(ahead - RING)

            self.load(ahead)

        for off, stage in zip(OFFS, (self.inbound, self.middle, self.settle, self.outbound)):

            @pl.when((t >= off) & (t < self.total + off))
            def _(off=off, stage=stage):
                stage(t - off)

    def finish(self):
        def drain(j, carry):
            self.reclaim(j)
            return carry

        lax.fori_loop(self.total - RING, self.total, drain, 0)
        for m, out in enumerate(self.outs):
            done(out.at[pl.ds(0, 3 * out.shape[0] // 4)], self.far_recv.at[m])


MB = 128
AQ, AK = 256, 512


def backward_kernel(
    kinds,
    info_ref, gain_ref, gate_ref, up_ref, down_ref, part_ref, low_part_ref, resid_ref, low_ref, w_ref, mixed_ref,
    q_ref, k_ref, v_ref, wide_ref, lse_ref, turn_ref, wq_ref, wkv_ref, normed_ref, x_ref,
    out_gate, out_up, out_down, out_out, out_heads, mid_out, gain_part, attn_out, down_out, dot_out,
    cot_full, attn_part, grad_out, grad_heads,
    *refs,
):
    refs = list(refs)

    def take(count):
        taken = refs[:count]
        del refs[:count]
        return taken

    zsum = GroupSum(
        kinds,
        [gate_ref, up_ref, down_ref, grad_out, grad_heads],
        [out_gate, out_up, out_down, out_out, out_heads],
        take(15),
    )
    scratch = take(5)
    mlp_reduce = Reduce(part_ref, scratch, take(7))
    low_reduce = Reduce(low_part_ref, scratch, take(7))
    attn_reduce = Reduce(attn_part, scratch, take(7))
    mine, = take(1)
    tok, width = mine.shape
    gather = Gather(mine, cot_full, token_place(tok, width), None, take(Gather.SEMS))
    bufs, resid_buf, out_buf, sum_buf, buf_sem, out_sem, sum_sem = take(7)
    out_total, mixed_cot, q_cot, dq_sum, dk_sum, dv_sum, kv_cot, head_total, dots, dots_mate, dots_col = take(11)
    dot_send, dot_recv, ready, w_mine, w_sem = take(5)
    span = 2 * tok
    heads_width = mixed_ref.shape[1]
    heads = heads_width // HD
    half = lax.axis_index("row")
    col = lax.axis_index("col")
    length = info_ref[0]
    near_x, near_y, mate = plane_peers()
    corner = {"col": 3 - col}
    blocks = span // MB

    def mid_loads(i):
        slot = lax.rem(i, 2)
        lines = pl.ds(pl.multiple_of(i * MB, MB), MB)
        return [
            pltpu.make_async_copy(cot_full.at[lines, :], bufs.at[slot, 0], buf_sem.at[slot, 0]),
            pltpu.make_async_copy(low_ref.at[lines, :], bufs.at[slot, 1], buf_sem.at[slot, 1]),
            pltpu.make_async_copy(resid_ref.at[lines, :], resid_buf.at[slot], buf_sem.at[slot, 2]),
        ]

    def mid_store(i):
        lines = pl.ds(pl.multiple_of(i * MB, MB), MB)
        return pltpu.make_async_copy(out_buf.at[:, pl.ds(0, width)], mid_out.at[lines, :], out_sem.at[0])

    def mid_item(i):
        slot = lax.rem(i, 2)

        @pl.when(i + 1 < blocks)
        def _():
            for c in mid_loads(i + 1):
                c.start()

        for c in mid_loads(i):
            c.wait()
        cot = bufs[slot, 0].astype(F32)
        resid = resid_buf[slot]
        scale = lax.rsqrt(jnp.mean(resid * resid, axis=1, keepdims=True) + EPSILON)
        weighed = cot * gain_ref[1:2, :]
        inner = jnp.sum(weighed * resid, axis=1, keepdims=True)
        mid = bufs[slot, 1].astype(F32) + weighed * scale - resid * (scale * scale * scale * inner / D)
        low = mid.astype(BF)
        lines = pl.ds(pl.multiple_of(i * MB, MB), MB)
        mixed_cot[lines, :] = contract(low, w_mine[...], 1, 1).astype(BF)
        out_total[...] += contract(mixed_ref[lines, :], low, 0, 0)

        @pl.when(i < blocks // 2)
        def _():
            @pl.when(i > 0)
            def _():
                mid_store(i - 1).wait()

            out_buf[:, pl.ds(0, width)] = mid[:, :width]
            mid_store(i).start()
            part = jnp.sum((cot * resid * scale)[:, :width], axis=0, keepdims=True)
            gain_part[...] += jnp.broadcast_to(part, gain_part.shape)

        @pl.when(i == blocks // 2)
        def _():
            mid_store(i - 1).wait()

    q_steps = span // AQ
    rows = heads * AQ
    pieces = [slice(h * HD, (h + 1) * HD) for h in range(heads)]

    def attn_item(q_step, tile, diagonal):
        stored = lax.rem(q_step + half * (q_steps // 2), q_steps)
        lines = pl.ds(pl.multiple_of(stored * AQ, AQ), AQ)
        key_tiles = span // AK
        keys = pl.ds(pl.multiple_of(lax.rem(tile + half * (key_tiles // 2), key_tiles) * AK, AK), AK)
        first = q_step * AQ
        q = jnp.concatenate([q_ref[lines, s] for s in pieces], axis=0)
        cot = jnp.concatenate([mixed_cot[lines, s] for s in pieces], axis=0)
        wide = jnp.concatenate([wide_ref[lines, s] for s in pieces], axis=0)
        place = first + lax.rem(lax.broadcasted_iota(jnp.int32, (1, rows), 1), AQ)
        log_total = jnp.where(place < length, lse_ref[q_step], -NEG_FILL)
        inner = jnp.sum(wide * cot.astype(F32), axis=1, keepdims=True)
        inner = jnp.broadcast_to(inner, (rows, LANES)).T[0:1, :]
        k_tile = k_ref[keys, :]
        v_tile = v_ref[keys, :]
        scores = contract(k_tile, q, 1, 1) * HD**-0.5 - log_total
        if diagonal:
            key_place = tile * AK + lax.broadcasted_iota(jnp.int32, (AK, rows), 0)
            scores = jnp.where(key_place <= place, scores, NEG_FILL)
        weights = jnp.exp(scores)
        prob_cot = contract(v_tile, cot, 1, 1)
        score_cot = (weights * (prob_cot - inner)).astype(BF)
        dv_sum[keys, :] += contract(weights.astype(BF), cot, 1, 0)
        dk_sum[keys, :] += contract(score_cot, q, 1, 0) * HD**-0.5
        dq = contract(score_cot, k_tile, 0, 0) * HD**-0.5

        @pl.when(tile == 0)
        def _():
            dq_sum[...] = dq

        @pl.when(tile > 0)
        def _():
            dq_sum[...] += dq

        if diagonal:
            cos, sin = turn_ref[lines, :HD], turn_ref[lines, HD:]
            for h in range(heads):
                part = dq_sum[h * AQ : (h + 1) * AQ, :]
                swapped = jnp.concatenate([part[:, HD // 2 :], -part[:, : HD // 2]], axis=1)
                q_cot[lines, h * HD : (h + 1) * HD] = (part * cos + swapped * sin).astype(BF)

    def attn_step(q_step):
        last = q_step * AQ // AK

        def body(tile, carry):
            attn_item(q_step, tile, False)
            return carry

        lax.fori_loop(0, last, body, 0)
        attn_item(q_step, last, True)

    def attn_finish():
        part = dk_sum[...]
        swapped = jnp.concatenate([part[:, HD // 2 :], -part[:, : HD // 2]], axis=1)
        kv_cot[:, :HD] = (part * turn_ref[:, :HD] + swapped * turn_ref[:, HD:]).astype(BF)
        kv_cot[:, HD:] = dv_sum[...].astype(BF)

    def head_loads(i):
        slot = lax.rem(i, 2)
        lines = pl.ds(pl.multiple_of(i * MB, MB), MB)
        return [
            pltpu.make_async_copy(normed_ref.at[lines, :], bufs.at[slot, 0], buf_sem.at[slot, 0]),
            pltpu.make_async_copy(x_ref.at[lines, :], bufs.at[slot, 1], buf_sem.at[slot, 1]),
        ]

    def head_store(i):
        lines = pl.ds(pl.multiple_of(i * MB, MB), MB)
        return pltpu.make_async_copy(bufs.at[lax.rem(i, 2), 2], attn_part.at[lines, :], out_sem.at[1])

    def head_item(i):
        slot = lax.rem(i, 2)

        @pl.when(i + 1 < blocks)
        def _():
            for c in head_loads(i + 1):
                c.start()

        for c in head_loads(i):
            c.wait()
        lines = pl.ds(pl.multiple_of(i * MB, MB), MB)
        qc = q_cot[lines, :]
        kv = kv_cot[lines, :]
        part = contract(qc, wq_ref[...], 1, 1) + contract(kv, wkv_ref[...], 1, 1)

        @pl.when(i > 0)
        def _():
            head_store(i - 1).wait()

        bufs[slot, 2] = part.astype(BF)
        head_store(i).start()
        inner = jnp.sum(part * gain_ref[0:1, :] * bufs[slot, 1].astype(F32), axis=1, keepdims=True)
        dots[pl.ds(i, 1), :] = jnp.broadcast_to(inner, (MB, LANES)).T[0:1, :]
        head_total[:, :heads_width] += contract(bufs[slot, 0], qc, 0, 0)
        head_total[:, heads_width:] += contract(bufs[slot, 0], kv, 0, 0)

    def head_finish():
        head_store(blocks - 1).wait()
        pieces = D // CC

        def store(i):
            lines = pl.ds(pl.multiple_of(i * CC, CC), CC)
            return pltpu.make_async_copy(sum_buf, grad_heads.at[lines, :], sum_sem.at[0])

        used = heads_width + 2 * HD
        for i in range(pieces):
            lines = pl.ds(i * CC, CC)
            sum_buf[:, :used] = head_total[lines, :].astype(BF)
            sum_buf[:, used:] = jnp.zeros((CC, CC - used), BF)
            store(i).start()
            store(i).wait()

    def grad_out_store():
        wide_out = out_total.shape[1] // CC
        for i in range(wide_out):
            cols = pl.ds(i * CC, CC)
            sum_buf[: heads_width, :] = out_total[:, cols].astype(BF)
            c = pltpu.make_async_copy(sum_buf.at[pl.ds(0, heads_width), :], grad_out.at[:, cols], sum_sem.at[0])
            c.start()
            c.wait()

    def dot_give():
        n = blocks // 2
        return remote(dots.at[pl.ds(n, n), :], dots_mate, dot_send.at[0], dot_recv.at[0], **mate)

    def dot_share():
        n = blocks // 2
        return [
            remote(dots.at[pl.ds(0, n), :], dots_col.at[s], dot_send.at[1 + s], dot_recv.at[1 + s], **peer)
            for s, peer in enumerate((near_x, near_y, corner))
        ]

    def emit(work, out, sem):
        for a in range(2):
            sum_total = work.total(a)
            h = tok // 4
            for b in range(2):
                lines = pl.ds(a * 2 * h + b * h, h)
                resid_sum = sum_total[b * h : (b + 1) * h]
                emit_buf[...] = resid_sum
                c = pltpu.make_async_copy(emit_buf, out.at[lines, :], sem)
                c.start()
                c.wait()

    emit_buf, = take(1)

    pltpu.make_async_copy(w_ref.at[pl.ds(pl.multiple_of(col * heads_width, heads_width), heads_width), :], w_mine, w_sem.at[0]).start()
    zsum.load(jnp.int32(0))
    gain_part[...] = jnp.zeros_like(gain_part)
    out_total[...] = jnp.zeros_like(out_total)
    head_total[...] = jnp.zeros_like(head_total)
    dk_sum[...] = jnp.zeros_like(dk_sum)
    dv_sum[...] = jnp.zeros_like(dv_sum)
    zsum.greet([near_x, near_y, corner, mate])

    at = {}

    def plan(tick, action):
        at.setdefault(tick, []).append(action)

    def start_all(copies):
        for c in copies:
            c.start()

    plan(0, mlp_reduce.begin)
    plan(T_ONE, lambda: [mlp_reduce.first(a) for a in range(2)])
    plan(T_TWO, lambda: [mlp_reduce.second(a) for a in range(2)])

    def own_block():
        for a in range(2):
            mine[mlp_reduce.lines(a), :] = mlp_reduce.total(a).astype(BF)
        gather.begin()

    plan(T_SUM, own_block)
    plan(T_GATHER, gather.first)
    plan(T_GATHER + 3, gather.second)

    def start_mid():
        gather.finish()
        mlp_reduce.finish()
        pltpu.make_async_copy(w_ref.at[pl.ds(0, heads_width), :], w_mine, w_sem.at[0]).wait()
        start_all(mid_loads(jnp.int32(0)))
        low_reduce.begin()

    plan(T_MID, start_mid)
    plan(T_MID + 4, lambda: [low_reduce.first(a) for a in range(2)])
    plan(T_MID + 9, lambda: [low_reduce.second(a) for a in range(2)])

    def low_done():
        emit(low_reduce, down_out, out_sem.at[2])
        low_reduce.finish()
        for i, peer in enumerate((near_x, near_y, mate)):
            pl.semaphore_signal(ready.at[i], inc=1, device_id=peer, device_id_type=MESH)

    plan(T_MID + 13, low_done)
    t_attn = T_MID + 1 + blocks // 2
    plan(t_attn, grad_out_store)
    t_head = t_attn + q_steps
    plan(t_head, lambda: (attn_finish(), start_all(head_loads(jnp.int32(0)))))
    t_last = t_head + 1 + blocks // 2

    def start_last():
        head_finish()
        dot_give().start()
        for i in range(3):
            pl.semaphore_wait(ready.at[i], 1)
        attn_reduce.begin()

    plan(t_last, start_last)

    def last_first():
        n = blocks // 2
        done(dots_mate, dot_recv.at[0])
        dot_give().wait_send()
        dots[pl.ds(0, n), :] = dots[pl.ds(0, n), :] + dots_mate[...]
        start_all(dot_share())
        for a in range(2):
            attn_reduce.first(a)

    plan(t_last + 3, last_first)
    plan(t_last + 7, lambda: [attn_reduce.second(a) for a in range(2)])

    def last_done():
        n = blocks // 2
        shares = dot_share()
        for c in shares:
            c.wait()
        terms = [dots[pl.ds(0, n), :], dots_col[0], dots_col[1], dots_col[2]]
        dot_out[...] = (terms[0] + terms[1]) + (terms[2] + terms[3])
        emit(attn_reduce, attn_out, out_sem.at[2])
        attn_reduce.finish()

    plan(t_last + 10, last_done)
    final = max(zsum.total + OFFS[3], t_last + 11)

    def tick(t, carry):
        zsum.tick(t)
        for when in sorted(at):

            @pl.when(t == when)
            def _(when=when):
                for action in at[when]:
                    action()

        @pl.when((t > T_MID) & (t < t_attn))
        def _():
            for e in range(2):
                mid_item((t - T_MID - 1) * 2 + e)

        @pl.when((t >= t_attn) & (t < t_head))
        def _():
            attn_step(t - t_attn)

        @pl.when((t > t_head) & (t < t_last))
        def _():
            for e in range(2):
                head_item((t - t_head - 1) * 2 + e)

        return carry

    lax.fori_loop(0, final, tick, 0)
    zsum.finish()


T_ONE, T_TWO, T_SUM, T_GATHER, T_MID = 2, 8, 12, 15, 22


def backward(info, gains, grads, mlp_part, low_part, resid, low, w_out_full, mixed, q, k, v, wide, lse, cos, sin,
             wq, wkv, normed, tokens_full, cid):
    span, full = normed.shape
    tok, width = span // 2, full // 4
    heads_width = mixed.shape[1]
    heads = heads_width // HD
    kinds = ["columns", "columns", "rows", "rows", "stack"]
    sources = [g.shape for g in grads] + [(heads_width, full), (full, CC)]
    outs = [jax.ShapeDtypeStruct(grad_plan(kd, s)[2], BF) for kd, s in zip(kinds, sources)]
    vmem = pl.BlockSpec(memory_space=pltpu.VMEM)
    dma = pltpu.SemaphoreType.DMA
    blocks = span // MB
    turn = jnp.concatenate([cos, sin], axis=1)
    lse = lse.reshape(span // QB, heads, QB // AQ, AQ).transpose(0, 2, 1, 3).reshape(span // AQ, 1, heads * AQ)
    shapes = outs + [
        jax.ShapeDtypeStruct((tok, width), F32),
        jax.ShapeDtypeStruct((8, width), F32),
        jax.ShapeDtypeStruct((tok, width), F32),
        jax.ShapeDtypeStruct((tok, width), F32),
        jax.ShapeDtypeStruct((blocks // 2, LANES), F32),
        jax.ShapeDtypeStruct((span, full), BF),
        jax.ShapeDtypeStruct((span, full), BF),
        jax.ShapeDtypeStruct((heads_width, full), BF),
        jax.ShapeDtypeStruct((full, CC), BF),
    ]
    out_specs = [ANY] * 5 + [ANY, vmem, ANY, ANY, vmem, ANY, ANY, ANY, ANY]
    scratch = (
        GroupSum.scratch(kinds)
        + Reduce.scratch(tok, full)
        + Reduce.sems() * 3
        + [pltpu.VMEM((tok, width), BF)]
        + Gather.sems()
        + [
            pltpu.VMEM((2, 3, MB, full), BF),
            pltpu.VMEM((2, MB, full), F32),
            pltpu.VMEM((MB, width), F32),
            pltpu.VMEM((CC, CC), BF),
            dma((2, 3)),
            dma((3,)),
            dma((1,)),
            pltpu.VMEM((heads_width, full), F32),
            pltpu.VMEM((span, heads_width), BF),
            pltpu.VMEM((span, heads_width), BF),
            pltpu.VMEM((heads * AQ, HD), F32),
            pltpu.VMEM((span, HD), F32),
            pltpu.VMEM((span, HD), F32),
            pltpu.VMEM((span, 2 * HD), BF),
            pltpu.VMEM((full, heads_width + 2 * HD), F32),
            pltpu.VMEM((blocks, LANES), F32),
            pltpu.VMEM((blocks // 2, LANES), F32),
            pltpu.VMEM((3, blocks // 2, LANES), F32),
            dma((4,)),
            dma((4,)),
            pltpu.SemaphoreType.REGULAR((3,)),
            pltpu.VMEM((heads_width, full), BF),
            dma((1,)),
            pltpu.VMEM((tok // 4, width), F32),
        ]
    )
    results = pl.pallas_call(
        functools.partial(backward_kernel, kinds),
        in_specs=[pl.BlockSpec(memory_space=pltpu.SMEM), vmem] + [ANY] * 8 + [vmem] * 9 + [ANY] * 2,
        out_specs=out_specs,
        out_shape=shapes,
        scratch_shapes=scratch,
        compiler_params=pltpu.CompilerParams(
            collective_id=cid, has_side_effects=True, vmem_limit_bytes=VMEM_ALL
        ),
        name="backward",
    )(info, gains, *grads, mlp_part, low_part, resid, low, w_out_full, mixed, q, k, v, wide, lse, turn, wq, wkv,
      normed, tokens_full)
    return results[:10]


def by_distance(stacked, dim):
    count = lax.axis_size("col")
    order = lax.axis_index("col") ^ jnp.arange(count)
    blocks = jnp.take(stacked, order, axis=0)
    return jnp.concatenate([blocks[i] for i in range(count)], axis=dim)


def plain_gather(x):
    cols = by_distance(lax.all_gather(x, "col"), 1)
    return jnp.concatenate([cols, swap(cols, "row", 1)], axis=0)


def plain_gather_heads(x):
    mine = lax.all_gather(x, "col", axis=1, tiled=True)
    half = x.shape[0] // 2
    other = swap(mine, "row", 1)
    other = jnp.concatenate([other[half:], other[:half]], axis=0)
    return jnp.concatenate([mine, other], axis=1)


def plain_reduce(part):
    span, full = part.shape
    count = lax.axis_size("col")
    width = full // count
    half = part[: span // 2].astype(F32) + swap(part[span // 2 :], "row", 1).astype(F32)
    order = lax.axis_index("col") ^ jnp.arange(count)
    blocks = jnp.stack([half[:, s * width : (s + 1) * width] for s in range(count)])
    return lax.psum_scatter(jnp.take(blocks, order, axis=0), "col", tiled=False)


def exchange(packs):
    if kernels_fit():
        return [p if s == 0 else swap(p, "col", s) for s, p in enumerate(packs)]
    count = len(packs)
    order = lax.axis_index("col") ^ jnp.arange(count)
    sent = jnp.take(jnp.stack(packs), order, axis=0)
    blocks = jnp.take(lax.all_to_all(sent, "col", 0, 0, tiled=True), order, axis=0)
    return [blocks[i] for i in range(count)]


def plain_group_sum(grads, kinds):
    outs = []
    count = lax.axis_size("col")
    order = lax.axis_index("col") ^ jnp.arange(count)
    for grad, kind in zip(grads, kinds):
        grad = lax.psum(grad.astype(F32), "dp").astype(BF)
        dim = 1 if kind == "rows" else 0
        blocks = jnp.stack(jnp.split(grad, count, axis=dim))
        blocks = lax.all_to_all(jnp.take(blocks, order, axis=0), "col", 0, 0, tiled=True)
        out_dim = 1 if kind == "columns" else 0
        outs.append(jnp.concatenate([blocks[i] for i in range(count)], axis=out_dim))
    return outs


def kernels_fit():
    return lax.axis_size("col") == 4 and lax.axis_size("dp") == 4 and lax.axis_size("row") == 2


def attn_forward_kernel(info_ref, q_ref, k_ref, v_ref, *refs):
    linked = len(refs) > 6
    if linked:
        side_ref, mixed_ref, wide_ref, lse_ref, peak_ref, side_out, score_ref, sum_ref, stage = refs[:9]
        gather = Gather(side_ref, side_out, token_place(*side_ref.shape), stage, refs[9:])
    else:
        mixed_ref, wide_ref, lse_ref, peak_ref, score_ref, sum_ref = refs
    heads = q_ref.shape[1] // HD
    span = k_ref.shape[0]
    rows = heads * QB
    length = info_ref[0]
    half = lax.axis_index("row")
    step = pl.program_id(0)
    first = step * QB
    key_tiles = span // FWD_KB
    steps = span // QB
    lines = pl.ds(pl.multiple_of(lax.rem(step + half * (steps // 2), steps) * QB, QB), QB)

    if linked:

        @pl.when(step == 0)
        def _():
            greet(list(gather.near))
            gather.begin()

        @pl.when(step == steps - 1)
        def _():
            gather.first()

    q = jnp.concatenate([q_ref[lines, h * HD : (h + 1) * HD] for h in range(heads)], axis=0)
    tiles = (first + QB) // FWD_KB
    plain = first // FWD_KB

    def tile_of(ref, tile):
        stored = lax.rem(tile + half * (key_tiles // 2), key_tiles)
        return ref[pl.ds(pl.multiple_of(stored * FWD_KB, FWD_KB), FWD_KB), :]

    def fold(values, running, op):
        for t in range(FWD_KB // LANES):
            running = op(running, values[:, t * LANES : (t + 1) * LANES])
        return running

    def scores_of(tile, top, diagonal):
        scores = contract(q, tile_of(k_ref, tile), 1, 1) * HD**-0.5
        if diagonal:
            place = first + lax.broadcasted_iota(jnp.int32, (QB, FWD_KB), 0)
            key_place = tile * FWD_KB + lax.broadcasted_iota(jnp.int32, (QB, FWD_KB), 1)
            allowed = (key_place <= place) & (key_place < length)
            scores = jnp.where(allowed[None], scores.reshape(heads, QB, FWD_KB), NEG_FILL)
            scores = scores.reshape(rows, FWD_KB)
        else:
            key_place = tile * FWD_KB + lax.broadcasted_iota(jnp.int32, (1, FWD_KB), 1)
            scores = jnp.where(key_place < length, scores, NEG_FILL)
        score_ref[tile] = scores
        return fold(scores, top, jnp.maximum)

    top = jnp.full((rows, LANES), NEG_FILL, F32)
    top = lax.fori_loop(0, plain, lambda tile, top: scores_of(tile, top, False), top)
    top = lax.fori_loop(plain, tiles, lambda tile, top: scores_of(tile, top, True), top)
    top = jnp.max(top, axis=1, keepdims=True)
    live = first + lax.broadcasted_iota(jnp.int32, (QB, 1), 0) < length
    peak = jnp.max(jnp.where(live[None], top.reshape(heads, QB, 1), NEG_FILL), axis=1)

    @pl.when(step == 0)
    def _():
        peak_ref[...] = jnp.full_like(peak_ref, NEG_FILL)

    peak_ref[...] = jnp.maximum(peak_ref[...], jnp.broadcast_to(peak, peak_ref.shape))
    sum_ref[...] = jnp.zeros_like(sum_ref)

    def weigh(tile, total):
        weights = jnp.exp(score_ref[tile] - top)
        sum_ref[...] += contract(weights.astype(BF), tile_of(v_ref, tile), 1, 0)
        return fold(weights, total, jnp.add)

    total = lax.fori_loop(0, tiles, weigh, jnp.zeros((rows, LANES), F32))
    total = jnp.sum(total, axis=1, keepdims=True)
    mixed = sum_ref[...] / total
    log_total = jnp.broadcast_to(top + jnp.log(total), (rows, LANES))
    lse_ref[step] = log_total.T[0:1, :]
    for h in range(heads):
        part = mixed[h * QB : (h + 1) * QB]
        mixed_ref[lines, h * HD : (h + 1) * HD] = part.astype(BF)
        wide_ref[lines, h * HD : (h + 1) * HD] = part

    if linked:

        @pl.when(step == steps - 1)
        def _():
            gather.second()
            gather.finish()


def attn_forward(info, q, k, v, side=None, cid=None):
    span, width = q.shape
    heads = width // HD
    steps = span // QB
    whole = lambda shape: pl.BlockSpec(shape, lambda i: (0,) * len(shape))
    pairs = heads * span * span // 2
    shapes = [
        jax.ShapeDtypeStruct((span, width), BF),
        jax.ShapeDtypeStruct((span, width), F32),
        jax.ShapeDtypeStruct((steps, 1, heads * QB), F32),
        jax.ShapeDtypeStruct((heads, LANES), F32),
    ]
    in_specs = [pl.BlockSpec(memory_space=pltpu.SMEM)] + [whole(a.shape) for a in (q, k, v)]
    out_specs = [whole(s.shape) for s in shapes]
    scratch = [
        pltpu.VMEM((span // FWD_KB, heads * QB, FWD_KB), F32),
        pltpu.VMEM((heads * QB, HD), F32),
    ]
    operands = [info, q, k, v]
    params = dict(vmem_limit_bytes=48 * MIB)
    if side is not None:
        tok, wide = side.shape
        operands.append(side)
        in_specs.append(ANY)
        out_specs.append(ANY)
        shapes.append(jax.ShapeDtypeStruct((2 * tok, 4 * wide), side.dtype))
        scratch += [pltpu.VMEM(side.shape, side.dtype)] + Gather.sems()
        params.update(collective_id=cid, has_side_effects=True)
    return pl.pallas_call(
        attn_forward_kernel,
        grid=(steps,),
        in_specs=in_specs,
        out_specs=out_specs,
        scratch_shapes=scratch,
        out_shape=shapes,
        compiler_params=pltpu.CompilerParams(**params),
        cost_estimate=pl.CostEstimate(
            flops=40 * pairs * HD // 4, transcendentals=pairs, bytes_accessed=8 * span * width
        ),
        name="attn_forward",
    )(*operands)


def turn_back(values, cos_ref, sin_ref):
    half = HD // 2
    swapped = jnp.concatenate([values[:, half:], -values[:, :half]], axis=1)
    return values * cos_ref[...] + swapped * sin_ref[...]


def attn_backward_kernel(
    info_ref, q_ref, k_ref, v_ref, cot_ref, wide_ref, lse_ref, cosq_ref, sinq_ref, cosk_ref, sink_ref,
    dq_ref, dk_ref, dv_ref, dq_sum, dk_sum, dv_sum,
):
    heads = q_ref.shape[1] // HD
    span = k_ref.shape[0]
    rows = heads * QB
    length = info_ref[0]
    half = info_ref[1]
    step = pl.program_id(0)
    first = step * QB
    key_tiles = span // BWD_KB

    @pl.when(step == 0)
    def _():
        dk_sum[...] = jnp.zeros_like(dk_sum)
        dv_sum[...] = jnp.zeros_like(dv_sum)

    dq_sum[...] = jnp.zeros_like(dq_sum)

    @pl.when(first < length)
    def _():
        pieces = [slice(h * HD, (h + 1) * HD) for h in range(heads)]
        q = jnp.concatenate([q_ref[:, s] for s in pieces], axis=0)
        cot = jnp.concatenate([cot_ref[:, s] for s in pieces], axis=0)
        wide = jnp.concatenate([wide_ref[:, s] for s in pieces], axis=0)
        log_total = lse_ref[0]
        inner = jnp.sum(wide * cot.astype(F32), axis=1, keepdims=True)
        inner = jnp.broadcast_to(inner, (rows, LANES)).T[0:1, :]

        def tile_step(tile, masked):
            stored = lax.rem(tile + half * (key_tiles // 2), key_tiles)
            keys = pl.ds(pl.multiple_of(stored * BWD_KB, BWD_KB), BWD_KB)
            k_tile = k_ref[keys, :]
            v_tile = v_ref[keys, :]
            scores = contract(k_tile, q, 1, 1) * HD**-0.5 - log_total
            if masked:
                key_place = tile * BWD_KB + lax.broadcasted_iota(jnp.int32, (BWD_KB, rows), 0)
                place = first + lax.rem(lax.broadcasted_iota(jnp.int32, (BWD_KB, rows), 1), QB)
                scores = jnp.where((key_place <= place) & (key_place < length), scores, NEG_FILL)
            weights = jnp.exp(scores)
            prob_cot = contract(v_tile, cot, 1, 1)
            score_cot = (weights * (prob_cot - inner)).astype(BF)
            dv_sum[keys, :] += contract(weights.astype(BF), cot, 1, 0)
            dk_sum[keys, :] += contract(score_cot, q, 1, 0) * HD**-0.5
            dq_sum[...] += contract(score_cot, k_tile, 0, 0) * HD**-0.5

        @pl.loop(0, first // BWD_KB)
        def _(tile):
            tile_step(tile, False)

        @pl.loop(first // BWD_KB, pl.cdiv(first + QB, BWD_KB))
        def _(tile):
            tile_step(tile, True)

    for h in range(heads):
        part = turn_back(dq_sum[h * QB : (h + 1) * QB, :], cosq_ref, sinq_ref)
        dq_ref[:, h * HD : (h + 1) * HD] = part.astype(dq_ref.dtype)

    @pl.when(step == pl.num_programs(0) - 1)
    def _():
        dk_ref[...] = turn_back(dk_sum[...], cosk_ref, sink_ref).astype(dk_ref.dtype)
        dv_ref[...] = dv_sum[...].astype(dv_ref.dtype)


def attn_backward(info, q, k, v, cot, wide, lse, cos, sin, kv_type):
    span, width = q.shape
    heads = width // HD
    steps = span // QB

    def stored(i, info_ref):
        return (lax.rem(i + info_ref[1] * (steps // 2), steps), 0)

    whole = pl.BlockSpec((span, HD), lambda i, info_ref: (0, 0))
    mine = pl.BlockSpec((QB, width), stored)
    turn = pl.BlockSpec((QB, HD), stored)
    pairs = heads * span * span // 2
    return pl.pallas_call(
        attn_backward_kernel,
        grid_spec=pltpu.PrefetchScalarGridSpec(
            num_scalar_prefetch=1,
            grid=(steps,),
            in_specs=[
                mine, whole, whole, mine, mine,
                pl.BlockSpec((1, 1, heads * QB), lambda i, info_ref: (i, 0, 0)),
                turn, turn, whole, whole,
            ],
            out_specs=[mine, whole, whole],
            scratch_shapes=[
                pltpu.VMEM((heads * QB, HD), F32),
                pltpu.VMEM((span, HD), F32),
                pltpu.VMEM((span, HD), F32),
            ],
        ),
        out_shape=[
            jax.ShapeDtypeStruct((span, width), BF),
            jax.ShapeDtypeStruct((span, HD), kv_type),
            jax.ShapeDtypeStruct((span, HD), kv_type),
        ],
        compiler_params=pltpu.CompilerParams(vmem_limit_bytes=40 * 2**20),
        cost_estimate=pl.CostEstimate(
            flops=60 * pairs * HD // 4, transcendentals=pairs, bytes_accessed=12 * span * width
        ),
        name="attn_backward",
    )(info, q, k, v, cot, wide, lse, cos, sin, cos, sin)


def head_kernel(x_ref, gain_ref, wq_ref, wkv_ref, cos_ref, sin_ref, normed_ref, q_ref, k_ref, v_ref, scale_ref):
    x = x_ref[...].astype(F32)
    scale = lax.rsqrt(jnp.mean(x * x, axis=1, keepdims=True) + EPSILON)
    scale_ref[...] = jnp.broadcast_to(scale, scale_ref.shape)
    normed = (x * scale * gain_ref[0:1, :]).astype(BF)
    normed_ref[...] = normed

    def turned(raw):
        pieces = []
        half = HD // 2
        for h in range(raw.shape[1] // HD):
            pieces += [-raw[:, h * HD + half : (h + 1) * HD], raw[:, h * HD : h * HD + half]]
        pieces = jnp.concatenate(pieces, axis=1)
        count = raw.shape[1] // HD
        cos = jnp.concatenate([cos_ref[...]] * count, axis=1)
        sin = jnp.concatenate([sin_ref[...]] * count, axis=1)
        return (raw * cos + pieces * sin).astype(BF)

    q_ref[...] = turned(contract(normed, wq_ref[...], 1, 0))
    keyval = contract(normed, wkv_ref[...], 1, 0)
    k_ref[...] = turned(keyval[:, :HD])
    v_ref[...] = keyval[:, HD:].astype(BF)


def project_heads(tokens_full, gains, wq, wkv, cos, sin):
    span, full = tokens_full.shape
    width = wq.shape[1]
    block = 512
    line = lambda n: pl.BlockSpec((block, n), lambda i: (i, 0))
    whole = lambda a: pl.BlockSpec(a.shape, lambda i: (0, 0))
    return pl.pallas_call(
        head_kernel,
        grid=(span // block,),
        in_specs=[line(full), whole(gains), whole(wq), whole(wkv), line(HD), line(HD)],
        out_specs=[line(full), line(width), line(HD), line(HD), line(LANES)],
        out_shape=[
            jax.ShapeDtypeStruct((span, full), BF),
            jax.ShapeDtypeStruct((span, width), BF),
            jax.ShapeDtypeStruct((span, HD), BF),
            jax.ShapeDtypeStruct((span, HD), BF),
            jax.ShapeDtypeStruct((span, LANES), F32),
        ],
        compiler_params=pltpu.CompilerParams(vmem_limit_bytes=48 * MIB),
        cost_estimate=pl.CostEstimate(
            flops=2 * span * full * (width + LANES), transcendentals=0, bytes_accessed=5 * span * full
        ),
        name="project_heads",
    )(tokens_full, gains, wq, wkv, cos, sin)


def project_out_kernel(mixed_ref, w_ref, x_ref, gain_ref, *refs):
    linked = len(refs) > 2
    step = pl.program_id(0)
    if linked:
        side_ref, resid_ref, normed_ref, side_out, stage = refs[:5]
        gather = Gather(side_ref, side_out, token_place(*side_ref.shape), stage, refs[5:])

        @pl.when(step == 0)
        def _():
            greet(list(gather.near))
            gather.begin()

        @pl.when(step == pl.num_programs(0) // 2)
        def _():
            gather.first()

    else:
        resid_ref, normed_ref = refs
    resid = x_ref[...].astype(F32) + contract(mixed_ref[...], w_ref[...], 1, 0)
    resid_ref[...] = resid
    scale = lax.rsqrt(jnp.mean(resid * resid, axis=1, keepdims=True) + EPSILON)
    normed_ref[...] = (resid * scale * gain_ref[1:2, :]).astype(BF)

    if linked:

        @pl.when(step == pl.num_programs(0) - 1)
        def _():
            gather.second()
            gather.finish()


def project_out(mixed_full, w_out_full, tokens_full, gains, side=None, cid=None):
    span, full = tokens_full.shape
    block = 256
    line = pl.BlockSpec((block, full), lambda i: (i, 0))
    operands = [mixed_full, w_out_full, tokens_full, gains]
    in_specs = [
        pl.BlockSpec((block, mixed_full.shape[1]), lambda i: (i, 0)),
        pl.BlockSpec(w_out_full.shape, lambda i: (0, 0), pipeline_mode=pl.Buffered(1)),
        line,
        pl.BlockSpec(gains.shape, lambda i: (0, 0)),
    ]
    out_specs = [line, line]
    shapes = [jax.ShapeDtypeStruct((span, full), F32), jax.ShapeDtypeStruct((span, full), BF)]
    scratch = []
    params = dict(vmem_limit_bytes=48 * MIB)
    if side is not None:
        tok, wide = side.shape
        operands.append(side)
        in_specs.append(ANY)
        out_specs.append(ANY)
        shapes.append(jax.ShapeDtypeStruct((2 * tok, 4 * wide), side.dtype))
        scratch += [pltpu.VMEM(side.shape, side.dtype)] + Gather.sems()
        params.update(collective_id=cid, has_side_effects=True)
    return pl.pallas_call(
        project_out_kernel,
        grid=(span // block,),
        in_specs=in_specs,
        out_specs=out_specs,
        out_shape=shapes,
        scratch_shapes=scratch,
        compiler_params=pltpu.CompilerParams(**params),
        cost_estimate=pl.CostEstimate(
            flops=2 * span * full * full, transcendentals=0, bytes_accessed=12 * span * full
        ),
        name="project_out",
    )(*operands)


def middle_kernel(
    cot_ref, resid_ref, low_ref, gain_ref, w_ref, mixed_ref,
    mixed_cot_ref, own_ref, grad_ref, gain_part_ref, total_ref,
):
    step = pl.program_id(0)
    last = pl.num_programs(0) - 1
    width = own_ref.shape[1]
    cot = cot_ref[...].astype(F32)
    resid = resid_ref[...]
    scale = lax.rsqrt(jnp.mean(resid * resid, axis=1, keepdims=True) + EPSILON)
    weighed = cot * gain_ref[1:2, :]
    inner = jnp.sum(weighed * resid, axis=1, keepdims=True)
    mid = low_ref[...].astype(F32) + weighed * scale - resid * (scale * scale * scale * inner / D)
    low = mid.astype(BF)
    mixed_cot_ref[...] = contract(low, w_ref[...], 1, 1).astype(BF)

    @pl.when(step == 0)
    def _():
        total_ref[...] = jnp.zeros_like(total_ref)
        gain_part_ref[...] = jnp.zeros_like(gain_part_ref)

    total_ref[...] += contract(mixed_ref[...], low, 0, 0)

    @pl.when(step <= last // 2)
    def _():
        own_ref[...] = mid[:, :width]
        part = jnp.sum((cot * resid * scale)[:, :width], axis=0, keepdims=True)
        gain_part_ref[...] += jnp.broadcast_to(part, gain_part_ref.shape)

    @pl.when(step == last)
    def _():
        grad_ref[...] = total_ref[...].astype(BF)


def middle(mlp_cot, resid_mid, out_low, gains, w_mine, mixed, width):
    span, full = resid_mid.shape
    heads_width = mixed.shape[1]
    block = 256
    steps = span // block
    line = pl.BlockSpec((block, full), lambda i: (i, 0))
    thin = pl.BlockSpec((block, heads_width), lambda i: (i, 0))
    return pl.pallas_call(
        middle_kernel,
        grid=(steps,),
        in_specs=[
            line, line, line,
            pl.BlockSpec(gains.shape, lambda i: (0, 0)),
            pl.BlockSpec(w_mine.shape, lambda i: (0, 0)),
            thin,
        ],
        out_specs=[
            thin,
            pl.BlockSpec((block, width), lambda i: (jnp.minimum(i, steps // 2 - 1), 0)),
            pl.BlockSpec((heads_width, full), lambda i: (0, 0)),
            pl.BlockSpec((8, width), lambda i: (0, 0)),
        ],
        out_shape=[
            jax.ShapeDtypeStruct((span, heads_width), BF),
            jax.ShapeDtypeStruct((span // 2, width), F32),
            jax.ShapeDtypeStruct((heads_width, full), BF),
            jax.ShapeDtypeStruct((8, width), F32),
        ],
        scratch_shapes=[pltpu.VMEM((heads_width, full), F32)],
        compiler_params=pltpu.CompilerParams(vmem_limit_bytes=48 * MIB),
        cost_estimate=pl.CostEstimate(
            flops=4 * span * full * heads_width, transcendentals=0, bytes_accessed=8 * span * full
        ),
        name="middle",
    )(mlp_cot, resid_mid, out_low, gains, w_mine, mixed)


def head_back_kernel(
    info_ref, qc_ref, kc_ref, vc_ref, wq_ref, wkv_ref, normed_ref, x_ref, gain_ref,
    part_ref, dot_ref, grad_ref, total_ref,
):
    step = pl.program_id(0)
    wide = qc_ref.shape[1]
    keyval = jnp.concatenate([kc_ref[...], vc_ref[...]], axis=1)
    counted = keyval * info_ref[2].astype(BF)
    part = contract(qc_ref[...], wq_ref[...], 1, 1) + contract(counted, wkv_ref[...], 1, 1)
    part_ref[...] = part.astype(BF)
    inner = jnp.sum(part * gain_ref[0:1, :] * x_ref[...].astype(F32), axis=1, keepdims=True)
    dot_ref[0] = jnp.broadcast_to(inner, (inner.shape[0], LANES)).T[0:1, :]

    @pl.when(step == 0)
    def _():
        total_ref[...] = jnp.zeros_like(total_ref)

    total_ref[:, :wide] += contract(normed_ref[...], qc_ref[...], 0, 0)
    total_ref[:, wide:] += contract(normed_ref[...], keyval, 0, 0)

    @pl.when(step == pl.num_programs(0) - 1)
    def _():
        used = wide + 2 * HD
        grad_ref[:, :used] = total_ref[...].astype(BF)
        grad_ref[:, used:] = jnp.zeros((grad_ref.shape[0], grad_ref.shape[1] - used), BF)


def head_back(info, query_cot, key_cot, value_cot, wq, wkv, normed, tokens_full, gains):
    span, full = normed.shape
    wide = query_cot.shape[1]
    block = 512
    steps = span // block
    line = lambda n: pl.BlockSpec((block, n), lambda i, info_ref: (i, 0))
    whole = lambda shape: pl.BlockSpec(shape, lambda i, info_ref: (0, 0))
    grad_width = max(CC, wide + 2 * HD)
    return pl.pallas_call(
        head_back_kernel,
        grid_spec=pltpu.PrefetchScalarGridSpec(
            num_scalar_prefetch=1,
            grid=(steps,),
            in_specs=[
                line(wide), line(HD), line(HD), whole(wq.shape), whole(wkv.shape), line(full), line(full),
                whole(gains.shape),
            ],
            out_specs=[
                line(full),
                pl.BlockSpec((1, 1, block), lambda i, info_ref: (i, 0, 0)),
                whole((full, grad_width)),
            ],
            scratch_shapes=[pltpu.VMEM((full, wide + 2 * HD), F32)],
        ),
        out_shape=[
            jax.ShapeDtypeStruct((span, full), BF),
            jax.ShapeDtypeStruct((steps, 1, block), F32),
            jax.ShapeDtypeStruct((full, grad_width), BF),
        ],
        compiler_params=pltpu.CompilerParams(vmem_limit_bytes=48 * MIB),
        cost_estimate=pl.CostEstimate(
            flops=4 * span * full * (wide + LANES), transcendentals=0, bytes_accessed=6 * span * full
        ),
        name="head_back",
    )(info, query_cot, key_cot, value_cot, wq, wkv, normed, tokens_full, gains)


def on_device(
    tokens, lengths, attn_gain, w_query, w_key, w_value, w_out, mlp_gain, w_gate, w_up, w_down, cotangent
):
    row_devices = lax.axis_size("row")
    col_devices = lax.axis_size("col")
    row = lax.axis_index("row")
    col = lax.axis_index("col")
    fit = kernels_fit()
    tok, width = tokens.shape
    span = tok * row_devices
    group = HQ // KV
    heads_row = HQ // row_devices
    heads = heads_row // col_devices
    head_width = heads * HD
    keyval_row = KV // row_devices
    units = w_gate.shape[1] // col_devices
    length = lengths[0]
    shared_key = heads < group
    sharers = max(1, group // heads)
    leader = (col % sharers == 0).astype(jnp.int32)
    info = jnp.stack([length, row, leader]).astype(jnp.int32)

    keyval = []
    for owner in range(col_devices):
        first = owner * heads // group * HD
        keyval += [w_key[:, first : first + HD], w_value[:, first : first + HD]]
    keyval = jnp.concatenate(keyval, axis=1)
    gains = jnp.concatenate([attn_gain[None], mlp_gain[None], jnp.zeros((6, width), F32)], axis=0)

    if fit:
        tokens_full, wq, wkv, gains = first_gather(tokens, w_query, keyval, gains, 1)
    else:
        tokens_full = plain_gather(tokens)
        def slices(weight, size):
            return [lax.dynamic_slice_in_dim(weight, (col ^ s) * size, size, 1) for s in range(col_devices)]

        wq = jnp.concatenate(exchange(slices(w_query, head_width)), axis=0)
        wkv = jnp.concatenate(exchange(slices(keyval, LANES)), axis=0)
        gains = by_distance(lax.all_gather(gains, "col"), 1)
    w_gate, w_up, tokens_full = lax.optimization_barrier((w_gate, w_up, tokens_full))
    place = lax.rem(jnp.arange(span, dtype=jnp.int32) + row * tok, span)
    frequency = ROPE_BASE ** (-jnp.arange(HD // 2, dtype=F32) * (2.0 / HD))
    angle = place.astype(F32)[:, None] * frequency[None, :]
    cos = jnp.tile(jnp.cos(angle), (1, 2))
    sin = jnp.tile(jnp.sin(angle), (1, 2))

    normed_attn, query, key, value, scale_a = project_heads(tokens_full, gains, wq, wkv, cos, sin)
    valid = (row * tok + jnp.arange(tok, dtype=jnp.int32) < length).astype(BF)
    cot_low = cotangent * valid[:, None]
    if fit:
        mixed, mixed_wide, log_total, peak, w_out_full = attn_forward(info, query, key, value, w_out, 7)
        mixed_full = gather_heads(mixed, 2)
        w_down, mixed_full = lax.optimization_barrier((w_down, mixed_full))
        resid_mid, normed_mlp, out_low = project_out(mixed_full, w_out_full, tokens_full, gains, cot_low, 8)
    else:
        mixed, mixed_wide, log_total, peak = attn_forward(info, query, key, value)
        mixed_full = plain_gather_heads(mixed)
        w_out_full = plain_gather(w_out)
        resid_mid, normed_mlp = project_out(mixed_full, w_out_full, tokens_full, gains)
        out_low = plain_gather(cot_low)

    def unit_slices(weight, dim):
        return [lax.dynamic_slice_in_dim(weight, (col ^ s) * units, units, dim) for s in range(col_devices)]

    gate_blocks = exchange(unit_slices(w_gate, 1))
    up_blocks = exchange(unit_slices(w_up, 1))
    down_blocks = exchange(unit_slices(w_down, 0))
    normed_mlp, gate_blocks, up_blocks = lax.optimization_barrier((normed_mlp, gate_blocks, up_blocks))
    w_gate_units = jnp.concatenate(gate_blocks, axis=0)
    w_up_units = jnp.concatenate(up_blocks, axis=0)
    gate = jnp.dot(normed_mlp, w_gate_units, preferred_element_type=F32)
    up = jnp.dot(normed_mlp, w_up_units, preferred_element_type=F32)
    gate_sigmoid = jax.nn.sigmoid(gate)
    hidden = (gate * gate_sigmoid * up).astype(BF)

    hidden, down_blocks = lax.optimization_barrier((hidden, down_blocks))
    w_down_units = jnp.concatenate(down_blocks, axis=1)
    grad_down = contract(hidden, out_low, 0, 0).astype(BF)
    hidden_cot = contract(out_low, w_down_units, 1, 1)
    gate_cot = (
        hidden_cot * up * gate_sigmoid * (1.0 + gate * (1.0 - gate_sigmoid))
    ).astype(BF)
    up_cot = (hidden_cot * gate * gate_sigmoid).astype(BF)
    mlp_part = (contract(gate_cot, w_gate_units, 1, 1) + contract(up_cot, w_up_units, 1, 1)).astype(BF)
    grad_gate = contract(normed_mlp, gate_cot, 0, 0).astype(BF)
    grad_up = contract(normed_mlp, up_cot, 0, 0).astype(BF)
    down_part = jnp.dot(hidden, w_down_units, preferred_element_type=F32).astype(BF)

    if fit:
        *sums, mid_cot, gain_m_part, attn_cot, down_sum, width_dot = backward(
            info, gains, [grad_gate, grad_up, grad_down], mlp_part, down_part, resid_mid, out_low, w_out_full,
            mixed, query, key, value, mixed_wide, log_total, cos, sin, wq, wkv, normed_attn, tokens_full, 3,
        )
        width_dot = width_dot.reshape(tok)
    else:
        mlp_cot = plain_gather(plain_reduce(mlp_part).astype(BF))
        down_sum = plain_reduce(down_part)
        w_mine = lax.dynamic_slice_in_dim(w_out_full, col * head_width, head_width, 0)
        mixed_cot, mid_cot, grad_out, gain_m_part = middle(
            mlp_cot, resid_mid, out_low, gains, w_mine, mixed, width
        )
        query_cot, key_cot, value_cot = attn_backward(
            info, query, key, value, mixed_cot, mixed_wide, log_total, cos, sin, F32 if shared_key else BF
        )
        if shared_key:
            for bit in range(sharers.bit_length() - 1):
                key_cot = key_cot + swap(key_cot, "col", 1 << bit)
                value_cot = value_cot + swap(value_cot, "col", 1 << bit)
            key_cot, value_cot = key_cot.astype(BF), value_cot.astype(BF)
        attn_part, dot_part, grad_heads = head_back(
            info, query_cot, key_cot, value_cot, wq, wkv, normed_attn, tokens_full, gains
        )
        dot_part = dot_part.reshape(span)
        width_dot = lax.psum(dot_part[:tok] + swap(dot_part[tok:], "row", 1), "col")
        attn_cot = plain_reduce(attn_part)
        sums = plain_group_sum(
            [grad_gate, grad_up, grad_down, grad_out, grad_heads], ["columns", "columns", "rows", "rows", "stack"]
        )
    output = (resid_mid[:tok, :width] + down_sum).astype(BF)
    own_in = tokens.astype(F32)
    scale_own = scale_a[:tok, :1]
    input_grad = (
        mid_cot
        + attn_cot * attn_gain * scale_own
        - own_in * (scale_own * scale_own * scale_own * width_dot[:, None] / D)
    )
    gain_a_part = jnp.sum(attn_cot * own_in * scale_own, axis=0)

    out_gate, out_up, out_down, out_out, out_heads = [g.astype(F32) for g in sums]
    out_heads = out_heads.reshape(col_devices, width, out_heads.shape[1])
    out_query = jnp.concatenate([out_heads[i, :, :head_width] for i in range(col_devices)], axis=1)
    leaders = range(0, col_devices, sharers)
    out_key = jnp.concatenate([out_heads[i, :, head_width : head_width + HD] for i in leaders], axis=1)
    out_value = jnp.concatenate(
        [out_heads[i, :, head_width + HD : head_width + 2 * HD] for i in leaders], axis=1
    )

    gain_sums = jnp.stack([gain_a_part, gain_m_part[0]])
    gain_sums = gain_sums + swap(gain_sums, "row", 1)
    step = 1
    while step < lax.axis_size("dp"):
        gain_sums = gain_sums + swap(gain_sums, "dp", step)
        step *= 2
    step = 1
    while step < lax.axis_size("dp"):
        peak = jnp.maximum(peak, swap(peak, "dp", step))
        step *= 2
    own_peaks = peak[:, 0]
    slots = jnp.arange(col_devices)[:, None]
    row_peaks = jnp.where(slots == col, own_peaks[None, :], NEG_FILL)
    step = 1
    while step < col_devices:
        row_peaks = jnp.maximum(row_peaks, swap(row_peaks, "col", step))
        step *= 2
    row_peaks = row_peaks.reshape(heads_row)
    clip_factor = CLIP_LEVEL / jnp.maximum(row_peaks, CLIP_LEVEL)
    query_scale = jnp.repeat(jnp.sqrt(clip_factor), HD)
    key_scale = jnp.repeat(jnp.sqrt(jnp.min(clip_factor.reshape(keyval_row, group), axis=1)), HD)
    clipped_query = (w_query.astype(F32) * query_scale[None, :]).astype(BF)
    clipped_key = (w_key.astype(F32) * key_scale[None, :]).astype(BF)
    return (
        output,
        input_grad,
        gain_sums[0],
        out_query,
        out_key,
        out_value,
        out_out,
        gain_sums[1],
        out_gate,
        out_up,
        out_down,
        own_peaks,
        clipped_query,
        clipped_key,
    )


def solution(mesh):
    in_specs = (
        P(("dp", "row"), "col"),
        P("dp"),
        P("col"),
        P("col", "row"),
        P("col", "row"),
        P("col", "row"),
        P("row", "col"),
        P("col"),
        P("col", "row"),
        P("col", "row"),
        P("row", "col"),
        P(("dp", "row"), "col"),
    )
    out_specs = (
        P(("dp", "row"), "col"),
        P(("dp", "row"), "col"),
        P("col"),
        P("col", "row"),
        P("col", "row"),
        P("col", "row"),
        P("row", "col"),
        P("col"),
        P("col", "row"),
        P("col", "row"),
        P("row", "col"),
        P(("row", "col")),
        P("col", "row"),
        P("col", "row"),
    )
    return jax.shard_map(
        on_device, mesh=mesh, in_specs=in_specs, out_specs=out_specs, check_vma=False
    )
```

```python
import functools

import jax
import jax.numpy as jnp
from jax import lax
from jax.experimental import pallas as pl
from jax.experimental.pallas import tpu as pltpu
from jax.sharding import PartitionSpec as P

D = 2048
HQ = 32
KV = 8
HD = 64
SEQ_LEN = 2048

EPSILON = 1e-05
NEG_FILL = -1e30
CLIP_LEVEL = 5.0
ROPE_BASE = 500000.0

BF = jnp.bfloat16
F32 = jnp.float32
LANES = 128
QB = 512
FWD_KB = 512
BWD_KB = 512
MESH = pl.DeviceIdType.MESH
ANY = pl.BlockSpec(memory_space=pl.ANY)
NCH = 4
CR, CC = 256, 512
HR = CR // 2
OFFS = (0, 2, 4, 7)
RING = 12
MIB = 2**20
VMEM_ALL = 63 * MIB


def contract(left, right, left_dim, right_dim):
    return lax.dot_general(
        left, right, (((left_dim,), (right_dim,)), ((), ())), preferred_element_type=F32
    )


def swap(values, axis, step):
    count = lax.axis_size(axis)
    return lax.ppermute(values, axis, [(i, i ^ step) for i in range(count)])


def flip(index, bit):
    return index + bit - 2 * bit * lax.rem(index // bit, 2)


def xor(index, step):
    return lax.rem(lax.rem(index, 2) + step % 2, 2) + 2 * lax.rem(index // 2 + step // 2, 2)


def remote(src, dst, send, recv, **where):
    return pltpu.make_async_remote_copy(
        src_ref=src, dst_ref=dst, send_sem=send, recv_sem=recv, device_id=where, device_id_type=MESH
    )


def done(ref, sem):
    pltpu.make_async_copy(ref, ref, sem).wait()


def greet(targets):
    barrier = pltpu.get_barrier_semaphore()
    for target in targets:
        pl.semaphore_signal(barrier, inc=1, device_id=target, device_id_type=MESH)
    pl.semaphore_wait(barrier, len(targets))


def plane_peers():
    row = lax.axis_index("row")
    col = lax.axis_index("col")
    return {"col": flip(col, 1)}, {"col": flip(col, 2)}, {"row": 1 - row}


def token_place(tok, width):
    rows = tok // NCH

    def place(ref, half, s, j, who):
        return ref.at[pl.ds(half * tok + j * rows, rows), pl.ds(s * width, width)]

    return place


def head_place(span, width):
    rows = span // NCH

    def place(ref, half, s, j, who):
        start = j * rows if half == 0 else ((j + NCH // 2) % NCH) * rows
        return ref.at[pl.ds(start, rows), pl.ds(pl.multiple_of((half * 4 + xor(who, s)) * width, LANES), width)]

    return place


class Gather:
    SEMS = 6

    def __init__(self, src, out, place, stage, sems):
        self.src, self.out, self.place, self.stage = src, out, place, stage
        self.own_send, self.relay_send, self.mate_send, self.recv, self.mate_recv, self.local = sems
        self.col = lax.axis_index("col")
        self.near = plane_peers()

    @staticmethod
    def sems():
        shapes = [(2, NCH), (NCH,), (4, NCH), (3, NCH), (4, NCH), (2,)]
        return [pltpu.SemaphoreType.DMA(s) for s in shapes]

    def chunk(self, j):
        rows = self.src.shape[0] // NCH
        return self.src.at[pl.ds(j * rows, rows), :]

    def here(self, half, s, j):
        return self.place(self.out, half, s, j, self.col)

    def own(self, axis, j):
        peer = self.near[axis]
        dst = self.place(self.out, 0, axis + 1, j, peer["col"])
        return remote(self.chunk(j), dst, self.own_send.at[axis, j], self.recv.at[axis, j], **peer)

    def relay(self, axis, j):
        peer = self.near[1 - axis]
        dst = self.place(self.out, 0, 3, j, peer["col"])
        return remote(self.here(0, axis + 1, j), dst, self.relay_send.at[j], self.recv.at[2, j], **peer)

    def mate(self, s, j):
        src = self.chunk(j) if s == 0 else self.here(0, s, j)
        dst = self.place(self.out, 1, s, j, self.col)
        return remote(src, dst, self.mate_send.at[s, j], self.mate_recv.at[s, j], **self.near[2])

    def load(self):
        return pltpu.make_async_copy(self.src, self.stage, self.local.at[0])

    def keep(self, j):
        rows = self.src.shape[0] // NCH
        whole = self.stage if self.stage is not None else self.src
        return pltpu.make_async_copy(whole.at[pl.ds(j * rows, rows), :], self.here(0, 0, j), self.local.at[1])

    def begin(self):
        half = NCH // 2
        if self.stage is not None:
            self.load().start()
        for i in range(NCH):
            self.own(0, i).start()
            self.own(1, (i + half) % NCH).start()
        for j in range(NCH):
            self.mate(0, j).start()

    def arrived(self, s, j):
        done(self.here(0, s, j), self.recv.at[s - 1, j])

    def first(self):
        half = NCH // 2
        for i in range(half):
            self.arrived(1, i)
            self.relay(0, i).start()
            self.mate(1, i).start()
            self.arrived(2, half + i)
            self.relay(1, half + i).start()
            self.mate(2, half + i).start()

    def second(self):
        half = NCH // 2
        if self.stage is not None:
            self.load().wait()
        for j in range(NCH):
            self.keep(j).start()
        for i in range(half):
            self.arrived(1, half + i)
            self.mate(1, half + i).start()
            self.arrived(2, i)
            self.mate(2, i).start()
        for i in range(half):
            for j in (i, half + i):
                self.arrived(3, j)
                self.mate(3, j).start()

    def finish(self):
        half = NCH // 2
        for s in range(4):
            for j in range(NCH):
                done(self.here(1, s, j), self.mate_recv.at[s, j])
                self.mate(s, j).wait_send()
        for j in range(NCH):
            self.own(0, j).wait_send()
            self.own(1, j).wait_send()
            self.relay(0 if j < half else 1, j).wait_send()
        whole = self.stage if self.stage is not None else self.src
        done(whole, self.local.at[1])


def gather_kernel(place_of, x_ref, out_ref, stage, *sems):
    near_x, near_y, mate = plane_peers()
    greet([near_x, near_y, mate])
    gather = Gather(x_ref, out_ref, place_of(*x_ref.shape), stage, sems)
    gather.begin()
    gather.first()
    gather.second()
    gather.finish()


def gather_call(x, shape, place_of, cid, name):
    return pl.pallas_call(
        functools.partial(gather_kernel, place_of),
        in_specs=[ANY],
        out_specs=ANY,
        out_shape=jax.ShapeDtypeStruct(shape, x.dtype),
        scratch_shapes=[pltpu.VMEM(x.shape, x.dtype)] + Gather.sems(),
        compiler_params=pltpu.CompilerParams(collective_id=cid, has_side_effects=True),
        name=name,
    )(x)


def gather_tokens(x, cid):
    tok, width = x.shape
    return gather_call(x, (2 * tok, 4 * width), token_place, cid, "gather_tokens")


def gather_heads(x, cid):
    span, width = x.shape
    return gather_call(x, (span, 8 * width), head_place, cid, "gather_heads")


class Reduce:
    def __init__(self, part, scratch, sems):
        self.part = part
        self.own, self.given, self.sent, self.got_one, self.got_two = scratch
        self.loads, self.mate_send, self.mate_recv, self.one_send, self.one_recv, self.two_send, self.two_recv = sems
        self.near = plane_peers()
        self.h = self.own.shape[0] // 2
        self.width = self.own.shape[1] // 4

    @staticmethod
    def scratch(tok, full):
        h, w = tok // 2, full // 4
        shapes = [(tok, full), (tok, full), (2, 3, h, w), (2, 2, h, w), (2, h, w)]
        return [pltpu.VMEM(s, BF) for s in shapes]

    @staticmethod
    def sems():
        return [pltpu.SemaphoreType.DMA((2,))] * 7

    def lines(self, a):
        return pl.ds(a * self.h, self.h)

    def give(self, a):
        src = self.part.at[pl.ds((2 + a) * self.h, self.h), :]
        return remote(src, self.given.at[self.lines(a), :], self.mate_send.at[a], self.mate_recv.at[a], **self.near[2])

    def load(self, a):
        return pltpu.make_async_copy(self.part.at[self.lines(a), :], self.own.at[self.lines(a), :], self.loads.at[a])

    def one(self, a):
        src = self.sent.at[a, pl.ds(0, 2)]
        return remote(src, self.got_one.at[a], self.one_send.at[a], self.one_recv.at[a], **self.near[a])

    def two(self, a):
        return remote(self.sent.at[a, 2], self.got_two.at[a], self.two_send.at[a], self.two_recv.at[a], **self.near[1 - a])

    def pair(self, a, s):
        cols = pl.ds(s * self.width, self.width)
        rows = self.lines(a)
        return self.own[rows, cols].astype(F32) + self.given[rows, cols].astype(F32)

    def begin(self):
        for a in range(2):
            self.give(a).start()
            self.load(a).start()

    def first(self, a):
        self.load(a).wait()
        done(self.given.at[self.lines(a), :], self.mate_recv.at[a])
        for i, s in enumerate((a + 1, 3)):
            self.sent[a, i] = self.pair(a, s).astype(BF)
        self.one(a).start()

    def second(self, a):
        done(self.got_one.at[a], self.one_recv.at[a])
        self.sent[a, 2] = (self.pair(a, 2 - a) + self.got_one[a, 1].astype(F32)).astype(BF)
        self.two(a).start()

    def total(self, a):
        done(self.got_two.at[a], self.two_recv.at[a])
        return self.pair(a, 0) + self.got_one[a, 0].astype(F32) + self.got_two[a].astype(F32)

    def finish(self):
        for a in range(2):
            self.give(a).wait_send()
            self.one(a).wait_send()
            self.two(a).wait_send()


def first_gather_kernel(
    x_ref, wq_ref, wkv_ref, gain_ref, out_ref, wq_out, wkv_out, gain_out,
    stage, wq_stage, wkv_stage, gain_stage, stage_sem, small_send, small_recv, *sems,
):
    near_x, near_y, mate = plane_peers()
    col = lax.axis_index("col")
    tok, width = x_ref.shape
    wide = wq_ref.shape[1] // 4
    thin = wkv_ref.shape[1] // 4

    def share(ref, owner, size):
        return ref.at[:, pl.ds(pl.multiple_of(owner * size, LANES), size)]

    loads = [
        pltpu.make_async_copy(share(wq_ref, col, wide), wq_stage, stage_sem.at[0]),
        pltpu.make_async_copy(share(wkv_ref, col, thin), wkv_stage, stage_sem.at[1]),
        pltpu.make_async_copy(gain_ref, gain_stage, stage_sem.at[2]),
    ]
    for c in loads:
        c.start()
    greet([near_x, near_y, {"col": 3 - col}, mate])
    smalls = []
    for s, peer in ((1, near_x), (2, near_y), (3, {"col": 3 - col})):
        owner = peer["col"]
        lines = pl.ds(s * width, width)
        smalls += [
            remote(share(wq_ref, owner, wide), wq_out.at[lines, :], small_send.at[0, s], small_recv.at[0, s], **peer),
            remote(share(wkv_ref, owner, thin), wkv_out.at[lines, :], small_send.at[1, s], small_recv.at[1, s], **peer),
            remote(gain_ref, gain_out.at[:, lines], small_send.at[2, s], small_recv.at[2, s], **peer),
        ]
    gather = Gather(x_ref, out_ref, token_place(tok, width), stage, sems)
    gather.begin()
    for c in smalls:
        c.start()
    lines = pl.ds(0, width)
    keeps = [
        pltpu.make_async_copy(wq_stage, wq_out.at[lines, :], stage_sem.at[3]),
        pltpu.make_async_copy(wkv_stage, wkv_out.at[lines, :], stage_sem.at[4]),
        pltpu.make_async_copy(gain_stage, gain_out.at[:, lines], stage_sem.at[5]),
    ]
    for load, keep in zip(loads, keeps):
        load.wait()
        keep.start()
    gather.first()
    gather.second()
    gather.finish()
    for c in smalls:
        c.wait()
    for c in keeps:
        c.wait()


def first_gather(x, wq, wkv, gains, cid):
    tok, width = x.shape
    wide, thin = wq.shape[1] // 4, wkv.shape[1] // 4
    return pl.pallas_call(
        first_gather_kernel,
        in_specs=[ANY] * 4,
        out_specs=[ANY] * 4,
        out_shape=[
            jax.ShapeDtypeStruct((2 * tok, 4 * width), BF),
            jax.ShapeDtypeStruct((4 * width, wide), BF),
            jax.ShapeDtypeStruct((4 * width, thin), BF),
            jax.ShapeDtypeStruct((8, 4 * width), F32),
        ],
        scratch_shapes=[
            pltpu.VMEM((tok, width), BF),
            pltpu.VMEM((width, wide), BF),
            pltpu.VMEM((width, thin), BF),
            pltpu.VMEM((8, width), F32),
            pltpu.SemaphoreType.DMA((6,)),
            pltpu.SemaphoreType.DMA((3, 4)),
            pltpu.SemaphoreType.DMA((3, 4)),
        ]
        + Gather.sems(),
        compiler_params=pltpu.CompilerParams(collective_id=cid, has_side_effects=True),
        name="first_gather",
    )(x, wq, wkv, gains)


def grad_plan(kind, shape):
    rows, cols = shape
    if kind == "columns":
        w = rows // 4
        high, n = rows // CR, w // CR
        return (
            high * (cols // CC), high,
            lambda i: lax.rem(i, high) // n, lambda i: lax.rem(i, high), lambda i: i // high,
            (w, 4 * cols), lambda c, i: (lax.rem(i, n) * CR, c * cols + i // high * CC),
        )
    high = rows // CR
    if kind == "rows":
        return (
            4 * high, high,
            lambda i: i // high, lambda i: lax.rem(i, high), lambda i: i // high,
            (4 * rows, cols // 4), lambda c, i: (c * rows + lax.rem(i, high) * CR, 0),
        )
    n = high // 4
    return (
        high, high,
        lambda i: i // n, lambda i: i, lambda i: 0,
        (rows, cols), lambda c, i: ((c * n + lax.rem(i, n)) * CR, 0),
    )


class GroupSum:
    def __init__(self, kinds, lefts, rights, outs, refs):
        (self.left, self.right, self.left_sem, self.right_sem, self.own, self.land, self.mids, self.tops, self.in_send, self.in_recv, self.mid_send,
         self.mid_recv, self.top_send, self.top_recv, self.out_send, self.out_recv, self.far_send, self.far_recv) = refs
        self.lefts, self.rights, self.outs = lefts, rights, outs
        self.plans = [grad_plan(k, (a.shape[1], b.shape[1])) for k, a, b in zip(kinds, lefts, rights)]
        self.counts = [p[0] for p in self.plans]
        self.begins = [sum(self.counts[:i]) for i in range(len(lefts))]
        groups = [p[0] // p[1] for p in self.plans]
        self.groups = [sum(groups[:i]) for i in range(len(lefts))]
        self.total = sum(self.counts)
        z = lax.axis_index("dp")
        self.col = lax.axis_index("col")
        self.is_mid = (z == 1) | (z == 2)
        self.is_end = jnp.logical_not(self.is_mid)
        left = z < 2
        self.inward = {"dp": jnp.where(left, z + 1, z - 1)}
        self.outward = {"dp": jnp.where(left, z - 1, z + 1)}
        self.kept = jnp.where(left, 0, 1)

    @staticmethod
    def scratch(kinds, span):
        dma = pltpu.SemaphoreType.DMA
        return (
            [pltpu.VMEM((2, span, CR), BF), pltpu.VMEM((2, span, CC), BF), dma((2,)), dma((2,))]
            + [pltpu.VMEM((RING, CR, CC), BF)] * 2
            + [pltpu.VMEM((RING, HR, CC), BF)] * 2
            + [dma((RING,))] * 6
            + [dma((RING, 2))] * 3
            + [dma((len(kinds),))]
        )

    def greet(self, others):
        barrier = pltpu.get_barrier_semaphore()
        targets = [self.inward] + others
        for target in targets:
            pl.semaphore_signal(barrier, inc=1, device_id=target, device_id_type=MESH)

        @pl.when(self.is_mid)
        def _():
            pl.semaphore_signal(barrier, inc=1, device_id=self.outward, device_id_type=MESH)
            pl.semaphore_wait(barrier, len(targets) + 1)

        @pl.when(self.is_end)
        def _():
            pl.semaphore_wait(barrier, len(targets))

    def rows(self, half):
        return pl.ds(pl.multiple_of(half * HR, HR), HR)

    def each(self, j, action):
        for m, count in enumerate(self.counts):

            @pl.when((j >= self.begins[m]) & (j < self.begins[m] + count))
            def _(m=m):
                action(m, j - self.begins[m])

    def left_load(self, m, i, j):
        lines = pl.ds(pl.multiple_of(self.plans[m][3](i) * CR, CR), CR)
        slot = lax.rem(j, 2)
        return pltpu.make_async_copy(self.lefts[m].at[:, lines], self.left.at[slot], self.left_sem.at[slot])

    def right_slot(self, m, i):
        return lax.rem(self.groups[m] + i // self.plans[m][1], 2)

    def right_load(self, m, i):
        lines = pl.ds(pl.multiple_of(self.plans[m][4](i) * CC, CC), CC)
        slot = self.right_slot(m, i)
        return pltpu.make_async_copy(self.rights[m].at[:, lines], self.right.at[slot], self.right_sem.at[slot])

    def fetch(self, j):
        def action(m, i):
            self.left_load(m, i, j).start()
            if self.resident[m] is None:

                @pl.when(lax.rem(i, self.plans[m][1]) == 0)
                def _():
                    self.right_load(m, i).start()

        self.each(j, action)

    def produce(self, j):
        slot = lax.rem(j, RING)

        def action(m, i):
            self.left_load(m, i, j).wait()
            if self.resident[m] is None:

                @pl.when(lax.rem(i, self.plans[m][1]) == 0)
                def _():
                    self.right_load(m, i).wait()

                right = self.right[self.right_slot(m, i)]
            else:
                right = self.resident[m][...]
            self.own[slot] = contract(self.left[lax.rem(j, 2)], right, 0, 0).astype(BF)

        self.each(j, action)

    def spread(self, j, half, src):
        slot = lax.rem(j, RING)

        def action(m, i):
            s = self.plans[m][2](i)
            r, q = self.plans[m][6](self.col, i)
            dst = self.outs[m].at[
                pl.ds(pl.multiple_of(r + half * HR, HR), HR), pl.ds(pl.multiple_of(q, CC), CC)
            ]

            @pl.when(s == 0)
            def _():
                pltpu.make_async_copy(src, dst, self.far_send.at[slot, half]).start()

            @pl.when(s > 0)
            def _():
                owner = lax.rem(lax.rem(self.col, 2) + lax.rem(s, 2), 2) + 2 * lax.rem(self.col // 2 + s // 2, 2)
                remote(src, dst, self.far_send.at[slot, half], self.far_recv.at[m], col=owner).start()

        self.each(j, action)

    def reclaim(self, j):
        slot = lax.rem(j, RING)
        for half in range(2):
            done(self.mids.at[slot], self.far_send.at[slot, half])

        @pl.when(self.is_mid)
        def _():
            done(self.mids.at[slot], self.mid_send.at[slot])
            done(self.mids.at[slot], self.top_send.at[slot])
            for half in range(2):
                done(self.mids.at[slot], self.out_send.at[slot, half])

        @pl.when(self.is_end)
        def _():
            done(self.own.at[slot], self.in_send.at[slot])

    def inbound(self, j):
        slot = lax.rem(j, RING)

        @pl.when(self.is_mid)
        def _():
            done(self.land.at[slot], self.in_recv.at[slot])
            self.own[slot] = (self.own[slot].astype(F32) + self.land[slot].astype(F32)).astype(BF)
            src = self.own.at[slot, self.rows(1 - self.kept)]
            remote(src, self.mids.at[slot], self.mid_send.at[slot], self.mid_recv.at[slot], **self.inward).start()

        @pl.when(self.is_end)
        def _():
            remote(
                self.own.at[slot], self.land.at[slot], self.in_send.at[slot], self.in_recv.at[slot], **self.inward
            ).start()

    def middle(self, j):
        slot = lax.rem(j, RING)

        @pl.when(self.is_mid)
        def _():
            done(self.mids.at[slot], self.mid_recv.at[slot])
            rows = self.rows(self.kept)
            self.own[slot, rows] = (self.own[slot, rows].astype(F32) + self.mids[slot].astype(F32)).astype(BF)
            src = self.own.at[slot, rows]
            remote(src, self.tops.at[slot], self.top_send.at[slot], self.top_recv.at[slot], **self.inward).start()
            remote(
                src, self.land.at[slot, rows], self.out_send.at[slot, self.kept], self.out_recv.at[slot, self.kept],
                **self.outward,
            ).start()
            self.spread(j, self.kept, src)

    def settle(self, j):
        slot = lax.rem(j, RING)

        @pl.when(self.is_mid)
        def _():
            done(self.tops.at[slot], self.top_recv.at[slot])
            half = 1 - self.kept
            src = self.tops.at[slot]
            remote(
                src, self.land.at[slot, self.rows(half)], self.out_send.at[slot, half], self.out_recv.at[slot, half],
                **self.outward,
            ).start()
            self.spread(j, half, src)

    def outbound(self, j):
        slot = lax.rem(j, RING)

        @pl.when(self.is_end)
        def _():
            for half in range(2):
                src = self.land.at[slot, pl.ds(half * HR, HR)]
                done(src, self.out_recv.at[slot, half])
                self.spread(j, half, src)

    def begin(self):
        self.fetch(jnp.int32(0))
        self.produce(jnp.int32(0))
        self.fetch(jnp.int32(1))

    def tick(self, t):
        for off, stage in zip(OFFS, (self.inbound, self.middle, self.settle, self.outbound)):

            @pl.when((t >= off) & (t < self.total + off))
            def _(off=off, stage=stage):
                stage(t - off)

        ahead = t + 1

        @pl.when(ahead < self.total)
        def _():
            @pl.when(ahead >= RING)
            def _():
                self.reclaim(ahead - RING)

            self.produce(ahead)

            @pl.when(ahead + 1 < self.total)
            def _():
                self.fetch(ahead + 1)

    def finish(self):
        def drain(j, carry):
            self.reclaim(j)
            return carry

        lax.fori_loop(self.total - RING, self.total, drain, 0)
        for m, out in enumerate(self.outs):
            done(out.at[pl.ds(0, 3 * out.shape[0] // 4)], self.far_recv.at[m])


MB = 128
AQ, AK = 256, 512


def backward_kernel(
    kinds,
    info_ref, gain_ref, mlp_ref, gate_ref, up_ref, hidden_ref, part_ref, low_part_ref, resid_ref, low_ref, w_ref, mixed_ref,
    wide_ref, normed_ref, x_ref, q_ref, k_ref, v_ref, lse_ref, turn_ref, wq_ref, wkv_ref,
    out_gate, out_up, out_down, out_out, out_heads, mid_out, gain_part, attn_out, down_out, dot_out,
    cot_full, attn_part, mid_low,
    *refs,
):
    refs = list(refs)

    def take(count):
        taken = refs[:count]
        del refs[:count]
        return taken

    zsum = GroupSum(
        kinds,
        [hidden_ref, mlp_ref, mlp_ref, mixed_ref, normed_ref],
        [low_ref, gate_ref, up_ref, mid_low, refs[0]],
        [out_down, out_gate, out_up, out_out, out_heads],
        refs[1:19],
    )
    heads_cot = refs[0]
    zsum.resident = [None, None, None, None, heads_cot]
    del refs[:19]
    scratch = take(5)
    mlp_reduce = Reduce(part_ref, scratch, take(7))
    low_reduce = Reduce(low_part_ref, scratch, take(7))
    attn_reduce = Reduce(attn_part, scratch, take(7))
    mine, = take(1)
    tok, width = mine.shape
    gather = Gather(mine, cot_full, token_place(tok, width), None, take(Gather.SEMS))
    bufs, resid_buf, out_buf, buf_sem, out_sem = take(5)
    mixed_cot, wide_buf, dq_sum, dk_sum, dv_sum, dots, dots_mate, dots_col = take(8)
    dot_send, dot_recv, ready, w_mine, w_sem = take(5)
    span = 2 * tok
    heads_width = q_ref.shape[1]
    heads = heads_width // HD
    half = lax.axis_index("row")
    col = lax.axis_index("col")
    length = info_ref[0]
    near_x, near_y, mate = plane_peers()
    corner = {"col": 3 - col}
    blocks = span // MB

    def mid_loads(i):
        slot = lax.rem(i, 2)
        lines = pl.ds(pl.multiple_of(i * MB, MB), MB)
        return [
            pltpu.make_async_copy(cot_full.at[lines, :], bufs.at[slot, 0], buf_sem.at[slot, 0]),
            pltpu.make_async_copy(low_ref.at[lines, :], bufs.at[slot, 1], buf_sem.at[slot, 1]),
            pltpu.make_async_copy(resid_ref.at[lines, :], resid_buf.at[slot], buf_sem.at[slot, 2]),
        ]

    def row_store(out, i):
        lines = pl.ds(pl.multiple_of(i * MB, MB), MB)
        return pltpu.make_async_copy(bufs.at[lax.rem(i, 2), 2], out.at[lines, :], out_sem.at[1])

    def mid_store(i):
        lines = pl.ds(pl.multiple_of(i * MB, MB), MB)
        return pltpu.make_async_copy(out_buf.at[:, pl.ds(0, width)], mid_out.at[lines, :], out_sem.at[0])

    def mid_item(i):
        slot = lax.rem(i, 2)

        @pl.when(i + 1 < blocks)
        def _():
            for c in mid_loads(i + 1):
                c.start()

        for c in mid_loads(i):
            c.wait()
        cot = bufs[slot, 0].astype(F32)
        resid = resid_buf[slot]
        scale = lax.rsqrt(jnp.mean(resid * resid, axis=1, keepdims=True) + EPSILON)
        weighed = cot * gain_ref[1:2, :]
        inner = jnp.sum(weighed * resid, axis=1, keepdims=True)
        mid = bufs[slot, 1].astype(F32) + weighed * scale - resid * (scale * scale * scale * inner / D)
        low = mid.astype(BF)
        lines = pl.ds(pl.multiple_of(i * MB, MB), MB)
        mixed_cot[lines, :] = contract(low, w_mine[...], 1, 1).astype(BF)

        @pl.when(i > 0)
        def _():
            row_store(mid_low, i - 1).wait()

        bufs[slot, 2] = low
        row_store(mid_low, i).start()

        @pl.when(i < blocks // 2)
        def _():
            @pl.when(i > 0)
            def _():
                mid_store(i - 1).wait()

            out_buf[:, pl.ds(0, width)] = mid[:, :width]
            mid_store(i).start()
            part = jnp.sum((cot * resid * scale)[:, :width], axis=0, keepdims=True)
            gain_part[...] += jnp.broadcast_to(part, gain_part.shape)

        @pl.when(i == blocks // 2)
        def _():
            mid_store(i - 1).wait()

    q_steps = span // AQ
    rows = heads * AQ
    pieces = [slice(h * HD, (h + 1) * HD) for h in range(heads)]

    def attn_item(q_step, tile, diagonal):
        stored = lax.rem(q_step + half * (q_steps // 2), q_steps)
        lines = pl.ds(pl.multiple_of(stored * AQ, AQ), AQ)
        key_tiles = span // AK
        keys = pl.ds(pl.multiple_of(lax.rem(tile + half * (key_tiles // 2), key_tiles) * AK, AK), AK)
        first = q_step * AQ
        q = jnp.concatenate([q_ref[lines, s] for s in pieces], axis=0)
        cot = jnp.concatenate([mixed_cot[lines, s] for s in pieces], axis=0)
        wide = jnp.concatenate([wide_buf[:, s] for s in pieces], axis=0)
        place = first + lax.rem(lax.broadcasted_iota(jnp.int32, (1, rows), 1), AQ)
        log_total = jnp.where(place < length, lse_ref[q_step], -NEG_FILL)
        inner = jnp.sum(wide * cot.astype(F32), axis=1, keepdims=True)
        inner = jnp.broadcast_to(inner, (rows, LANES)).T[0:1, :]
        k_tile = k_ref[keys, :]
        v_tile = v_ref[keys, :]
        scores = contract(k_tile, q, 1, 1) * HD**-0.5 - log_total
        if diagonal:
            key_place = tile * AK + lax.broadcasted_iota(jnp.int32, (AK, rows), 0)
            scores = jnp.where(key_place <= place, scores, NEG_FILL)
        weights = jnp.exp(scores)
        prob_cot = contract(v_tile, cot, 1, 1)
        score_cot = (weights * (prob_cot - inner)).astype(BF)
        dv_sum[keys, :] += contract(weights.astype(BF), cot, 1, 0)
        dk_sum[keys, :] += contract(score_cot, q, 1, 0) * HD**-0.5
        dq = contract(score_cot, k_tile, 0, 0) * HD**-0.5

        @pl.when(tile == 0)
        def _():
            dq_sum[...] = dq

        @pl.when(tile > 0)
        def _():
            dq_sum[...] += dq

        if diagonal:
            cos, sin = turn_ref[lines, :HD], turn_ref[lines, HD:]
            for h in range(heads):
                part = dq_sum[h * AQ : (h + 1) * AQ, :]
                swapped = jnp.concatenate([part[:, HD // 2 :], -part[:, : HD // 2]], axis=1)
                heads_cot[lines, h * HD : (h + 1) * HD] = (part * cos + swapped * sin).astype(BF)

    starts = [0]
    for n in range(q_steps):
        starts.append(starts[-1] + n * AQ // AK + 1)
    attn_items = starts.pop()

    def wide_load(q_step):
        stored = lax.rem(q_step + half * (q_steps // 2), q_steps)
        lines = pl.ds(pl.multiple_of(stored * AQ, AQ), AQ)
        return pltpu.make_async_copy(wide_ref.at[lines, :], wide_buf, w_sem.at[1])

    def attn_one(n):
        q_step = sum([jnp.where(n >= start, 1, 0) for start in starts[1:]], jnp.int32(0))
        tile = n - sum([jnp.where(n >= b, b - a, 0) for a, b in zip(starts, starts[1:])], jnp.int32(0))
        last = q_step * AQ // AK

        @pl.when(tile == 0)
        def _():
            wide_load(q_step).wait()

        @pl.when(tile < last)
        def _():
            attn_item(q_step, tile, False)

        @pl.when(tile == last)
        def _():
            attn_item(q_step, tile, True)

            @pl.when(q_step + 1 < q_steps)
            def _():
                wide_load(q_step + 1).start()

    def attn_finish():
        part = dk_sum[...]
        swapped = jnp.concatenate([part[:, HD // 2 :], -part[:, : HD // 2]], axis=1)
        heads_cot[:, heads_width : heads_width + HD] = (part * turn_ref[:, :HD] + swapped * turn_ref[:, HD:]).astype(BF)
        heads_cot[:, heads_width + HD : heads_width + 2 * HD] = dv_sum[...].astype(BF)

    def head_load(i):
        slot = lax.rem(i, 2)
        lines = pl.ds(pl.multiple_of(i * MB, MB), MB)
        return pltpu.make_async_copy(x_ref.at[lines, :], bufs.at[slot, 1], buf_sem.at[slot, 1])

    def head_item(i):
        slot = lax.rem(i, 2)

        @pl.when(i + 1 < blocks)
        def _():
            head_load(i + 1).start()

        head_load(i).wait()
        lines = pl.ds(pl.multiple_of(i * MB, MB), MB)
        part = contract(heads_cot[lines, :heads_width], wq_ref[...], 1, 1)
        part += contract(heads_cot[lines, heads_width : heads_width + 2 * HD], wkv_ref[...], 1, 1)

        @pl.when(i > 0)
        def _():
            row_store(attn_part, i - 1).wait()

        bufs[slot, 2] = part.astype(BF)
        row_store(attn_part, i).start()
        inner = jnp.sum(part * gain_ref[0:1, :] * bufs[slot, 1].astype(F32), axis=1, keepdims=True)
        dots[pl.ds(i, 1), :] = jnp.broadcast_to(inner, (MB, LANES)).T[0:1, :]

    def dot_give():
        n = blocks // 2
        return remote(dots.at[pl.ds(n, n), :], dots_mate, dot_send.at[0], dot_recv.at[0], **mate)

    def dot_share():
        n = blocks // 2
        return [
            remote(dots.at[pl.ds(0, n), :], dots_col.at[s], dot_send.at[1 + s], dot_recv.at[1 + s], **peer)
            for s, peer in enumerate((near_x, near_y, corner))
        ]

    def emit(work, out, sem):
        for a in range(2):
            sum_total = work.total(a)
            h = tok // 4
            for b in range(2):
                lines = pl.ds(a * 2 * h + b * h, h)
                resid_sum = sum_total[b * h : (b + 1) * h]
                emit_buf[...] = resid_sum
                c = pltpu.make_async_copy(emit_buf, out.at[lines, :], sem)
                c.start()
                c.wait()

    emit_buf, = take(1)

    pltpu.make_async_copy(w_ref.at[pl.ds(pl.multiple_of(col * heads_width, heads_width), heads_width), :], w_mine, w_sem.at[0]).start()
    gain_part[...] = jnp.zeros_like(gain_part)
    heads_cot[:, heads_width + 2 * HD :] = jnp.zeros((span, CC - heads_width - 2 * HD), BF)
    zsum.begin()
    dk_sum[...] = jnp.zeros_like(dk_sum)
    dv_sum[...] = jnp.zeros_like(dv_sum)
    zsum.greet([near_x, near_y, corner, mate])

    at = {}

    def plan(tick, action):
        at.setdefault(tick, []).append(action)

    def start_all(copies):
        for c in copies:
            c.start()

    plan(0, mlp_reduce.begin)
    plan(T_ONE, lambda: [mlp_reduce.first(a) for a in range(2)])
    plan(T_TWO, lambda: [mlp_reduce.second(a) for a in range(2)])

    def own_block():
        for a in range(2):
            mine[mlp_reduce.lines(a), :] = mlp_reduce.total(a).astype(BF)
        gather.begin()

    plan(T_SUM, own_block)
    plan(T_GATHER, gather.first)
    plan(T_GATHER + 3, gather.second)

    def start_mid():
        gather.finish()
        mlp_reduce.finish()
        pltpu.make_async_copy(w_ref.at[pl.ds(0, heads_width), :], w_mine, w_sem.at[0]).wait()
        start_all(mid_loads(jnp.int32(0)))
        low_reduce.begin()

    plan(T_MID, start_mid)
    plan(T_MID + 4, lambda: [low_reduce.first(a) for a in range(2)])
    plan(T_MID + 9, lambda: [low_reduce.second(a) for a in range(2)])

    def low_done():
        emit(low_reduce, down_out, out_sem.at[2])
        low_reduce.finish()
        for i, peer in enumerate((near_x, near_y, mate)):
            pl.semaphore_signal(ready.at[i], inc=1, device_id=peer, device_id_type=MESH)

    plan(T_MID + 13, low_done)
    t_attn = T_MID + 1 + blocks // N_MID
    plan(t_attn, lambda: (row_store(mid_low, blocks - 1).wait(), wide_load(jnp.int32(0)).start()))
    t_head = t_attn + 1 + attn_items // N_ATTN
    plan(t_head, lambda: (attn_finish(), head_load(jnp.int32(0)).start()))
    t_last = t_head + 1 + blocks // N_HEAD

    def start_last():
        row_store(attn_part, blocks - 1).wait()
        dot_give().start()
        for i in range(3):
            pl.semaphore_wait(ready.at[i], 1)
        attn_reduce.begin()

    plan(t_last, start_last)

    def last_first():
        n = blocks // 2
        done(dots_mate, dot_recv.at[0])
        dot_give().wait_send()
        dots[pl.ds(0, n), :] = dots[pl.ds(0, n), :] + dots_mate[...]
        start_all(dot_share())
        for a in range(2):
            attn_reduce.first(a)

    plan(t_last + 3, last_first)
    plan(t_last + 7, lambda: [attn_reduce.second(a) for a in range(2)])

    def last_done():
        n = blocks // 2
        shares = dot_share()
        for c in shares:
            c.wait()
        terms = [dots[pl.ds(0, n), :], dots_col[0], dots_col[1], dots_col[2]]
        dot_out[...] = (terms[0] + terms[1]) + (terms[2] + terms[3])
        emit(attn_reduce, attn_out, out_sem.at[2])
        attn_reduce.finish()

    plan(t_last + 10, last_done)
    final = max(zsum.total + OFFS[3], t_last + 11)

    def tick(t, carry):
        zsum.tick(t)
        for when in sorted(at):

            @pl.when(t == when)
            def _(when=when):
                for action in at[when]:
                    action()

        @pl.when((t > T_MID) & (t < t_attn))
        def _():
            for e in range(N_MID):
                mid_item((t - T_MID - 1) * N_MID + e)

        @pl.when((t > t_attn) & (t < t_head))
        def _():
            def body(e, carry):
                attn_one((t - t_attn - 1) * N_ATTN + e)
                return carry

            lax.fori_loop(0, N_ATTN, body, 0)

        @pl.when((t > t_head) & (t < t_last))
        def _():
            for e in range(N_HEAD):
                head_item((t - t_head - 1) * N_HEAD + e)

        return carry

    lax.fori_loop(0, final, tick, 0)
    zsum.finish()


T_ONE, T_TWO, T_SUM, T_GATHER, T_MID = 2, 7, 10, 12, 19
N_MID, N_ATTN, N_HEAD = 2, 2, 4


def backward(info, gains, normed_mlp, gate_cot, up_cot, hidden, mlp_part, low_part, resid, low, w_out_full, mixed, q, k, v, wide, lse, cos, sin,
             wq, wkv, normed, tokens_full, cid):
    span, full = normed.shape
    tok, width = span // 2, full // 4
    heads_width = mixed.shape[1]
    heads = heads_width // HD
    units = hidden.shape[1]
    kinds = ["rows", "columns", "columns", "rows", "stack"]
    sources = [(units, full), (full, units), (full, units), (heads_width, full), (full, CC)]
    outs = [jax.ShapeDtypeStruct(grad_plan(kd, s)[5], BF) for kd, s in zip(kinds, sources)]
    outs = [outs[i] for i in (1, 2, 0, 3, 4)]
    vmem = pl.BlockSpec(memory_space=pltpu.VMEM)
    dma = pltpu.SemaphoreType.DMA
    blocks = span // MB
    turn = jnp.concatenate([cos, sin], axis=1)
    lse = lse.reshape(span // QB, heads, QB // AQ, AQ).transpose(0, 2, 1, 3).reshape(span // AQ, 1, heads * AQ)
    shapes = outs + [
        jax.ShapeDtypeStruct((tok, width), F32),
        jax.ShapeDtypeStruct((8, width), F32),
        jax.ShapeDtypeStruct((tok, width), F32),
        jax.ShapeDtypeStruct((tok, width), F32),
        jax.ShapeDtypeStruct((blocks // 2, LANES), F32),
        jax.ShapeDtypeStruct((span, full), BF),
        jax.ShapeDtypeStruct((span, full), BF),
        jax.ShapeDtypeStruct((span, full), BF),
    ]
    out_specs = [ANY] * 5 + [ANY, vmem, ANY, ANY, vmem, ANY, ANY, ANY]
    scratch = (
        [pltpu.VMEM((span, CC), BF)]
        + GroupSum.scratch(kinds, span)
        + Reduce.scratch(tok, full)
        + Reduce.sems() * 3
        + [pltpu.VMEM((tok, width), BF)]
        + Gather.sems()
        + [
            pltpu.VMEM((2, 3, MB, full), BF),
            pltpu.VMEM((2, MB, full), F32),
            pltpu.VMEM((MB, width), F32),
            dma((2, 3)),
            dma((3,)),
            pltpu.VMEM((span, heads_width), BF),
            pltpu.VMEM((AQ, heads_width), F32),
            pltpu.VMEM((heads * AQ, HD), F32),
            pltpu.VMEM((span, HD), F32),
            pltpu.VMEM((span, HD), F32),
            pltpu.VMEM((blocks, LANES), F32),
            pltpu.VMEM((blocks // 2, LANES), F32),
            pltpu.VMEM((3, blocks // 2, LANES), F32),
            dma((4,)),
            dma((4,)),
            pltpu.SemaphoreType.REGULAR((3,)),
            pltpu.VMEM((heads_width, full), BF),
            dma((2,)),
            pltpu.VMEM((tok // 4, width), F32),
        ]
    )
    results = pl.pallas_call(
        functools.partial(backward_kernel, kinds),
        in_specs=[pl.BlockSpec(memory_space=pltpu.SMEM), vmem] + [ANY] * 13 + [vmem] * 7,
        out_specs=out_specs,
        out_shape=shapes,
        scratch_shapes=scratch,
        compiler_params=pltpu.CompilerParams(
            collective_id=cid, has_side_effects=True, vmem_limit_bytes=VMEM_ALL
        ),
        name="backward",
    )(info, gains, normed_mlp, gate_cot, up_cot, hidden, mlp_part, low_part, resid, low, w_out_full, mixed, wide, normed,
      tokens_full, q, k, v, lse, turn, wq, wkv)
    return results[:10]


def by_distance(stacked, dim):
    count = lax.axis_size("col")
    order = lax.axis_index("col") ^ jnp.arange(count)
    blocks = jnp.take(stacked, order, axis=0)
    return jnp.concatenate([blocks[i] for i in range(count)], axis=dim)


def plain_gather(x):
    cols = by_distance(lax.all_gather(x, "col"), 1)
    return jnp.concatenate([cols, swap(cols, "row", 1)], axis=0)


def plain_gather_heads(x):
    mine = lax.all_gather(x, "col", axis=1, tiled=True)
    half = x.shape[0] // 2
    other = swap(mine, "row", 1)
    other = jnp.concatenate([other[half:], other[:half]], axis=0)
    return jnp.concatenate([mine, other], axis=1)


def plain_reduce(part):
    span, full = part.shape
    count = lax.axis_size("col")
    width = full // count
    half = part[: span // 2].astype(F32) + swap(part[span // 2 :], "row", 1).astype(F32)
    order = lax.axis_index("col") ^ jnp.arange(count)
    blocks = jnp.stack([half[:, s * width : (s + 1) * width] for s in range(count)])
    return lax.psum_scatter(jnp.take(blocks, order, axis=0), "col", tiled=False)


def exchange(packs):
    if kernels_fit():
        return [p if s == 0 else swap(p, "col", s) for s, p in enumerate(packs)]
    count = len(packs)
    order = lax.axis_index("col") ^ jnp.arange(count)
    sent = jnp.take(jnp.stack(packs), order, axis=0)
    blocks = jnp.take(lax.all_to_all(sent, "col", 0, 0, tiled=True), order, axis=0)
    return [blocks[i] for i in range(count)]


def plain_group_sum(grads, kinds):
    outs = []
    count = lax.axis_size("col")
    order = lax.axis_index("col") ^ jnp.arange(count)
    for grad, kind in zip(grads, kinds):
        grad = lax.psum(grad.astype(F32), "dp").astype(BF)
        dim = 1 if kind == "rows" else 0
        blocks = jnp.stack(jnp.split(grad, count, axis=dim))
        blocks = lax.all_to_all(jnp.take(blocks, order, axis=0), "col", 0, 0, tiled=True)
        out_dim = 1 if kind == "columns" else 0
        outs.append(jnp.concatenate([blocks[i] for i in range(count)], axis=out_dim))
    return outs


def kernels_fit():
    return lax.axis_size("col") == 4 and lax.axis_size("dp") == 4 and lax.axis_size("row") == 2


def attn_forward_kernel(info_ref, q_ref, k_ref, v_ref, *refs):
    linked = len(refs) > 6
    if linked:
        side_ref, mixed_ref, wide_ref, lse_ref, peak_ref, side_out, score_ref, sum_ref, stage = refs[:9]
        gather = Gather(side_ref, side_out, token_place(*side_ref.shape), stage, refs[9:])
    else:
        mixed_ref, wide_ref, lse_ref, peak_ref, score_ref, sum_ref = refs
    heads = q_ref.shape[1] // HD
    span = k_ref.shape[0]
    rows = heads * QB
    length = info_ref[0]
    half = lax.axis_index("row")
    step = pl.program_id(0)
    first = step * QB
    key_tiles = span // FWD_KB
    steps = span // QB
    lines = pl.ds(pl.multiple_of(lax.rem(step + half * (steps // 2), steps) * QB, QB), QB)

    if linked:

        @pl.when(step == 0)
        def _():
            greet(list(gather.near))
            gather.begin()

        @pl.when(step == steps - 1)
        def _():
            gather.first()

    q = jnp.concatenate([q_ref[lines, h * HD : (h + 1) * HD] for h in range(heads)], axis=0)
    tiles = (first + QB) // FWD_KB
    plain = first // FWD_KB

    def tile_of(ref, tile):
        stored = lax.rem(tile + half * (key_tiles // 2), key_tiles)
        return ref[pl.ds(pl.multiple_of(stored * FWD_KB, FWD_KB), FWD_KB), :]

    def fold(values, running, op):
        for t in range(FWD_KB // LANES):
            running = op(running, values[:, t * LANES : (t + 1) * LANES])
        return running

    def scores_of(tile, top, diagonal):
        scores = contract(q, tile_of(k_ref, tile), 1, 1) * HD**-0.5
        if diagonal:
            place = first + lax.broadcasted_iota(jnp.int32, (QB, FWD_KB), 0)
            key_place = tile * FWD_KB + lax.broadcasted_iota(jnp.int32, (QB, FWD_KB), 1)
            allowed = (key_place <= place) & (key_place < length)
            scores = jnp.where(allowed[None], scores.reshape(heads, QB, FWD_KB), NEG_FILL)
            scores = scores.reshape(rows, FWD_KB)
        else:
            key_place = tile * FWD_KB + lax.broadcasted_iota(jnp.int32, (1, FWD_KB), 1)
            scores = jnp.where(key_place < length, scores, NEG_FILL)
        score_ref[tile] = scores
        return fold(scores, top, jnp.maximum)

    top = jnp.full((rows, LANES), NEG_FILL, F32)
    top = lax.fori_loop(0, plain, lambda tile, top: scores_of(tile, top, False), top)
    top = lax.fori_loop(plain, tiles, lambda tile, top: scores_of(tile, top, True), top)
    top = jnp.max(top, axis=1, keepdims=True)
    live = first + lax.broadcasted_iota(jnp.int32, (QB, 1), 0) < length
    peak = jnp.max(jnp.where(live[None], top.reshape(heads, QB, 1), NEG_FILL), axis=1)

    @pl.when(step == 0)
    def _():
        peak_ref[...] = jnp.full_like(peak_ref, NEG_FILL)

    peak_ref[...] = jnp.maximum(peak_ref[...], jnp.broadcast_to(peak, peak_ref.shape))
    sum_ref[...] = jnp.zeros_like(sum_ref)

    def weigh(tile, total):
        weights = jnp.exp(score_ref[tile] - top)
        sum_ref[...] += contract(weights.astype(BF), tile_of(v_ref, tile), 1, 0)
        return fold(weights, total, jnp.add)

    total = lax.fori_loop(0, tiles, weigh, jnp.zeros((rows, LANES), F32))
    total = jnp.sum(total, axis=1, keepdims=True)
    mixed = sum_ref[...] / total
    log_total = jnp.broadcast_to(top + jnp.log(total), (rows, LANES))
    lse_ref[step] = log_total.T[0:1, :]
    for h in range(heads):
        part = mixed[h * QB : (h + 1) * QB]
        mixed_ref[lines, h * HD : (h + 1) * HD] = part.astype(BF)
        wide_ref[lines, h * HD : (h + 1) * HD] = part

    if linked:

        @pl.when(step == steps - 1)
        def _():
            gather.second()
            gather.finish()


def attn_forward(info, q, k, v, side=None, cid=None):
    span, width = q.shape
    heads = width // HD
    steps = span // QB
    whole = lambda shape: pl.BlockSpec(shape, lambda i: (0,) * len(shape))
    pairs = heads * span * span // 2
    shapes = [
        jax.ShapeDtypeStruct((span, width), BF),
        jax.ShapeDtypeStruct((span, width), F32),
        jax.ShapeDtypeStruct((steps, 1, heads * QB), F32),
        jax.ShapeDtypeStruct((heads, LANES), F32),
    ]
    in_specs = [pl.BlockSpec(memory_space=pltpu.SMEM)] + [whole(a.shape) for a in (q, k, v)]
    out_specs = [whole(s.shape) for s in shapes]
    scratch = [
        pltpu.VMEM((span // FWD_KB, heads * QB, FWD_KB), F32),
        pltpu.VMEM((heads * QB, HD), F32),
    ]
    operands = [info, q, k, v]
    params = dict(vmem_limit_bytes=48 * MIB)
    if side is not None:
        tok, wide = side.shape
        operands.append(side)
        in_specs.append(ANY)
        out_specs.append(ANY)
        shapes.append(jax.ShapeDtypeStruct((2 * tok, 4 * wide), side.dtype))
        scratch += [pltpu.VMEM(side.shape, side.dtype)] + Gather.sems()
        params.update(collective_id=cid, has_side_effects=True)
    return pl.pallas_call(
        attn_forward_kernel,
        grid=(steps,),
        in_specs=in_specs,
        out_specs=out_specs,
        scratch_shapes=scratch,
        out_shape=shapes,
        compiler_params=pltpu.CompilerParams(**params),
        cost_estimate=pl.CostEstimate(
            flops=40 * pairs * HD // 4, transcendentals=pairs, bytes_accessed=8 * span * width
        ),
        name="attn_forward",
    )(*operands)


def turn_back(values, cos_ref, sin_ref):
    half = HD // 2
    swapped = jnp.concatenate([values[:, half:], -values[:, :half]], axis=1)
    return values * cos_ref[...] + swapped * sin_ref[...]


def attn_backward_kernel(
    info_ref, q_ref, k_ref, v_ref, cot_ref, wide_ref, lse_ref, cosq_ref, sinq_ref, cosk_ref, sink_ref,
    dq_ref, dk_ref, dv_ref, dq_sum, dk_sum, dv_sum,
):
    heads = q_ref.shape[1] // HD
    span = k_ref.shape[0]
    rows = heads * QB
    length = info_ref[0]
    half = info_ref[1]
    step = pl.program_id(0)
    first = step * QB
    key_tiles = span // BWD_KB

    @pl.when(step == 0)
    def _():
        dk_sum[...] = jnp.zeros_like(dk_sum)
        dv_sum[...] = jnp.zeros_like(dv_sum)

    dq_sum[...] = jnp.zeros_like(dq_sum)

    @pl.when(first < length)
    def _():
        pieces = [slice(h * HD, (h + 1) * HD) for h in range(heads)]
        q = jnp.concatenate([q_ref[:, s] for s in pieces], axis=0)
        cot = jnp.concatenate([cot_ref[:, s] for s in pieces], axis=0)
        wide = jnp.concatenate([wide_ref[:, s] for s in pieces], axis=0)
        log_total = lse_ref[0]
        inner = jnp.sum(wide * cot.astype(F32), axis=1, keepdims=True)
        inner = jnp.broadcast_to(inner, (rows, LANES)).T[0:1, :]

        def tile_step(tile, masked):
            stored = lax.rem(tile + half * (key_tiles // 2), key_tiles)
            keys = pl.ds(pl.multiple_of(stored * BWD_KB, BWD_KB), BWD_KB)
            k_tile = k_ref[keys, :]
            v_tile = v_ref[keys, :]
            scores = contract(k_tile, q, 1, 1) * HD**-0.5 - log_total
            if masked:
                key_place = tile * BWD_KB + lax.broadcasted_iota(jnp.int32, (BWD_KB, rows), 0)
                place = first + lax.rem(lax.broadcasted_iota(jnp.int32, (BWD_KB, rows), 1), QB)
                scores = jnp.where((key_place <= place) & (key_place < length), scores, NEG_FILL)
            weights = jnp.exp(scores)
            prob_cot = contract(v_tile, cot, 1, 1)
            score_cot = (weights * (prob_cot - inner)).astype(BF)
            dv_sum[keys, :] += contract(weights.astype(BF), cot, 1, 0)
            dk_sum[keys, :] += contract(score_cot, q, 1, 0) * HD**-0.5
            dq_sum[...] += contract(score_cot, k_tile, 0, 0) * HD**-0.5

        @pl.loop(0, first // BWD_KB)
        def _(tile):
            tile_step(tile, False)

        @pl.loop(first // BWD_KB, pl.cdiv(first + QB, BWD_KB))
        def _(tile):
            tile_step(tile, True)

    for h in range(heads):
        part = turn_back(dq_sum[h * QB : (h + 1) * QB, :], cosq_ref, sinq_ref)
        dq_ref[:, h * HD : (h + 1) * HD] = part.astype(dq_ref.dtype)

    @pl.when(step == pl.num_programs(0) - 1)
    def _():
        dk_ref[...] = turn_back(dk_sum[...], cosk_ref, sink_ref).astype(dk_ref.dtype)
        dv_ref[...] = dv_sum[...].astype(dv_ref.dtype)


def attn_backward(info, q, k, v, cot, wide, lse, cos, sin, kv_type):
    span, width = q.shape
    heads = width // HD
    steps = span // QB

    def stored(i, info_ref):
        return (lax.rem(i + info_ref[1] * (steps // 2), steps), 0)

    whole = pl.BlockSpec((span, HD), lambda i, info_ref: (0, 0))
    mine = pl.BlockSpec((QB, width), stored)
    turn = pl.BlockSpec((QB, HD), stored)
    pairs = heads * span * span // 2
    return pl.pallas_call(
        attn_backward_kernel,
        grid_spec=pltpu.PrefetchScalarGridSpec(
            num_scalar_prefetch=1,
            grid=(steps,),
            in_specs=[
                mine, whole, whole, mine, mine,
                pl.BlockSpec((1, 1, heads * QB), lambda i, info_ref: (i, 0, 0)),
                turn, turn, whole, whole,
            ],
            out_specs=[mine, whole, whole],
            scratch_shapes=[
                pltpu.VMEM((heads * QB, HD), F32),
                pltpu.VMEM((span, HD), F32),
                pltpu.VMEM((span, HD), F32),
            ],
        ),
        out_shape=[
            jax.ShapeDtypeStruct((span, width), BF),
            jax.ShapeDtypeStruct((span, HD), kv_type),
            jax.ShapeDtypeStruct((span, HD), kv_type),
        ],
        compiler_params=pltpu.CompilerParams(vmem_limit_bytes=40 * 2**20),
        cost_estimate=pl.CostEstimate(
            flops=60 * pairs * HD // 4, transcendentals=pairs, bytes_accessed=12 * span * width
        ),
        name="attn_backward",
    )(info, q, k, v, cot, wide, lse, cos, sin, cos, sin)


def head_kernel(x_ref, gain_ref, wq_ref, wkv_ref, cos_ref, sin_ref, normed_ref, q_ref, k_ref, v_ref, scale_ref):
    x = x_ref[...].astype(F32)
    scale = lax.rsqrt(jnp.mean(x * x, axis=1, keepdims=True) + EPSILON)
    scale_ref[...] = jnp.broadcast_to(scale, scale_ref.shape)
    normed = (x * scale * gain_ref[0:1, :]).astype(BF)
    normed_ref[...] = normed

    def turned(raw):
        pieces = []
        half = HD // 2
        for h in range(raw.shape[1] // HD):
            pieces += [-raw[:, h * HD + half : (h + 1) * HD], raw[:, h * HD : h * HD + half]]
        pieces = jnp.concatenate(pieces, axis=1)
        count = raw.shape[1] // HD
        cos = jnp.concatenate([cos_ref[...]] * count, axis=1)
        sin = jnp.concatenate([sin_ref[...]] * count, axis=1)
        return (raw * cos + pieces * sin).astype(BF)

    q_ref[...] = turned(contract(normed, wq_ref[...], 1, 0))
    keyval = contract(normed, wkv_ref[...], 1, 0)
    k_ref[...] = turned(keyval[:, :HD])
    v_ref[...] = keyval[:, HD:].astype(BF)


def project_heads(tokens_full, gains, wq, wkv, cos, sin):
    span, full = tokens_full.shape
    width = wq.shape[1]
    block = 512
    line = lambda n: pl.BlockSpec((block, n), lambda i: (i, 0))
    whole = lambda a: pl.BlockSpec(a.shape, lambda i: (0, 0))
    return pl.pallas_call(
        head_kernel,
        grid=(span // block,),
        in_specs=[line(full), whole(gains), whole(wq), whole(wkv), line(HD), line(HD)],
        out_specs=[line(full), line(width), line(HD), line(HD), line(LANES)],
        out_shape=[
            jax.ShapeDtypeStruct((span, full), BF),
            jax.ShapeDtypeStruct((span, width), BF),
            jax.ShapeDtypeStruct((span, HD), BF),
            jax.ShapeDtypeStruct((span, HD), BF),
            jax.ShapeDtypeStruct((span, LANES), F32),
        ],
        compiler_params=pltpu.CompilerParams(vmem_limit_bytes=48 * MIB),
        cost_estimate=pl.CostEstimate(
            flops=2 * span * full * (width + LANES), transcendentals=0, bytes_accessed=5 * span * full
        ),
        name="project_heads",
    )(tokens_full, gains, wq, wkv, cos, sin)


def project_out_kernel(mixed_ref, w_ref, x_ref, gain_ref, *refs):
    linked = len(refs) > 2
    step = pl.program_id(0)
    if linked:
        side_ref, resid_ref, normed_ref, side_out, stage = refs[:5]
        gather = Gather(side_ref, side_out, token_place(*side_ref.shape), stage, refs[5:])

        @pl.when(step == 0)
        def _():
            greet(list(gather.near))
            gather.begin()

        @pl.when(step == pl.num_programs(0) // 2)
        def _():
            gather.first()

    else:
        resid_ref, normed_ref = refs
    resid = x_ref[...].astype(F32) + contract(mixed_ref[...], w_ref[...], 1, 0)
    resid_ref[...] = resid
    scale = lax.rsqrt(jnp.mean(resid * resid, axis=1, keepdims=True) + EPSILON)
    normed_ref[...] = (resid * scale * gain_ref[1:2, :]).astype(BF)

    if linked:

        @pl.when(step == pl.num_programs(0) - 1)
        def _():
            gather.second()
            gather.finish()


def project_out(mixed_full, w_out_full, tokens_full, gains, side=None, cid=None):
    span, full = tokens_full.shape
    block = 256
    line = pl.BlockSpec((block, full), lambda i: (i, 0))
    operands = [mixed_full, w_out_full, tokens_full, gains]
    in_specs = [
        pl.BlockSpec((block, mixed_full.shape[1]), lambda i: (i, 0)),
        pl.BlockSpec(w_out_full.shape, lambda i: (0, 0), pipeline_mode=pl.Buffered(1)),
        line,
        pl.BlockSpec(gains.shape, lambda i: (0, 0)),
    ]
    out_specs = [line, line]
    shapes = [jax.ShapeDtypeStruct((span, full), F32), jax.ShapeDtypeStruct((span, full), BF)]
    scratch = []
    params = dict(vmem_limit_bytes=48 * MIB)
    if side is not None:
        tok, wide = side.shape
        operands.append(side)
        in_specs.append(ANY)
        out_specs.append(ANY)
        shapes.append(jax.ShapeDtypeStruct((2 * tok, 4 * wide), side.dtype))
        scratch += [pltpu.VMEM(side.shape, side.dtype)] + Gather.sems()
        params.update(collective_id=cid, has_side_effects=True)
    return pl.pallas_call(
        project_out_kernel,
        grid=(span // block,),
        in_specs=in_specs,
        out_specs=out_specs,
        out_shape=shapes,
        scratch_shapes=scratch,
        compiler_params=pltpu.CompilerParams(**params),
        cost_estimate=pl.CostEstimate(
            flops=2 * span * full * full, transcendentals=0, bytes_accessed=12 * span * full
        ),
        name="project_out",
    )(*operands)


def middle_kernel(
    cot_ref, resid_ref, low_ref, gain_ref, w_ref, mixed_ref,
    mixed_cot_ref, own_ref, grad_ref, gain_part_ref, total_ref,
):
    step = pl.program_id(0)
    last = pl.num_programs(0) - 1
    width = own_ref.shape[1]
    cot = cot_ref[...].astype(F32)
    resid = resid_ref[...]
    scale = lax.rsqrt(jnp.mean(resid * resid, axis=1, keepdims=True) + EPSILON)
    weighed = cot * gain_ref[1:2, :]
    inner = jnp.sum(weighed * resid, axis=1, keepdims=True)
    mid = low_ref[...].astype(F32) + weighed * scale - resid * (scale * scale * scale * inner / D)
    low = mid.astype(BF)
    mixed_cot_ref[...] = contract(low, w_ref[...], 1, 1).astype(BF)

    @pl.when(step == 0)
    def _():
        total_ref[...] = jnp.zeros_like(total_ref)
        gain_part_ref[...] = jnp.zeros_like(gain_part_ref)

    total_ref[...] += contract(mixed_ref[...], low, 0, 0)

    @pl.when(step <= last // 2)
    def _():
        own_ref[...] = mid[:, :width]
        part = jnp.sum((cot * resid * scale)[:, :width], axis=0, keepdims=True)
        gain_part_ref[...] += jnp.broadcast_to(part, gain_part_ref.shape)

    @pl.when(step == last)
    def _():
        grad_ref[...] = total_ref[...].astype(BF)


def middle(mlp_cot, resid_mid, out_low, gains, w_mine, mixed, width):
    span, full = resid_mid.shape
    heads_width = mixed.shape[1]
    block = 256
    steps = span // block
    line = pl.BlockSpec((block, full), lambda i: (i, 0))
    thin = pl.BlockSpec((block, heads_width), lambda i: (i, 0))
    return pl.pallas_call(
        middle_kernel,
        grid=(steps,),
        in_specs=[
            line, line, line,
            pl.BlockSpec(gains.shape, lambda i: (0, 0)),
            pl.BlockSpec(w_mine.shape, lambda i: (0, 0)),
            thin,
        ],
        out_specs=[
            thin,
            pl.BlockSpec((block, width), lambda i: (jnp.minimum(i, steps // 2 - 1), 0)),
            pl.BlockSpec((heads_width, full), lambda i: (0, 0)),
            pl.BlockSpec((8, width), lambda i: (0, 0)),
        ],
        out_shape=[
            jax.ShapeDtypeStruct((span, heads_width), BF),
            jax.ShapeDtypeStruct((span // 2, width), F32),
            jax.ShapeDtypeStruct((heads_width, full), BF),
            jax.ShapeDtypeStruct((8, width), F32),
        ],
        scratch_shapes=[pltpu.VMEM((heads_width, full), F32)],
        compiler_params=pltpu.CompilerParams(vmem_limit_bytes=48 * MIB),
        cost_estimate=pl.CostEstimate(
            flops=4 * span * full * heads_width, transcendentals=0, bytes_accessed=8 * span * full
        ),
        name="middle",
    )(mlp_cot, resid_mid, out_low, gains, w_mine, mixed)


def head_back_kernel(
    info_ref, qc_ref, kc_ref, vc_ref, wq_ref, wkv_ref, normed_ref, x_ref, gain_ref,
    part_ref, dot_ref, grad_ref, total_ref,
):
    step = pl.program_id(0)
    wide = qc_ref.shape[1]
    keyval = jnp.concatenate([kc_ref[...], vc_ref[...]], axis=1)
    counted = keyval * info_ref[2].astype(BF)
    part = contract(qc_ref[...], wq_ref[...], 1, 1) + contract(counted, wkv_ref[...], 1, 1)
    part_ref[...] = part.astype(BF)
    inner = jnp.sum(part * gain_ref[0:1, :] * x_ref[...].astype(F32), axis=1, keepdims=True)
    dot_ref[0] = jnp.broadcast_to(inner, (inner.shape[0], LANES)).T[0:1, :]

    @pl.when(step == 0)
    def _():
        total_ref[...] = jnp.zeros_like(total_ref)

    total_ref[:, :wide] += contract(normed_ref[...], qc_ref[...], 0, 0)
    total_ref[:, wide:] += contract(normed_ref[...], keyval, 0, 0)

    @pl.when(step == pl.num_programs(0) - 1)
    def _():
        used = wide + 2 * HD
        grad_ref[:, :used] = total_ref[...].astype(BF)
        grad_ref[:, used:] = jnp.zeros((grad_ref.shape[0], grad_ref.shape[1] - used), BF)


def head_back(info, query_cot, key_cot, value_cot, wq, wkv, normed, tokens_full, gains):
    span, full = normed.shape
    wide = query_cot.shape[1]
    block = 512
    steps = span // block
    line = lambda n: pl.BlockSpec((block, n), lambda i, info_ref: (i, 0))
    whole = lambda shape: pl.BlockSpec(shape, lambda i, info_ref: (0, 0))
    grad_width = max(CC, wide + 2 * HD)
    return pl.pallas_call(
        head_back_kernel,
        grid_spec=pltpu.PrefetchScalarGridSpec(
            num_scalar_prefetch=1,
            grid=(steps,),
            in_specs=[
                line(wide), line(HD), line(HD), whole(wq.shape), whole(wkv.shape), line(full), line(full),
                whole(gains.shape),
            ],
            out_specs=[
                line(full),
                pl.BlockSpec((1, 1, block), lambda i, info_ref: (i, 0, 0)),
                whole((full, grad_width)),
            ],
            scratch_shapes=[pltpu.VMEM((full, wide + 2 * HD), F32)],
        ),
        out_shape=[
            jax.ShapeDtypeStruct((span, full), BF),
            jax.ShapeDtypeStruct((steps, 1, block), F32),
            jax.ShapeDtypeStruct((full, grad_width), BF),
        ],
        compiler_params=pltpu.CompilerParams(vmem_limit_bytes=48 * MIB),
        cost_estimate=pl.CostEstimate(
            flops=4 * span * full * (wide + LANES), transcendentals=0, bytes_accessed=6 * span * full
        ),
        name="head_back",
    )(info, query_cot, key_cot, value_cot, wq, wkv, normed, tokens_full, gains)


def on_device(
    tokens, lengths, attn_gain, w_query, w_key, w_value, w_out, mlp_gain, w_gate, w_up, w_down, cotangent
):
    row_devices = lax.axis_size("row")
    col_devices = lax.axis_size("col")
    row = lax.axis_index("row")
    col = lax.axis_index("col")
    fit = kernels_fit()
    tok, width = tokens.shape
    span = tok * row_devices
    group = HQ // KV
    heads_row = HQ // row_devices
    heads = heads_row // col_devices
    head_width = heads * HD
    keyval_row = KV // row_devices
    units = w_gate.shape[1] // col_devices
    length = lengths[0]
    shared_key = heads < group
    sharers = max(1, group // heads)
    leader = (col % sharers == 0).astype(jnp.int32)
    info = jnp.stack([length, row, leader]).astype(jnp.int32)

    keyval = []
    for owner in range(col_devices):
        first = owner * heads // group * HD
        keyval += [w_key[:, first : first + HD], w_value[:, first : first + HD]]
    keyval = jnp.concatenate(keyval, axis=1)
    gains = jnp.concatenate([attn_gain[None], mlp_gain[None], jnp.zeros((6, width), F32)], axis=0)

    if fit:
        tokens_full, wq, wkv, gains = first_gather(tokens, w_query, keyval, gains, 1)
    else:
        tokens_full = plain_gather(tokens)
        def slices(weight, size):
            return [lax.dynamic_slice_in_dim(weight, (col ^ s) * size, size, 1) for s in range(col_devices)]

        wq = jnp.concatenate(exchange(slices(w_query, head_width)), axis=0)
        wkv = jnp.concatenate(exchange(slices(keyval, LANES)), axis=0)
        gains = by_distance(lax.all_gather(gains, "col"), 1)
    w_gate, w_up, tokens_full = lax.optimization_barrier((w_gate, w_up, tokens_full))
    place = lax.rem(jnp.arange(span, dtype=jnp.int32) + row * tok, span)
    frequency = ROPE_BASE ** (-jnp.arange(HD // 2, dtype=F32) * (2.0 / HD))
    angle = place.astype(F32)[:, None] * frequency[None, :]
    cos = jnp.tile(jnp.cos(angle), (1, 2))
    sin = jnp.tile(jnp.sin(angle), (1, 2))

    normed_attn, query, key, value, scale_a = project_heads(tokens_full, gains, wq, wkv, cos, sin)
    valid = (row * tok + jnp.arange(tok, dtype=jnp.int32) < length).astype(BF)
    cot_low = cotangent * valid[:, None]
    if fit:
        mixed, mixed_wide, log_total, peak, w_out_full = attn_forward(info, query, key, value, w_out, 7)
        mixed_full = gather_heads(mixed, 2)
        w_down, mixed_full = lax.optimization_barrier((w_down, mixed_full))
        resid_mid, normed_mlp, out_low = project_out(mixed_full, w_out_full, tokens_full, gains, cot_low, 8)
    else:
        mixed, mixed_wide, log_total, peak = attn_forward(info, query, key, value)
        mixed_full = plain_gather_heads(mixed)
        w_out_full = plain_gather(w_out)
        resid_mid, normed_mlp = project_out(mixed_full, w_out_full, tokens_full, gains)
        out_low = plain_gather(cot_low)

    def unit_slices(weight, dim):
        return [lax.dynamic_slice_in_dim(weight, (col ^ s) * units, units, dim) for s in range(col_devices)]

    gate_blocks = exchange(unit_slices(w_gate, 1))
    up_blocks = exchange(unit_slices(w_up, 1))
    down_blocks = exchange(unit_slices(w_down, 0))
    normed_mlp, gate_blocks, up_blocks = lax.optimization_barrier((normed_mlp, gate_blocks, up_blocks))
    w_gate_units = jnp.concatenate(gate_blocks, axis=0)
    w_up_units = jnp.concatenate(up_blocks, axis=0)
    gate = jnp.dot(normed_mlp, w_gate_units, preferred_element_type=F32)
    up = jnp.dot(normed_mlp, w_up_units, preferred_element_type=F32)
    gate_sigmoid = jax.nn.sigmoid(gate)
    hidden = (gate * gate_sigmoid * up).astype(BF)

    hidden, down_blocks = lax.optimization_barrier((hidden, down_blocks))
    w_down_units = jnp.concatenate(down_blocks, axis=1)
    hidden_cot = contract(out_low, w_down_units, 1, 1)
    gate_cot = (
        hidden_cot * up * gate_sigmoid * (1.0 + gate * (1.0 - gate_sigmoid))
    ).astype(BF)
    up_cot = (hidden_cot * gate * gate_sigmoid).astype(BF)
    mlp_part = (contract(gate_cot, w_gate_units, 1, 1) + contract(up_cot, w_up_units, 1, 1)).astype(BF)
    down_part = jnp.dot(hidden, w_down_units, preferred_element_type=F32).astype(BF)

    if fit:
        *sums, mid_cot, gain_m_part, attn_cot, down_sum, width_dot = backward(
            info, gains, normed_mlp, gate_cot, up_cot, hidden, mlp_part, down_part, resid_mid, out_low, w_out_full,
            mixed, query, key, value, mixed_wide, log_total, cos, sin, wq, wkv, normed_attn, tokens_full, 3,
        )
        width_dot = width_dot.reshape(tok)
    else:
        mlp_cot = plain_gather(plain_reduce(mlp_part).astype(BF))
        down_sum = plain_reduce(down_part)
        w_mine = lax.dynamic_slice_in_dim(w_out_full, col * head_width, head_width, 0)
        mixed_cot, mid_cot, grad_out, gain_m_part = middle(
            mlp_cot, resid_mid, out_low, gains, w_mine, mixed, width
        )
        query_cot, key_cot, value_cot = attn_backward(
            info, query, key, value, mixed_cot, mixed_wide, log_total, cos, sin, F32 if shared_key else BF
        )
        if shared_key:
            for bit in range(sharers.bit_length() - 1):
                key_cot = key_cot + swap(key_cot, "col", 1 << bit)
                value_cot = value_cot + swap(value_cot, "col", 1 << bit)
            key_cot, value_cot = key_cot.astype(BF), value_cot.astype(BF)
        attn_part, dot_part, grad_heads = head_back(
            info, query_cot, key_cot, value_cot, wq, wkv, normed_attn, tokens_full, gains
        )
        dot_part = dot_part.reshape(span)
        width_dot = lax.psum(dot_part[:tok] + swap(dot_part[tok:], "row", 1), "col")
        attn_cot = plain_reduce(attn_part)
        grad_gate = contract(normed_mlp, gate_cot, 0, 0).astype(BF)
        grad_up = contract(normed_mlp, up_cot, 0, 0).astype(BF)
        grad_down = contract(hidden, out_low, 0, 0).astype(BF)
        sums = plain_group_sum(
            [grad_gate, grad_up, grad_down, grad_out, grad_heads], ["columns", "columns", "rows", "rows", "stack"]
        )
    output = (resid_mid[:tok, :width] + down_sum).astype(BF)
    own_in = tokens.astype(F32)
    scale_own = scale_a[:tok, :1]
    input_grad = (
        mid_cot
        + attn_cot * attn_gain * scale_own
        - own_in * (scale_own * scale_own * scale_own * width_dot[:, None] / D)
    )
    gain_a_part = jnp.sum(attn_cot * own_in * scale_own, axis=0)

    out_gate, out_up, out_down, out_out, out_heads = [g.astype(F32) for g in sums]
    out_heads = out_heads.reshape(col_devices, width, out_heads.shape[1])
    out_query = jnp.concatenate([out_heads[i, :, :head_width] for i in range(col_devices)], axis=1)
    leaders = range(0, col_devices, sharers)
    out_key = jnp.concatenate([out_heads[i, :, head_width : head_width + HD] for i in leaders], axis=1)
    out_value = jnp.concatenate(
        [out_heads[i, :, head_width + HD : head_width + 2 * HD] for i in leaders], axis=1
    )

    gain_sums = jnp.stack([gain_a_part, gain_m_part[0]])
    gain_sums = gain_sums + swap(gain_sums, "row", 1)
    step = 1
    while step < lax.axis_size("dp"):
        gain_sums = gain_sums + swap(gain_sums, "dp", step)
        step *= 2
    step = 1
    while step < lax.axis_size("dp"):
        peak = jnp.maximum(peak, swap(peak, "dp", step))
        step *= 2
    own_peaks = peak[:, 0]
    slots = jnp.arange(col_devices)[:, None]
    row_peaks = jnp.where(slots == col, own_peaks[None, :], NEG_FILL)
    step = 1
    while step < col_devices:
        row_peaks = jnp.maximum(row_peaks, swap(row_peaks, "col", step))
        step *= 2
    row_peaks = row_peaks.reshape(heads_row)
    clip_factor = CLIP_LEVEL / jnp.maximum(row_peaks, CLIP_LEVEL)
    query_scale = jnp.repeat(jnp.sqrt(clip_factor), HD)
    key_scale = jnp.repeat(jnp.sqrt(jnp.min(clip_factor.reshape(keyval_row, group), axis=1)), HD)
    clipped_query = (w_query.astype(F32) * query_scale[None, :]).astype(BF)
    clipped_key = (w_key.astype(F32) * key_scale[None, :]).astype(BF)
    return (
        output,
        input_grad,
        gain_sums[0],
        out_query,
        out_key,
        out_value,
        out_out,
        gain_sums[1],
        out_gate,
        out_up,
        out_down,
        own_peaks,
        clipped_query,
        clipped_key,
    )


def solution(mesh):
    in_specs = (
        P(("dp", "row"), "col"),
        P("dp"),
        P("col"),
        P("col", "row"),
        P("col", "row"),
        P("col", "row"),
        P("row", "col"),
        P("col"),
        P("col", "row"),
        P("col", "row"),
        P("row", "col"),
        P(("dp", "row"), "col"),
    )
    out_specs = (
        P(("dp", "row"), "col"),
        P(("dp", "row"), "col"),
        P("col"),
        P("col", "row"),
        P("col", "row"),
        P("col", "row"),
        P("row", "col"),
        P("col"),
        P("col", "row"),
        P("col", "row"),
        P("row", "col"),
        P(("row", "col")),
        P("col", "row"),
        P("col", "row"),
    )
    return jax.shard_map(
        on_device, mesh=mesh, in_specs=in_specs, out_specs=out_specs, check_vma=False
    )
```

```python
import functools

import jax
import jax.numpy as jnp
from jax import lax
from jax.experimental import pallas as pl
from jax.experimental.pallas import tpu as pltpu
from jax.sharding import PartitionSpec as P

D = 2048
HQ = 32
KV = 8
HD = 64
SEQ_LEN = 2048

EPSILON = 1e-05
NEG_FILL = -1e30
CLIP_LEVEL = 5.0
ROPE_BASE = 500000.0

BF = jnp.bfloat16
F32 = jnp.float32
LANES = 128
QB = 512
FWD_KB = 512
BWD_KB = 512
MESH = pl.DeviceIdType.MESH
ANY = pl.BlockSpec(memory_space=pl.ANY)
NCH = 4
CR, CC = 256, 512
HR = CR // 2
OFFS = (0, 2, 4, 7)
RING = 12
MIB = 2**20
VMEM_ALL = 63 * MIB


def contract(left, right, left_dim, right_dim):
    return lax.dot_general(
        left, right, (((left_dim,), (right_dim,)), ((), ())), preferred_element_type=F32
    )


def swap(values, axis, step):
    count = lax.axis_size(axis)
    return lax.ppermute(values, axis, [(i, i ^ step) for i in range(count)])


def flip(index, bit):
    return index + bit - 2 * bit * lax.rem(index // bit, 2)


def xor(index, step):
    return lax.rem(lax.rem(index, 2) + step % 2, 2) + 2 * lax.rem(index // 2 + step // 2, 2)


def remote(src, dst, send, recv, **where):
    return pltpu.make_async_remote_copy(
        src_ref=src, dst_ref=dst, send_sem=send, recv_sem=recv, device_id=where, device_id_type=MESH
    )


def done(ref, sem):
    pltpu.make_async_copy(ref, ref, sem).wait()


def greet(targets):
    barrier = pltpu.get_barrier_semaphore()
    for target in targets:
        pl.semaphore_signal(barrier, inc=1, device_id=target, device_id_type=MESH)
    pl.semaphore_wait(barrier, len(targets))


def plane_peers():
    row = lax.axis_index("row")
    col = lax.axis_index("col")
    return {"col": flip(col, 1)}, {"col": flip(col, 2)}, {"row": 1 - row}


def token_place(tok, width):
    rows = tok // NCH

    def place(ref, half, s, j, who):
        return ref.at[pl.ds(half * tok + j * rows, rows), pl.ds(s * width, width)]

    return place


def head_place(span, width):
    rows = span // NCH

    def place(ref, half, s, j, who):
        start = j * rows if half == 0 else ((j + NCH // 2) % NCH) * rows
        return ref.at[pl.ds(start, rows), pl.ds(pl.multiple_of((half * 4 + xor(who, s)) * width, LANES), width)]

    return place


class Gather:
    SEMS = 6

    def __init__(self, src, out, place, stage, sems):
        self.src, self.out, self.place, self.stage = src, out, place, stage
        self.own_send, self.relay_send, self.mate_send, self.recv, self.mate_recv, self.local = sems
        self.col = lax.axis_index("col")
        self.near = plane_peers()

    @staticmethod
    def sems():
        shapes = [(2, NCH), (NCH,), (4, NCH), (3, NCH), (4, NCH), (2,)]
        return [pltpu.SemaphoreType.DMA(s) for s in shapes]

    def chunk(self, j):
        rows = self.src.shape[0] // NCH
        return self.src.at[pl.ds(j * rows, rows), :]

    def here(self, half, s, j):
        return self.place(self.out, half, s, j, self.col)

    def own(self, axis, j):
        peer = self.near[axis]
        dst = self.place(self.out, 0, axis + 1, j, peer["col"])
        return remote(self.chunk(j), dst, self.own_send.at[axis, j], self.recv.at[axis, j], **peer)

    def relay(self, axis, j):
        peer = self.near[1 - axis]
        dst = self.place(self.out, 0, 3, j, peer["col"])
        return remote(self.here(0, axis + 1, j), dst, self.relay_send.at[j], self.recv.at[2, j], **peer)

    def mate(self, s, j):
        src = self.chunk(j) if s == 0 else self.here(0, s, j)
        dst = self.place(self.out, 1, s, j, self.col)
        return remote(src, dst, self.mate_send.at[s, j], self.mate_recv.at[s, j], **self.near[2])

    def load(self):
        return pltpu.make_async_copy(self.src, self.stage, self.local.at[0])

    def keep(self, j):
        rows = self.src.shape[0] // NCH
        whole = self.stage if self.stage is not None else self.src
        return pltpu.make_async_copy(whole.at[pl.ds(j * rows, rows), :], self.here(0, 0, j), self.local.at[1])

    def begin(self):
        half = NCH // 2
        if self.stage is not None:
            self.load().start()
        for i in range(NCH):
            self.own(0, i).start()
            self.own(1, (i + half) % NCH).start()
        for j in range(NCH):
            self.mate(0, j).start()

    def arrived(self, s, j):
        done(self.here(0, s, j), self.recv.at[s - 1, j])

    def first(self):
        half = NCH // 2
        for i in range(half):
            self.arrived(1, i)
            self.relay(0, i).start()
            self.mate(1, i).start()
            self.arrived(2, half + i)
            self.relay(1, half + i).start()
            self.mate(2, half + i).start()

    def second(self):
        half = NCH // 2
        if self.stage is not None:
            self.load().wait()
        for j in range(NCH):
            self.keep(j).start()
        for i in range(half):
            self.arrived(1, half + i)
            self.mate(1, half + i).start()
            self.arrived(2, i)
            self.mate(2, i).start()
        for i in range(half):
            for j in (i, half + i):
                self.arrived(3, j)
                self.mate(3, j).start()

    def finish(self):
        half = NCH // 2
        for s in range(4):
            for j in range(NCH):
                done(self.here(1, s, j), self.mate_recv.at[s, j])
                self.mate(s, j).wait_send()
        for j in range(NCH):
            self.own(0, j).wait_send()
            self.own(1, j).wait_send()
            self.relay(0 if j < half else 1, j).wait_send()
        whole = self.stage if self.stage is not None else self.src
        done(whole, self.local.at[1])


def gather_kernel(place_of, x_ref, out_ref, stage, *sems):
    near_x, near_y, mate = plane_peers()
    greet([near_x, near_y, mate])
    gather = Gather(x_ref, out_ref, place_of(*x_ref.shape), stage, sems)
    gather.begin()
    gather.first()
    gather.second()
    gather.finish()


def gather_call(x, shape, place_of, cid, name):
    return pl.pallas_call(
        functools.partial(gather_kernel, place_of),
        in_specs=[ANY],
        out_specs=ANY,
        out_shape=jax.ShapeDtypeStruct(shape, x.dtype),
        scratch_shapes=[pltpu.VMEM(x.shape, x.dtype)] + Gather.sems(),
        compiler_params=pltpu.CompilerParams(collective_id=cid, has_side_effects=True),
        name=name,
    )(x)


def gather_tokens(x, cid):
    tok, width = x.shape
    return gather_call(x, (2 * tok, 4 * width), token_place, cid, "gather_tokens")


def gather_heads(x, cid):
    span, width = x.shape
    return gather_call(x, (span, 8 * width), head_place, cid, "gather_heads")


class Reduce:
    def __init__(self, part, scratch, sems):
        self.part = part
        self.own, self.given, self.sent, self.got_one, self.got_two = scratch
        self.loads, self.mate_send, self.mate_recv, self.one_send, self.one_recv, self.two_send, self.two_recv = sems
        self.near = plane_peers()
        self.h = self.own.shape[0] // 2
        self.width = self.own.shape[1] // 4

    @staticmethod
    def scratch(tok, full):
        h, w = tok // 2, full // 4
        shapes = [(tok, full), (tok, full), (2, 3, h, w), (2, 2, h, w), (2, h, w)]
        return [pltpu.VMEM(s, BF) for s in shapes]

    @staticmethod
    def sems():
        return [pltpu.SemaphoreType.DMA((2,))] * 7

    def lines(self, a):
        return pl.ds(a * self.h, self.h)

    def give(self, a):
        src = self.part.at[pl.ds((2 + a) * self.h, self.h), :]
        return remote(src, self.given.at[self.lines(a), :], self.mate_send.at[a], self.mate_recv.at[a], **self.near[2])

    def load(self, a):
        return pltpu.make_async_copy(self.part.at[self.lines(a), :], self.own.at[self.lines(a), :], self.loads.at[a])

    def one(self, a):
        src = self.sent.at[a, pl.ds(0, 2)]
        return remote(src, self.got_one.at[a], self.one_send.at[a], self.one_recv.at[a], **self.near[a])

    def two(self, a):
        return remote(self.sent.at[a, 2], self.got_two.at[a], self.two_send.at[a], self.two_recv.at[a], **self.near[1 - a])

    def pair(self, a, s):
        cols = pl.ds(s * self.width, self.width)
        rows = self.lines(a)
        return self.own[rows, cols].astype(F32) + self.given[rows, cols].astype(F32)

    def begin(self):
        for a in range(2):
            self.give(a).start()
            self.load(a).start()

    def first(self, a):
        self.load(a).wait()
        done(self.given.at[self.lines(a), :], self.mate_recv.at[a])
        for i, s in enumerate((a + 1, 3)):
            self.sent[a, i] = self.pair(a, s).astype(BF)
        self.one(a).start()

    def second(self, a):
        done(self.got_one.at[a], self.one_recv.at[a])
        self.sent[a, 2] = (self.pair(a, 2 - a) + self.got_one[a, 1].astype(F32)).astype(BF)
        self.two(a).start()

    def total(self, a):
        done(self.got_two.at[a], self.two_recv.at[a])
        return self.pair(a, 0) + self.got_one[a, 0].astype(F32) + self.got_two[a].astype(F32)

    def finish(self):
        for a in range(2):
            self.give(a).wait_send()
            self.one(a).wait_send()
            self.two(a).wait_send()


def first_gather_kernel(
    x_ref, wq_ref, wkv_ref, gain_ref, out_ref, wq_out, wkv_out, gain_out,
    stage, wq_stage, wkv_stage, gain_stage, stage_sem, small_send, small_recv, *sems,
):
    near_x, near_y, mate = plane_peers()
    col = lax.axis_index("col")
    tok, width = x_ref.shape
    wide = wq_ref.shape[1] // 4
    thin = wkv_ref.shape[1] // 4

    def share(ref, owner, size):
        return ref.at[:, pl.ds(pl.multiple_of(owner * size, LANES), size)]

    loads = [
        pltpu.make_async_copy(share(wq_ref, col, wide), wq_stage, stage_sem.at[0]),
        pltpu.make_async_copy(share(wkv_ref, col, thin), wkv_stage, stage_sem.at[1]),
        pltpu.make_async_copy(gain_ref, gain_stage, stage_sem.at[2]),
    ]
    for c in loads:
        c.start()
    greet([near_x, near_y, {"col": 3 - col}, mate])
    smalls = []
    for s, peer in ((1, near_x), (2, near_y), (3, {"col": 3 - col})):
        owner = peer["col"]
        lines = pl.ds(s * width, width)
        smalls += [
            remote(share(wq_ref, owner, wide), wq_out.at[lines, :], small_send.at[0, s], small_recv.at[0, s], **peer),
            remote(share(wkv_ref, owner, thin), wkv_out.at[lines, :], small_send.at[1, s], small_recv.at[1, s], **peer),
            remote(gain_ref, gain_out.at[:, lines], small_send.at[2, s], small_recv.at[2, s], **peer),
        ]
    gather = Gather(x_ref, out_ref, token_place(tok, width), stage, sems)
    gather.begin()
    for c in smalls:
        c.start()
    lines = pl.ds(0, width)
    keeps = [
        pltpu.make_async_copy(wq_stage, wq_out.at[lines, :], stage_sem.at[3]),
        pltpu.make_async_copy(wkv_stage, wkv_out.at[lines, :], stage_sem.at[4]),
        pltpu.make_async_copy(gain_stage, gain_out.at[:, lines], stage_sem.at[5]),
    ]
    for load, keep in zip(loads, keeps):
        load.wait()
        keep.start()
    gather.first()
    gather.second()
    gather.finish()
    for c in smalls:
        c.wait()
    for c in keeps:
        c.wait()


def first_gather(x, wq, wkv, gains, cid):
    tok, width = x.shape
    wide, thin = wq.shape[1] // 4, wkv.shape[1] // 4
    return pl.pallas_call(
        first_gather_kernel,
        in_specs=[ANY] * 4,
        out_specs=[ANY] * 4,
        out_shape=[
            jax.ShapeDtypeStruct((2 * tok, 4 * width), BF),
            jax.ShapeDtypeStruct((4 * width, wide), BF),
            jax.ShapeDtypeStruct((4 * width, thin), BF),
            jax.ShapeDtypeStruct((8, 4 * width), F32),
        ],
        scratch_shapes=[
            pltpu.VMEM((tok, width), BF),
            pltpu.VMEM((width, wide), BF),
            pltpu.VMEM((width, thin), BF),
            pltpu.VMEM((8, width), F32),
            pltpu.SemaphoreType.DMA((6,)),
            pltpu.SemaphoreType.DMA((3, 4)),
            pltpu.SemaphoreType.DMA((3, 4)),
        ]
        + Gather.sems(),
        compiler_params=pltpu.CompilerParams(collective_id=cid, has_side_effects=True),
        name="first_gather",
    )(x, wq, wkv, gains)


def grad_plan(kind, shape):
    rows, cols = shape
    if kind == "columns":
        w = rows // 4
        high, n = rows // CR, w // CR
        return (
            high * (cols // CC), high,
            lambda i: lax.rem(i, high) // n, lambda i: lax.rem(i, high), lambda i: i // high,
            (w, 4 * cols), lambda c, i: (lax.rem(i, n) * CR, c * cols + i // high * CC),
        )
    high = rows // CR
    if kind == "rows":
        return (
            4 * high, high,
            lambda i: i // high, lambda i: lax.rem(i, high), lambda i: i // high,
            (4 * rows, cols // 4), lambda c, i: (c * rows + lax.rem(i, high) * CR, 0),
        )
    n = high // 4
    return (
        high, high,
        lambda i: i // n, lambda i: i, lambda i: 0,
        (rows, cols), lambda c, i: ((c * n + lax.rem(i, n)) * CR, 0),
    )


class GroupSum:
    def __init__(self, kinds, lefts, rights, outs, refs):
        (self.left, self.right, self.left_sem, self.right_sem, self.own, self.land, self.mids, self.tops, self.in_send, self.in_recv, self.mid_send,
         self.mid_recv, self.top_send, self.top_recv, self.out_send, self.out_recv, self.far_send, self.far_recv) = refs
        self.lefts, self.rights, self.outs = lefts, rights, outs
        self.plans = [grad_plan(k, (a.shape[1], b.shape[1])) for k, a, b in zip(kinds, lefts, rights)]
        self.counts = [p[0] for p in self.plans]
        self.begins = [sum(self.counts[:i]) for i in range(len(lefts))]
        groups = [p[0] // p[1] for p in self.plans]
        self.groups = [sum(groups[:i]) for i in range(len(lefts))]
        self.total = sum(self.counts)
        z = lax.axis_index("dp")
        self.col = lax.axis_index("col")
        self.is_mid = (z == 1) | (z == 2)
        self.is_end = jnp.logical_not(self.is_mid)
        left = z < 2
        self.inward = {"dp": jnp.where(left, z + 1, z - 1)}
        self.outward = {"dp": jnp.where(left, z - 1, z + 1)}
        self.kept = jnp.where(left, 0, 1)

    @staticmethod
    def scratch(kinds, span):
        dma = pltpu.SemaphoreType.DMA
        return (
            [pltpu.VMEM((2, span, CR), BF), pltpu.VMEM((2, span, CC), BF), dma((2,)), dma((2,))]
            + [pltpu.VMEM((RING, CR, CC), BF)] * 2
            + [pltpu.VMEM((RING, HR, CC), BF)] * 2
            + [dma((RING,))] * 6
            + [dma((RING, 2))] * 3
            + [dma((len(kinds),))]
        )

    def greet(self, others):
        barrier = pltpu.get_barrier_semaphore()
        targets = [self.inward] + others
        for target in targets:
            pl.semaphore_signal(barrier, inc=1, device_id=target, device_id_type=MESH)

        @pl.when(self.is_mid)
        def _():
            pl.semaphore_signal(barrier, inc=1, device_id=self.outward, device_id_type=MESH)
            pl.semaphore_wait(barrier, len(targets) + 1)

        @pl.when(self.is_end)
        def _():
            pl.semaphore_wait(barrier, len(targets))

    def rows(self, half):
        return pl.ds(pl.multiple_of(half * HR, HR), HR)

    def each(self, j, action):
        for m, count in enumerate(self.counts):

            @pl.when((j >= self.begins[m]) & (j < self.begins[m] + count))
            def _(m=m):
                action(m, j - self.begins[m])

    def left_load(self, m, i, j):
        lines = pl.ds(pl.multiple_of(self.plans[m][3](i) * CR, CR), CR)
        slot = lax.rem(j, 2)
        return pltpu.make_async_copy(self.lefts[m].at[:, lines], self.left.at[slot], self.left_sem.at[slot])

    def right_slot(self, m, i):
        return lax.rem(self.groups[m] + i // self.plans[m][1], 2)

    def right_load(self, m, i):
        lines = pl.ds(pl.multiple_of(self.plans[m][4](i) * CC, CC), CC)
        slot = self.right_slot(m, i)
        return pltpu.make_async_copy(self.rights[m].at[:, lines], self.right.at[slot], self.right_sem.at[slot])

    def fetch(self, j):
        def action(m, i):
            self.left_load(m, i, j).start()
            if self.resident[m] is None:

                @pl.when(lax.rem(i, self.plans[m][1]) == 0)
                def _():
                    self.right_load(m, i).start()

        self.each(j, action)

    def produce(self, j):
        slot = lax.rem(j, RING)

        def action(m, i):
            self.left_load(m, i, j).wait()
            if self.resident[m] is None:

                @pl.when(lax.rem(i, self.plans[m][1]) == 0)
                def _():
                    self.right_load(m, i).wait()

                right = self.right[self.right_slot(m, i)]
            else:
                right = self.resident[m][...]
            self.own[slot] = contract(self.left[lax.rem(j, 2)], right, 0, 0).astype(BF)

        self.each(j, action)

    def spread(self, j, half, src):
        slot = lax.rem(j, RING)

        def action(m, i):
            s = self.plans[m][2](i)
            r, q = self.plans[m][6](self.col, i)
            dst = self.outs[m].at[
                pl.ds(pl.multiple_of(r + half * HR, HR), HR), pl.ds(pl.multiple_of(q, CC), CC)
            ]

            @pl.when(s == 0)
            def _():
                pltpu.make_async_copy(src, dst, self.far_send.at[slot, half]).start()

            @pl.when(s > 0)
            def _():
                owner = lax.rem(lax.rem(self.col, 2) + lax.rem(s, 2), 2) + 2 * lax.rem(self.col // 2 + s // 2, 2)
                remote(src, dst, self.far_send.at[slot, half], self.far_recv.at[m], col=owner).start()

        self.each(j, action)

    def reclaim(self, j):
        slot = lax.rem(j, RING)
        for half in range(2):
            done(self.mids.at[slot], self.far_send.at[slot, half])

        @pl.when(self.is_mid)
        def _():
            done(self.mids.at[slot], self.mid_send.at[slot])
            done(self.mids.at[slot], self.top_send.at[slot])
            for half in range(2):
                done(self.mids.at[slot], self.out_send.at[slot, half])

        @pl.when(self.is_end)
        def _():
            done(self.own.at[slot], self.in_send.at[slot])

    def inbound(self, j):
        slot = lax.rem(j, RING)

        @pl.when(self.is_mid)
        def _():
            done(self.land.at[slot], self.in_recv.at[slot])
            self.own[slot] = (self.own[slot].astype(F32) + self.land[slot].astype(F32)).astype(BF)
            src = self.own.at[slot, self.rows(1 - self.kept)]
            remote(src, self.mids.at[slot], self.mid_send.at[slot], self.mid_recv.at[slot], **self.inward).start()

        @pl.when(self.is_end)
        def _():
            remote(
                self.own.at[slot], self.land.at[slot], self.in_send.at[slot], self.in_recv.at[slot], **self.inward
            ).start()

    def middle(self, j):
        slot = lax.rem(j, RING)

        @pl.when(self.is_mid)
        def _():
            done(self.mids.at[slot], self.mid_recv.at[slot])
            rows = self.rows(self.kept)
            self.own[slot, rows] = (self.own[slot, rows].astype(F32) + self.mids[slot].astype(F32)).astype(BF)
            src = self.own.at[slot, rows]
            remote(src, self.tops.at[slot], self.top_send.at[slot], self.top_recv.at[slot], **self.inward).start()
            remote(
                src, self.land.at[slot, rows], self.out_send.at[slot, self.kept], self.out_recv.at[slot, self.kept],
                **self.outward,
            ).start()
            self.spread(j, self.kept, src)

    def settle(self, j):
        slot = lax.rem(j, RING)

        @pl.when(self.is_mid)
        def _():
            done(self.tops.at[slot], self.top_recv.at[slot])
            half = 1 - self.kept
            src = self.tops.at[slot]
            remote(
                src, self.land.at[slot, self.rows(half)], self.out_send.at[slot, half], self.out_recv.at[slot, half],
                **self.outward,
            ).start()
            self.spread(j, half, src)

    def outbound(self, j):
        slot = lax.rem(j, RING)

        @pl.when(self.is_end)
        def _():
            for half in range(2):
                src = self.land.at[slot, pl.ds(half * HR, HR)]
                done(src, self.out_recv.at[slot, half])
                self.spread(j, half, src)

    def begin(self):
        self.fetch(jnp.int32(0))
        self.produce(jnp.int32(0))
        self.fetch(jnp.int32(1))

    def tick(self, t):
        for off, stage in zip(OFFS, (self.inbound, self.middle, self.settle, self.outbound)):

            @pl.when((t >= off) & (t < self.total + off))
            def _(off=off, stage=stage):
                stage(t - off)

        ahead = t + 1

        @pl.when(ahead < self.total)
        def _():
            @pl.when(ahead >= RING)
            def _():
                self.reclaim(ahead - RING)

            self.produce(ahead)

            @pl.when(ahead + 1 < self.total)
            def _():
                self.fetch(ahead + 1)

    def finish(self):
        def drain(j, carry):
            self.reclaim(j)
            return carry

        lax.fori_loop(self.total - RING, self.total, drain, 0)
        for m, out in enumerate(self.outs):
            done(out.at[pl.ds(0, 3 * out.shape[0] // 4)], self.far_recv.at[m])


MB = 128
AQ, AK = 256, 512


def backward_kernel(
    kinds,
    info_ref, gain_ref, mlp_ref, gate_ref, up_ref, hidden_ref, part_ref, low_part_ref, resid_ref, low_ref, w_ref, mixed_ref,
    wide_ref, normed_ref, x_ref, q_ref, k_ref, v_ref, lse_ref, turn_ref, wq_ref, wkv_ref,
    out_gate, out_up, out_down, out_out, out_heads, mid_out, gain_part, attn_out, down_out, dot_out,
    cot_full, attn_part, mid_low,
    *refs,
):
    refs = list(refs)

    def take(count):
        taken = refs[:count]
        del refs[:count]
        return taken

    zsum = GroupSum(
        kinds,
        [hidden_ref, mlp_ref, mlp_ref, mixed_ref, normed_ref],
        [low_ref, gate_ref, up_ref, mid_low, refs[0]],
        [out_down, out_gate, out_up, out_out, out_heads],
        refs[1:19],
    )
    heads_cot = refs[0]
    zsum.resident = [None, None, None, None, heads_cot]
    del refs[:19]
    scratch = take(5)
    mlp_reduce = Reduce(part_ref, scratch, take(7))
    low_reduce = Reduce(low_part_ref, scratch, take(7))
    attn_reduce = Reduce(attn_part, scratch, take(7))
    mine, = take(1)
    tok, width = mine.shape
    gather = Gather(mine, cot_full, token_place(tok, width), None, take(Gather.SEMS))
    bufs, resid_buf, out_buf, buf_sem, out_sem = take(5)
    mixed_cot, wide_buf, dq_sum, dk_sum, dv_sum, dots, dots_mate, dots_col = take(8)
    dot_send, dot_recv, ready, w_mine, w_sem = take(5)
    span = 2 * tok
    heads_width = q_ref.shape[1]
    heads = heads_width // HD
    half = lax.axis_index("row")
    col = lax.axis_index("col")
    length = info_ref[0]
    near_x, near_y, mate = plane_peers()
    corner = {"col": 3 - col}
    blocks = span // MB

    def mid_loads(i):
        slot = lax.rem(i, 2)
        lines = pl.ds(pl.multiple_of(i * MB, MB), MB)
        return [
            pltpu.make_async_copy(cot_full.at[lines, :], bufs.at[slot, 0], buf_sem.at[slot, 0]),
            pltpu.make_async_copy(low_ref.at[lines, :], bufs.at[slot, 1], buf_sem.at[slot, 1]),
            pltpu.make_async_copy(resid_ref.at[lines, :], resid_buf.at[slot], buf_sem.at[slot, 2]),
        ]

    def row_store(out, i):
        lines = pl.ds(pl.multiple_of(i * MB, MB), MB)
        return pltpu.make_async_copy(bufs.at[lax.rem(i, 2), 2], out.at[lines, :], out_sem.at[1])

    def mid_store(i):
        lines = pl.ds(pl.multiple_of(i * MB, MB), MB)
        return pltpu.make_async_copy(out_buf.at[:, pl.ds(0, width)], mid_out.at[lines, :], out_sem.at[0])

    def mid_item(i):
        slot = lax.rem(i, 2)

        @pl.when(i + 1 < blocks)
        def _():
            for c in mid_loads(i + 1):
                c.start()

        for c in mid_loads(i):
            c.wait()
        cot = bufs[slot, 0].astype(F32)
        resid = resid_buf[slot]
        scale = lax.rsqrt(jnp.mean(resid * resid, axis=1, keepdims=True) + EPSILON)
        weighed = cot * gain_ref[1:2, :]
        inner = jnp.sum(weighed * resid, axis=1, keepdims=True)
        mid = bufs[slot, 1].astype(F32) + weighed * scale - resid * (scale * scale * scale * inner / D)
        low = mid.astype(BF)
        lines = pl.ds(pl.multiple_of(i * MB, MB), MB)
        mixed_cot[lines, :] = contract(low, w_mine[...], 1, 1).astype(BF)

        @pl.when(i > 0)
        def _():
            row_store(mid_low, i - 1).wait()

        bufs[slot, 2] = low
        row_store(mid_low, i).start()

        @pl.when(i < blocks // 2)
        def _():
            @pl.when(i > 0)
            def _():
                mid_store(i - 1).wait()

            out_buf[:, pl.ds(0, width)] = mid[:, :width]
            mid_store(i).start()
            part = jnp.sum((cot * resid * scale)[:, :width], axis=0, keepdims=True)
            gain_part[...] += jnp.broadcast_to(part, gain_part.shape)

        @pl.when(i == blocks // 2)
        def _():
            mid_store(i - 1).wait()

    q_steps = span // AQ
    rows = heads * AQ
    pieces = [slice(h * HD, (h + 1) * HD) for h in range(heads)]

    def attn_item(q_step, tile, diagonal):
        stored = lax.rem(q_step + half * (q_steps // 2), q_steps)
        lines = pl.ds(pl.multiple_of(stored * AQ, AQ), AQ)
        key_tiles = span // AK
        keys = pl.ds(pl.multiple_of(lax.rem(tile + half * (key_tiles // 2), key_tiles) * AK, AK), AK)
        first = q_step * AQ
        q = jnp.concatenate([q_ref[lines, s] for s in pieces], axis=0)
        cot = jnp.concatenate([mixed_cot[lines, s] for s in pieces], axis=0)
        wide = jnp.concatenate([wide_buf[:, s] for s in pieces], axis=0)
        place = first + lax.rem(lax.broadcasted_iota(jnp.int32, (1, rows), 1), AQ)
        log_total = jnp.where(place < length, lse_ref[q_step], -NEG_FILL)
        inner = jnp.sum(wide * cot.astype(F32), axis=1, keepdims=True)
        inner = jnp.broadcast_to(inner, (rows, LANES)).T[0:1, :]
        k_tile = k_ref[keys, :]
        v_tile = v_ref[keys, :]
        scores = contract(k_tile, q, 1, 1) * HD**-0.5 - log_total
        if diagonal:
            key_place = tile * AK + lax.broadcasted_iota(jnp.int32, (AK, rows), 0)
            scores = jnp.where(key_place <= place, scores, NEG_FILL)
        weights = jnp.exp(scores)
        prob_cot = contract(v_tile, cot, 1, 1)
        score_cot = (weights * (prob_cot - inner)).astype(BF)
        dv_sum[keys, :] += contract(weights.astype(BF), cot, 1, 0)
        dk_sum[keys, :] += contract(score_cot, q, 1, 0) * HD**-0.5
        dq = contract(score_cot, k_tile, 0, 0) * HD**-0.5

        @pl.when(tile == 0)
        def _():
            dq_sum[...] = dq

        @pl.when(tile > 0)
        def _():
            dq_sum[...] += dq

        if diagonal:
            cos, sin = turn_ref[lines, :HD], turn_ref[lines, HD:]
            for h in range(heads):
                part = dq_sum[h * AQ : (h + 1) * AQ, :]
                swapped = jnp.concatenate([part[:, HD // 2 :], -part[:, : HD // 2]], axis=1)
                heads_cot[lines, h * HD : (h + 1) * HD] = (part * cos + swapped * sin).astype(BF)

    starts = [0]
    for n in range(q_steps):
        starts.append(starts[-1] + n * AQ // AK + 1)
    attn_items = starts.pop()

    def wide_load(q_step):
        stored = lax.rem(q_step + half * (q_steps // 2), q_steps)
        lines = pl.ds(pl.multiple_of(stored * AQ, AQ), AQ)
        return pltpu.make_async_copy(wide_ref.at[lines, :], wide_buf, w_sem.at[1])

    def attn_one(n):
        q_step = sum([jnp.where(n >= start, 1, 0) for start in starts[1:]], jnp.int32(0))
        tile = n - sum([jnp.where(n >= b, b - a, 0) for a, b in zip(starts, starts[1:])], jnp.int32(0))
        last = q_step * AQ // AK

        @pl.when(tile == 0)
        def _():
            wide_load(q_step).wait()

        @pl.when(tile < last)
        def _():
            attn_item(q_step, tile, False)

        @pl.when(tile == last)
        def _():
            attn_item(q_step, tile, True)

            @pl.when(q_step + 1 < q_steps)
            def _():
                wide_load(q_step + 1).start()

    def attn_finish():
        part = dk_sum[...]
        swapped = jnp.concatenate([part[:, HD // 2 :], -part[:, : HD // 2]], axis=1)
        heads_cot[:, heads_width : heads_width + HD] = (part * turn_ref[:, :HD] + swapped * turn_ref[:, HD:]).astype(BF)
        heads_cot[:, heads_width + HD : heads_width + 2 * HD] = dv_sum[...].astype(BF)

    def head_load(i):
        slot = lax.rem(i, 2)
        lines = pl.ds(pl.multiple_of(i * MB, MB), MB)
        return pltpu.make_async_copy(x_ref.at[lines, :], bufs.at[slot, 1], buf_sem.at[slot, 1])

    def head_item(i):
        slot = lax.rem(i, 2)

        @pl.when(i + 1 < blocks)
        def _():
            head_load(i + 1).start()

        head_load(i).wait()
        lines = pl.ds(pl.multiple_of(i * MB, MB), MB)
        part = contract(heads_cot[lines, :heads_width], wq_ref[...], 1, 1)
        part += contract(heads_cot[lines, heads_width : heads_width + 2 * HD], wkv_ref[...], 1, 1)

        @pl.when(i > 0)
        def _():
            row_store(attn_part, i - 1).wait()

        bufs[slot, 2] = part.astype(BF)
        row_store(attn_part, i).start()
        inner = jnp.sum(part * gain_ref[0:1, :] * bufs[slot, 1].astype(F32), axis=1, keepdims=True)
        dots[pl.ds(i, 1), :] = jnp.broadcast_to(inner, (MB, LANES)).T[0:1, :]

    def dot_give():
        n = blocks // 2
        return remote(dots.at[pl.ds(n, n), :], dots_mate, dot_send.at[0], dot_recv.at[0], **mate)

    def dot_share():
        n = blocks // 2
        return [
            remote(dots.at[pl.ds(0, n), :], dots_col.at[s], dot_send.at[1 + s], dot_recv.at[1 + s], **peer)
            for s, peer in enumerate((near_x, near_y, corner))
        ]

    def emit(work, out, sem):
        for a in range(2):
            sum_total = work.total(a)
            h = tok // 4
            for b in range(2):
                lines = pl.ds(a * 2 * h + b * h, h)
                resid_sum = sum_total[b * h : (b + 1) * h]
                emit_buf[...] = resid_sum
                c = pltpu.make_async_copy(emit_buf, out.at[lines, :], sem)
                c.start()
                c.wait()

    emit_buf, = take(1)

    pltpu.make_async_copy(w_ref.at[pl.ds(pl.multiple_of(col * heads_width, heads_width), heads_width), :], w_mine, w_sem.at[0]).start()
    gain_part[...] = jnp.zeros_like(gain_part)
    heads_cot[:, heads_width + 2 * HD :] = jnp.zeros((span, CC - heads_width - 2 * HD), BF)
    zsum.begin()
    dk_sum[...] = jnp.zeros_like(dk_sum)
    dv_sum[...] = jnp.zeros_like(dv_sum)
    zsum.greet([near_x, near_y, corner, mate])

    at = {}

    def plan(tick, action):
        at.setdefault(tick, []).append(action)

    def start_all(copies):
        for c in copies:
            c.start()

    plan(0, mlp_reduce.begin)
    plan(T_ONE, lambda: [mlp_reduce.first(a) for a in range(2)])
    plan(T_TWO, lambda: [mlp_reduce.second(a) for a in range(2)])

    def own_block():
        for a in range(2):
            mine[mlp_reduce.lines(a), :] = mlp_reduce.total(a).astype(BF)
        gather.begin()

    plan(T_SUM, own_block)
    plan(T_GATHER, gather.first)
    plan(T_GATHER + 3, gather.second)

    def start_mid():
        gather.finish()
        mlp_reduce.finish()
        pltpu.make_async_copy(w_ref.at[pl.ds(0, heads_width), :], w_mine, w_sem.at[0]).wait()
        start_all(mid_loads(jnp.int32(0)))
        low_reduce.begin()

    plan(T_MID, start_mid)
    plan(T_MID + 4, lambda: [low_reduce.first(a) for a in range(2)])
    plan(T_MID + 9, lambda: [low_reduce.second(a) for a in range(2)])

    def low_done():
        emit(low_reduce, down_out, out_sem.at[2])
        low_reduce.finish()
        for i, peer in enumerate((near_x, near_y, mate)):
            pl.semaphore_signal(ready.at[i], inc=1, device_id=peer, device_id_type=MESH)

    plan(T_MID + 13, low_done)
    t_attn = T_MID + 1 + blocks // N_MID
    plan(t_attn, lambda: (row_store(mid_low, blocks - 1).wait(), wide_load(jnp.int32(0)).start()))
    t_head = t_attn + 1 + attn_items // N_ATTN
    plan(t_head, lambda: (attn_finish(), head_load(jnp.int32(0)).start()))
    t_last = t_head + 1 + blocks // N_HEAD

    def start_last():
        row_store(attn_part, blocks - 1).wait()
        dot_give().start()
        for i in range(3):
            pl.semaphore_wait(ready.at[i], 1)
        attn_reduce.begin()

    plan(t_last, start_last)

    def last_first():
        n = blocks // 2
        done(dots_mate, dot_recv.at[0])
        dot_give().wait_send()
        dots[pl.ds(0, n), :] = dots[pl.ds(0, n), :] + dots_mate[...]
        start_all(dot_share())
        for a in range(2):
            attn_reduce.first(a)

    plan(t_last + 3, last_first)
    plan(t_last + 7, lambda: [attn_reduce.second(a) for a in range(2)])

    def last_done():
        n = blocks // 2
        shares = dot_share()
        for c in shares:
            c.wait()
        terms = [dots[pl.ds(0, n), :], dots_col[0], dots_col[1], dots_col[2]]
        dot_out[...] = (terms[0] + terms[1]) + (terms[2] + terms[3])
        emit(attn_reduce, attn_out, out_sem.at[2])
        attn_reduce.finish()

    plan(t_last + 10, last_done)
    final = max(zsum.total + OFFS[3], t_last + 11)

    def tick(t, carry):
        zsum.tick(t)
        for when in sorted(at):

            @pl.when(t == when)
            def _(when=when):
                for action in at[when]:
                    action()

        @pl.when((t > T_MID) & (t < t_attn))
        def _():
            for e in range(N_MID):
                mid_item((t - T_MID - 1) * N_MID + e)

        @pl.when((t > t_attn) & (t < t_head))
        def _():
            def body(e, carry):
                attn_one((t - t_attn - 1) * N_ATTN + e)
                return carry

            lax.fori_loop(0, N_ATTN, body, 0)

        @pl.when((t > t_head) & (t < t_last))
        def _():
            for e in range(N_HEAD):
                head_item((t - t_head - 1) * N_HEAD + e)

        return carry

    lax.fori_loop(0, final, tick, 0)
    zsum.finish()


T_ONE, T_TWO, T_SUM, T_GATHER, T_MID = 2, 7, 10, 12, 19
N_MID, N_ATTN, N_HEAD = 2, 2, 4


def backward(info, gains, normed_mlp, gate_cot, up_cot, hidden, mlp_part, low_part, resid, low, w_out_full, mixed, q, k, v, wide, lse, cos, sin,
             wq, wkv, normed, tokens_full, cid):
    span, full = normed.shape
    tok, width = span // 2, full // 4
    heads_width = mixed.shape[1]
    heads = heads_width // HD
    units = hidden.shape[1]
    kinds = ["rows", "columns", "columns", "rows", "stack"]
    sources = [(units, full), (full, units), (full, units), (heads_width, full), (full, CC)]
    outs = [jax.ShapeDtypeStruct(grad_plan(kd, s)[5], BF) for kd, s in zip(kinds, sources)]
    outs = [outs[i] for i in (1, 2, 0, 3, 4)]
    vmem = pl.BlockSpec(memory_space=pltpu.VMEM)
    dma = pltpu.SemaphoreType.DMA
    blocks = span // MB
    turn = jnp.concatenate([cos, sin], axis=1)
    lse = lse.reshape(span // QB, heads, QB // AQ, AQ).transpose(0, 2, 1, 3).reshape(span // AQ, 1, heads * AQ)
    shapes = outs + [
        jax.ShapeDtypeStruct((tok, width), F32),
        jax.ShapeDtypeStruct((8, width), F32),
        jax.ShapeDtypeStruct((tok, width), F32),
        jax.ShapeDtypeStruct((tok, width), F32),
        jax.ShapeDtypeStruct((blocks // 2, LANES), F32),
        jax.ShapeDtypeStruct((span, full), BF),
        jax.ShapeDtypeStruct((span, full), BF),
        jax.ShapeDtypeStruct((span, full), BF),
    ]
    out_specs = [ANY] * 5 + [ANY, vmem, ANY, ANY, vmem, ANY, ANY, ANY]
    scratch = (
        [pltpu.VMEM((span, CC), BF)]
        + GroupSum.scratch(kinds, span)
        + Reduce.scratch(tok, full)
        + Reduce.sems() * 3
        + [pltpu.VMEM((tok, width), BF)]
        + Gather.sems()
        + [
            pltpu.VMEM((2, 3, MB, full), BF),
            pltpu.VMEM((2, MB, full), F32),
            pltpu.VMEM((MB, width), F32),
            dma((2, 3)),
            dma((3,)),
            pltpu.VMEM((span, heads_width), BF),
            pltpu.VMEM((AQ, heads_width), F32),
            pltpu.VMEM((heads * AQ, HD), F32),
            pltpu.VMEM((span, HD), F32),
            pltpu.VMEM((span, HD), F32),
            pltpu.VMEM((blocks, LANES), F32),
            pltpu.VMEM((blocks // 2, LANES), F32),
            pltpu.VMEM((3, blocks // 2, LANES), F32),
            dma((4,)),
            dma((4,)),
            pltpu.SemaphoreType.REGULAR((3,)),
            pltpu.VMEM((heads_width, full), BF),
            dma((2,)),
            pltpu.VMEM((tok // 4, width), F32),
        ]
    )
    results = pl.pallas_call(
        functools.partial(backward_kernel, kinds),
        in_specs=[pl.BlockSpec(memory_space=pltpu.SMEM), vmem] + [ANY] * 13 + [vmem] * 7,
        out_specs=out_specs,
        out_shape=shapes,
        scratch_shapes=scratch,
        compiler_params=pltpu.CompilerParams(
            collective_id=cid, has_side_effects=True, vmem_limit_bytes=VMEM_ALL
        ),
        name="backward",
    )(info, gains, normed_mlp, gate_cot, up_cot, hidden, mlp_part, low_part, resid, low, w_out_full, mixed, wide, normed,
      tokens_full, q, k, v, lse, turn, wq, wkv)
    return results[:10]


def by_distance(stacked, dim):
    count = lax.axis_size("col")
    order = lax.axis_index("col") ^ jnp.arange(count)
    blocks = jnp.take(stacked, order, axis=0)
    return jnp.concatenate([blocks[i] for i in range(count)], axis=dim)


def plain_gather(x):
    cols = by_distance(lax.all_gather(x, "col"), 1)
    return jnp.concatenate([cols, swap(cols, "row", 1)], axis=0)


def plain_gather_heads(x):
    mine = lax.all_gather(x, "col", axis=1, tiled=True)
    half = x.shape[0] // 2
    other = swap(mine, "row", 1)
    other = jnp.concatenate([other[half:], other[:half]], axis=0)
    return jnp.concatenate([mine, other], axis=1)


def plain_reduce(part):
    span, full = part.shape
    count = lax.axis_size("col")
    width = full // count
    half = part[: span // 2].astype(F32) + swap(part[span // 2 :], "row", 1).astype(F32)
    order = lax.axis_index("col") ^ jnp.arange(count)
    blocks = jnp.stack([half[:, s * width : (s + 1) * width] for s in range(count)])
    return lax.psum_scatter(jnp.take(blocks, order, axis=0), "col", tiled=False)


def exchange(packs):
    if kernels_fit():
        return [p if s == 0 else swap(p, "col", s) for s, p in enumerate(packs)]
    count = len(packs)
    order = lax.axis_index("col") ^ jnp.arange(count)
    sent = jnp.take(jnp.stack(packs), order, axis=0)
    blocks = jnp.take(lax.all_to_all(sent, "col", 0, 0, tiled=True), order, axis=0)
    return [blocks[i] for i in range(count)]


def plain_group_sum(grads, kinds):
    outs = []
    count = lax.axis_size("col")
    order = lax.axis_index("col") ^ jnp.arange(count)
    for grad, kind in zip(grads, kinds):
        grad = lax.psum(grad.astype(F32), "dp").astype(BF)
        dim = 1 if kind == "rows" else 0
        blocks = jnp.stack(jnp.split(grad, count, axis=dim))
        blocks = lax.all_to_all(jnp.take(blocks, order, axis=0), "col", 0, 0, tiled=True)
        out_dim = 1 if kind == "columns" else 0
        outs.append(jnp.concatenate([blocks[i] for i in range(count)], axis=out_dim))
    return outs


def kernels_fit():
    return lax.axis_size("col") == 4 and lax.axis_size("dp") == 4 and lax.axis_size("row") == 2


def attn_forward_kernel(info_ref, q_ref, k_ref, v_ref, *refs):
    linked = len(refs) > 6
    if linked:
        side_ref, mixed_ref, wide_ref, lse_ref, peak_ref, side_out, score_ref, sum_ref, stage = refs[:9]
        gather = Gather(side_ref, side_out, token_place(*side_ref.shape), stage, refs[9:])
    else:
        mixed_ref, wide_ref, lse_ref, peak_ref, score_ref, sum_ref = refs
    heads = q_ref.shape[1] // HD
    span = k_ref.shape[0]
    rows = heads * QB
    length = info_ref[0]
    half = lax.axis_index("row")
    step = pl.program_id(0)
    first = step * QB
    key_tiles = span // FWD_KB
    steps = span // QB
    lines = pl.ds(pl.multiple_of(lax.rem(step + half * (steps // 2), steps) * QB, QB), QB)

    if linked:

        @pl.when(step == 0)
        def _():
            greet(list(gather.near))
            gather.begin()

        @pl.when(step == steps - 1)
        def _():
            gather.first()

    q = jnp.concatenate([q_ref[lines, h * HD : (h + 1) * HD] for h in range(heads)], axis=0)
    tiles = (first + QB) // FWD_KB
    plain = first // FWD_KB

    def tile_of(ref, tile):
        stored = lax.rem(tile + half * (key_tiles // 2), key_tiles)
        return ref[pl.ds(pl.multiple_of(stored * FWD_KB, FWD_KB), FWD_KB), :]

    def fold(values, running, op):
        for t in range(FWD_KB // LANES):
            running = op(running, values[:, t * LANES : (t + 1) * LANES])
        return running

    def scores_of(tile, top, diagonal):
        scores = contract(q, tile_of(k_ref, tile), 1, 1) * HD**-0.5
        if diagonal:
            place = first + lax.broadcasted_iota(jnp.int32, (QB, FWD_KB), 0)
            key_place = tile * FWD_KB + lax.broadcasted_iota(jnp.int32, (QB, FWD_KB), 1)
            allowed = (key_place <= place) & (key_place < length)
            scores = jnp.where(allowed[None], scores.reshape(heads, QB, FWD_KB), NEG_FILL)
            scores = scores.reshape(rows, FWD_KB)
        else:
            key_place = tile * FWD_KB + lax.broadcasted_iota(jnp.int32, (1, FWD_KB), 1)
            scores = jnp.where(key_place < length, scores, NEG_FILL)
        score_ref[tile] = scores
        return fold(scores, top, jnp.maximum)

    top = jnp.full((rows, LANES), NEG_FILL, F32)
    top = lax.fori_loop(0, plain, lambda tile, top: scores_of(tile, top, False), top)
    top = lax.fori_loop(plain, tiles, lambda tile, top: scores_of(tile, top, True), top)
    top = jnp.max(top, axis=1, keepdims=True)
    live = first + lax.broadcasted_iota(jnp.int32, (QB, 1), 0) < length
    peak = jnp.max(jnp.where(live[None], top.reshape(heads, QB, 1), NEG_FILL), axis=1)

    @pl.when(step == 0)
    def _():
        peak_ref[...] = jnp.full_like(peak_ref, NEG_FILL)

    peak_ref[...] = jnp.maximum(peak_ref[...], jnp.broadcast_to(peak, peak_ref.shape))
    sum_ref[...] = jnp.zeros_like(sum_ref)

    def weigh(tile, total):
        weights = jnp.exp(score_ref[tile] - top)
        sum_ref[...] += contract(weights.astype(BF), tile_of(v_ref, tile), 1, 0)
        return fold(weights, total, jnp.add)

    total = lax.fori_loop(0, tiles, weigh, jnp.zeros((rows, LANES), F32))
    total = jnp.sum(total, axis=1, keepdims=True)
    mixed = sum_ref[...] / total
    log_total = jnp.broadcast_to(top + jnp.log(total), (rows, LANES))
    lse_ref[step] = log_total.T[0:1, :]
    for h in range(heads):
        part = mixed[h * QB : (h + 1) * QB]
        mixed_ref[lines, h * HD : (h + 1) * HD] = part.astype(BF)
        wide_ref[lines, h * HD : (h + 1) * HD] = part

    if linked:

        @pl.when(step == steps - 1)
        def _():
            gather.second()
            gather.finish()


def attn_forward(info, q, k, v, side=None, cid=None):
    span, width = q.shape
    heads = width // HD
    steps = span // QB
    whole = lambda shape: pl.BlockSpec(shape, lambda i: (0,) * len(shape))
    pairs = heads * span * span // 2
    shapes = [
        jax.ShapeDtypeStruct((span, width), BF),
        jax.ShapeDtypeStruct((span, width), F32),
        jax.ShapeDtypeStruct((steps, 1, heads * QB), F32),
        jax.ShapeDtypeStruct((heads, LANES), F32),
    ]
    in_specs = [pl.BlockSpec(memory_space=pltpu.SMEM)] + [whole(a.shape) for a in (q, k, v)]
    out_specs = [whole(s.shape) for s in shapes]
    scratch = [
        pltpu.VMEM((span // FWD_KB, heads * QB, FWD_KB), F32),
        pltpu.VMEM((heads * QB, HD), F32),
    ]
    operands = [info, q, k, v]
    params = dict(vmem_limit_bytes=48 * MIB)
    if side is not None:
        tok, wide = side.shape
        operands.append(side)
        in_specs.append(ANY)
        out_specs.append(ANY)
        shapes.append(jax.ShapeDtypeStruct((2 * tok, 4 * wide), side.dtype))
        scratch += [pltpu.VMEM(side.shape, side.dtype)] + Gather.sems()
        params.update(collective_id=cid, has_side_effects=True)
    return pl.pallas_call(
        attn_forward_kernel,
        grid=(steps,),
        in_specs=in_specs,
        out_specs=out_specs,
        scratch_shapes=scratch,
        out_shape=shapes,
        compiler_params=pltpu.CompilerParams(**params),
        cost_estimate=pl.CostEstimate(
            flops=40 * pairs * HD // 4, transcendentals=pairs, bytes_accessed=8 * span * width
        ),
        name="attn_forward",
    )(*operands)


def turn_back(values, cos_ref, sin_ref):
    half = HD // 2
    swapped = jnp.concatenate([values[:, half:], -values[:, :half]], axis=1)
    return values * cos_ref[...] + swapped * sin_ref[...]


def attn_backward_kernel(
    info_ref, q_ref, k_ref, v_ref, cot_ref, wide_ref, lse_ref, cosq_ref, sinq_ref, cosk_ref, sink_ref,
    dq_ref, dk_ref, dv_ref, dq_sum, dk_sum, dv_sum,
):
    heads = q_ref.shape[1] // HD
    span = k_ref.shape[0]
    rows = heads * QB
    length = info_ref[0]
    half = info_ref[1]
    step = pl.program_id(0)
    first = step * QB
    key_tiles = span // BWD_KB

    @pl.when(step == 0)
    def _():
        dk_sum[...] = jnp.zeros_like(dk_sum)
        dv_sum[...] = jnp.zeros_like(dv_sum)

    dq_sum[...] = jnp.zeros_like(dq_sum)

    @pl.when(first < length)
    def _():
        pieces = [slice(h * HD, (h + 1) * HD) for h in range(heads)]
        q = jnp.concatenate([q_ref[:, s] for s in pieces], axis=0)
        cot = jnp.concatenate([cot_ref[:, s] for s in pieces], axis=0)
        wide = jnp.concatenate([wide_ref[:, s] for s in pieces], axis=0)
        log_total = lse_ref[0]
        inner = jnp.sum(wide * cot.astype(F32), axis=1, keepdims=True)
        inner = jnp.broadcast_to(inner, (rows, LANES)).T[0:1, :]

        def tile_step(tile, masked):
            stored = lax.rem(tile + half * (key_tiles // 2), key_tiles)
            keys = pl.ds(pl.multiple_of(stored * BWD_KB, BWD_KB), BWD_KB)
            k_tile = k_ref[keys, :]
            v_tile = v_ref[keys, :]
            scores = contract(k_tile, q, 1, 1) * HD**-0.5 - log_total
            if masked:
                key_place = tile * BWD_KB + lax.broadcasted_iota(jnp.int32, (BWD_KB, rows), 0)
                place = first + lax.rem(lax.broadcasted_iota(jnp.int32, (BWD_KB, rows), 1), QB)
                scores = jnp.where((key_place <= place) & (key_place < length), scores, NEG_FILL)
            weights = jnp.exp(scores)
            prob_cot = contract(v_tile, cot, 1, 1)
            score_cot = (weights * (prob_cot - inner)).astype(BF)
            dv_sum[keys, :] += contract(weights.astype(BF), cot, 1, 0)
            dk_sum[keys, :] += contract(score_cot, q, 1, 0) * HD**-0.5
            dq_sum[...] += contract(score_cot, k_tile, 0, 0) * HD**-0.5

        @pl.loop(0, first // BWD_KB)
        def _(tile):
            tile_step(tile, False)

        @pl.loop(first // BWD_KB, pl.cdiv(first + QB, BWD_KB))
        def _(tile):
            tile_step(tile, True)

    for h in range(heads):
        part = turn_back(dq_sum[h * QB : (h + 1) * QB, :], cosq_ref, sinq_ref)
        dq_ref[:, h * HD : (h + 1) * HD] = part.astype(dq_ref.dtype)

    @pl.when(step == pl.num_programs(0) - 1)
    def _():
        dk_ref[...] = turn_back(dk_sum[...], cosk_ref, sink_ref).astype(dk_ref.dtype)
        dv_ref[...] = dv_sum[...].astype(dv_ref.dtype)


def attn_backward(info, q, k, v, cot, wide, lse, cos, sin, kv_type):
    span, width = q.shape
    heads = width // HD
    steps = span // QB

    def stored(i, info_ref):
        return (lax.rem(i + info_ref[1] * (steps // 2), steps), 0)

    whole = pl.BlockSpec((span, HD), lambda i, info_ref: (0, 0))
    mine = pl.BlockSpec((QB, width), stored)
    turn = pl.BlockSpec((QB, HD), stored)
    pairs = heads * span * span // 2
    return pl.pallas_call(
        attn_backward_kernel,
        grid_spec=pltpu.PrefetchScalarGridSpec(
            num_scalar_prefetch=1,
            grid=(steps,),
            in_specs=[
                mine, whole, whole, mine, mine,
                pl.BlockSpec((1, 1, heads * QB), lambda i, info_ref: (i, 0, 0)),
                turn, turn, whole, whole,
            ],
            out_specs=[mine, whole, whole],
            scratch_shapes=[
                pltpu.VMEM((heads * QB, HD), F32),
                pltpu.VMEM((span, HD), F32),
                pltpu.VMEM((span, HD), F32),
            ],
        ),
        out_shape=[
            jax.ShapeDtypeStruct((span, width), BF),
            jax.ShapeDtypeStruct((span, HD), kv_type),
            jax.ShapeDtypeStruct((span, HD), kv_type),
        ],
        compiler_params=pltpu.CompilerParams(vmem_limit_bytes=40 * 2**20),
        cost_estimate=pl.CostEstimate(
            flops=60 * pairs * HD // 4, transcendentals=pairs, bytes_accessed=12 * span * width
        ),
        name="attn_backward",
    )(info, q, k, v, cot, wide, lse, cos, sin, cos, sin)


def head_kernel(x_ref, gain_ref, wq_ref, wkv_ref, cos_ref, sin_ref, normed_ref, q_ref, k_ref, v_ref, scale_ref):
    x = x_ref[...].astype(F32)
    scale = lax.rsqrt(jnp.mean(x * x, axis=1, keepdims=True) + EPSILON)
    scale_ref[...] = jnp.broadcast_to(scale, scale_ref.shape)
    normed = (x * scale * gain_ref[0:1, :]).astype(BF)
    normed_ref[...] = normed

    def turned(raw):
        pieces = []
        half = HD // 2
        for h in range(raw.shape[1] // HD):
            pieces += [-raw[:, h * HD + half : (h + 1) * HD], raw[:, h * HD : h * HD + half]]
        pieces = jnp.concatenate(pieces, axis=1)
        count = raw.shape[1] // HD
        cos = jnp.concatenate([cos_ref[...]] * count, axis=1)
        sin = jnp.concatenate([sin_ref[...]] * count, axis=1)
        return (raw * cos + pieces * sin).astype(BF)

    q_ref[...] = turned(contract(normed, wq_ref[...], 1, 0))
    keyval = contract(normed, wkv_ref[...], 1, 0)
    k_ref[...] = turned(keyval[:, :HD])
    v_ref[...] = keyval[:, HD:].astype(BF)


def project_heads(tokens_full, gains, wq, wkv, cos, sin):
    span, full = tokens_full.shape
    width = wq.shape[1]
    block = 512
    line = lambda n: pl.BlockSpec((block, n), lambda i: (i, 0))
    whole = lambda a: pl.BlockSpec(a.shape, lambda i: (0, 0))
    return pl.pallas_call(
        head_kernel,
        grid=(span // block,),
        in_specs=[line(full), whole(gains), whole(wq), whole(wkv), line(HD), line(HD)],
        out_specs=[line(full), line(width), line(HD), line(HD), line(LANES)],
        out_shape=[
            jax.ShapeDtypeStruct((span, full), BF),
            jax.ShapeDtypeStruct((span, width), BF),
            jax.ShapeDtypeStruct((span, HD), BF),
            jax.ShapeDtypeStruct((span, HD), BF),
            jax.ShapeDtypeStruct((span, LANES), F32),
        ],
        compiler_params=pltpu.CompilerParams(vmem_limit_bytes=48 * MIB),
        cost_estimate=pl.CostEstimate(
            flops=2 * span * full * (width + LANES), transcendentals=0, bytes_accessed=5 * span * full
        ),
        name="project_heads",
    )(tokens_full, gains, wq, wkv, cos, sin)


def project_out_kernel(mixed_ref, w_ref, x_ref, gain_ref, *refs):
    linked = len(refs) > 2
    step = pl.program_id(0)
    if linked:
        side_ref, resid_ref, normed_ref, side_out, stage = refs[:5]
        gather = Gather(side_ref, side_out, token_place(*side_ref.shape), stage, refs[5:])

        @pl.when(step == 0)
        def _():
            greet(list(gather.near))
            gather.begin()

        @pl.when(step == pl.num_programs(0) // 2)
        def _():
            gather.first()

    else:
        resid_ref, normed_ref = refs
    resid = x_ref[...].astype(F32) + contract(mixed_ref[...], w_ref[...], 1, 0)
    resid_ref[...] = resid
    scale = lax.rsqrt(jnp.mean(resid * resid, axis=1, keepdims=True) + EPSILON)
    normed_ref[...] = (resid * scale * gain_ref[1:2, :]).astype(BF)

    if linked:

        @pl.when(step == pl.num_programs(0) - 1)
        def _():
            gather.second()
            gather.finish()


def project_out(mixed_full, w_out_full, tokens_full, gains, side=None, cid=None):
    span, full = tokens_full.shape
    block = 256
    line = pl.BlockSpec((block, full), lambda i: (i, 0))
    operands = [mixed_full, w_out_full, tokens_full, gains]
    in_specs = [
        pl.BlockSpec((block, mixed_full.shape[1]), lambda i: (i, 0)),
        pl.BlockSpec(w_out_full.shape, lambda i: (0, 0), pipeline_mode=pl.Buffered(1)),
        line,
        pl.BlockSpec(gains.shape, lambda i: (0, 0)),
    ]
    out_specs = [line, line]
    shapes = [jax.ShapeDtypeStruct((span, full), F32), jax.ShapeDtypeStruct((span, full), BF)]
    scratch = []
    params = dict(vmem_limit_bytes=48 * MIB)
    if side is not None:
        tok, wide = side.shape
        operands.append(side)
        in_specs.append(ANY)
        out_specs.append(ANY)
        shapes.append(jax.ShapeDtypeStruct((2 * tok, 4 * wide), side.dtype))
        scratch += [pltpu.VMEM(side.shape, side.dtype)] + Gather.sems()
        params.update(collective_id=cid, has_side_effects=True)
    return pl.pallas_call(
        project_out_kernel,
        grid=(span // block,),
        in_specs=in_specs,
        out_specs=out_specs,
        out_shape=shapes,
        scratch_shapes=scratch,
        compiler_params=pltpu.CompilerParams(**params),
        cost_estimate=pl.CostEstimate(
            flops=2 * span * full * full, transcendentals=0, bytes_accessed=12 * span * full
        ),
        name="project_out",
    )(*operands)


def middle_kernel(
    cot_ref, resid_ref, low_ref, gain_ref, w_ref, mixed_ref,
    mixed_cot_ref, own_ref, grad_ref, gain_part_ref, total_ref,
):
    step = pl.program_id(0)
    last = pl.num_programs(0) - 1
    width = own_ref.shape[1]
    cot = cot_ref[...].astype(F32)
    resid = resid_ref[...]
    scale = lax.rsqrt(jnp.mean(resid * resid, axis=1, keepdims=True) + EPSILON)
    weighed = cot * gain_ref[1:2, :]
    inner = jnp.sum(weighed * resid, axis=1, keepdims=True)
    mid = low_ref[...].astype(F32) + weighed * scale - resid * (scale * scale * scale * inner / D)
    low = mid.astype(BF)
    mixed_cot_ref[...] = contract(low, w_ref[...], 1, 1).astype(BF)

    @pl.when(step == 0)
    def _():
        total_ref[...] = jnp.zeros_like(total_ref)
        gain_part_ref[...] = jnp.zeros_like(gain_part_ref)

    total_ref[...] += contract(mixed_ref[...], low, 0, 0)

    @pl.when(step <= last // 2)
    def _():
        own_ref[...] = mid[:, :width]
        part = jnp.sum((cot * resid * scale)[:, :width], axis=0, keepdims=True)
        gain_part_ref[...] += jnp.broadcast_to(part, gain_part_ref.shape)

    @pl.when(step == last)
    def _():
        grad_ref[...] = total_ref[...].astype(BF)


def middle(mlp_cot, resid_mid, out_low, gains, w_mine, mixed, width):
    span, full = resid_mid.shape
    heads_width = mixed.shape[1]
    block = 256
    steps = span // block
    line = pl.BlockSpec((block, full), lambda i: (i, 0))
    thin = pl.BlockSpec((block, heads_width), lambda i: (i, 0))
    return pl.pallas_call(
        middle_kernel,
        grid=(steps,),
        in_specs=[
            line, line, line,
            pl.BlockSpec(gains.shape, lambda i: (0, 0)),
            pl.BlockSpec(w_mine.shape, lambda i: (0, 0)),
            thin,
        ],
        out_specs=[
            thin,
            pl.BlockSpec((block, width), lambda i: (jnp.minimum(i, steps // 2 - 1), 0)),
            pl.BlockSpec((heads_width, full), lambda i: (0, 0)),
            pl.BlockSpec((8, width), lambda i: (0, 0)),
        ],
        out_shape=[
            jax.ShapeDtypeStruct((span, heads_width), BF),
            jax.ShapeDtypeStruct((span // 2, width), F32),
            jax.ShapeDtypeStruct((heads_width, full), BF),
            jax.ShapeDtypeStruct((8, width), F32),
        ],
        scratch_shapes=[pltpu.VMEM((heads_width, full), F32)],
        compiler_params=pltpu.CompilerParams(vmem_limit_bytes=48 * MIB),
        cost_estimate=pl.CostEstimate(
            flops=4 * span * full * heads_width, transcendentals=0, bytes_accessed=8 * span * full
        ),
        name="middle",
    )(mlp_cot, resid_mid, out_low, gains, w_mine, mixed)


def head_back_kernel(
    info_ref, qc_ref, kc_ref, vc_ref, wq_ref, wkv_ref, normed_ref, x_ref, gain_ref,
    part_ref, dot_ref, grad_ref, total_ref,
):
    step = pl.program_id(0)
    wide = qc_ref.shape[1]
    keyval = jnp.concatenate([kc_ref[...], vc_ref[...]], axis=1)
    counted = keyval * info_ref[2].astype(BF)
    part = contract(qc_ref[...], wq_ref[...], 1, 1) + contract(counted, wkv_ref[...], 1, 1)
    part_ref[...] = part.astype(BF)
    inner = jnp.sum(part * gain_ref[0:1, :] * x_ref[...].astype(F32), axis=1, keepdims=True)
    dot_ref[0] = jnp.broadcast_to(inner, (inner.shape[0], LANES)).T[0:1, :]

    @pl.when(step == 0)
    def _():
        total_ref[...] = jnp.zeros_like(total_ref)

    total_ref[:, :wide] += contract(normed_ref[...], qc_ref[...], 0, 0)
    total_ref[:, wide:] += contract(normed_ref[...], keyval, 0, 0)

    @pl.when(step == pl.num_programs(0) - 1)
    def _():
        used = wide + 2 * HD
        grad_ref[:, :used] = total_ref[...].astype(BF)
        grad_ref[:, used:] = jnp.zeros((grad_ref.shape[0], grad_ref.shape[1] - used), BF)


def head_back(info, query_cot, key_cot, value_cot, wq, wkv, normed, tokens_full, gains):
    span, full = normed.shape
    wide = query_cot.shape[1]
    block = 512
    steps = span // block
    line = lambda n: pl.BlockSpec((block, n), lambda i, info_ref: (i, 0))
    whole = lambda shape: pl.BlockSpec(shape, lambda i, info_ref: (0, 0))
    grad_width = max(CC, wide + 2 * HD)
    return pl.pallas_call(
        head_back_kernel,
        grid_spec=pltpu.PrefetchScalarGridSpec(
            num_scalar_prefetch=1,
            grid=(steps,),
            in_specs=[
                line(wide), line(HD), line(HD), whole(wq.shape), whole(wkv.shape), line(full), line(full),
                whole(gains.shape),
            ],
            out_specs=[
                line(full),
                pl.BlockSpec((1, 1, block), lambda i, info_ref: (i, 0, 0)),
                whole((full, grad_width)),
            ],
            scratch_shapes=[pltpu.VMEM((full, wide + 2 * HD), F32)],
        ),
        out_shape=[
            jax.ShapeDtypeStruct((span, full), BF),
            jax.ShapeDtypeStruct((steps, 1, block), F32),
            jax.ShapeDtypeStruct((full, grad_width), BF),
        ],
        compiler_params=pltpu.CompilerParams(vmem_limit_bytes=48 * MIB),
        cost_estimate=pl.CostEstimate(
            flops=4 * span * full * (wide + LANES), transcendentals=0, bytes_accessed=6 * span * full
        ),
        name="head_back",
    )(info, query_cot, key_cot, value_cot, wq, wkv, normed, tokens_full, gains)


def fill_units(out, pieces, part, sem):
    mine = lax.rem(lax.axis_index("dp"), 2)
    rows = out.shape[0] // 8
    copies = []
    for s in range(4):
        for which, piece in ((mine, pieces[0]), (1 - mine, pieces[1])):
            lines = pl.ds(pl.multiple_of(s * 2 * rows + which * rows, rows), rows)
            src = piece.at[pl.ds((2 * s + part) * rows, rows), :]
            copies.append(pltpu.make_async_copy(src, out.at[lines, :], sem.at[len(copies)]))
    return copies


def hidden_kernel(x_ref, *refs):
    pieces = refs[:2]
    gate_ref, up_ref, hidden_ref, w_gate, w_up, gate_sem, up_sem = refs[2:]

    @pl.when(pl.program_id(0) == 0)
    def _():
        copies = fill_units(w_gate, pieces, 0, gate_sem) + fill_units(w_up, pieces, 1, up_sem)
        for c in copies:
            c.start()
        for c in copies:
            c.wait()

    gate = contract(x_ref[...], w_gate[...], 1, 0)
    gate_ref[...] = gate
    up = contract(x_ref[...], w_up[...], 1, 0)
    up_ref[...] = up
    hidden_ref[...] = (gate * jax.nn.sigmoid(gate) * up).astype(BF)


def hidden_units(normed, pieces):
    span, full = normed.shape
    units = pieces[0].shape[1]
    block = 256
    thin = pl.BlockSpec((block, units), lambda i: (i, 0))
    return pl.pallas_call(
        hidden_kernel,
        grid=(span // block,),
        in_specs=[pl.BlockSpec((block, full), lambda i: (i, 0))] + [ANY] * 2,
        out_specs=[thin] * 3,
        out_shape=[
            jax.ShapeDtypeStruct((span, units), F32),
            jax.ShapeDtypeStruct((span, units), F32),
            jax.ShapeDtypeStruct((span, units), BF),
        ],
        scratch_shapes=[
            pltpu.VMEM((full, units), BF),
            pltpu.VMEM((full, units), BF),
            pltpu.SemaphoreType.DMA((8,)),
            pltpu.SemaphoreType.DMA((8,)),
        ],
        compiler_params=pltpu.CompilerParams(vmem_limit_bytes=48 * MIB),
        cost_estimate=pl.CostEstimate(
            flops=4 * span * full * units, transcendentals=span * units, bytes_accessed=6 * span * full
        ),
        name="hidden_units",
    )(normed, *pieces)


def hidden_back_kernel(low_ref, gate_ref, up_ref, hidden_ref, own_ref, *refs):
    pieces, down_pieces = refs[:2], refs[2:5]
    gate_cot_ref, up_cot_ref, part_ref, low_part_ref, w_gate, w_up, w_down, gate_sem, up_sem, down_sem = refs[5:]
    units = w_down.shape[0]
    width = w_down.shape[1] // 4

    @pl.when(pl.program_id(0) == 0)
    def _():
        mine = own_ref.at[pl.ds(pl.multiple_of(lax.axis_index("col") * units, units), units), :]
        copies = [
            pltpu.make_async_copy(p, w_down.at[:, pl.ds(s * width, width)], down_sem.at[s])
            for s, p in enumerate((mine, *down_pieces))
        ]
        copies += fill_units(w_gate, pieces, 0, gate_sem) + fill_units(w_up, pieces, 1, up_sem)
        for c in copies:
            c.start()
        for c in copies:
            c.wait()

    hidden_cot = contract(low_ref[...], w_down[...], 1, 1)
    gate = gate_ref[...]
    sig = jax.nn.sigmoid(gate)
    gate_cot = (hidden_cot * up_ref[...] * sig * (1.0 + gate * (1.0 - sig))).astype(BF)
    up_cot = (hidden_cot * gate * sig).astype(BF)
    gate_cot_ref[...] = gate_cot
    up_cot_ref[...] = up_cot
    part = contract(gate_cot, w_gate[...], 1, 1) + contract(up_cot, w_up[...], 1, 1)
    part_ref[...] = part.astype(BF)
    low_part_ref[...] = contract(hidden_ref[...], w_down[...], 1, 0).astype(BF)


def hidden_back(low, gate, up, hidden, w_down, pieces, down_pieces):
    span, full = low.shape
    units = gate.shape[1]
    block = 256
    thin = pl.BlockSpec((block, units), lambda i: (i, 0))
    line = pl.BlockSpec((block, full), lambda i: (i, 0))
    return pl.pallas_call(
        hidden_back_kernel,
        grid=(span // block,),
        in_specs=[line, thin, thin, thin] + [ANY] * 6,
        out_specs=[thin, thin, line, line],
        out_shape=[jax.ShapeDtypeStruct((span, units), BF)] * 2 + [jax.ShapeDtypeStruct((span, full), BF)] * 2,
        scratch_shapes=[
            pltpu.VMEM((full, units), BF),
            pltpu.VMEM((full, units), BF),
            pltpu.VMEM((units, full), BF),
            pltpu.SemaphoreType.DMA((8,)),
            pltpu.SemaphoreType.DMA((8,)),
            pltpu.SemaphoreType.DMA((4,)),
        ],
        compiler_params=pltpu.CompilerParams(vmem_limit_bytes=52 * MIB),
        cost_estimate=pl.CostEstimate(
            flops=8 * span * full * units, transcendentals=span * units, bytes_accessed=12 * span * full
        ),
        name="hidden_back",
    )(low, gate, up, hidden, w_down, *pieces, *down_pieces)


def on_device(
    tokens, lengths, attn_gain, w_query, w_key, w_value, w_out, mlp_gain, w_gate, w_up, w_down, cotangent
):
    row_devices = lax.axis_size("row")
    col_devices = lax.axis_size("col")
    row = lax.axis_index("row")
    col = lax.axis_index("col")
    fit = kernels_fit()
    tok, width = tokens.shape
    span = tok * row_devices
    group = HQ // KV
    heads_row = HQ // row_devices
    heads = heads_row // col_devices
    head_width = heads * HD
    keyval_row = KV // row_devices
    units = w_gate.shape[1] // col_devices
    length = lengths[0]
    shared_key = heads < group
    sharers = max(1, group // heads)
    leader = (col % sharers == 0).astype(jnp.int32)
    info = jnp.stack([length, row, leader]).astype(jnp.int32)

    keyval = []
    for owner in range(col_devices):
        first = owner * heads // group * HD
        keyval += [w_key[:, first : first + HD], w_value[:, first : first + HD]]
    keyval = jnp.concatenate(keyval, axis=1)
    gains = jnp.concatenate([attn_gain[None], mlp_gain[None], jnp.zeros((6, width), F32)], axis=0)

    if fit:
        tokens_full, wq, wkv, gains = first_gather(tokens, w_query, keyval, gains, 1)
    else:
        tokens_full = plain_gather(tokens)
        def slices(weight, size):
            return [lax.dynamic_slice_in_dim(weight, (col ^ s) * size, size, 1) for s in range(col_devices)]

        wq = jnp.concatenate(exchange(slices(w_query, head_width)), axis=0)
        wkv = jnp.concatenate(exchange(slices(keyval, LANES)), axis=0)
        gains = by_distance(lax.all_gather(gains, "col"), 1)
    w_gate, w_up, tokens_full = lax.optimization_barrier((w_gate, w_up, tokens_full))
    place = lax.rem(jnp.arange(span, dtype=jnp.int32) + row * tok, span)
    frequency = ROPE_BASE ** (-jnp.arange(HD // 2, dtype=F32) * (2.0 / HD))
    angle = place.astype(F32)[:, None] * frequency[None, :]
    cos = jnp.tile(jnp.cos(angle), (1, 2))
    sin = jnp.tile(jnp.sin(angle), (1, 2))

    normed_attn, query, key, value, scale_a = project_heads(tokens_full, gains, wq, wkv, cos, sin)
    valid = (row * tok + jnp.arange(tok, dtype=jnp.int32) < length).astype(BF)
    cot_low = cotangent * valid[:, None]
    def unit_pieces():
        rows = width // 2
        start = lax.rem(lax.axis_index("dp"), 2) * rows
        near = [
            jnp.concatenate(
                [lax.dynamic_slice(w, (start, (col ^ s) * units), (rows, units)) for w in (w_gate, w_up)], axis=0
            )
            for s in range(col_devices)
        ]
        return jnp.concatenate(exchange(near), axis=0)

    def unit_slices(weight, dim):
        return [lax.dynamic_slice_in_dim(weight, (col ^ s) * units, units, dim) for s in range(col_devices)]

    if fit:
        near_units = unit_pieces()
        mixed, mixed_wide, log_total, peak, w_out_full = attn_forward(info, query, key, value, w_out, 7)
        mixed, near_units = lax.optimization_barrier((mixed, near_units))
        moved = swap(peak, "dp", 1)
        pieces = [near_units, swap(near_units, "dp", 1)]
        mixed_full = gather_heads(mixed, 2)
        w_down, mixed_full, moved = lax.optimization_barrier((w_down, mixed_full, moved))
        peak = jnp.maximum(peak, moved)
        moved = swap(peak, "dp", 2)
        down_pieces = [
            swap(lax.dynamic_slice_in_dim(w_down, (col ^ s) * units, units, 0), "col", s) for s in range(1, col_devices)
        ]
        resid_mid, normed_mlp, out_low = project_out(mixed_full, w_out_full, tokens_full, gains, cot_low, 8)
        normed_mlp, moved = lax.optimization_barrier((normed_mlp, moved))
        own_peaks = jnp.maximum(peak, moved)[:, 0]
        row_peaks = jnp.where(jnp.arange(col_devices)[:, None] == col, own_peaks[None, :], NEG_FILL)
        moved = swap(row_peaks, "col", 1)
        gate, up, hidden = hidden_units(normed_mlp, pieces)
        hidden, moved = lax.optimization_barrier((hidden, moved))
        row_peaks = jnp.maximum(row_peaks, moved)
        moved = swap(row_peaks, "col", 2)
        gate_cot, up_cot, mlp_part, down_part = hidden_back(
            out_low, gate, up, hidden, w_down, pieces, down_pieces
        )
        mlp_part, moved = lax.optimization_barrier((mlp_part, moved))
        row_peaks = jnp.maximum(row_peaks, moved)
    else:
        mixed, mixed_wide, log_total, peak = attn_forward(info, query, key, value)
        mixed_full = plain_gather_heads(mixed)
        w_out_full = plain_gather(w_out)
        resid_mid, normed_mlp = project_out(mixed_full, w_out_full, tokens_full, gains)
        out_low = plain_gather(cot_low)
        w_gate_units = jnp.concatenate(exchange(unit_slices(w_gate, 1)), axis=0)
        w_up_units = jnp.concatenate(exchange(unit_slices(w_up, 1)), axis=0)
        w_down_units = jnp.concatenate(exchange(unit_slices(w_down, 0)), axis=1)
        gate = jnp.dot(normed_mlp, w_gate_units, preferred_element_type=F32)
        up = jnp.dot(normed_mlp, w_up_units, preferred_element_type=F32)
        gate_sigmoid = jax.nn.sigmoid(gate)
        hidden = (gate * gate_sigmoid * up).astype(BF)
        hidden_cot = contract(out_low, w_down_units, 1, 1)
        gate_cot = (
            hidden_cot * up * gate_sigmoid * (1.0 + gate * (1.0 - gate_sigmoid))
        ).astype(BF)
        up_cot = (hidden_cot * gate * gate_sigmoid).astype(BF)
        mlp_part = (contract(gate_cot, w_gate_units, 1, 1) + contract(up_cot, w_up_units, 1, 1)).astype(BF)
        down_part = jnp.dot(hidden, w_down_units, preferred_element_type=F32).astype(BF)

    if fit:
        *sums, mid_cot, gain_m_part, attn_cot, down_sum, width_dot = backward(
            info, gains, normed_mlp, gate_cot, up_cot, hidden, mlp_part, down_part, resid_mid, out_low, w_out_full,
            mixed, query, key, value, mixed_wide, log_total, cos, sin, wq, wkv, normed_attn, tokens_full, 3,
        )
        width_dot = width_dot.reshape(tok)
    else:
        mlp_cot = plain_gather(plain_reduce(mlp_part).astype(BF))
        down_sum = plain_reduce(down_part)
        w_mine = lax.dynamic_slice_in_dim(w_out_full, col * head_width, head_width, 0)
        mixed_cot, mid_cot, grad_out, gain_m_part = middle(
            mlp_cot, resid_mid, out_low, gains, w_mine, mixed, width
        )
        query_cot, key_cot, value_cot = attn_backward(
            info, query, key, value, mixed_cot, mixed_wide, log_total, cos, sin, F32 if shared_key else BF
        )
        if shared_key:
            for bit in range(sharers.bit_length() - 1):
                key_cot = key_cot + swap(key_cot, "col", 1 << bit)
                value_cot = value_cot + swap(value_cot, "col", 1 << bit)
            key_cot, value_cot = key_cot.astype(BF), value_cot.astype(BF)
        attn_part, dot_part, grad_heads = head_back(
            info, query_cot, key_cot, value_cot, wq, wkv, normed_attn, tokens_full, gains
        )
        dot_part = dot_part.reshape(span)
        width_dot = lax.psum(dot_part[:tok] + swap(dot_part[tok:], "row", 1), "col")
        attn_cot = plain_reduce(attn_part)
        grad_gate = contract(normed_mlp, gate_cot, 0, 0).astype(BF)
        grad_up = contract(normed_mlp, up_cot, 0, 0).astype(BF)
        grad_down = contract(hidden, out_low, 0, 0).astype(BF)
        sums = plain_group_sum(
            [grad_gate, grad_up, grad_down, grad_out, grad_heads], ["columns", "columns", "rows", "rows", "stack"]
        )
    output = (resid_mid[:tok, :width] + down_sum).astype(BF)
    own_in = tokens.astype(F32)
    scale_own = scale_a[:tok, :1]
    input_grad = (
        mid_cot
        + attn_cot * attn_gain * scale_own
        - own_in * (scale_own * scale_own * scale_own * width_dot[:, None] / D)
    )
    gain_a_part = jnp.sum(attn_cot * own_in * scale_own, axis=0)

    out_gate, out_up, out_down, out_out, out_heads = [g.astype(F32) for g in sums]
    out_heads = out_heads.reshape(col_devices, width, out_heads.shape[1])
    out_query = jnp.concatenate([out_heads[i, :, :head_width] for i in range(col_devices)], axis=1)
    leaders = range(0, col_devices, sharers)
    out_key = jnp.concatenate([out_heads[i, :, head_width : head_width + HD] for i in leaders], axis=1)
    out_value = jnp.concatenate(
        [out_heads[i, :, head_width + HD : head_width + 2 * HD] for i in leaders], axis=1
    )

    gain_sums = jnp.stack([gain_a_part, gain_m_part[0]])
    gain_sums = gain_sums + swap(gain_sums, "row", 1)
    step = 1
    while step < lax.axis_size("dp"):
        gain_sums = gain_sums + swap(gain_sums, "dp", step)
        step *= 2
    if not fit:
        own_peaks = lax.pmax(peak, "dp")[:, 0]
        row_peaks = lax.all_gather(own_peaks, "col")
    row_peaks = row_peaks.reshape(heads_row)
    clip_factor = CLIP_LEVEL / jnp.maximum(row_peaks, CLIP_LEVEL)
    query_scale = jnp.repeat(jnp.sqrt(clip_factor), HD)
    key_scale = jnp.repeat(jnp.sqrt(jnp.min(clip_factor.reshape(keyval_row, group), axis=1)), HD)
    clipped_query = (w_query.astype(F32) * query_scale[None, :]).astype(BF)
    clipped_key = (w_key.astype(F32) * key_scale[None, :]).astype(BF)
    return (
        output,
        input_grad,
        gain_sums[0],
        out_query,
        out_key,
        out_value,
        out_out,
        gain_sums[1],
        out_gate,
        out_up,
        out_down,
        own_peaks,
        clipped_query,
        clipped_key,
    )


def solution(mesh):
    in_specs = (
        P(("dp", "row"), "col"),
        P("dp"),
        P("col"),
        P("col", "row"),
        P("col", "row"),
        P("col", "row"),
        P("row", "col"),
        P("col"),
        P("col", "row"),
        P("col", "row"),
        P("row", "col"),
        P(("dp", "row"), "col"),
    )
    out_specs = (
        P(("dp", "row"), "col"),
        P(("dp", "row"), "col"),
        P("col"),
        P("col", "row"),
        P("col", "row"),
        P("col", "row"),
        P("row", "col"),
        P("col"),
        P("col", "row"),
        P("col", "row"),
        P("row", "col"),
        P(("row", "col")),
        P("col", "row"),
        P("col", "row"),
    )
    return jax.shard_map(
        on_device, mesh=mesh, in_specs=in_specs, out_specs=out_specs, check_vma=False
    )
```

```python
import functools

import jax
import jax.numpy as jnp
from jax import lax
from jax.experimental import pallas as pl
from jax.experimental.pallas import tpu as pltpu
from jax.sharding import PartitionSpec as P

D = 2048
HQ = 32
KV = 8
HD = 64
SEQ_LEN = 2048

EPSILON = 1e-05
NEG_FILL = -1e30
CLIP_LEVEL = 5.0
ROPE_BASE = 500000.0

BF = jnp.bfloat16
F32 = jnp.float32
LANES = 128
QB = 512
FWD_KB = 512
BWD_KB = 512
MESH = pl.DeviceIdType.MESH
ANY = pl.BlockSpec(memory_space=pl.ANY)
NCH = 4
CR, CC = 256, 512
HR = CR // 2
OFFS = (0, 2, 4, 7)
RING = 12
MIB = 2**20
VMEM_ALL = 63 * MIB


def contract(left, right, left_dim, right_dim):
    return lax.dot_general(
        left, right, (((left_dim,), (right_dim,)), ((), ())), preferred_element_type=F32
    )


def swap(values, axis, step):
    count = lax.axis_size(axis)
    return lax.ppermute(values, axis, [(i, i ^ step) for i in range(count)])


def flip(index, bit):
    return index + bit - 2 * bit * lax.rem(index // bit, 2)


def xor(index, step):
    return lax.rem(lax.rem(index, 2) + step % 2, 2) + 2 * lax.rem(index // 2 + step // 2, 2)


def remote(src, dst, send, recv, **where):
    return pltpu.make_async_remote_copy(
        src_ref=src, dst_ref=dst, send_sem=send, recv_sem=recv, device_id=where, device_id_type=MESH
    )


def done(ref, sem):
    pltpu.make_async_copy(ref, ref, sem).wait()


def greet(targets):
    barrier = pltpu.get_barrier_semaphore()
    for target in targets:
        pl.semaphore_signal(barrier, inc=1, device_id=target, device_id_type=MESH)
    pl.semaphore_wait(barrier, len(targets))


def plane_peers():
    row = lax.axis_index("row")
    col = lax.axis_index("col")
    return {"col": flip(col, 1)}, {"col": flip(col, 2)}, {"row": 1 - row}


def token_place(tok, width):
    rows = tok // NCH

    def place(ref, half, s, j, who):
        return ref.at[pl.ds(half * tok + j * rows, rows), pl.ds(s * width, width)]

    return place


def head_place(span, width):
    rows = span // NCH

    def place(ref, half, s, j, who):
        start = j * rows if half == 0 else ((j + NCH // 2) % NCH) * rows
        return ref.at[pl.ds(start, rows), pl.ds(pl.multiple_of((half * 4 + xor(who, s)) * width, LANES), width)]

    return place


class Gather:
    SEMS = 6

    def __init__(self, src, out, place, stage, sems):
        self.src, self.out, self.place, self.stage = src, out, place, stage
        self.own_send, self.relay_send, self.mate_send, self.recv, self.mate_recv, self.local = sems
        self.col = lax.axis_index("col")
        self.near = plane_peers()

    @staticmethod
    def sems():
        shapes = [(2, NCH), (NCH,), (4, NCH), (3, NCH), (4, NCH), (2,)]
        return [pltpu.SemaphoreType.DMA(s) for s in shapes]

    def chunk(self, j):
        rows = self.src.shape[0] // NCH
        return self.src.at[pl.ds(j * rows, rows), :]

    def here(self, half, s, j):
        return self.place(self.out, half, s, j, self.col)

    def own(self, axis, j):
        peer = self.near[axis]
        dst = self.place(self.out, 0, axis + 1, j, peer["col"])
        return remote(self.chunk(j), dst, self.own_send.at[axis, j], self.recv.at[axis, j], **peer)

    def relay(self, axis, j):
        peer = self.near[1 - axis]
        dst = self.place(self.out, 0, 3, j, peer["col"])
        return remote(self.here(0, axis + 1, j), dst, self.relay_send.at[j], self.recv.at[2, j], **peer)

    def mate(self, s, j):
        src = self.chunk(j) if s == 0 else self.here(0, s, j)
        dst = self.place(self.out, 1, s, j, self.col)
        return remote(src, dst, self.mate_send.at[s, j], self.mate_recv.at[s, j], **self.near[2])

    def load(self):
        return pltpu.make_async_copy(self.src, self.stage, self.local.at[0])

    def keep(self, j):
        rows = self.src.shape[0] // NCH
        whole = self.stage if self.stage is not None else self.src
        return pltpu.make_async_copy(whole.at[pl.ds(j * rows, rows), :], self.here(0, 0, j), self.local.at[1])

    def begin(self):
        half = NCH // 2
        if self.stage is not None:
            self.load().start()
        for i in range(NCH):
            self.own(0, i).start()
            self.own(1, (i + half) % NCH).start()
        for j in range(NCH):
            self.mate(0, j).start()

    def arrived(self, s, j):
        done(self.here(0, s, j), self.recv.at[s - 1, j])

    def first(self):
        half = NCH // 2
        for i in range(half):
            self.arrived(1, i)
            self.relay(0, i).start()
            self.mate(1, i).start()
            self.arrived(2, half + i)
            self.relay(1, half + i).start()
            self.mate(2, half + i).start()

    def second(self):
        half = NCH // 2
        if self.stage is not None:
            self.load().wait()
        for j in range(NCH):
            self.keep(j).start()
        for i in range(half):
            self.arrived(1, half + i)
            self.mate(1, half + i).start()
            self.arrived(2, i)
            self.mate(2, i).start()
        for i in range(half):
            for j in (i, half + i):
                self.arrived(3, j)
                self.mate(3, j).start()

    def finish(self):
        half = NCH // 2
        for s in range(4):
            for j in range(NCH):
                done(self.here(1, s, j), self.mate_recv.at[s, j])
                self.mate(s, j).wait_send()
        for j in range(NCH):
            self.own(0, j).wait_send()
            self.own(1, j).wait_send()
            self.relay(0 if j < half else 1, j).wait_send()
        whole = self.stage if self.stage is not None else self.src
        done(whole, self.local.at[1])


def gather_kernel(place_of, x_ref, out_ref, stage, *sems):
    near_x, near_y, mate = plane_peers()
    greet([near_x, near_y, mate])
    gather = Gather(x_ref, out_ref, place_of(*x_ref.shape), stage, sems)
    gather.begin()
    gather.first()
    gather.second()
    gather.finish()


def gather_call(x, shape, place_of, cid, name):
    return pl.pallas_call(
        functools.partial(gather_kernel, place_of),
        in_specs=[ANY],
        out_specs=ANY,
        out_shape=jax.ShapeDtypeStruct(shape, x.dtype),
        scratch_shapes=[pltpu.VMEM(x.shape, x.dtype)] + Gather.sems(),
        compiler_params=pltpu.CompilerParams(collective_id=cid, has_side_effects=True),
        name=name,
    )(x)


def gather_tokens(x, cid):
    tok, width = x.shape
    return gather_call(x, (2 * tok, 4 * width), token_place, cid, "gather_tokens")


def gather_heads(x, cid):
    span, width = x.shape
    return gather_call(x, (span, 8 * width), head_place, cid, "gather_heads")


class Reduce:
    def __init__(self, part, scratch, sems):
        self.part = part
        self.own, self.given, self.sent, self.got_one, self.got_two = scratch
        self.loads, self.mate_send, self.mate_recv, self.one_send, self.one_recv, self.two_send, self.two_recv = sems
        self.near = plane_peers()
        self.h = self.own.shape[0] // 2
        self.width = self.own.shape[1] // 4

    @staticmethod
    def scratch(tok, full):
        h, w = tok // 2, full // 4
        shapes = [(tok, full), (tok, full), (2, 3, h, w), (2, 2, h, w), (2, h, w)]
        return [pltpu.VMEM(s, BF) for s in shapes]

    @staticmethod
    def sems():
        return [pltpu.SemaphoreType.DMA((2,))] * 7

    def lines(self, a):
        return pl.ds(a * self.h, self.h)

    def give(self, a):
        src = self.part.at[pl.ds((2 + a) * self.h, self.h), :]
        return remote(src, self.given.at[self.lines(a), :], self.mate_send.at[a], self.mate_recv.at[a], **self.near[2])

    def load(self, a):
        return pltpu.make_async_copy(self.part.at[self.lines(a), :], self.own.at[self.lines(a), :], self.loads.at[a])

    def one(self, a):
        src = self.sent.at[a, pl.ds(0, 2)]
        return remote(src, self.got_one.at[a], self.one_send.at[a], self.one_recv.at[a], **self.near[a])

    def two(self, a):
        return remote(self.sent.at[a, 2], self.got_two.at[a], self.two_send.at[a], self.two_recv.at[a], **self.near[1 - a])

    def pair(self, a, s):
        cols = pl.ds(s * self.width, self.width)
        rows = self.lines(a)
        return self.own[rows, cols].astype(F32) + self.given[rows, cols].astype(F32)

    def begin(self):
        for a in range(2):
            self.give(a).start()
            self.load(a).start()

    def first(self, a):
        self.load(a).wait()
        done(self.given.at[self.lines(a), :], self.mate_recv.at[a])
        for i, s in enumerate((a + 1, 3)):
            self.sent[a, i] = self.pair(a, s).astype(BF)
        self.one(a).start()

    def second(self, a):
        done(self.got_one.at[a], self.one_recv.at[a])
        self.sent[a, 2] = (self.pair(a, 2 - a) + self.got_one[a, 1].astype(F32)).astype(BF)
        self.two(a).start()

    def total(self, a):
        done(self.got_two.at[a], self.two_recv.at[a])
        return self.pair(a, 0) + self.got_one[a, 0].astype(F32) + self.got_two[a].astype(F32)

    def finish(self):
        for a in range(2):
            self.give(a).wait_send()
            self.one(a).wait_send()
            self.two(a).wait_send()


def first_gather_kernel(
    x_ref, wq_ref, wkv_ref, gain_ref, out_ref, wq_out, wkv_out, gain_out,
    stage, wq_stage, wkv_stage, gain_stage, stage_sem, small_send, small_recv, *sems,
):
    near_x, near_y, mate = plane_peers()
    col = lax.axis_index("col")
    tok, width = x_ref.shape
    wide = wq_ref.shape[1] // 4
    thin = wkv_ref.shape[1] // 4

    def share(ref, owner, size):
        return ref.at[:, pl.ds(pl.multiple_of(owner * size, LANES), size)]

    loads = [
        pltpu.make_async_copy(share(wq_ref, col, wide), wq_stage, stage_sem.at[0]),
        pltpu.make_async_copy(share(wkv_ref, col, thin), wkv_stage, stage_sem.at[1]),
        pltpu.make_async_copy(gain_ref, gain_stage, stage_sem.at[2]),
    ]
    for c in loads:
        c.start()
    greet([near_x, near_y, {"col": 3 - col}, mate])
    smalls = []
    for s, peer in ((1, near_x), (2, near_y), (3, {"col": 3 - col})):
        owner = peer["col"]
        lines = pl.ds(s * width, width)
        smalls += [
            remote(share(wq_ref, owner, wide), wq_out.at[lines, :], small_send.at[0, s], small_recv.at[0, s], **peer),
            remote(share(wkv_ref, owner, thin), wkv_out.at[lines, :], small_send.at[1, s], small_recv.at[1, s], **peer),
            remote(gain_ref, gain_out.at[:, lines], small_send.at[2, s], small_recv.at[2, s], **peer),
        ]
    gather = Gather(x_ref, out_ref, token_place(tok, width), stage, sems)
    gather.begin()
    for c in smalls:
        c.start()
    lines = pl.ds(0, width)
    keeps = [
        pltpu.make_async_copy(wq_stage, wq_out.at[lines, :], stage_sem.at[3]),
        pltpu.make_async_copy(wkv_stage, wkv_out.at[lines, :], stage_sem.at[4]),
        pltpu.make_async_copy(gain_stage, gain_out.at[:, lines], stage_sem.at[5]),
    ]
    for load, keep in zip(loads, keeps):
        load.wait()
        keep.start()
    gather.first()
    gather.second()
    gather.finish()
    for c in smalls:
        c.wait()
    for c in keeps:
        c.wait()


def first_gather(x, wq, wkv, gains, cid):
    tok, width = x.shape
    wide, thin = wq.shape[1] // 4, wkv.shape[1] // 4
    return pl.pallas_call(
        first_gather_kernel,
        in_specs=[ANY] * 4,
        out_specs=[ANY] * 4,
        out_shape=[
            jax.ShapeDtypeStruct((2 * tok, 4 * width), BF),
            jax.ShapeDtypeStruct((4 * width, wide), BF),
            jax.ShapeDtypeStruct((4 * width, thin), BF),
            jax.ShapeDtypeStruct((8, 4 * width), F32),
        ],
        scratch_shapes=[
            pltpu.VMEM((tok, width), BF),
            pltpu.VMEM((width, wide), BF),
            pltpu.VMEM((width, thin), BF),
            pltpu.VMEM((8, width), F32),
            pltpu.SemaphoreType.DMA((6,)),
            pltpu.SemaphoreType.DMA((3, 4)),
            pltpu.SemaphoreType.DMA((3, 4)),
        ]
        + Gather.sems(),
        compiler_params=pltpu.CompilerParams(collective_id=cid, has_side_effects=True),
        name="first_gather",
    )(x, wq, wkv, gains)


def grad_plan(kind, shape):
    rows, cols = shape
    if kind == "columns":
        w = rows // 4
        high, n = rows // CR, w // CR
        return (
            high * (cols // CC), high,
            lambda i: lax.rem(i, high) // n, lambda i: lax.rem(i, high), lambda i: i // high,
            (w, 4 * cols), lambda c, i: (lax.rem(i, n) * CR, c * cols + i // high * CC),
        )
    high = rows // CR
    if kind == "rows":
        return (
            4 * high, high,
            lambda i: i // high, lambda i: lax.rem(i, high), lambda i: i // high,
            (4 * rows, cols // 4), lambda c, i: (c * rows + lax.rem(i, high) * CR, 0),
        )
    n = high // 4
    return (
        high, high,
        lambda i: i // n, lambda i: i, lambda i: 0,
        (rows, cols), lambda c, i: ((c * n + lax.rem(i, n)) * CR, 0),
    )


class GroupSum:
    def __init__(self, kinds, lefts, rights, outs, refs):
        (self.left, self.right, self.left_sem, self.right_sem, self.own, self.land, self.mids, self.tops, self.in_send, self.in_recv, self.mid_send,
         self.mid_recv, self.top_send, self.top_recv, self.out_send, self.out_recv, self.far_send, self.far_recv) = refs
        self.lefts, self.rights, self.outs = lefts, rights, outs
        self.plans = [grad_plan(k, (a.shape[1], b.shape[1])) for k, a, b in zip(kinds, lefts, rights)]
        self.counts = [p[0] for p in self.plans]
        self.begins = [sum(self.counts[:i]) for i in range(len(lefts))]
        groups = [p[0] // p[1] for p in self.plans]
        self.groups = [sum(groups[:i]) for i in range(len(lefts))]
        self.total = sum(self.counts)
        z = lax.axis_index("dp")
        self.col = lax.axis_index("col")
        self.is_mid = (z == 1) | (z == 2)
        self.is_end = jnp.logical_not(self.is_mid)
        left = z < 2
        self.inward = {"dp": jnp.where(left, z + 1, z - 1)}
        self.outward = {"dp": jnp.where(left, z - 1, z + 1)}
        self.kept = jnp.where(left, 0, 1)

    @staticmethod
    def scratch(kinds, span):
        dma = pltpu.SemaphoreType.DMA
        return (
            [pltpu.VMEM((2, span, CR), BF), pltpu.VMEM((2, span, CC), BF), dma((2,)), dma((2,))]
            + [pltpu.VMEM((RING, CR, CC), BF)] * 2
            + [pltpu.VMEM((RING, HR, CC), BF)] * 2
            + [dma((RING,))] * 6
            + [dma((RING, 2))] * 3
            + [dma((len(kinds),))]
        )

    def greet(self, others):
        barrier = pltpu.get_barrier_semaphore()
        targets = [self.inward] + others
        for target in targets:
            pl.semaphore_signal(barrier, inc=1, device_id=target, device_id_type=MESH)

        @pl.when(self.is_mid)
        def _():
            pl.semaphore_signal(barrier, inc=1, device_id=self.outward, device_id_type=MESH)
            pl.semaphore_wait(barrier, len(targets) + 1)

        @pl.when(self.is_end)
        def _():
            pl.semaphore_wait(barrier, len(targets))

    def rows(self, half):
        return pl.ds(pl.multiple_of(half * HR, HR), HR)

    def each(self, j, action):
        for m, count in enumerate(self.counts):

            @pl.when((j >= self.begins[m]) & (j < self.begins[m] + count))
            def _(m=m):
                action(m, j - self.begins[m])

    def left_load(self, m, i, j):
        lines = pl.ds(pl.multiple_of(self.plans[m][3](i) * CR, CR), CR)
        slot = lax.rem(j, 2)
        return pltpu.make_async_copy(self.lefts[m].at[:, lines], self.left.at[slot], self.left_sem.at[slot])

    def right_slot(self, m, i):
        return lax.rem(self.groups[m] + i // self.plans[m][1], 2)

    def right_load(self, m, i):
        lines = pl.ds(pl.multiple_of(self.plans[m][4](i) * CC, CC), CC)
        slot = self.right_slot(m, i)
        return pltpu.make_async_copy(self.rights[m].at[:, lines], self.right.at[slot], self.right_sem.at[slot])

    def fetch(self, j):
        def action(m, i):
            self.left_load(m, i, j).start()
            if self.resident[m] is None:

                @pl.when(lax.rem(i, self.plans[m][1]) == 0)
                def _():
                    self.right_load(m, i).start()

        self.each(j, action)

    def produce(self, j):
        slot = lax.rem(j, RING)

        def action(m, i):
            self.left_load(m, i, j).wait()
            if self.resident[m] is None:

                @pl.when(lax.rem(i, self.plans[m][1]) == 0)
                def _():
                    self.right_load(m, i).wait()

                right = self.right[self.right_slot(m, i)]
            else:
                right = self.resident[m][...]
            self.own[slot] = contract(self.left[lax.rem(j, 2)], right, 0, 0).astype(BF)

        self.each(j, action)

    def spread(self, j, half, src):
        slot = lax.rem(j, RING)

        def action(m, i):
            s = self.plans[m][2](i)
            r, q = self.plans[m][6](self.col, i)
            dst = self.outs[m].at[
                pl.ds(pl.multiple_of(r + half * HR, HR), HR), pl.ds(pl.multiple_of(q, CC), CC)
            ]

            @pl.when(s == 0)
            def _():
                pltpu.make_async_copy(src, dst, self.far_send.at[slot, half]).start()

            @pl.when(s > 0)
            def _():
                owner = lax.rem(lax.rem(self.col, 2) + lax.rem(s, 2), 2) + 2 * lax.rem(self.col // 2 + s // 2, 2)
                remote(src, dst, self.far_send.at[slot, half], self.far_recv.at[m], col=owner).start()

        self.each(j, action)

    def reclaim(self, j):
        slot = lax.rem(j, RING)
        for half in range(2):
            done(self.mids.at[slot], self.far_send.at[slot, half])

        @pl.when(self.is_mid)
        def _():
            done(self.mids.at[slot], self.mid_send.at[slot])
            done(self.mids.at[slot], self.top_send.at[slot])
            for half in range(2):
                done(self.mids.at[slot], self.out_send.at[slot, half])

        @pl.when(self.is_end)
        def _():
            done(self.own.at[slot], self.in_send.at[slot])

    def inbound(self, j):
        slot = lax.rem(j, RING)

        @pl.when(self.is_mid)
        def _():
            done(self.land.at[slot], self.in_recv.at[slot])
            self.own[slot] = (self.own[slot].astype(F32) + self.land[slot].astype(F32)).astype(BF)
            src = self.own.at[slot, self.rows(1 - self.kept)]
            remote(src, self.mids.at[slot], self.mid_send.at[slot], self.mid_recv.at[slot], **self.inward).start()

        @pl.when(self.is_end)
        def _():
            remote(
                self.own.at[slot], self.land.at[slot], self.in_send.at[slot], self.in_recv.at[slot], **self.inward
            ).start()

    def middle(self, j):
        slot = lax.rem(j, RING)

        @pl.when(self.is_mid)
        def _():
            done(self.mids.at[slot], self.mid_recv.at[slot])
            rows = self.rows(self.kept)
            self.own[slot, rows] = (self.own[slot, rows].astype(F32) + self.mids[slot].astype(F32)).astype(BF)
            src = self.own.at[slot, rows]
            remote(src, self.tops.at[slot], self.top_send.at[slot], self.top_recv.at[slot], **self.inward).start()
            remote(
                src, self.land.at[slot, rows], self.out_send.at[slot, self.kept], self.out_recv.at[slot, self.kept],
                **self.outward,
            ).start()
            self.spread(j, self.kept, src)

    def settle(self, j):
        slot = lax.rem(j, RING)

        @pl.when(self.is_mid)
        def _():
            done(self.tops.at[slot], self.top_recv.at[slot])
            half = 1 - self.kept
            src = self.tops.at[slot]
            remote(
                src, self.land.at[slot, self.rows(half)], self.out_send.at[slot, half], self.out_recv.at[slot, half],
                **self.outward,
            ).start()
            self.spread(j, half, src)

    def outbound(self, j):
        slot = lax.rem(j, RING)

        @pl.when(self.is_end)
        def _():
            for half in range(2):
                src = self.land.at[slot, pl.ds(half * HR, HR)]
                done(src, self.out_recv.at[slot, half])
                self.spread(j, half, src)

    def begin(self):
        self.fetch(jnp.int32(0))
        self.produce(jnp.int32(0))
        self.fetch(jnp.int32(1))

    def tick(self, t):
        for off, stage in zip(OFFS, (self.inbound, self.middle, self.settle, self.outbound)):

            @pl.when((t >= off) & (t < self.total + off))
            def _(off=off, stage=stage):
                stage(t - off)

        ahead = t + 1

        @pl.when(ahead < self.total)
        def _():
            @pl.when(ahead >= RING)
            def _():
                self.reclaim(ahead - RING)

            self.produce(ahead)

            @pl.when(ahead + 1 < self.total)
            def _():
                self.fetch(ahead + 1)

    def finish(self):
        def drain(j, carry):
            self.reclaim(j)
            return carry

        lax.fori_loop(self.total - RING, self.total, drain, 0)
        for m, out in enumerate(self.outs):
            done(out.at[pl.ds(0, 3 * out.shape[0] // 4)], self.far_recv.at[m])


MB = 128
AQ, AK = 256, 512


def backward_kernel(
    kinds,
    info_ref, gain_ref, mlp_ref, gate_ref, up_ref, hidden_ref, part_ref, low_part_ref, resid_ref, low_ref, w_ref, mixed_ref,
    wide_ref, normed_ref, x_ref, q_ref, k_ref, v_ref, lse_ref, turn_ref, wq_ref, wkv_ref,
    out_gate, out_up, out_down, out_out, out_heads, mid_out, gain_part, attn_out, down_out, dot_out,
    cot_full, attn_part, mid_low,
    *refs,
):
    refs = list(refs)

    def take(count):
        taken = refs[:count]
        del refs[:count]
        return taken

    zsum = GroupSum(
        kinds,
        [hidden_ref, mlp_ref, mlp_ref, mixed_ref, normed_ref],
        [low_ref, gate_ref, up_ref, mid_low, refs[0]],
        [out_down, out_gate, out_up, out_out, out_heads],
        refs[1:19],
    )
    heads_cot = refs[0]
    zsum.resident = [None, None, None, None, heads_cot]
    del refs[:19]
    scratch = take(5)
    mlp_reduce = Reduce(part_ref, scratch, take(7))
    low_reduce = Reduce(low_part_ref, scratch, take(7))
    attn_reduce = Reduce(attn_part, scratch, take(7))
    mine, = take(1)
    tok, width = mine.shape
    gather = Gather(mine, cot_full, token_place(tok, width), None, take(Gather.SEMS))
    bufs, resid_buf, out_buf, buf_sem, out_sem = take(5)
    mixed_cot, wide_buf, dq_sum, dk_sum, dv_sum, dots, dots_mate, dots_col = take(8)
    dot_send, dot_recv, ready, w_mine, w_sem = take(5)
    span = 2 * tok
    heads_width = q_ref.shape[1]
    heads = heads_width // HD
    half = lax.axis_index("row")
    col = lax.axis_index("col")
    length = info_ref[0]
    near_x, near_y, mate = plane_peers()
    corner = {"col": 3 - col}
    blocks = span // MB

    def mid_loads(i):
        slot = lax.rem(i, 2)
        lines = pl.ds(pl.multiple_of(i * MB, MB), MB)
        return [
            pltpu.make_async_copy(cot_full.at[lines, :], bufs.at[slot, 0], buf_sem.at[slot, 0]),
            pltpu.make_async_copy(low_ref.at[lines, :], bufs.at[slot, 1], buf_sem.at[slot, 1]),
            pltpu.make_async_copy(resid_ref.at[lines, :], resid_buf.at[slot], buf_sem.at[slot, 2]),
        ]

    def row_store(out, i):
        lines = pl.ds(pl.multiple_of(i * MB, MB), MB)
        return pltpu.make_async_copy(bufs.at[lax.rem(i, 2), 2], out.at[lines, :], out_sem.at[1])

    def mid_store(i):
        lines = pl.ds(pl.multiple_of(i * MB, MB), MB)
        return pltpu.make_async_copy(out_buf.at[:, pl.ds(0, width)], mid_out.at[lines, :], out_sem.at[0])

    def mid_item(i):
        slot = lax.rem(i, 2)

        @pl.when(i + 1 < blocks)
        def _():
            for c in mid_loads(i + 1):
                c.start()

        for c in mid_loads(i):
            c.wait()
        cot = bufs[slot, 0].astype(F32)
        resid = resid_buf[slot]
        scale = lax.rsqrt(jnp.mean(resid * resid, axis=1, keepdims=True) + EPSILON)
        weighed = cot * gain_ref[1:2, :]
        inner = jnp.sum(weighed * resid, axis=1, keepdims=True)
        mid = bufs[slot, 1].astype(F32) + weighed * scale - resid * (scale * scale * scale * inner / D)
        low = mid.astype(BF)
        lines = pl.ds(pl.multiple_of(i * MB, MB), MB)
        mixed_cot[lines, :] = contract(low, w_mine[...], 1, 1).astype(BF)

        @pl.when(i > 0)
        def _():
            row_store(mid_low, i - 1).wait()

        bufs[slot, 2] = low
        row_store(mid_low, i).start()

        @pl.when(i < blocks // 2)
        def _():
            @pl.when(i > 0)
            def _():
                mid_store(i - 1).wait()

            out_buf[:, pl.ds(0, width)] = mid[:, :width]
            mid_store(i).start()
            part = jnp.sum((cot * resid * scale)[:, :width], axis=0, keepdims=True)
            gain_part[...] += jnp.broadcast_to(part, gain_part.shape)

        @pl.when(i == blocks // 2)
        def _():
            mid_store(i - 1).wait()

    q_steps = span // AQ
    rows = heads * AQ
    pieces = [slice(h * HD, (h + 1) * HD) for h in range(heads)]

    def attn_item(q_step, tile, diagonal):
        stored = lax.rem(q_step + half * (q_steps // 2), q_steps)
        lines = pl.ds(pl.multiple_of(stored * AQ, AQ), AQ)
        key_tiles = span // AK
        keys = pl.ds(pl.multiple_of(lax.rem(tile + half * (key_tiles // 2), key_tiles) * AK, AK), AK)
        first = q_step * AQ
        q = jnp.concatenate([q_ref[lines, s] for s in pieces], axis=0)
        cot = jnp.concatenate([mixed_cot[lines, s] for s in pieces], axis=0)
        wide = jnp.concatenate([wide_buf[:, s] for s in pieces], axis=0)
        place = first + lax.rem(lax.broadcasted_iota(jnp.int32, (1, rows), 1), AQ)
        log_total = jnp.where(place < length, lse_ref[q_step], -NEG_FILL)
        inner = jnp.sum(wide * cot.astype(F32), axis=1, keepdims=True)
        inner = jnp.broadcast_to(inner, (rows, LANES)).T[0:1, :]
        k_tile = k_ref[keys, :]
        v_tile = v_ref[keys, :]
        scores = contract(k_tile, q, 1, 1) * HD**-0.5 - log_total
        if diagonal:
            key_place = tile * AK + lax.broadcasted_iota(jnp.int32, (AK, rows), 0)
            scores = jnp.where(key_place <= place, scores, NEG_FILL)
        weights = jnp.exp(scores)
        prob_cot = contract(v_tile, cot, 1, 1)
        score_cot = (weights * (prob_cot - inner)).astype(BF)
        dv_sum[keys, :] += contract(weights.astype(BF), cot, 1, 0)
        dk_sum[keys, :] += contract(score_cot, q, 1, 0) * HD**-0.5
        dq = contract(score_cot, k_tile, 0, 0) * HD**-0.5

        @pl.when(tile == 0)
        def _():
            dq_sum[...] = dq

        @pl.when(tile > 0)
        def _():
            dq_sum[...] += dq

        if diagonal:
            cos, sin = turn_ref[lines, :HD], turn_ref[lines, HD:]
            for h in range(heads):
                part = dq_sum[h * AQ : (h + 1) * AQ, :]
                swapped = jnp.concatenate([part[:, HD // 2 :], -part[:, : HD // 2]], axis=1)
                heads_cot[lines, h * HD : (h + 1) * HD] = (part * cos + swapped * sin).astype(BF)

    starts = [0]
    for n in range(q_steps):
        starts.append(starts[-1] + n * AQ // AK + 1)
    attn_items = starts.pop()

    def wide_load(q_step):
        stored = lax.rem(q_step + half * (q_steps // 2), q_steps)
        lines = pl.ds(pl.multiple_of(stored * AQ, AQ), AQ)
        return pltpu.make_async_copy(wide_ref.at[lines, :], wide_buf, w_sem.at[1])

    def attn_one(n):
        q_step = sum([jnp.where(n >= start, 1, 0) for start in starts[1:]], jnp.int32(0))
        tile = n - sum([jnp.where(n >= b, b - a, 0) for a, b in zip(starts, starts[1:])], jnp.int32(0))
        last = q_step * AQ // AK

        @pl.when(tile == 0)
        def _():
            wide_load(q_step).wait()

        @pl.when(tile < last)
        def _():
            attn_item(q_step, tile, False)

        @pl.when(tile == last)
        def _():
            attn_item(q_step, tile, True)

            @pl.when(q_step + 1 < q_steps)
            def _():
                wide_load(q_step + 1).start()

    def attn_finish():
        part = dk_sum[...]
        swapped = jnp.concatenate([part[:, HD // 2 :], -part[:, : HD // 2]], axis=1)
        heads_cot[:, heads_width : heads_width + HD] = (part * turn_ref[:, :HD] + swapped * turn_ref[:, HD:]).astype(BF)
        heads_cot[:, heads_width + HD : heads_width + 2 * HD] = dv_sum[...].astype(BF)

    def head_load(i):
        slot = lax.rem(i, 2)
        lines = pl.ds(pl.multiple_of(i * MB, MB), MB)
        return pltpu.make_async_copy(x_ref.at[lines, :], bufs.at[slot, 1], buf_sem.at[slot, 1])

    def head_item(i):
        slot = lax.rem(i, 2)

        @pl.when(i + 1 < blocks)
        def _():
            head_load(i + 1).start()

        head_load(i).wait()
        lines = pl.ds(pl.multiple_of(i * MB, MB), MB)
        part = contract(heads_cot[lines, :heads_width], wq_ref[...], 1, 1)
        part += contract(heads_cot[lines, heads_width : heads_width + 2 * HD], wkv_ref[...], 1, 1)

        @pl.when(i > 0)
        def _():
            row_store(attn_part, i - 1).wait()

        bufs[slot, 2] = part.astype(BF)
        row_store(attn_part, i).start()
        inner = jnp.sum(part * gain_ref[0:1, :] * bufs[slot, 1].astype(F32), axis=1, keepdims=True)
        dots[pl.ds(i, 1), :] = jnp.broadcast_to(inner, (MB, LANES)).T[0:1, :]

    def dot_give():
        n = blocks // 2
        return remote(dots.at[pl.ds(n, n), :], dots_mate, dot_send.at[0], dot_recv.at[0], **mate)

    def dot_share():
        n = blocks // 2
        return [
            remote(dots.at[pl.ds(0, n), :], dots_col.at[s], dot_send.at[1 + s], dot_recv.at[1 + s], **peer)
            for s, peer in enumerate((near_x, near_y, corner))
        ]

    def emit(work, out, sem):
        for a in range(2):
            sum_total = work.total(a)
            h = tok // 4
            for b in range(2):
                lines = pl.ds(a * 2 * h + b * h, h)
                resid_sum = sum_total[b * h : (b + 1) * h]
                emit_buf[...] = resid_sum
                c = pltpu.make_async_copy(emit_buf, out.at[lines, :], sem)
                c.start()
                c.wait()

    emit_buf, = take(1)

    pltpu.make_async_copy(w_ref.at[pl.ds(pl.multiple_of(col * heads_width, heads_width), heads_width), :], w_mine, w_sem.at[0]).start()
    gain_part[...] = jnp.zeros_like(gain_part)
    heads_cot[:, heads_width + 2 * HD :] = jnp.zeros((span, CC - heads_width - 2 * HD), BF)
    zsum.begin()
    dk_sum[...] = jnp.zeros_like(dk_sum)
    dv_sum[...] = jnp.zeros_like(dv_sum)
    zsum.greet([near_x, near_y, corner, mate])

    at = {}

    def plan(tick, action):
        at.setdefault(tick, []).append(action)

    def start_all(copies):
        for c in copies:
            c.start()

    plan(0, mlp_reduce.begin)
    plan(T_ONE, lambda: [mlp_reduce.first(a) for a in range(2)])
    plan(T_TWO, lambda: [mlp_reduce.second(a) for a in range(2)])

    def own_block():
        for a in range(2):
            mine[mlp_reduce.lines(a), :] = mlp_reduce.total(a).astype(BF)
        gather.begin()

    plan(T_SUM, own_block)
    plan(T_GATHER, gather.first)
    plan(T_GATHER + 3, gather.second)

    def start_mid():
        gather.finish()
        mlp_reduce.finish()
        pltpu.make_async_copy(w_ref.at[pl.ds(0, heads_width), :], w_mine, w_sem.at[0]).wait()
        start_all(mid_loads(jnp.int32(0)))
        low_reduce.begin()

    plan(T_MID, start_mid)
    plan(T_MID + 4, lambda: [low_reduce.first(a) for a in range(2)])
    plan(T_MID + 9, lambda: [low_reduce.second(a) for a in range(2)])

    def low_done():
        emit(low_reduce, down_out, out_sem.at[2])
        low_reduce.finish()
        for i, peer in enumerate((near_x, near_y, mate)):
            pl.semaphore_signal(ready.at[i], inc=1, device_id=peer, device_id_type=MESH)

    plan(T_MID + 13, low_done)
    t_attn = T_MID + 1 + blocks // N_MID
    plan(t_attn, lambda: (row_store(mid_low, blocks - 1).wait(), wide_load(jnp.int32(0)).start()))
    t_head = t_attn + 1 + attn_items // N_ATTN
    plan(t_head, lambda: (attn_finish(), head_load(jnp.int32(0)).start()))
    t_last = t_head + 1 + blocks // N_HEAD

    def start_last():
        row_store(attn_part, blocks - 1).wait()
        dot_give().start()
        for i in range(3):
            pl.semaphore_wait(ready.at[i], 1)
        attn_reduce.begin()

    plan(t_last, start_last)

    def last_first():
        n = blocks // 2
        done(dots_mate, dot_recv.at[0])
        dot_give().wait_send()
        dots[pl.ds(0, n), :] = dots[pl.ds(0, n), :] + dots_mate[...]
        start_all(dot_share())
        for a in range(2):
            attn_reduce.first(a)

    plan(t_last + 3, last_first)
    plan(t_last + 7, lambda: [attn_reduce.second(a) for a in range(2)])

    def last_done():
        n = blocks // 2
        shares = dot_share()
        for c in shares:
            c.wait()
        terms = [dots[pl.ds(0, n), :], dots_col[0], dots_col[1], dots_col[2]]
        dot_out[...] = (terms[0] + terms[1]) + (terms[2] + terms[3])
        emit(attn_reduce, attn_out, out_sem.at[2])
        attn_reduce.finish()

    plan(t_last + 10, last_done)
    final = max(zsum.total + OFFS[3], t_last + 11)

    def tick(t, carry):
        zsum.tick(t)
        for when in sorted(at):

            @pl.when(t == when)
            def _(when=when):
                for action in at[when]:
                    action()

        @pl.when((t > T_MID) & (t < t_attn))
        def _():
            for e in range(N_MID):
                mid_item((t - T_MID - 1) * N_MID + e)

        @pl.when((t > t_attn) & (t < t_head))
        def _():
            def body(e, carry):
                attn_one((t - t_attn - 1) * N_ATTN + e)
                return carry

            lax.fori_loop(0, N_ATTN, body, 0)

        @pl.when((t > t_head) & (t < t_last))
        def _():
            for e in range(N_HEAD):
                head_item((t - t_head - 1) * N_HEAD + e)

        return carry

    lax.fori_loop(0, final, tick, 0)
    zsum.finish()


T_ONE, T_TWO, T_SUM, T_GATHER, T_MID = 2, 7, 10, 12, 19
N_MID, N_ATTN, N_HEAD = 2, 2, 4


def backward(info, gains, normed_mlp, gate_cot, up_cot, hidden, mlp_part, low_part, resid, low, w_out_full, mixed, q, k, v, wide, lse, cos, sin,
             wq, wkv, normed, tokens_full, cid):
    span, full = normed.shape
    tok, width = span // 2, full // 4
    heads_width = mixed.shape[1]
    heads = heads_width // HD
    units = hidden.shape[1]
    kinds = ["rows", "columns", "columns", "rows", "stack"]
    sources = [(units, full), (full, units), (full, units), (heads_width, full), (full, CC)]
    outs = [jax.ShapeDtypeStruct(grad_plan(kd, s)[5], BF) for kd, s in zip(kinds, sources)]
    outs = [outs[i] for i in (1, 2, 0, 3, 4)]
    vmem = pl.BlockSpec(memory_space=pltpu.VMEM)
    dma = pltpu.SemaphoreType.DMA
    blocks = span // MB
    turn = jnp.concatenate([cos, sin], axis=1)
    lse = lse.reshape(span // QB, heads, QB // AQ, AQ).transpose(0, 2, 1, 3).reshape(span // AQ, 1, heads * AQ)
    shapes = outs + [
        jax.ShapeDtypeStruct((tok, width), F32),
        jax.ShapeDtypeStruct((8, width), F32),
        jax.ShapeDtypeStruct((tok, width), F32),
        jax.ShapeDtypeStruct((tok, width), F32),
        jax.ShapeDtypeStruct((blocks // 2, LANES), F32),
        jax.ShapeDtypeStruct((span, full), BF),
        jax.ShapeDtypeStruct((span, full), BF),
        jax.ShapeDtypeStruct((span, full), BF),
    ]
    out_specs = [ANY] * 5 + [ANY, vmem, ANY, ANY, vmem, ANY, ANY, ANY]
    scratch = (
        [pltpu.VMEM((span, CC), BF)]
        + GroupSum.scratch(kinds, span)
        + Reduce.scratch(tok, full)
        + Reduce.sems() * 3
        + [pltpu.VMEM((tok, width), BF)]
        + Gather.sems()
        + [
            pltpu.VMEM((2, 3, MB, full), BF),
            pltpu.VMEM((2, MB, full), F32),
            pltpu.VMEM((MB, width), F32),
            dma((2, 3)),
            dma((3,)),
            pltpu.VMEM((span, heads_width), BF),
            pltpu.VMEM((AQ, heads_width), F32),
            pltpu.VMEM((heads * AQ, HD), F32),
            pltpu.VMEM((span, HD), F32),
            pltpu.VMEM((span, HD), F32),
            pltpu.VMEM((blocks, LANES), F32),
            pltpu.VMEM((blocks // 2, LANES), F32),
            pltpu.VMEM((3, blocks // 2, LANES), F32),
            dma((4,)),
            dma((4,)),
            pltpu.SemaphoreType.REGULAR((3,)),
            pltpu.VMEM((heads_width, full), BF),
            dma((2,)),
            pltpu.VMEM((tok // 4, width), F32),
        ]
    )
    results = pl.pallas_call(
        functools.partial(backward_kernel, kinds),
        in_specs=[pl.BlockSpec(memory_space=pltpu.SMEM), vmem] + [ANY] * 13 + [vmem] * 7,
        out_specs=out_specs,
        out_shape=shapes,
        scratch_shapes=scratch,
        compiler_params=pltpu.CompilerParams(
            collective_id=cid, has_side_effects=True, vmem_limit_bytes=VMEM_ALL
        ),
        name="backward",
    )(info, gains, normed_mlp, gate_cot, up_cot, hidden, mlp_part, low_part, resid, low, w_out_full, mixed, wide, normed,
      tokens_full, q, k, v, lse, turn, wq, wkv)
    return results[:10]


def by_distance(stacked, dim):
    count = lax.axis_size("col")
    order = lax.axis_index("col") ^ jnp.arange(count)
    blocks = jnp.take(stacked, order, axis=0)
    return jnp.concatenate([blocks[i] for i in range(count)], axis=dim)


def plain_gather(x):
    cols = by_distance(lax.all_gather(x, "col"), 1)
    return jnp.concatenate([cols, swap(cols, "row", 1)], axis=0)


def plain_gather_heads(x):
    mine = lax.all_gather(x, "col", axis=1, tiled=True)
    half = x.shape[0] // 2
    other = swap(mine, "row", 1)
    other = jnp.concatenate([other[half:], other[:half]], axis=0)
    return jnp.concatenate([mine, other], axis=1)


def plain_reduce(part):
    span, full = part.shape
    count = lax.axis_size("col")
    width = full // count
    half = part[: span // 2].astype(F32) + swap(part[span // 2 :], "row", 1).astype(F32)
    order = lax.axis_index("col") ^ jnp.arange(count)
    blocks = jnp.stack([half[:, s * width : (s + 1) * width] for s in range(count)])
    return lax.psum_scatter(jnp.take(blocks, order, axis=0), "col", tiled=False)


def exchange(packs):
    if kernels_fit():
        return [p if s == 0 else swap(p, "col", s) for s, p in enumerate(packs)]
    count = len(packs)
    order = lax.axis_index("col") ^ jnp.arange(count)
    sent = jnp.take(jnp.stack(packs), order, axis=0)
    blocks = jnp.take(lax.all_to_all(sent, "col", 0, 0, tiled=True), order, axis=0)
    return [blocks[i] for i in range(count)]


def plain_group_sum(grads, kinds):
    outs = []
    count = lax.axis_size("col")
    order = lax.axis_index("col") ^ jnp.arange(count)
    for grad, kind in zip(grads, kinds):
        grad = lax.psum(grad.astype(F32), "dp").astype(BF)
        dim = 1 if kind == "rows" else 0
        blocks = jnp.stack(jnp.split(grad, count, axis=dim))
        blocks = lax.all_to_all(jnp.take(blocks, order, axis=0), "col", 0, 0, tiled=True)
        out_dim = 1 if kind == "columns" else 0
        outs.append(jnp.concatenate([blocks[i] for i in range(count)], axis=out_dim))
    return outs


def kernels_fit():
    return lax.axis_size("col") == 4 and lax.axis_size("dp") == 4 and lax.axis_size("row") == 2


def attn_forward_kernel(info_ref, q_ref, k_ref, v_ref, *refs):
    linked = len(refs) > 6
    if linked:
        side_ref, mixed_ref, wide_ref, lse_ref, peak_ref, side_out, score_ref, sum_ref, stage = refs[:9]
        gather = Gather(side_ref, side_out, token_place(*side_ref.shape), stage, refs[9:])
    else:
        mixed_ref, wide_ref, lse_ref, peak_ref, score_ref, sum_ref = refs
    heads = q_ref.shape[1] // HD
    span = k_ref.shape[0]
    rows = heads * QB
    length = info_ref[0]
    half = lax.axis_index("row")
    step = pl.program_id(0)
    first = step * QB
    key_tiles = span // FWD_KB
    steps = span // QB
    lines = pl.ds(pl.multiple_of(lax.rem(step + half * (steps // 2), steps) * QB, QB), QB)

    if linked:

        @pl.when(step == 0)
        def _():
            greet(list(gather.near))
            gather.begin()

        @pl.when(step == steps - 1)
        def _():
            gather.first()

    q = jnp.concatenate([q_ref[lines, h * HD : (h + 1) * HD] for h in range(heads)], axis=0)
    tiles = (first + QB) // FWD_KB
    plain = first // FWD_KB

    def tile_of(ref, tile):
        stored = lax.rem(tile + half * (key_tiles // 2), key_tiles)
        return ref[pl.ds(pl.multiple_of(stored * FWD_KB, FWD_KB), FWD_KB), :]

    def fold(values, running, op):
        for t in range(FWD_KB // LANES):
            running = op(running, values[:, t * LANES : (t + 1) * LANES])
        return running

    def scores_of(tile, top, diagonal):
        scores = contract(q, tile_of(k_ref, tile), 1, 1) * HD**-0.5
        if diagonal:
            place = first + lax.broadcasted_iota(jnp.int32, (QB, FWD_KB), 0)
            key_place = tile * FWD_KB + lax.broadcasted_iota(jnp.int32, (QB, FWD_KB), 1)
            allowed = (key_place <= place) & (key_place < length)
            scores = jnp.where(allowed[None], scores.reshape(heads, QB, FWD_KB), NEG_FILL)
            scores = scores.reshape(rows, FWD_KB)
        else:
            key_place = tile * FWD_KB + lax.broadcasted_iota(jnp.int32, (1, FWD_KB), 1)
            scores = jnp.where(key_place < length, scores, NEG_FILL)
        score_ref[tile] = scores
        return fold(scores, top, jnp.maximum)

    top = jnp.full((rows, LANES), NEG_FILL, F32)
    top = lax.fori_loop(0, plain, lambda tile, top: scores_of(tile, top, False), top)
    top = lax.fori_loop(plain, tiles, lambda tile, top: scores_of(tile, top, True), top)
    top = jnp.max(top, axis=1, keepdims=True)
    live = first + lax.broadcasted_iota(jnp.int32, (QB, 1), 0) < length
    peak = jnp.max(jnp.where(live[None], top.reshape(heads, QB, 1), NEG_FILL), axis=1)

    @pl.when(step == 0)
    def _():
        peak_ref[...] = jnp.full_like(peak_ref, NEG_FILL)

    peak_ref[...] = jnp.maximum(peak_ref[...], jnp.broadcast_to(peak, peak_ref.shape))
    sum_ref[...] = jnp.zeros_like(sum_ref)

    def weigh(tile, total):
        weights = jnp.exp(score_ref[tile] - top)
        sum_ref[...] += contract(weights.astype(BF), tile_of(v_ref, tile), 1, 0)
        return fold(weights, total, jnp.add)

    total = lax.fori_loop(0, tiles, weigh, jnp.zeros((rows, LANES), F32))
    total = jnp.sum(total, axis=1, keepdims=True)
    mixed = sum_ref[...] / total
    log_total = jnp.broadcast_to(top + jnp.log(total), (rows, LANES))
    lse_ref[step] = log_total.T[0:1, :]
    for h in range(heads):
        part = mixed[h * QB : (h + 1) * QB]
        mixed_ref[lines, h * HD : (h + 1) * HD] = part.astype(BF)
        wide_ref[lines, h * HD : (h + 1) * HD] = part

    if linked:

        @pl.when(step == steps - 1)
        def _():
            gather.second()
            gather.finish()


def attn_forward(info, q, k, v, side=None, cid=None):
    span, width = q.shape
    heads = width // HD
    steps = span // QB
    whole = lambda shape: pl.BlockSpec(shape, lambda i: (0,) * len(shape))
    pairs = heads * span * span // 2
    shapes = [
        jax.ShapeDtypeStruct((span, width), BF),
        jax.ShapeDtypeStruct((span, width), F32),
        jax.ShapeDtypeStruct((steps, 1, heads * QB), F32),
        jax.ShapeDtypeStruct((heads, LANES), F32),
    ]
    in_specs = [pl.BlockSpec(memory_space=pltpu.SMEM)] + [whole(a.shape) for a in (q, k, v)]
    out_specs = [whole(s.shape) for s in shapes]
    scratch = [
        pltpu.VMEM((span // FWD_KB, heads * QB, FWD_KB), F32),
        pltpu.VMEM((heads * QB, HD), F32),
    ]
    operands = [info, q, k, v]
    params = dict(vmem_limit_bytes=48 * MIB)
    if side is not None:
        tok, wide = side.shape
        operands.append(side)
        in_specs.append(ANY)
        out_specs.append(ANY)
        shapes.append(jax.ShapeDtypeStruct((2 * tok, 4 * wide), side.dtype))
        scratch += [pltpu.VMEM(side.shape, side.dtype)] + Gather.sems()
        params.update(collective_id=cid, has_side_effects=True)
    return pl.pallas_call(
        attn_forward_kernel,
        grid=(steps,),
        in_specs=in_specs,
        out_specs=out_specs,
        scratch_shapes=scratch,
        out_shape=shapes,
        compiler_params=pltpu.CompilerParams(**params),
        cost_estimate=pl.CostEstimate(
            flops=40 * pairs * HD // 4, transcendentals=pairs, bytes_accessed=8 * span * width
        ),
        name="attn_forward",
    )(*operands)


def turn_back(values, cos_ref, sin_ref):
    half = HD // 2
    swapped = jnp.concatenate([values[:, half:], -values[:, :half]], axis=1)
    return values * cos_ref[...] + swapped * sin_ref[...]


def attn_backward_kernel(
    info_ref, q_ref, k_ref, v_ref, cot_ref, wide_ref, lse_ref, cosq_ref, sinq_ref, cosk_ref, sink_ref,
    dq_ref, dk_ref, dv_ref, dq_sum, dk_sum, dv_sum,
):
    heads = q_ref.shape[1] // HD
    span = k_ref.shape[0]
    rows = heads * QB
    length = info_ref[0]
    half = info_ref[1]
    step = pl.program_id(0)
    first = step * QB
    key_tiles = span // BWD_KB

    @pl.when(step == 0)
    def _():
        dk_sum[...] = jnp.zeros_like(dk_sum)
        dv_sum[...] = jnp.zeros_like(dv_sum)

    dq_sum[...] = jnp.zeros_like(dq_sum)

    @pl.when(first < length)
    def _():
        pieces = [slice(h * HD, (h + 1) * HD) for h in range(heads)]
        q = jnp.concatenate([q_ref[:, s] for s in pieces], axis=0)
        cot = jnp.concatenate([cot_ref[:, s] for s in pieces], axis=0)
        wide = jnp.concatenate([wide_ref[:, s] for s in pieces], axis=0)
        log_total = lse_ref[0]
        inner = jnp.sum(wide * cot.astype(F32), axis=1, keepdims=True)
        inner = jnp.broadcast_to(inner, (rows, LANES)).T[0:1, :]

        def tile_step(tile, masked):
            stored = lax.rem(tile + half * (key_tiles // 2), key_tiles)
            keys = pl.ds(pl.multiple_of(stored * BWD_KB, BWD_KB), BWD_KB)
            k_tile = k_ref[keys, :]
            v_tile = v_ref[keys, :]
            scores = contract(k_tile, q, 1, 1) * HD**-0.5 - log_total
            if masked:
                key_place = tile * BWD_KB + lax.broadcasted_iota(jnp.int32, (BWD_KB, rows), 0)
                place = first + lax.rem(lax.broadcasted_iota(jnp.int32, (BWD_KB, rows), 1), QB)
                scores = jnp.where((key_place <= place) & (key_place < length), scores, NEG_FILL)
            weights = jnp.exp(scores)
            prob_cot = contract(v_tile, cot, 1, 1)
            score_cot = (weights * (prob_cot - inner)).astype(BF)
            dv_sum[keys, :] += contract(weights.astype(BF), cot, 1, 0)
            dk_sum[keys, :] += contract(score_cot, q, 1, 0) * HD**-0.5
            dq_sum[...] += contract(score_cot, k_tile, 0, 0) * HD**-0.5

        @pl.loop(0, first // BWD_KB)
        def _(tile):
            tile_step(tile, False)

        @pl.loop(first // BWD_KB, pl.cdiv(first + QB, BWD_KB))
        def _(tile):
            tile_step(tile, True)

    for h in range(heads):
        part = turn_back(dq_sum[h * QB : (h + 1) * QB, :], cosq_ref, sinq_ref)
        dq_ref[:, h * HD : (h + 1) * HD] = part.astype(dq_ref.dtype)

    @pl.when(step == pl.num_programs(0) - 1)
    def _():
        dk_ref[...] = turn_back(dk_sum[...], cosk_ref, sink_ref).astype(dk_ref.dtype)
        dv_ref[...] = dv_sum[...].astype(dv_ref.dtype)


def attn_backward(info, q, k, v, cot, wide, lse, cos, sin, kv_type):
    span, width = q.shape
    heads = width // HD
    steps = span // QB

    def stored(i, info_ref):
        return (lax.rem(i + info_ref[1] * (steps // 2), steps), 0)

    whole = pl.BlockSpec((span, HD), lambda i, info_ref: (0, 0))
    mine = pl.BlockSpec((QB, width), stored)
    turn = pl.BlockSpec((QB, HD), stored)
    pairs = heads * span * span // 2
    return pl.pallas_call(
        attn_backward_kernel,
        grid_spec=pltpu.PrefetchScalarGridSpec(
            num_scalar_prefetch=1,
            grid=(steps,),
            in_specs=[
                mine, whole, whole, mine, mine,
                pl.BlockSpec((1, 1, heads * QB), lambda i, info_ref: (i, 0, 0)),
                turn, turn, whole, whole,
            ],
            out_specs=[mine, whole, whole],
            scratch_shapes=[
                pltpu.VMEM((heads * QB, HD), F32),
                pltpu.VMEM((span, HD), F32),
                pltpu.VMEM((span, HD), F32),
            ],
        ),
        out_shape=[
            jax.ShapeDtypeStruct((span, width), BF),
            jax.ShapeDtypeStruct((span, HD), kv_type),
            jax.ShapeDtypeStruct((span, HD), kv_type),
        ],
        compiler_params=pltpu.CompilerParams(vmem_limit_bytes=40 * 2**20),
        cost_estimate=pl.CostEstimate(
            flops=60 * pairs * HD // 4, transcendentals=pairs, bytes_accessed=12 * span * width
        ),
        name="attn_backward",
    )(info, q, k, v, cot, wide, lse, cos, sin, cos, sin)


def head_kernel(x_ref, gain_ref, wq_ref, wkv_ref, cos_ref, sin_ref, normed_ref, q_ref, k_ref, v_ref, scale_ref):
    x = x_ref[...].astype(F32)
    scale = lax.rsqrt(jnp.mean(x * x, axis=1, keepdims=True) + EPSILON)
    scale_ref[...] = jnp.broadcast_to(scale, scale_ref.shape)
    normed = (x * scale * gain_ref[0:1, :]).astype(BF)
    normed_ref[...] = normed

    def turned(raw):
        pieces = []
        half = HD // 2
        for h in range(raw.shape[1] // HD):
            pieces += [-raw[:, h * HD + half : (h + 1) * HD], raw[:, h * HD : h * HD + half]]
        pieces = jnp.concatenate(pieces, axis=1)
        count = raw.shape[1] // HD
        cos = jnp.concatenate([cos_ref[...]] * count, axis=1)
        sin = jnp.concatenate([sin_ref[...]] * count, axis=1)
        return (raw * cos + pieces * sin).astype(BF)

    q_ref[...] = turned(contract(normed, wq_ref[...], 1, 0))
    keyval = contract(normed, wkv_ref[...], 1, 0)
    k_ref[...] = turned(keyval[:, :HD])
    v_ref[...] = keyval[:, HD:].astype(BF)


def project_heads(tokens_full, gains, wq, wkv, cos, sin):
    span, full = tokens_full.shape
    width = wq.shape[1]
    block = 512
    line = lambda n: pl.BlockSpec((block, n), lambda i: (i, 0))
    whole = lambda a: pl.BlockSpec(a.shape, lambda i: (0, 0))
    return pl.pallas_call(
        head_kernel,
        grid=(span // block,),
        in_specs=[line(full), whole(gains), whole(wq), whole(wkv), line(HD), line(HD)],
        out_specs=[line(full), line(width), line(HD), line(HD), line(LANES)],
        out_shape=[
            jax.ShapeDtypeStruct((span, full), BF),
            jax.ShapeDtypeStruct((span, width), BF),
            jax.ShapeDtypeStruct((span, HD), BF),
            jax.ShapeDtypeStruct((span, HD), BF),
            jax.ShapeDtypeStruct((span, LANES), F32),
        ],
        compiler_params=pltpu.CompilerParams(vmem_limit_bytes=48 * MIB),
        cost_estimate=pl.CostEstimate(
            flops=2 * span * full * (width + LANES), transcendentals=0, bytes_accessed=5 * span * full
        ),
        name="project_heads",
    )(tokens_full, gains, wq, wkv, cos, sin)


def project_out_kernel(mixed_ref, w_ref, x_ref, gain_ref, *refs):
    linked = len(refs) > 2
    step = pl.program_id(0)
    if linked:
        side_ref, resid_ref, normed_ref, side_out, stage = refs[:5]
        gather = Gather(side_ref, side_out, token_place(*side_ref.shape), stage, refs[5:])

        @pl.when(step == 0)
        def _():
            greet(list(gather.near))
            gather.begin()

        @pl.when(step == pl.num_programs(0) // 2)
        def _():
            gather.first()

    else:
        resid_ref, normed_ref = refs
    resid = x_ref[...].astype(F32) + contract(mixed_ref[...], w_ref[...], 1, 0)
    resid_ref[...] = resid
    scale = lax.rsqrt(jnp.mean(resid * resid, axis=1, keepdims=True) + EPSILON)
    normed_ref[...] = (resid * scale * gain_ref[1:2, :]).astype(BF)

    if linked:

        @pl.when(step == pl.num_programs(0) - 1)
        def _():
            gather.second()
            gather.finish()


def project_out(mixed_full, w_out_full, tokens_full, gains, side=None, cid=None):
    span, full = tokens_full.shape
    block = 256
    line = pl.BlockSpec((block, full), lambda i: (i, 0))
    operands = [mixed_full, w_out_full, tokens_full, gains]
    in_specs = [
        pl.BlockSpec((block, mixed_full.shape[1]), lambda i: (i, 0)),
        pl.BlockSpec(w_out_full.shape, lambda i: (0, 0), pipeline_mode=pl.Buffered(1)),
        line,
        pl.BlockSpec(gains.shape, lambda i: (0, 0)),
    ]
    out_specs = [line, line]
    shapes = [jax.ShapeDtypeStruct((span, full), F32), jax.ShapeDtypeStruct((span, full), BF)]
    scratch = []
    params = dict(vmem_limit_bytes=48 * MIB)
    if side is not None:
        tok, wide = side.shape
        operands.append(side)
        in_specs.append(ANY)
        out_specs.append(ANY)
        shapes.append(jax.ShapeDtypeStruct((2 * tok, 4 * wide), side.dtype))
        scratch += [pltpu.VMEM(side.shape, side.dtype)] + Gather.sems()
        params.update(collective_id=cid, has_side_effects=True)
    return pl.pallas_call(
        project_out_kernel,
        grid=(span // block,),
        in_specs=in_specs,
        out_specs=out_specs,
        out_shape=shapes,
        scratch_shapes=scratch,
        compiler_params=pltpu.CompilerParams(**params),
        cost_estimate=pl.CostEstimate(
            flops=2 * span * full * full, transcendentals=0, bytes_accessed=12 * span * full
        ),
        name="project_out",
    )(*operands)


def middle_kernel(
    cot_ref, resid_ref, low_ref, gain_ref, w_ref, mixed_ref,
    mixed_cot_ref, own_ref, grad_ref, gain_part_ref, total_ref,
):
    step = pl.program_id(0)
    last = pl.num_programs(0) - 1
    width = own_ref.shape[1]
    cot = cot_ref[...].astype(F32)
    resid = resid_ref[...]
    scale = lax.rsqrt(jnp.mean(resid * resid, axis=1, keepdims=True) + EPSILON)
    weighed = cot * gain_ref[1:2, :]
    inner = jnp.sum(weighed * resid, axis=1, keepdims=True)
    mid = low_ref[...].astype(F32) + weighed * scale - resid * (scale * scale * scale * inner / D)
    low = mid.astype(BF)
    mixed_cot_ref[...] = contract(low, w_ref[...], 1, 1).astype(BF)

    @pl.when(step == 0)
    def _():
        total_ref[...] = jnp.zeros_like(total_ref)
        gain_part_ref[...] = jnp.zeros_like(gain_part_ref)

    total_ref[...] += contract(mixed_ref[...], low, 0, 0)

    @pl.when(step <= last // 2)
    def _():
        own_ref[...] = mid[:, :width]
        part = jnp.sum((cot * resid * scale)[:, :width], axis=0, keepdims=True)
        gain_part_ref[...] += jnp.broadcast_to(part, gain_part_ref.shape)

    @pl.when(step == last)
    def _():
        grad_ref[...] = total_ref[...].astype(BF)


def middle(mlp_cot, resid_mid, out_low, gains, w_mine, mixed, width):
    span, full = resid_mid.shape
    heads_width = mixed.shape[1]
    block = 256
    steps = span // block
    line = pl.BlockSpec((block, full), lambda i: (i, 0))
    thin = pl.BlockSpec((block, heads_width), lambda i: (i, 0))
    return pl.pallas_call(
        middle_kernel,
        grid=(steps,),
        in_specs=[
            line, line, line,
            pl.BlockSpec(gains.shape, lambda i: (0, 0)),
            pl.BlockSpec(w_mine.shape, lambda i: (0, 0)),
            thin,
        ],
        out_specs=[
            thin,
            pl.BlockSpec((block, width), lambda i: (jnp.minimum(i, steps // 2 - 1), 0)),
            pl.BlockSpec((heads_width, full), lambda i: (0, 0)),
            pl.BlockSpec((8, width), lambda i: (0, 0)),
        ],
        out_shape=[
            jax.ShapeDtypeStruct((span, heads_width), BF),
            jax.ShapeDtypeStruct((span // 2, width), F32),
            jax.ShapeDtypeStruct((heads_width, full), BF),
            jax.ShapeDtypeStruct((8, width), F32),
        ],
        scratch_shapes=[pltpu.VMEM((heads_width, full), F32)],
        compiler_params=pltpu.CompilerParams(vmem_limit_bytes=48 * MIB),
        cost_estimate=pl.CostEstimate(
            flops=4 * span * full * heads_width, transcendentals=0, bytes_accessed=8 * span * full
        ),
        name="middle",
    )(mlp_cot, resid_mid, out_low, gains, w_mine, mixed)


def head_back_kernel(
    info_ref, qc_ref, kc_ref, vc_ref, wq_ref, wkv_ref, normed_ref, x_ref, gain_ref,
    part_ref, dot_ref, grad_ref, total_ref,
):
    step = pl.program_id(0)
    wide = qc_ref.shape[1]
    keyval = jnp.concatenate([kc_ref[...], vc_ref[...]], axis=1)
    counted = keyval * info_ref[2].astype(BF)
    part = contract(qc_ref[...], wq_ref[...], 1, 1) + contract(counted, wkv_ref[...], 1, 1)
    part_ref[...] = part.astype(BF)
    inner = jnp.sum(part * gain_ref[0:1, :] * x_ref[...].astype(F32), axis=1, keepdims=True)
    dot_ref[0] = jnp.broadcast_to(inner, (inner.shape[0], LANES)).T[0:1, :]

    @pl.when(step == 0)
    def _():
        total_ref[...] = jnp.zeros_like(total_ref)

    total_ref[:, :wide] += contract(normed_ref[...], qc_ref[...], 0, 0)
    total_ref[:, wide:] += contract(normed_ref[...], keyval, 0, 0)

    @pl.when(step == pl.num_programs(0) - 1)
    def _():
        used = wide + 2 * HD
        grad_ref[:, :used] = total_ref[...].astype(BF)
        grad_ref[:, used:] = jnp.zeros((grad_ref.shape[0], grad_ref.shape[1] - used), BF)


def head_back(info, query_cot, key_cot, value_cot, wq, wkv, normed, tokens_full, gains):
    span, full = normed.shape
    wide = query_cot.shape[1]
    block = 512
    steps = span // block
    line = lambda n: pl.BlockSpec((block, n), lambda i, info_ref: (i, 0))
    whole = lambda shape: pl.BlockSpec(shape, lambda i, info_ref: (0, 0))
    grad_width = max(CC, wide + 2 * HD)
    return pl.pallas_call(
        head_back_kernel,
        grid_spec=pltpu.PrefetchScalarGridSpec(
            num_scalar_prefetch=1,
            grid=(steps,),
            in_specs=[
                line(wide), line(HD), line(HD), whole(wq.shape), whole(wkv.shape), line(full), line(full),
                whole(gains.shape),
            ],
            out_specs=[
                line(full),
                pl.BlockSpec((1, 1, block), lambda i, info_ref: (i, 0, 0)),
                whole((full, grad_width)),
            ],
            scratch_shapes=[pltpu.VMEM((full, wide + 2 * HD), F32)],
        ),
        out_shape=[
            jax.ShapeDtypeStruct((span, full), BF),
            jax.ShapeDtypeStruct((steps, 1, block), F32),
            jax.ShapeDtypeStruct((full, grad_width), BF),
        ],
        compiler_params=pltpu.CompilerParams(vmem_limit_bytes=48 * MIB),
        cost_estimate=pl.CostEstimate(
            flops=4 * span * full * (wide + LANES), transcendentals=0, bytes_accessed=6 * span * full
        ),
        name="head_back",
    )(info, query_cot, key_cot, value_cot, wq, wkv, normed, tokens_full, gains)


def fill_units(out, pieces, part, sem):
    mine = lax.rem(lax.axis_index("dp"), 2)
    rows = out.shape[0] // 8
    copies = []
    for s in range(4):
        for which, piece in ((mine, pieces[0]), (1 - mine, pieces[1])):
            lines = pl.ds(pl.multiple_of(s * 2 * rows + which * rows, rows), rows)
            src = piece.at[pl.ds((2 * s + part) * rows, rows), :]
            copies.append(pltpu.make_async_copy(src, out.at[lines, :], sem.at[len(copies)]))
    return copies


def hidden_kernel(x_ref, *refs):
    pieces = refs[:2]
    gate_ref, up_ref, hidden_ref, w_gate, w_up, gate_sem, up_sem = refs[2:]

    @pl.when(pl.program_id(0) == 0)
    def _():
        copies = fill_units(w_gate, pieces, 0, gate_sem) + fill_units(w_up, pieces, 1, up_sem)
        for c in copies:
            c.start()
        for c in copies:
            c.wait()

    gate = contract(x_ref[...], w_gate[...], 1, 0)
    gate_ref[...] = gate
    up = contract(x_ref[...], w_up[...], 1, 0)
    up_ref[...] = up
    hidden_ref[...] = (gate * jax.nn.sigmoid(gate) * up).astype(BF)


def hidden_units(normed, pieces):
    span, full = normed.shape
    units = pieces[0].shape[1]
    block = 256
    thin = pl.BlockSpec((block, units), lambda i: (i, 0))
    return pl.pallas_call(
        hidden_kernel,
        grid=(span // block,),
        in_specs=[pl.BlockSpec((block, full), lambda i: (i, 0))] + [ANY] * 2,
        out_specs=[thin] * 3,
        out_shape=[
            jax.ShapeDtypeStruct((span, units), F32),
            jax.ShapeDtypeStruct((span, units), F32),
            jax.ShapeDtypeStruct((span, units), BF),
        ],
        scratch_shapes=[
            pltpu.VMEM((full, units), BF),
            pltpu.VMEM((full, units), BF),
            pltpu.SemaphoreType.DMA((8,)),
            pltpu.SemaphoreType.DMA((8,)),
        ],
        compiler_params=pltpu.CompilerParams(vmem_limit_bytes=48 * MIB),
        cost_estimate=pl.CostEstimate(
            flops=4 * span * full * units, transcendentals=span * units, bytes_accessed=6 * span * full
        ),
        name="hidden_units",
    )(normed, *pieces)


def hidden_back_kernel(low_ref, gate_ref, up_ref, hidden_ref, own_ref, *refs):
    pieces, down_pieces = refs[:2], refs[2:5]
    gate_cot_ref, up_cot_ref, part_ref, low_part_ref, w_gate, w_up, w_down, gate_sem, up_sem, down_sem = refs[5:]
    units = w_down.shape[0]
    width = w_down.shape[1] // 4

    @pl.when(pl.program_id(0) == 0)
    def _():
        mine = own_ref.at[pl.ds(pl.multiple_of(lax.axis_index("col") * units, units), units), :]
        copies = [
            pltpu.make_async_copy(p, w_down.at[:, pl.ds(s * width, width)], down_sem.at[s])
            for s, p in enumerate((mine, *down_pieces))
        ]
        copies += fill_units(w_gate, pieces, 0, gate_sem) + fill_units(w_up, pieces, 1, up_sem)
        for c in copies:
            c.start()
        for c in copies:
            c.wait()

    hidden_cot = contract(low_ref[...], w_down[...], 1, 1)
    gate = gate_ref[...]
    sig = jax.nn.sigmoid(gate)
    gate_cot = (hidden_cot * up_ref[...] * sig * (1.0 + gate * (1.0 - sig))).astype(BF)
    up_cot = (hidden_cot * gate * sig).astype(BF)
    gate_cot_ref[...] = gate_cot
    up_cot_ref[...] = up_cot
    part = contract(gate_cot, w_gate[...], 1, 1) + contract(up_cot, w_up[...], 1, 1)
    part_ref[...] = part.astype(BF)
    low_part_ref[...] = contract(hidden_ref[...], w_down[...], 1, 0).astype(BF)


def hidden_back(low, gate, up, hidden, w_down, pieces, down_pieces):
    span, full = low.shape
    units = gate.shape[1]
    block = 256
    thin = pl.BlockSpec((block, units), lambda i: (i, 0))
    line = pl.BlockSpec((block, full), lambda i: (i, 0))
    return pl.pallas_call(
        hidden_back_kernel,
        grid=(span // block,),
        in_specs=[line, thin, thin, thin] + [ANY] * 6,
        out_specs=[thin, thin, line, line],
        out_shape=[jax.ShapeDtypeStruct((span, units), BF)] * 2 + [jax.ShapeDtypeStruct((span, full), BF)] * 2,
        scratch_shapes=[
            pltpu.VMEM((full, units), BF),
            pltpu.VMEM((full, units), BF),
            pltpu.VMEM((units, full), BF),
            pltpu.SemaphoreType.DMA((8,)),
            pltpu.SemaphoreType.DMA((8,)),
            pltpu.SemaphoreType.DMA((4,)),
        ],
        compiler_params=pltpu.CompilerParams(vmem_limit_bytes=52 * MIB),
        cost_estimate=pl.CostEstimate(
            flops=8 * span * full * units, transcendentals=span * units, bytes_accessed=12 * span * full
        ),
        name="hidden_back",
    )(low, gate, up, hidden, w_down, *pieces, *down_pieces)


def on_device(
    tokens, lengths, attn_gain, w_query, w_key, w_value, w_out, mlp_gain, w_gate, w_up, w_down, cotangent
):
    row_devices = lax.axis_size("row")
    col_devices = lax.axis_size("col")
    row = lax.axis_index("row")
    col = lax.axis_index("col")
    fit = kernels_fit()
    tok, width = tokens.shape
    span = tok * row_devices
    group = HQ // KV
    heads_row = HQ // row_devices
    heads = heads_row // col_devices
    head_width = heads * HD
    keyval_row = KV // row_devices
    units = w_gate.shape[1] // col_devices
    length = lengths[0]
    shared_key = heads < group
    sharers = max(1, group // heads)
    leader = (col % sharers == 0).astype(jnp.int32)
    info = jnp.stack([length, row, leader]).astype(jnp.int32)

    keyval = []
    for owner in range(col_devices):
        first = owner * heads // group * HD
        keyval += [w_key[:, first : first + HD], w_value[:, first : first + HD]]
    keyval = jnp.concatenate(keyval, axis=1)
    gains = jnp.concatenate([attn_gain[None], mlp_gain[None], jnp.zeros((6, width), F32)], axis=0)

    if fit:
        tokens_full, wq, wkv, gains = first_gather(tokens, w_query, keyval, gains, 1)
    else:
        tokens_full = plain_gather(tokens)
        def slices(weight, size):
            return [lax.dynamic_slice_in_dim(weight, (col ^ s) * size, size, 1) for s in range(col_devices)]

        wq = jnp.concatenate(exchange(slices(w_query, head_width)), axis=0)
        wkv = jnp.concatenate(exchange(slices(keyval, LANES)), axis=0)
        gains = by_distance(lax.all_gather(gains, "col"), 1)
    w_gate, w_up, tokens_full = lax.optimization_barrier((w_gate, w_up, tokens_full))
    place = lax.rem(jnp.arange(span, dtype=jnp.int32) + row * tok, span)
    frequency = ROPE_BASE ** (-jnp.arange(HD // 2, dtype=F32) * (2.0 / HD))
    angle = place.astype(F32)[:, None] * frequency[None, :]
    cos = jnp.tile(jnp.cos(angle), (1, 2))
    sin = jnp.tile(jnp.sin(angle), (1, 2))

    normed_attn, query, key, value, scale_a = project_heads(tokens_full, gains, wq, wkv, cos, sin)
    valid = (row * tok + jnp.arange(tok, dtype=jnp.int32) < length).astype(BF)
    cot_low = cotangent * valid[:, None]
    def unit_pieces():
        rows = width // 2
        start = lax.rem(lax.axis_index("dp"), 2) * rows
        near = [
            jnp.concatenate(
                [lax.dynamic_slice(w, (start, (col ^ s) * units), (rows, units)) for w in (w_gate, w_up)], axis=0
            )
            for s in range(col_devices)
        ]
        return jnp.concatenate(exchange(near), axis=0)

    def unit_slices(weight, dim):
        return [lax.dynamic_slice_in_dim(weight, (col ^ s) * units, units, dim) for s in range(col_devices)]

    if fit:
        near_units = unit_pieces()
        mixed, mixed_wide, log_total, peak, w_out_full = attn_forward(info, query, key, value, w_out, 7)
        mixed, near_units = lax.optimization_barrier((mixed, near_units))
        pieces = [near_units, swap(near_units, "dp", 1)]
        mixed_full = gather_heads(mixed, 2)
        resid_mid, normed_mlp, out_low = project_out(mixed_full, w_out_full, tokens_full, gains, cot_low, 8)
        w_down, normed_mlp = lax.optimization_barrier((w_down, normed_mlp))
        down_pieces = [
            swap(lax.dynamic_slice_in_dim(w_down, (col ^ s) * units, units, 0), "col", s) for s in range(1, col_devices)
        ]
        gate, up, hidden = hidden_units(normed_mlp, pieces)
        hidden, peak = lax.optimization_barrier((hidden, peak))
        moved = [swap(peak, "dp", step) for step in (1, 2, 3)]
        gate_cot, up_cot, mlp_part, down_part = hidden_back(
            out_low, gate, up, hidden, w_down, pieces, down_pieces
        )
        mlp_part, moved = lax.optimization_barrier((mlp_part, moved))
        for other in moved:
            peak = jnp.maximum(peak, other)
    else:
        mixed, mixed_wide, log_total, peak = attn_forward(info, query, key, value)
        mixed_full = plain_gather_heads(mixed)
        w_out_full = plain_gather(w_out)
        resid_mid, normed_mlp = project_out(mixed_full, w_out_full, tokens_full, gains)
        out_low = plain_gather(cot_low)
        w_gate_units = jnp.concatenate(exchange(unit_slices(w_gate, 1)), axis=0)
        w_up_units = jnp.concatenate(exchange(unit_slices(w_up, 1)), axis=0)
        w_down_units = jnp.concatenate(exchange(unit_slices(w_down, 0)), axis=1)
        gate = jnp.dot(normed_mlp, w_gate_units, preferred_element_type=F32)
        up = jnp.dot(normed_mlp, w_up_units, preferred_element_type=F32)
        gate_sigmoid = jax.nn.sigmoid(gate)
        hidden = (gate * gate_sigmoid * up).astype(BF)
        hidden_cot = contract(out_low, w_down_units, 1, 1)
        gate_cot = (
            hidden_cot * up * gate_sigmoid * (1.0 + gate * (1.0 - gate_sigmoid))
        ).astype(BF)
        up_cot = (hidden_cot * gate * gate_sigmoid).astype(BF)
        mlp_part = (contract(gate_cot, w_gate_units, 1, 1) + contract(up_cot, w_up_units, 1, 1)).astype(BF)
        down_part = jnp.dot(hidden, w_down_units, preferred_element_type=F32).astype(BF)

    if fit:
        *sums, mid_cot, gain_m_part, attn_cot, down_sum, width_dot = backward(
            info, gains, normed_mlp, gate_cot, up_cot, hidden, mlp_part, down_part, resid_mid, out_low, w_out_full,
            mixed, query, key, value, mixed_wide, log_total, cos, sin, wq, wkv, normed_attn, tokens_full, 3,
        )
        width_dot = width_dot.reshape(tok)
    else:
        mlp_cot = plain_gather(plain_reduce(mlp_part).astype(BF))
        down_sum = plain_reduce(down_part)
        w_mine = lax.dynamic_slice_in_dim(w_out_full, col * head_width, head_width, 0)
        mixed_cot, mid_cot, grad_out, gain_m_part = middle(
            mlp_cot, resid_mid, out_low, gains, w_mine, mixed, width
        )
        query_cot, key_cot, value_cot = attn_backward(
            info, query, key, value, mixed_cot, mixed_wide, log_total, cos, sin, F32 if shared_key else BF
        )
        if shared_key:
            for bit in range(sharers.bit_length() - 1):
                key_cot = key_cot + swap(key_cot, "col", 1 << bit)
                value_cot = value_cot + swap(value_cot, "col", 1 << bit)
            key_cot, value_cot = key_cot.astype(BF), value_cot.astype(BF)
        attn_part, dot_part, grad_heads = head_back(
            info, query_cot, key_cot, value_cot, wq, wkv, normed_attn, tokens_full, gains
        )
        dot_part = dot_part.reshape(span)
        width_dot = lax.psum(dot_part[:tok] + swap(dot_part[tok:], "row", 1), "col")
        attn_cot = plain_reduce(attn_part)
        grad_gate = contract(normed_mlp, gate_cot, 0, 0).astype(BF)
        grad_up = contract(normed_mlp, up_cot, 0, 0).astype(BF)
        grad_down = contract(hidden, out_low, 0, 0).astype(BF)
        sums = plain_group_sum(
            [grad_gate, grad_up, grad_down, grad_out, grad_heads], ["columns", "columns", "rows", "rows", "stack"]
        )
    output = (resid_mid[:tok, :width] + down_sum).astype(BF)
    own_in = tokens.astype(F32)
    scale_own = scale_a[:tok, :1]
    input_grad = (
        mid_cot
        + attn_cot * attn_gain * scale_own
        - own_in * (scale_own * scale_own * scale_own * width_dot[:, None] / D)
    )
    gain_a_part = jnp.sum(attn_cot * own_in * scale_own, axis=0)

    out_gate, out_up, out_down, out_out, out_heads = [g.astype(F32) for g in sums]
    out_heads = out_heads.reshape(col_devices, width, out_heads.shape[1])
    out_query = jnp.concatenate([out_heads[i, :, :head_width] for i in range(col_devices)], axis=1)
    leaders = range(0, col_devices, sharers)
    out_key = jnp.concatenate([out_heads[i, :, head_width : head_width + HD] for i in leaders], axis=1)
    out_value = jnp.concatenate(
        [out_heads[i, :, head_width + HD : head_width + 2 * HD] for i in leaders], axis=1
    )

    gain_sums = jnp.stack([gain_a_part, gain_m_part[0]])
    if fit:
        grown, hops = [out_gate, out_up, out_down], [("row", 1), ("dp", 1), ("dp", 2)]
        for n, (axis, step) in enumerate(hops):
            other = swap(gain_sums, axis, step)
            other, grown[n] = lax.optimization_barrier((other, grown[n]))
            gain_sums = gain_sums + other
        out_gate, out_up, out_down = grown
        own_peaks = peak[:, 0]
        row_peaks = jnp.where(jnp.arange(col_devices)[:, None] == col, own_peaks[None, :], NEG_FILL)
        row_peaks = jnp.maximum(row_peaks, swap(row_peaks, "col", 1))
        row_peaks = jnp.maximum(row_peaks, swap(row_peaks, "col", 2))
    else:
        gain_sums = lax.psum(gain_sums, ("dp", "row"))
        own_peaks = lax.pmax(peak, "dp")[:, 0]
        row_peaks = lax.all_gather(own_peaks, "col")
    row_peaks = row_peaks.reshape(heads_row)
    clip_factor = CLIP_LEVEL / jnp.maximum(row_peaks, CLIP_LEVEL)
    query_scale = jnp.repeat(jnp.sqrt(clip_factor), HD)
    key_scale = jnp.repeat(jnp.sqrt(jnp.min(clip_factor.reshape(keyval_row, group), axis=1)), HD)
    clipped_query = (w_query.astype(F32) * query_scale[None, :]).astype(BF)
    clipped_key = (w_key.astype(F32) * key_scale[None, :]).astype(BF)
    return (
        output,
        input_grad,
        gain_sums[0],
        out_query,
        out_key,
        out_value,
        out_out,
        gain_sums[1],
        out_gate,
        out_up,
        out_down,
        own_peaks,
        clipped_query,
        clipped_key,
    )


def solution(mesh):
    in_specs = (
        P(("dp", "row"), "col"),
        P("dp"),
        P("col"),
        P("col", "row"),
        P("col", "row"),
        P("col", "row"),
        P("row", "col"),
        P("col"),
        P("col", "row"),
        P("col", "row"),
        P("row", "col"),
        P(("dp", "row"), "col"),
    )
    out_specs = (
        P(("dp", "row"), "col"),
        P(("dp", "row"), "col"),
        P("col"),
        P("col", "row"),
        P("col", "row"),
        P("col", "row"),
        P("row", "col"),
        P("col"),
        P("col", "row"),
        P("col", "row"),
        P("row", "col"),
        P(("row", "col")),
        P("col", "row"),
        P("col", "row"),
    )
    return jax.shard_map(
        on_device, mesh=mesh, in_specs=in_specs, out_specs=out_specs, check_vma=False
    )
```

```python
import functools

import jax
import jax.numpy as jnp
from jax import lax
from jax.experimental import pallas as pl
from jax.experimental.pallas import tpu as pltpu
from jax.sharding import PartitionSpec as P

D = 2048
HQ = 32
KV = 8
HD = 64
SEQ_LEN = 2048

EPSILON = 1e-05
NEG_FILL = -1e30
CLIP_LEVEL = 5.0
ROPE_BASE = 500000.0

BF = jnp.bfloat16
F32 = jnp.float32
LANES = 128
QB = 512
FWD_KB = 512
BWD_KB = 512
MESH = pl.DeviceIdType.MESH
ANY = pl.BlockSpec(memory_space=pl.ANY)
NCH = 4
CR, CC = 256, 512
HR = CR // 2
OFFS = (0, 2, 4, 7)
RING = 12
MIB = 2**20
VMEM_ALL = 63 * MIB


def contract(left, right, left_dim, right_dim):
    return lax.dot_general(
        left, right, (((left_dim,), (right_dim,)), ((), ())), preferred_element_type=F32
    )


def swap(values, axis, step):
    count = lax.axis_size(axis)
    return lax.ppermute(values, axis, [(i, i ^ step) for i in range(count)])


def flip(index, bit):
    return index + bit - 2 * bit * lax.rem(index // bit, 2)


def xor(index, step):
    return lax.rem(lax.rem(index, 2) + step % 2, 2) + 2 * lax.rem(index // 2 + step // 2, 2)


def remote(src, dst, send, recv, **where):
    return pltpu.make_async_remote_copy(
        src_ref=src, dst_ref=dst, send_sem=send, recv_sem=recv, device_id=where, device_id_type=MESH
    )


def done(ref, sem):
    pltpu.make_async_copy(ref, ref, sem).wait()


def greet(targets):
    barrier = pltpu.get_barrier_semaphore()
    for target in targets:
        pl.semaphore_signal(barrier, inc=1, device_id=target, device_id_type=MESH)
    pl.semaphore_wait(barrier, len(targets))


def plane_peers():
    row = lax.axis_index("row")
    col = lax.axis_index("col")
    return {"col": flip(col, 1)}, {"col": flip(col, 2)}, {"row": 1 - row}


def token_place(tok, width):
    rows = tok // NCH

    def place(ref, half, s, j, who):
        return ref.at[pl.ds(half * tok + j * rows, rows), pl.ds(s * width, width)]

    return place


def head_place(span, width):
    rows = span // NCH

    def place(ref, half, s, j, who):
        start = j * rows if half == 0 else ((j + NCH // 2) % NCH) * rows
        return ref.at[pl.ds(start, rows), pl.ds(pl.multiple_of((half * 4 + xor(who, s)) * width, LANES), width)]

    return place


class Gather:
    SEMS = 6

    def __init__(self, src, out, place, stage, sems):
        self.src, self.out, self.place, self.stage = src, out, place, stage
        self.own_send, self.relay_send, self.mate_send, self.recv, self.mate_recv, self.local = sems
        self.col = lax.axis_index("col")
        self.near = plane_peers()

    @staticmethod
    def sems():
        shapes = [(2, NCH), (NCH,), (4, NCH), (3, NCH), (4, NCH), (2,)]
        return [pltpu.SemaphoreType.DMA(s) for s in shapes]

    def chunk(self, j):
        rows = self.src.shape[0] // NCH
        return self.src.at[pl.ds(j * rows, rows), :]

    def here(self, half, s, j):
        return self.place(self.out, half, s, j, self.col)

    def own(self, axis, j):
        peer = self.near[axis]
        dst = self.place(self.out, 0, axis + 1, j, peer["col"])
        return remote(self.chunk(j), dst, self.own_send.at[axis, j], self.recv.at[axis, j], **peer)

    def relay(self, axis, j):
        peer = self.near[1 - axis]
        dst = self.place(self.out, 0, 3, j, peer["col"])
        return remote(self.here(0, axis + 1, j), dst, self.relay_send.at[j], self.recv.at[2, j], **peer)

    def mate(self, s, j):
        src = self.chunk(j) if s == 0 else self.here(0, s, j)
        dst = self.place(self.out, 1, s, j, self.col)
        return remote(src, dst, self.mate_send.at[s, j], self.mate_recv.at[s, j], **self.near[2])

    def load(self):
        return pltpu.make_async_copy(self.src, self.stage, self.local.at[0])

    def keep(self, j):
        rows = self.src.shape[0] // NCH
        whole = self.stage if self.stage is not None else self.src
        return pltpu.make_async_copy(whole.at[pl.ds(j * rows, rows), :], self.here(0, 0, j), self.local.at[1])

    def begin(self):
        half = NCH // 2
        if self.stage is not None:
            self.load().start()
        for i in range(NCH):
            self.own(0, i).start()
            self.own(1, (i + half) % NCH).start()
        for j in range(NCH):
            self.mate(0, j).start()

    def arrived(self, s, j):
        done(self.here(0, s, j), self.recv.at[s - 1, j])

    def first(self):
        half = NCH // 2
        for i in range(half):
            self.arrived(1, i)
            self.relay(0, i).start()
            self.mate(1, i).start()
            self.arrived(2, half + i)
            self.relay(1, half + i).start()
            self.mate(2, half + i).start()

    def second(self):
        half = NCH // 2
        if self.stage is not None:
            self.load().wait()
        for j in range(NCH):
            self.keep(j).start()
        for i in range(half):
            self.arrived(1, half + i)
            self.mate(1, half + i).start()
            self.arrived(2, i)
            self.mate(2, i).start()
        for i in range(half):
            for j in (i, half + i):
                self.arrived(3, j)
                self.mate(3, j).start()

    def finish(self):
        half = NCH // 2
        for s in range(4):
            for j in range(NCH):
                done(self.here(1, s, j), self.mate_recv.at[s, j])
                self.mate(s, j).wait_send()
        for j in range(NCH):
            self.own(0, j).wait_send()
            self.own(1, j).wait_send()
            self.relay(0 if j < half else 1, j).wait_send()
        whole = self.stage if self.stage is not None else self.src
        done(whole, self.local.at[1])


def gather_kernel(place_of, x_ref, out_ref, stage, *sems):
    near_x, near_y, mate = plane_peers()
    greet([near_x, near_y, mate])
    gather = Gather(x_ref, out_ref, place_of(*x_ref.shape), stage, sems)
    gather.begin()
    gather.first()
    gather.second()
    gather.finish()


def gather_call(x, shape, place_of, cid, name):
    return pl.pallas_call(
        functools.partial(gather_kernel, place_of),
        in_specs=[ANY],
        out_specs=ANY,
        out_shape=jax.ShapeDtypeStruct(shape, x.dtype),
        scratch_shapes=[pltpu.VMEM(x.shape, x.dtype)] + Gather.sems(),
        compiler_params=pltpu.CompilerParams(collective_id=cid, has_side_effects=True),
        name=name,
    )(x)


def gather_tokens(x, cid):
    tok, width = x.shape
    return gather_call(x, (2 * tok, 4 * width), token_place, cid, "gather_tokens")


def gather_heads(x, cid):
    span, width = x.shape
    return gather_call(x, (span, 8 * width), head_place, cid, "gather_heads")


class Reduce:
    def __init__(self, part, scratch, sems):
        self.part = part
        self.own, self.given, self.sent, self.got_one, self.got_two = scratch
        self.loads, self.mate_send, self.mate_recv, self.one_send, self.one_recv, self.two_send, self.two_recv = sems
        self.near = plane_peers()
        self.h = self.own.shape[0] // 2
        self.width = self.own.shape[1] // 4

    @staticmethod
    def scratch(tok, full):
        h, w = tok // 2, full // 4
        shapes = [(tok, full), (tok, full), (2, 3, h, w), (2, 2, h, w), (2, h, w)]
        return [pltpu.VMEM(s, BF) for s in shapes]

    @staticmethod
    def sems():
        return [pltpu.SemaphoreType.DMA((2,))] * 7

    def lines(self, a):
        return pl.ds(a * self.h, self.h)

    def give(self, a):
        src = self.part.at[pl.ds((2 + a) * self.h, self.h), :]
        return remote(src, self.given.at[self.lines(a), :], self.mate_send.at[a], self.mate_recv.at[a], **self.near[2])

    def load(self, a):
        return pltpu.make_async_copy(self.part.at[self.lines(a), :], self.own.at[self.lines(a), :], self.loads.at[a])

    def one(self, a):
        src = self.sent.at[a, pl.ds(0, 2)]
        return remote(src, self.got_one.at[a], self.one_send.at[a], self.one_recv.at[a], **self.near[a])

    def two(self, a):
        return remote(self.sent.at[a, 2], self.got_two.at[a], self.two_send.at[a], self.two_recv.at[a], **self.near[1 - a])

    def pair(self, a, s):
        cols = pl.ds(s * self.width, self.width)
        rows = self.lines(a)
        return self.own[rows, cols].astype(F32) + self.given[rows, cols].astype(F32)

    def begin(self):
        for a in range(2):
            self.give(a).start()
            self.load(a).start()

    def first(self, a):
        self.load(a).wait()
        done(self.given.at[self.lines(a), :], self.mate_recv.at[a])
        for i, s in enumerate((a + 1, 3)):
            self.sent[a, i] = self.pair(a, s).astype(BF)
        self.one(a).start()

    def second(self, a):
        done(self.got_one.at[a], self.one_recv.at[a])
        self.sent[a, 2] = (self.pair(a, 2 - a) + self.got_one[a, 1].astype(F32)).astype(BF)
        self.two(a).start()

    def total(self, a):
        done(self.got_two.at[a], self.two_recv.at[a])
        return self.pair(a, 0) + self.got_one[a, 0].astype(F32) + self.got_two[a].astype(F32)

    def finish(self):
        for a in range(2):
            self.give(a).wait_send()
            self.one(a).wait_send()
            self.two(a).wait_send()


def first_gather_kernel(
    x_ref, wq_ref, wkv_ref, gain_ref, out_ref, wq_out, wkv_out, gain_out,
    stage, wq_stage, wkv_stage, gain_stage, stage_sem, small_send, small_recv, *sems,
):
    near_x, near_y, mate = plane_peers()
    col = lax.axis_index("col")
    tok, width = x_ref.shape
    wide = wq_ref.shape[1] // 4
    thin = wkv_ref.shape[1] // 4

    def share(ref, owner, size):
        return ref.at[:, pl.ds(pl.multiple_of(owner * size, LANES), size)]

    loads = [
        pltpu.make_async_copy(share(wq_ref, col, wide), wq_stage, stage_sem.at[0]),
        pltpu.make_async_copy(share(wkv_ref, col, thin), wkv_stage, stage_sem.at[1]),
        pltpu.make_async_copy(gain_ref, gain_stage, stage_sem.at[2]),
    ]
    for c in loads:
        c.start()
    greet([near_x, near_y, {"col": 3 - col}, mate])
    smalls = []
    for s, peer in ((1, near_x), (2, near_y), (3, {"col": 3 - col})):
        owner = peer["col"]
        lines = pl.ds(s * width, width)
        smalls += [
            remote(share(wq_ref, owner, wide), wq_out.at[lines, :], small_send.at[0, s], small_recv.at[0, s], **peer),
            remote(share(wkv_ref, owner, thin), wkv_out.at[lines, :], small_send.at[1, s], small_recv.at[1, s], **peer),
            remote(gain_ref, gain_out.at[:, lines], small_send.at[2, s], small_recv.at[2, s], **peer),
        ]
    gather = Gather(x_ref, out_ref, token_place(tok, width), stage, sems)
    gather.begin()
    for c in smalls:
        c.start()
    lines = pl.ds(0, width)
    keeps = [
        pltpu.make_async_copy(wq_stage, wq_out.at[lines, :], stage_sem.at[3]),
        pltpu.make_async_copy(wkv_stage, wkv_out.at[lines, :], stage_sem.at[4]),
        pltpu.make_async_copy(gain_stage, gain_out.at[:, lines], stage_sem.at[5]),
    ]
    for load, keep in zip(loads, keeps):
        load.wait()
        keep.start()
    gather.first()
    gather.second()
    gather.finish()
    for c in smalls:
        c.wait()
    for c in keeps:
        c.wait()


def first_gather(x, wq, wkv, gains, cid):
    tok, width = x.shape
    wide, thin = wq.shape[1] // 4, wkv.shape[1] // 4
    return pl.pallas_call(
        first_gather_kernel,
        in_specs=[ANY] * 4,
        out_specs=[ANY] * 4,
        out_shape=[
            jax.ShapeDtypeStruct((2 * tok, 4 * width), BF),
            jax.ShapeDtypeStruct((4 * width, wide), BF),
            jax.ShapeDtypeStruct((4 * width, thin), BF),
            jax.ShapeDtypeStruct((8, 4 * width), F32),
        ],
        scratch_shapes=[
            pltpu.VMEM((tok, width), BF),
            pltpu.VMEM((width, wide), BF),
            pltpu.VMEM((width, thin), BF),
            pltpu.VMEM((8, width), F32),
            pltpu.SemaphoreType.DMA((6,)),
            pltpu.SemaphoreType.DMA((3, 4)),
            pltpu.SemaphoreType.DMA((3, 4)),
        ]
        + Gather.sems(),
        compiler_params=pltpu.CompilerParams(collective_id=cid, has_side_effects=True),
        name="first_gather",
    )(x, wq, wkv, gains)


def grad_plan(kind, shape):
    rows, cols = shape
    if kind == "columns":
        w = rows // 4
        high, n = rows // CR, w // CR
        return (
            high * (cols // CC), high,
            lambda i: lax.rem(i, high) // n, lambda i: lax.rem(i, high), lambda i: i // high,
            (w, 4 * cols), lambda c, i: (lax.rem(i, n) * CR, c * cols + i // high * CC),
        )
    high = rows // CR
    if kind == "rows":
        return (
            4 * high, high,
            lambda i: i // high, lambda i: lax.rem(i, high), lambda i: i // high,
            (4 * rows, cols // 4), lambda c, i: (c * rows + lax.rem(i, high) * CR, 0),
        )
    n = high // 4
    return (
        high, high,
        lambda i: i // n, lambda i: i, lambda i: 0,
        (rows, cols), lambda c, i: ((c * n + lax.rem(i, n)) * CR, 0),
    )


class GroupSum:
    def __init__(self, kinds, lefts, rights, outs, refs):
        (self.left, self.right, self.left_sem, self.right_sem, self.own, self.land, self.mids, self.tops, self.in_send, self.in_recv, self.mid_send,
         self.mid_recv, self.top_send, self.top_recv, self.out_send, self.out_recv, self.far_send, self.far_recv) = refs
        self.lefts, self.rights, self.outs = lefts, rights, outs
        self.plans = [grad_plan(k, (a.shape[1], b.shape[1])) for k, a, b in zip(kinds, lefts, rights)]
        self.counts = [p[0] for p in self.plans]
        self.begins = [sum(self.counts[:i]) for i in range(len(lefts))]
        groups = [p[0] // p[1] for p in self.plans]
        self.groups = [sum(groups[:i]) for i in range(len(lefts))]
        self.total = sum(self.counts)
        z = lax.axis_index("dp")
        self.col = lax.axis_index("col")
        self.is_mid = (z == 1) | (z == 2)
        self.is_end = jnp.logical_not(self.is_mid)
        left = z < 2
        self.inward = {"dp": jnp.where(left, z + 1, z - 1)}
        self.outward = {"dp": jnp.where(left, z - 1, z + 1)}
        self.kept = jnp.where(left, 0, 1)

    @staticmethod
    def scratch(kinds, span):
        dma = pltpu.SemaphoreType.DMA
        return (
            [pltpu.VMEM((2, span, CR), BF), pltpu.VMEM((2, span, CC), BF), dma((2,)), dma((2,))]
            + [pltpu.VMEM((RING, CR, CC), BF)] * 2
            + [pltpu.VMEM((RING, HR, CC), BF)] * 2
            + [dma((RING,))] * 6
            + [dma((RING, 2))] * 3
            + [dma((len(kinds),))]
        )

    def greet(self, others):
        barrier = pltpu.get_barrier_semaphore()
        targets = [self.inward] + others
        for target in targets:
            pl.semaphore_signal(barrier, inc=1, device_id=target, device_id_type=MESH)

        @pl.when(self.is_mid)
        def _():
            pl.semaphore_signal(barrier, inc=1, device_id=self.outward, device_id_type=MESH)
            pl.semaphore_wait(barrier, len(targets) + 1)

        @pl.when(self.is_end)
        def _():
            pl.semaphore_wait(barrier, len(targets))

    def rows(self, half):
        return pl.ds(pl.multiple_of(half * HR, HR), HR)

    def each(self, j, action):
        for m, count in enumerate(self.counts):

            @pl.when((j >= self.begins[m]) & (j < self.begins[m] + count))
            def _(m=m):
                action(m, j - self.begins[m])

    def left_load(self, m, i, j):
        lines = pl.ds(pl.multiple_of(self.plans[m][3](i) * CR, CR), CR)
        slot = lax.rem(j, 2)
        return pltpu.make_async_copy(self.lefts[m].at[:, lines], self.left.at[slot], self.left_sem.at[slot])

    def right_slot(self, m, i):
        return lax.rem(self.groups[m] + i // self.plans[m][1], 2)

    def right_load(self, m, i):
        lines = pl.ds(pl.multiple_of(self.plans[m][4](i) * CC, CC), CC)
        slot = self.right_slot(m, i)
        return pltpu.make_async_copy(self.rights[m].at[:, lines], self.right.at[slot], self.right_sem.at[slot])

    def fetch(self, j):
        def action(m, i):
            self.left_load(m, i, j).start()
            if self.resident[m] is None:

                @pl.when(lax.rem(i, self.plans[m][1]) == 0)
                def _():
                    self.right_load(m, i).start()

        self.each(j, action)

    def produce(self, j):
        slot = lax.rem(j, RING)

        def action(m, i):
            self.left_load(m, i, j).wait()
            if self.resident[m] is None:

                @pl.when(lax.rem(i, self.plans[m][1]) == 0)
                def _():
                    self.right_load(m, i).wait()

                right = self.right[self.right_slot(m, i)]
            else:
                right = self.resident[m][...]
            self.own[slot] = contract(self.left[lax.rem(j, 2)], right, 0, 0).astype(BF)

        self.each(j, action)

    def spread(self, j, half, src):
        slot = lax.rem(j, RING)

        def action(m, i):
            s = self.plans[m][2](i)
            r, q = self.plans[m][6](self.col, i)
            dst = self.outs[m].at[
                pl.ds(pl.multiple_of(r + half * HR, HR), HR), pl.ds(pl.multiple_of(q, CC), CC)
            ]

            @pl.when(s == 0)
            def _():
                pltpu.make_async_copy(src, dst, self.far_send.at[slot, half]).start()

            @pl.when(s > 0)
            def _():
                owner = lax.rem(lax.rem(self.col, 2) + lax.rem(s, 2), 2) + 2 * lax.rem(self.col // 2 + s // 2, 2)
                remote(src, dst, self.far_send.at[slot, half], self.far_recv.at[m], col=owner).start()

        self.each(j, action)

    def reclaim(self, j):
        slot = lax.rem(j, RING)
        for half in range(2):
            done(self.mids.at[slot], self.far_send.at[slot, half])

        @pl.when(self.is_mid)
        def _():
            done(self.mids.at[slot], self.mid_send.at[slot])
            done(self.mids.at[slot], self.top_send.at[slot])
            for half in range(2):
                done(self.mids.at[slot], self.out_send.at[slot, half])

        @pl.when(self.is_end)
        def _():
            done(self.own.at[slot], self.in_send.at[slot])

    def inbound(self, j):
        slot = lax.rem(j, RING)

        @pl.when(self.is_mid)
        def _():
            done(self.land.at[slot], self.in_recv.at[slot])
            self.own[slot] = (self.own[slot].astype(F32) + self.land[slot].astype(F32)).astype(BF)
            src = self.own.at[slot, self.rows(1 - self.kept)]
            remote(src, self.mids.at[slot], self.mid_send.at[slot], self.mid_recv.at[slot], **self.inward).start()

        @pl.when(self.is_end)
        def _():
            remote(
                self.own.at[slot], self.land.at[slot], self.in_send.at[slot], self.in_recv.at[slot], **self.inward
            ).start()

    def middle(self, j):
        slot = lax.rem(j, RING)

        @pl.when(self.is_mid)
        def _():
            done(self.mids.at[slot], self.mid_recv.at[slot])
            rows = self.rows(self.kept)
            self.own[slot, rows] = (self.own[slot, rows].astype(F32) + self.mids[slot].astype(F32)).astype(BF)
            src = self.own.at[slot, rows]
            remote(src, self.tops.at[slot], self.top_send.at[slot], self.top_recv.at[slot], **self.inward).start()
            remote(
                src, self.land.at[slot, rows], self.out_send.at[slot, self.kept], self.out_recv.at[slot, self.kept],
                **self.outward,
            ).start()
            self.spread(j, self.kept, src)

    def settle(self, j):
        slot = lax.rem(j, RING)

        @pl.when(self.is_mid)
        def _():
            done(self.tops.at[slot], self.top_recv.at[slot])
            half = 1 - self.kept
            src = self.tops.at[slot]
            remote(
                src, self.land.at[slot, self.rows(half)], self.out_send.at[slot, half], self.out_recv.at[slot, half],
                **self.outward,
            ).start()
            self.spread(j, half, src)

    def outbound(self, j):
        slot = lax.rem(j, RING)

        @pl.when(self.is_end)
        def _():
            for half in range(2):
                src = self.land.at[slot, pl.ds(half * HR, HR)]
                done(src, self.out_recv.at[slot, half])
                self.spread(j, half, src)

    def begin(self):
        self.fetch(jnp.int32(0))
        self.produce(jnp.int32(0))
        self.fetch(jnp.int32(1))

    def tick(self, t):
        for off, stage in zip(OFFS, (self.inbound, self.middle, self.settle, self.outbound)):

            @pl.when((t >= off) & (t < self.total + off))
            def _(off=off, stage=stage):
                stage(t - off)

        ahead = t + 1

        @pl.when(ahead < self.total)
        def _():
            @pl.when(ahead >= RING)
            def _():
                self.reclaim(ahead - RING)

            self.produce(ahead)

            @pl.when(ahead + 1 < self.total)
            def _():
                self.fetch(ahead + 1)

    def finish(self):
        def drain(j, carry):
            self.reclaim(j)
            return carry

        lax.fori_loop(self.total - RING, self.total, drain, 0)
        for m, out in enumerate(self.outs):
            done(out.at[pl.ds(0, 3 * out.shape[0] // 4)], self.far_recv.at[m])


MB = 128
AQ, AK = 256, 512


def backward_kernel(
    kinds,
    info_ref, gain_ref, mlp_ref, gate_ref, up_ref, hidden_ref, part_ref, low_part_ref, resid_ref, low_ref, w_ref, mixed_ref,
    wide_ref, normed_ref, x_ref, q_ref, k_ref, v_ref, lse_ref, turn_ref, wq_ref, wkv_ref,
    out_gate, out_up, out_down, out_out, out_heads, mid_out, gain_part, attn_out, down_out, dot_out,
    cot_full, attn_part, mid_low,
    *refs,
):
    refs = list(refs)

    def take(count):
        taken = refs[:count]
        del refs[:count]
        return taken

    zsum = GroupSum(
        kinds,
        [hidden_ref, mlp_ref, mlp_ref, mixed_ref, normed_ref],
        [low_ref, gate_ref, up_ref, mid_low, refs[0]],
        [out_down, out_gate, out_up, out_out, out_heads],
        refs[1:19],
    )
    heads_cot = refs[0]
    zsum.resident = [None, None, None, None, heads_cot]
    del refs[:19]
    scratch = take(5)
    mlp_reduce = Reduce(part_ref, scratch, take(7))
    low_reduce = Reduce(low_part_ref, scratch, take(7))
    attn_reduce = Reduce(attn_part, scratch, take(7))
    mine, = take(1)
    tok, width = mine.shape
    gather = Gather(mine, cot_full, token_place(tok, width), None, take(Gather.SEMS))
    bufs, resid_buf, out_buf, buf_sem, out_sem = take(5)
    mixed_cot, wide_buf, dq_sum, dk_sum, dv_sum, dots, dots_mate, dots_col = take(8)
    dot_send, dot_recv, ready, w_mine, w_sem = take(5)
    span = 2 * tok
    heads_width = q_ref.shape[1]
    heads = heads_width // HD
    half = lax.axis_index("row")
    col = lax.axis_index("col")
    length = info_ref[0]
    near_x, near_y, mate = plane_peers()
    corner = {"col": 3 - col}
    blocks = span // MB

    def mid_loads(i):
        slot = lax.rem(i, 2)
        lines = pl.ds(pl.multiple_of(i * MB, MB), MB)
        return [
            pltpu.make_async_copy(cot_full.at[lines, :], bufs.at[slot, 0], buf_sem.at[slot, 0]),
            pltpu.make_async_copy(low_ref.at[lines, :], bufs.at[slot, 1], buf_sem.at[slot, 1]),
            pltpu.make_async_copy(resid_ref.at[lines, :], resid_buf.at[slot], buf_sem.at[slot, 2]),
        ]

    def row_store(out, i):
        lines = pl.ds(pl.multiple_of(i * MB, MB), MB)
        return pltpu.make_async_copy(bufs.at[lax.rem(i, 2), 2], out.at[lines, :], out_sem.at[1])

    def mid_store(i):
        lines = pl.ds(pl.multiple_of(i * MB, MB), MB)
        return pltpu.make_async_copy(out_buf.at[:, pl.ds(0, width)], mid_out.at[lines, :], out_sem.at[0])

    def mid_item(i):
        slot = lax.rem(i, 2)

        @pl.when(i + 1 < blocks)
        def _():
            for c in mid_loads(i + 1):
                c.start()

        for c in mid_loads(i):
            c.wait()
        cot = bufs[slot, 0].astype(F32)
        resid = resid_buf[slot]
        scale = lax.rsqrt(jnp.mean(resid * resid, axis=1, keepdims=True) + EPSILON)
        weighed = cot * gain_ref[1:2, :]
        inner = jnp.sum(weighed * resid, axis=1, keepdims=True)
        mid = bufs[slot, 1].astype(F32) + weighed * scale - resid * (scale * scale * scale * inner / D)
        low = mid.astype(BF)
        lines = pl.ds(pl.multiple_of(i * MB, MB), MB)
        mixed_cot[lines, :] = contract(low, w_mine[...], 1, 1).astype(BF)

        @pl.when(i > 0)
        def _():
            row_store(mid_low, i - 1).wait()

        bufs[slot, 2] = low
        row_store(mid_low, i).start()

        @pl.when(i < blocks // 2)
        def _():
            @pl.when(i > 0)
            def _():
                mid_store(i - 1).wait()

            out_buf[:, pl.ds(0, width)] = mid[:, :width]
            mid_store(i).start()
            part = jnp.sum((cot * resid * scale)[:, :width], axis=0, keepdims=True)
            gain_part[...] += jnp.broadcast_to(part, gain_part.shape)

        @pl.when(i == blocks // 2)
        def _():
            mid_store(i - 1).wait()

    q_steps = span // AQ
    rows = heads * AQ
    pieces = [slice(h * HD, (h + 1) * HD) for h in range(heads)]

    def attn_item(q_step, tile, diagonal):
        stored = lax.rem(q_step + half * (q_steps // 2), q_steps)
        lines = pl.ds(pl.multiple_of(stored * AQ, AQ), AQ)
        key_tiles = span // AK
        keys = pl.ds(pl.multiple_of(lax.rem(tile + half * (key_tiles // 2), key_tiles) * AK, AK), AK)
        first = q_step * AQ
        q = jnp.concatenate([q_ref[lines, s] for s in pieces], axis=0)
        cot = jnp.concatenate([mixed_cot[lines, s] for s in pieces], axis=0)
        wide = jnp.concatenate([wide_buf[:, s] for s in pieces], axis=0)
        place = first + lax.rem(lax.broadcasted_iota(jnp.int32, (1, rows), 1), AQ)
        log_total = jnp.where(place < length, lse_ref[q_step], -NEG_FILL)
        inner = jnp.sum(wide * cot.astype(F32), axis=1, keepdims=True)
        inner = jnp.broadcast_to(inner, (rows, LANES)).T[0:1, :]
        k_tile = k_ref[keys, :]
        v_tile = v_ref[keys, :]
        scores = contract(k_tile, q, 1, 1) * HD**-0.5 - log_total
        if diagonal:
            key_place = tile * AK + lax.broadcasted_iota(jnp.int32, (AK, rows), 0)
            scores = jnp.where(key_place <= place, scores, NEG_FILL)
        weights = jnp.exp(scores)
        prob_cot = contract(v_tile, cot, 1, 1)
        score_cot = (weights * (prob_cot - inner)).astype(BF)
        dv_sum[keys, :] += contract(weights.astype(BF), cot, 1, 0)
        dk_sum[keys, :] += contract(score_cot, q, 1, 0) * HD**-0.5
        dq = contract(score_cot, k_tile, 0, 0) * HD**-0.5

        @pl.when(tile == 0)
        def _():
            dq_sum[...] = dq

        @pl.when(tile > 0)
        def _():
            dq_sum[...] += dq

        if diagonal:
            cos, sin = turn_ref[lines, :HD], turn_ref[lines, HD:]
            for h in range(heads):
                part = dq_sum[h * AQ : (h + 1) * AQ, :]
                swapped = jnp.concatenate([part[:, HD // 2 :], -part[:, : HD // 2]], axis=1)
                heads_cot[lines, h * HD : (h + 1) * HD] = (part * cos + swapped * sin).astype(BF)

    starts = [0]
    for n in range(q_steps):
        starts.append(starts[-1] + n * AQ // AK + 1)
    attn_items = starts.pop()

    def wide_load(q_step):
        stored = lax.rem(q_step + half * (q_steps // 2), q_steps)
        lines = pl.ds(pl.multiple_of(stored * AQ, AQ), AQ)
        return pltpu.make_async_copy(wide_ref.at[lines, :], wide_buf, w_sem.at[1])

    def attn_one(n):
        q_step = sum([jnp.where(n >= start, 1, 0) for start in starts[1:]], jnp.int32(0))
        tile = n - sum([jnp.where(n >= b, b - a, 0) for a, b in zip(starts, starts[1:])], jnp.int32(0))
        last = q_step * AQ // AK

        @pl.when(tile == 0)
        def _():
            wide_load(q_step).wait()

        @pl.when(tile < last)
        def _():
            attn_item(q_step, tile, False)

        @pl.when(tile == last)
        def _():
            attn_item(q_step, tile, True)

            @pl.when(q_step + 1 < q_steps)
            def _():
                wide_load(q_step + 1).start()

    def attn_finish():
        part = dk_sum[...]
        swapped = jnp.concatenate([part[:, HD // 2 :], -part[:, : HD // 2]], axis=1)
        heads_cot[:, heads_width : heads_width + HD] = (part * turn_ref[:, :HD] + swapped * turn_ref[:, HD:]).astype(BF)
        heads_cot[:, heads_width + HD : heads_width + 2 * HD] = dv_sum[...].astype(BF)

    def head_load(i):
        slot = lax.rem(i, 2)
        lines = pl.ds(pl.multiple_of(i * MB, MB), MB)
        return pltpu.make_async_copy(x_ref.at[lines, :], bufs.at[slot, 1], buf_sem.at[slot, 1])

    def head_item(i):
        slot = lax.rem(i, 2)

        @pl.when(i + 1 < blocks)
        def _():
            head_load(i + 1).start()

        head_load(i).wait()
        lines = pl.ds(pl.multiple_of(i * MB, MB), MB)
        part = contract(heads_cot[lines, :heads_width], wq_ref[...], 1, 1)
        part += contract(heads_cot[lines, heads_width : heads_width + 2 * HD], wkv_ref[...], 1, 1)

        @pl.when(i > 0)
        def _():
            row_store(attn_part, i - 1).wait()

        bufs[slot, 2] = part.astype(BF)
        row_store(attn_part, i).start()
        inner = jnp.sum(part * gain_ref[0:1, :] * bufs[slot, 1].astype(F32), axis=1, keepdims=True)
        dots[pl.ds(i, 1), :] = jnp.broadcast_to(inner, (MB, LANES)).T[0:1, :]

    def dot_give():
        n = blocks // 2
        return remote(dots.at[pl.ds(n, n), :], dots_mate, dot_send.at[0], dot_recv.at[0], **mate)

    def dot_share():
        n = blocks // 2
        return [
            remote(dots.at[pl.ds(0, n), :], dots_col.at[s], dot_send.at[1 + s], dot_recv.at[1 + s], **peer)
            for s, peer in enumerate((near_x, near_y, corner))
        ]

    def emit(work, out, sem):
        for a in range(2):
            sum_total = work.total(a)
            h = tok // 4
            for b in range(2):
                lines = pl.ds(a * 2 * h + b * h, h)
                resid_sum = sum_total[b * h : (b + 1) * h]
                emit_buf[...] = resid_sum
                c = pltpu.make_async_copy(emit_buf, out.at[lines, :], sem)
                c.start()
                c.wait()

    emit_buf, = take(1)

    pltpu.make_async_copy(w_ref.at[pl.ds(pl.multiple_of(col * heads_width, heads_width), heads_width), :], w_mine, w_sem.at[0]).start()
    gain_part[...] = jnp.zeros_like(gain_part)
    heads_cot[:, heads_width + 2 * HD :] = jnp.zeros((span, CC - heads_width - 2 * HD), BF)
    zsum.begin()
    dk_sum[...] = jnp.zeros_like(dk_sum)
    dv_sum[...] = jnp.zeros_like(dv_sum)
    zsum.greet([near_x, near_y, corner, mate])

    at = {}

    def plan(tick, action):
        at.setdefault(tick, []).append(action)

    def start_all(copies):
        for c in copies:
            c.start()

    plan(0, mlp_reduce.begin)
    plan(T_ONE, lambda: [mlp_reduce.first(a) for a in range(2)])
    plan(T_TWO, lambda: [mlp_reduce.second(a) for a in range(2)])

    def own_block():
        for a in range(2):
            mine[mlp_reduce.lines(a), :] = mlp_reduce.total(a).astype(BF)
        gather.begin()

    plan(T_SUM, own_block)
    plan(T_GATHER, gather.first)
    plan(T_GATHER + 3, gather.second)

    def start_mid():
        gather.finish()
        mlp_reduce.finish()
        pltpu.make_async_copy(w_ref.at[pl.ds(0, heads_width), :], w_mine, w_sem.at[0]).wait()
        start_all(mid_loads(jnp.int32(0)))
        low_reduce.begin()

    plan(T_MID, start_mid)
    plan(T_MID + 4, lambda: [low_reduce.first(a) for a in range(2)])
    plan(T_MID + 9, lambda: [low_reduce.second(a) for a in range(2)])

    def low_done():
        emit(low_reduce, down_out, out_sem.at[2])
        low_reduce.finish()
        for i, peer in enumerate((near_x, near_y, mate)):
            pl.semaphore_signal(ready.at[i], inc=1, device_id=peer, device_id_type=MESH)

    plan(T_MID + 13, low_done)
    t_attn = T_MID + 1 + blocks // N_MID
    plan(t_attn, lambda: (row_store(mid_low, blocks - 1).wait(), wide_load(jnp.int32(0)).start()))
    t_head = t_attn + 1 + attn_items // N_ATTN
    plan(t_head, lambda: (attn_finish(), head_load(jnp.int32(0)).start()))
    t_last = t_head + 1 + blocks // N_HEAD

    def start_last():
        row_store(attn_part, blocks - 1).wait()
        dot_give().start()
        for i in range(3):
            pl.semaphore_wait(ready.at[i], 1)
        attn_reduce.begin()

    plan(t_last, start_last)

    def last_first():
        n = blocks // 2
        done(dots_mate, dot_recv.at[0])
        dot_give().wait_send()
        dots[pl.ds(0, n), :] = dots[pl.ds(0, n), :] + dots_mate[...]
        start_all(dot_share())
        for a in range(2):
            attn_reduce.first(a)

    plan(t_last + 3, last_first)
    plan(t_last + 7, lambda: [attn_reduce.second(a) for a in range(2)])

    def last_done():
        n = blocks // 2
        shares = dot_share()
        for c in shares:
            c.wait()
        terms = [dots[pl.ds(0, n), :], dots_col[0], dots_col[1], dots_col[2]]
        dot_out[...] = (terms[0] + terms[1]) + (terms[2] + terms[3])
        emit(attn_reduce, attn_out, out_sem.at[2])
        attn_reduce.finish()

    plan(t_last + 10, last_done)
    final = max(zsum.total + OFFS[3], t_last + 11)

    def tick(t, carry):
        zsum.tick(t)
        for when in sorted(at):

            @pl.when(t == when)
            def _(when=when):
                for action in at[when]:
                    action()

        @pl.when((t > T_MID) & (t < t_attn))
        def _():
            for e in range(N_MID):
                mid_item((t - T_MID - 1) * N_MID + e)

        @pl.when((t > t_attn) & (t < t_head))
        def _():
            def body(e, carry):
                attn_one((t - t_attn - 1) * N_ATTN + e)
                return carry

            lax.fori_loop(0, N_ATTN, body, 0)

        @pl.when((t > t_head) & (t < t_last))
        def _():
            for e in range(N_HEAD):
                head_item((t - t_head - 1) * N_HEAD + e)

        return carry

    lax.fori_loop(0, final, tick, 0)
    zsum.finish()


T_ONE, T_TWO, T_SUM, T_GATHER, T_MID = 2, 7, 10, 12, 19
N_MID, N_ATTN, N_HEAD = 2, 2, 4


def backward(info, gains, normed_mlp, gate_cot, up_cot, hidden, mlp_part, low_part, resid, low, w_out_full, mixed, q, k, v, wide, lse, cos, sin,
             wq, wkv, normed, tokens_full, cid):
    span, full = normed.shape
    tok, width = span // 2, full // 4
    heads_width = mixed.shape[1]
    heads = heads_width // HD
    units = hidden.shape[1]
    kinds = ["rows", "columns", "columns", "rows", "stack"]
    sources = [(units, full), (full, units), (full, units), (heads_width, full), (full, CC)]
    outs = [jax.ShapeDtypeStruct(grad_plan(kd, s)[5], BF) for kd, s in zip(kinds, sources)]
    outs = [outs[i] for i in (1, 2, 0, 3, 4)]
    vmem = pl.BlockSpec(memory_space=pltpu.VMEM)
    dma = pltpu.SemaphoreType.DMA
    blocks = span // MB
    turn = jnp.concatenate([cos, sin], axis=1)
    lse = lse.reshape(span // QB, heads, QB // AQ, AQ).transpose(0, 2, 1, 3).reshape(span // AQ, 1, heads * AQ)
    shapes = outs + [
        jax.ShapeDtypeStruct((tok, width), F32),
        jax.ShapeDtypeStruct((8, width), F32),
        jax.ShapeDtypeStruct((tok, width), F32),
        jax.ShapeDtypeStruct((tok, width), F32),
        jax.ShapeDtypeStruct((blocks // 2, LANES), F32),
        jax.ShapeDtypeStruct((span, full), BF),
        jax.ShapeDtypeStruct((span, full), BF),
        jax.ShapeDtypeStruct((span, full), BF),
    ]
    out_specs = [ANY] * 5 + [ANY, vmem, ANY, ANY, vmem, ANY, ANY, ANY]
    scratch = (
        [pltpu.VMEM((span, CC), BF)]
        + GroupSum.scratch(kinds, span)
        + Reduce.scratch(tok, full)
        + Reduce.sems() * 3
        + [pltpu.VMEM((tok, width), BF)]
        + Gather.sems()
        + [
            pltpu.VMEM((2, 3, MB, full), BF),
            pltpu.VMEM((2, MB, full), F32),
            pltpu.VMEM((MB, width), F32),
            dma((2, 3)),
            dma((3,)),
            pltpu.VMEM((span, heads_width), BF),
            pltpu.VMEM((AQ, heads_width), F32),
            pltpu.VMEM((heads * AQ, HD), F32),
            pltpu.VMEM((span, HD), F32),
            pltpu.VMEM((span, HD), F32),
            pltpu.VMEM((blocks, LANES), F32),
            pltpu.VMEM((blocks // 2, LANES), F32),
            pltpu.VMEM((3, blocks // 2, LANES), F32),
            dma((4,)),
            dma((4,)),
            pltpu.SemaphoreType.REGULAR((3,)),
            pltpu.VMEM((heads_width, full), BF),
            dma((2,)),
            pltpu.VMEM((tok // 4, width), F32),
        ]
    )
    results = pl.pallas_call(
        functools.partial(backward_kernel, kinds),
        in_specs=[pl.BlockSpec(memory_space=pltpu.SMEM), vmem] + [ANY] * 13 + [vmem] * 7,
        out_specs=out_specs,
        out_shape=shapes,
        scratch_shapes=scratch,
        compiler_params=pltpu.CompilerParams(
            collective_id=cid, has_side_effects=True, vmem_limit_bytes=VMEM_ALL
        ),
        name="backward",
    )(info, gains, normed_mlp, gate_cot, up_cot, hidden, mlp_part, low_part, resid, low, w_out_full, mixed, wide, normed,
      tokens_full, q, k, v, lse, turn, wq, wkv)
    return results[:10]


def by_distance(stacked, dim):
    count = lax.axis_size("col")
    order = lax.axis_index("col") ^ jnp.arange(count)
    blocks = jnp.take(stacked, order, axis=0)
    return jnp.concatenate([blocks[i] for i in range(count)], axis=dim)


def plain_gather(x):
    cols = by_distance(lax.all_gather(x, "col"), 1)
    return jnp.concatenate([cols, swap(cols, "row", 1)], axis=0)


def plain_gather_heads(x):
    mine = lax.all_gather(x, "col", axis=1, tiled=True)
    half = x.shape[0] // 2
    other = swap(mine, "row", 1)
    other = jnp.concatenate([other[half:], other[:half]], axis=0)
    return jnp.concatenate([mine, other], axis=1)


def plain_reduce(part):
    span, full = part.shape
    count = lax.axis_size("col")
    width = full // count
    half = part[: span // 2].astype(F32) + swap(part[span // 2 :], "row", 1).astype(F32)
    order = lax.axis_index("col") ^ jnp.arange(count)
    blocks = jnp.stack([half[:, s * width : (s + 1) * width] for s in range(count)])
    return lax.psum_scatter(jnp.take(blocks, order, axis=0), "col", tiled=False)


def exchange(packs):
    if kernels_fit():
        return [p if s == 0 else swap(p, "col", s) for s, p in enumerate(packs)]
    count = len(packs)
    order = lax.axis_index("col") ^ jnp.arange(count)
    sent = jnp.take(jnp.stack(packs), order, axis=0)
    blocks = jnp.take(lax.all_to_all(sent, "col", 0, 0, tiled=True), order, axis=0)
    return [blocks[i] for i in range(count)]


def plain_group_sum(grads, kinds):
    outs = []
    count = lax.axis_size("col")
    order = lax.axis_index("col") ^ jnp.arange(count)
    for grad, kind in zip(grads, kinds):
        grad = lax.psum(grad.astype(F32), "dp").astype(BF)
        dim = 1 if kind == "rows" else 0
        blocks = jnp.stack(jnp.split(grad, count, axis=dim))
        blocks = lax.all_to_all(jnp.take(blocks, order, axis=0), "col", 0, 0, tiled=True)
        out_dim = 1 if kind == "columns" else 0
        outs.append(jnp.concatenate([blocks[i] for i in range(count)], axis=out_dim))
    return outs


def kernels_fit():
    return lax.axis_size("col") == 4 and lax.axis_size("dp") == 4 and lax.axis_size("row") == 2


def attn_forward_kernel(info_ref, q_ref, k_ref, v_ref, *refs):
    linked = len(refs) > 6
    if linked:
        side_ref, mixed_ref, wide_ref, lse_ref, peak_ref, side_out, score_ref, sum_ref, stage = refs[:9]
        gather = Gather(side_ref, side_out, token_place(*side_ref.shape), stage, refs[9:])
    else:
        mixed_ref, wide_ref, lse_ref, peak_ref, score_ref, sum_ref = refs
    heads = q_ref.shape[1] // HD
    span = k_ref.shape[0]
    rows = heads * QB
    length = info_ref[0]
    half = lax.axis_index("row")
    step = pl.program_id(0)
    first = step * QB
    key_tiles = span // FWD_KB
    steps = span // QB
    lines = pl.ds(pl.multiple_of(lax.rem(step + half * (steps // 2), steps) * QB, QB), QB)

    if linked:

        @pl.when(step == 0)
        def _():
            greet(list(gather.near))
            gather.begin()

        @pl.when(step == steps - 1)
        def _():
            gather.first()

    q = jnp.concatenate([q_ref[lines, h * HD : (h + 1) * HD] for h in range(heads)], axis=0)
    tiles = (first + QB) // FWD_KB
    plain = first // FWD_KB

    def tile_of(ref, tile):
        stored = lax.rem(tile + half * (key_tiles // 2), key_tiles)
        return ref[pl.ds(pl.multiple_of(stored * FWD_KB, FWD_KB), FWD_KB), :]

    def fold(values, running, op):
        for t in range(FWD_KB // LANES):
            running = op(running, values[:, t * LANES : (t + 1) * LANES])
        return running

    def scores_of(tile, top, diagonal):
        scores = contract(q, tile_of(k_ref, tile), 1, 1) * HD**-0.5
        if diagonal:
            place = first + lax.broadcasted_iota(jnp.int32, (QB, FWD_KB), 0)
            key_place = tile * FWD_KB + lax.broadcasted_iota(jnp.int32, (QB, FWD_KB), 1)
            allowed = (key_place <= place) & (key_place < length)
            scores = jnp.where(allowed[None], scores.reshape(heads, QB, FWD_KB), NEG_FILL)
            scores = scores.reshape(rows, FWD_KB)
        else:
            key_place = tile * FWD_KB + lax.broadcasted_iota(jnp.int32, (1, FWD_KB), 1)
            scores = jnp.where(key_place < length, scores, NEG_FILL)
        score_ref[tile] = scores
        return fold(scores, top, jnp.maximum)

    top = jnp.full((rows, LANES), NEG_FILL, F32)
    top = lax.fori_loop(0, plain, lambda tile, top: scores_of(tile, top, False), top)
    top = lax.fori_loop(plain, tiles, lambda tile, top: scores_of(tile, top, True), top)
    top = jnp.max(top, axis=1, keepdims=True)
    live = first + lax.broadcasted_iota(jnp.int32, (QB, 1), 0) < length
    peak = jnp.max(jnp.where(live[None], top.reshape(heads, QB, 1), NEG_FILL), axis=1)

    @pl.when(step == 0)
    def _():
        peak_ref[...] = jnp.full_like(peak_ref, NEG_FILL)

    peak_ref[...] = jnp.maximum(peak_ref[...], jnp.broadcast_to(peak, peak_ref.shape))
    sum_ref[...] = jnp.zeros_like(sum_ref)

    def weigh(tile, total):
        weights = jnp.exp(score_ref[tile] - top)
        sum_ref[...] += contract(weights.astype(BF), tile_of(v_ref, tile), 1, 0)
        return fold(weights, total, jnp.add)

    total = lax.fori_loop(0, tiles, weigh, jnp.zeros((rows, LANES), F32))
    total = jnp.sum(total, axis=1, keepdims=True)
    mixed = sum_ref[...] / total
    log_total = jnp.broadcast_to(top + jnp.log(total), (rows, LANES))
    lse_ref[step] = log_total.T[0:1, :]
    for h in range(heads):
        part = mixed[h * QB : (h + 1) * QB]
        mixed_ref[lines, h * HD : (h + 1) * HD] = part.astype(BF)
        wide_ref[lines, h * HD : (h + 1) * HD] = part

    if linked:

        @pl.when(step == steps - 1)
        def _():
            gather.second()
            gather.finish()


def attn_forward(info, q, k, v, side=None, cid=None):
    span, width = q.shape
    heads = width // HD
    steps = span // QB
    whole = lambda shape: pl.BlockSpec(shape, lambda i: (0,) * len(shape))
    pairs = heads * span * span // 2
    shapes = [
        jax.ShapeDtypeStruct((span, width), BF),
        jax.ShapeDtypeStruct((span, width), F32),
        jax.ShapeDtypeStruct((steps, 1, heads * QB), F32),
        jax.ShapeDtypeStruct((heads, LANES), F32),
    ]
    in_specs = [pl.BlockSpec(memory_space=pltpu.SMEM)] + [whole(a.shape) for a in (q, k, v)]
    out_specs = [whole(s.shape) for s in shapes]
    scratch = [
        pltpu.VMEM((span // FWD_KB, heads * QB, FWD_KB), F32),
        pltpu.VMEM((heads * QB, HD), F32),
    ]
    operands = [info, q, k, v]
    params = dict(vmem_limit_bytes=48 * MIB)
    if side is not None:
        tok, wide = side.shape
        operands.append(side)
        in_specs.append(ANY)
        out_specs.append(ANY)
        shapes.append(jax.ShapeDtypeStruct((2 * tok, 4 * wide), side.dtype))
        scratch += [pltpu.VMEM(side.shape, side.dtype)] + Gather.sems()
        params.update(collective_id=cid, has_side_effects=True)
    return pl.pallas_call(
        attn_forward_kernel,
        grid=(steps,),
        in_specs=in_specs,
        out_specs=out_specs,
        scratch_shapes=scratch,
        out_shape=shapes,
        compiler_params=pltpu.CompilerParams(**params),
        cost_estimate=pl.CostEstimate(
            flops=40 * pairs * HD // 4, transcendentals=pairs, bytes_accessed=8 * span * width
        ),
        name="attn_forward",
    )(*operands)


def turn_back(values, cos_ref, sin_ref):
    half = HD // 2
    swapped = jnp.concatenate([values[:, half:], -values[:, :half]], axis=1)
    return values * cos_ref[...] + swapped * sin_ref[...]


def attn_backward_kernel(
    info_ref, q_ref, k_ref, v_ref, cot_ref, wide_ref, lse_ref, cosq_ref, sinq_ref, cosk_ref, sink_ref,
    dq_ref, dk_ref, dv_ref, dq_sum, dk_sum, dv_sum,
):
    heads = q_ref.shape[1] // HD
    span = k_ref.shape[0]
    rows = heads * QB
    length = info_ref[0]
    half = info_ref[1]
    step = pl.program_id(0)
    first = step * QB
    key_tiles = span // BWD_KB

    @pl.when(step == 0)
    def _():
        dk_sum[...] = jnp.zeros_like(dk_sum)
        dv_sum[...] = jnp.zeros_like(dv_sum)

    dq_sum[...] = jnp.zeros_like(dq_sum)

    @pl.when(first < length)
    def _():
        pieces = [slice(h * HD, (h + 1) * HD) for h in range(heads)]
        q = jnp.concatenate([q_ref[:, s] for s in pieces], axis=0)
        cot = jnp.concatenate([cot_ref[:, s] for s in pieces], axis=0)
        wide = jnp.concatenate([wide_ref[:, s] for s in pieces], axis=0)
        log_total = lse_ref[0]
        inner = jnp.sum(wide * cot.astype(F32), axis=1, keepdims=True)
        inner = jnp.broadcast_to(inner, (rows, LANES)).T[0:1, :]

        def tile_step(tile, masked):
            stored = lax.rem(tile + half * (key_tiles // 2), key_tiles)
            keys = pl.ds(pl.multiple_of(stored * BWD_KB, BWD_KB), BWD_KB)
            k_tile = k_ref[keys, :]
            v_tile = v_ref[keys, :]
            scores = contract(k_tile, q, 1, 1) * HD**-0.5 - log_total
            if masked:
                key_place = tile * BWD_KB + lax.broadcasted_iota(jnp.int32, (BWD_KB, rows), 0)
                place = first + lax.rem(lax.broadcasted_iota(jnp.int32, (BWD_KB, rows), 1), QB)
                scores = jnp.where((key_place <= place) & (key_place < length), scores, NEG_FILL)
            weights = jnp.exp(scores)
            prob_cot = contract(v_tile, cot, 1, 1)
            score_cot = (weights * (prob_cot - inner)).astype(BF)
            dv_sum[keys, :] += contract(weights.astype(BF), cot, 1, 0)
            dk_sum[keys, :] += contract(score_cot, q, 1, 0) * HD**-0.5
            dq_sum[...] += contract(score_cot, k_tile, 0, 0) * HD**-0.5

        @pl.loop(0, first // BWD_KB)
        def _(tile):
            tile_step(tile, False)

        @pl.loop(first // BWD_KB, pl.cdiv(first + QB, BWD_KB))
        def _(tile):
            tile_step(tile, True)

    for h in range(heads):
        part = turn_back(dq_sum[h * QB : (h + 1) * QB, :], cosq_ref, sinq_ref)
        dq_ref[:, h * HD : (h + 1) * HD] = part.astype(dq_ref.dtype)

    @pl.when(step == pl.num_programs(0) - 1)
    def _():
        dk_ref[...] = turn_back(dk_sum[...], cosk_ref, sink_ref).astype(dk_ref.dtype)
        dv_ref[...] = dv_sum[...].astype(dv_ref.dtype)


def attn_backward(info, q, k, v, cot, wide, lse, cos, sin, kv_type):
    span, width = q.shape
    heads = width // HD
    steps = span // QB

    def stored(i, info_ref):
        return (lax.rem(i + info_ref[1] * (steps // 2), steps), 0)

    whole = pl.BlockSpec((span, HD), lambda i, info_ref: (0, 0))
    mine = pl.BlockSpec((QB, width), stored)
    turn = pl.BlockSpec((QB, HD), stored)
    pairs = heads * span * span // 2
    return pl.pallas_call(
        attn_backward_kernel,
        grid_spec=pltpu.PrefetchScalarGridSpec(
            num_scalar_prefetch=1,
            grid=(steps,),
            in_specs=[
                mine, whole, whole, mine, mine,
                pl.BlockSpec((1, 1, heads * QB), lambda i, info_ref: (i, 0, 0)),
                turn, turn, whole, whole,
            ],
            out_specs=[mine, whole, whole],
            scratch_shapes=[
                pltpu.VMEM((heads * QB, HD), F32),
                pltpu.VMEM((span, HD), F32),
                pltpu.VMEM((span, HD), F32),
            ],
        ),
        out_shape=[
            jax.ShapeDtypeStruct((span, width), BF),
            jax.ShapeDtypeStruct((span, HD), kv_type),
            jax.ShapeDtypeStruct((span, HD), kv_type),
        ],
        compiler_params=pltpu.CompilerParams(vmem_limit_bytes=40 * 2**20),
        cost_estimate=pl.CostEstimate(
            flops=60 * pairs * HD // 4, transcendentals=pairs, bytes_accessed=12 * span * width
        ),
        name="attn_backward",
    )(info, q, k, v, cot, wide, lse, cos, sin, cos, sin)


def head_kernel(x_ref, gain_ref, wq_ref, wkv_ref, cos_ref, sin_ref, normed_ref, q_ref, k_ref, v_ref, scale_ref):
    x = x_ref[...].astype(F32)
    scale = lax.rsqrt(jnp.mean(x * x, axis=1, keepdims=True) + EPSILON)
    scale_ref[...] = jnp.broadcast_to(scale, scale_ref.shape)
    normed = (x * scale * gain_ref[0:1, :]).astype(BF)
    normed_ref[...] = normed

    def turned(raw):
        pieces = []
        half = HD // 2
        for h in range(raw.shape[1] // HD):
            pieces += [-raw[:, h * HD + half : (h + 1) * HD], raw[:, h * HD : h * HD + half]]
        pieces = jnp.concatenate(pieces, axis=1)
        count = raw.shape[1] // HD
        cos = jnp.concatenate([cos_ref[...]] * count, axis=1)
        sin = jnp.concatenate([sin_ref[...]] * count, axis=1)
        return (raw * cos + pieces * sin).astype(BF)

    q_ref[...] = turned(contract(normed, wq_ref[...], 1, 0))
    keyval = contract(normed, wkv_ref[...], 1, 0)
    k_ref[...] = turned(keyval[:, :HD])
    v_ref[...] = keyval[:, HD:].astype(BF)


def project_heads(tokens_full, gains, wq, wkv, cos, sin):
    span, full = tokens_full.shape
    width = wq.shape[1]
    block = 512
    line = lambda n: pl.BlockSpec((block, n), lambda i: (i, 0))
    whole = lambda a: pl.BlockSpec(a.shape, lambda i: (0, 0))
    return pl.pallas_call(
        head_kernel,
        grid=(span // block,),
        in_specs=[line(full), whole(gains), whole(wq), whole(wkv), line(HD), line(HD)],
        out_specs=[line(full), line(width), line(HD), line(HD), line(LANES)],
        out_shape=[
            jax.ShapeDtypeStruct((span, full), BF),
            jax.ShapeDtypeStruct((span, width), BF),
            jax.ShapeDtypeStruct((span, HD), BF),
            jax.ShapeDtypeStruct((span, HD), BF),
            jax.ShapeDtypeStruct((span, LANES), F32),
        ],
        compiler_params=pltpu.CompilerParams(vmem_limit_bytes=48 * MIB),
        cost_estimate=pl.CostEstimate(
            flops=2 * span * full * (width + LANES), transcendentals=0, bytes_accessed=5 * span * full
        ),
        name="project_heads",
    )(tokens_full, gains, wq, wkv, cos, sin)


def project_out_kernel(mixed_ref, w_ref, x_ref, gain_ref, *refs):
    linked = len(refs) > 2
    step = pl.program_id(0)
    if linked:
        side_ref, resid_ref, normed_ref, side_out, stage = refs[:5]
        gather = Gather(side_ref, side_out, token_place(*side_ref.shape), stage, refs[5:])

        @pl.when(step == 0)
        def _():
            greet(list(gather.near))
            gather.begin()

        @pl.when(step == pl.num_programs(0) // 2)
        def _():
            gather.first()

    else:
        resid_ref, normed_ref = refs
    resid = x_ref[...].astype(F32) + contract(mixed_ref[...], w_ref[...], 1, 0)
    resid_ref[...] = resid
    scale = lax.rsqrt(jnp.mean(resid * resid, axis=1, keepdims=True) + EPSILON)
    normed_ref[...] = (resid * scale * gain_ref[1:2, :]).astype(BF)

    if linked:

        @pl.when(step == pl.num_programs(0) - 1)
        def _():
            gather.second()
            gather.finish()


def project_out(mixed_full, w_out_full, tokens_full, gains, side=None, cid=None):
    span, full = tokens_full.shape
    block = 256
    line = pl.BlockSpec((block, full), lambda i: (i, 0))
    operands = [mixed_full, w_out_full, tokens_full, gains]
    in_specs = [
        pl.BlockSpec((block, mixed_full.shape[1]), lambda i: (i, 0)),
        pl.BlockSpec(w_out_full.shape, lambda i: (0, 0), pipeline_mode=pl.Buffered(1)),
        line,
        pl.BlockSpec(gains.shape, lambda i: (0, 0)),
    ]
    out_specs = [line, line]
    shapes = [jax.ShapeDtypeStruct((span, full), F32), jax.ShapeDtypeStruct((span, full), BF)]
    scratch = []
    params = dict(vmem_limit_bytes=48 * MIB)
    if side is not None:
        tok, wide = side.shape
        operands.append(side)
        in_specs.append(ANY)
        out_specs.append(ANY)
        shapes.append(jax.ShapeDtypeStruct((2 * tok, 4 * wide), side.dtype))
        scratch += [pltpu.VMEM(side.shape, side.dtype)] + Gather.sems()
        params.update(collective_id=cid, has_side_effects=True)
    return pl.pallas_call(
        project_out_kernel,
        grid=(span // block,),
        in_specs=in_specs,
        out_specs=out_specs,
        out_shape=shapes,
        scratch_shapes=scratch,
        compiler_params=pltpu.CompilerParams(**params),
        cost_estimate=pl.CostEstimate(
            flops=2 * span * full * full, transcendentals=0, bytes_accessed=12 * span * full
        ),
        name="project_out",
    )(*operands)


def middle_kernel(
    cot_ref, resid_ref, low_ref, gain_ref, w_ref, mixed_ref,
    mixed_cot_ref, own_ref, grad_ref, gain_part_ref, total_ref,
):
    step = pl.program_id(0)
    last = pl.num_programs(0) - 1
    width = own_ref.shape[1]
    cot = cot_ref[...].astype(F32)
    resid = resid_ref[...]
    scale = lax.rsqrt(jnp.mean(resid * resid, axis=1, keepdims=True) + EPSILON)
    weighed = cot * gain_ref[1:2, :]
    inner = jnp.sum(weighed * resid, axis=1, keepdims=True)
    mid = low_ref[...].astype(F32) + weighed * scale - resid * (scale * scale * scale * inner / D)
    low = mid.astype(BF)
    mixed_cot_ref[...] = contract(low, w_ref[...], 1, 1).astype(BF)

    @pl.when(step == 0)
    def _():
        total_ref[...] = jnp.zeros_like(total_ref)
        gain_part_ref[...] = jnp.zeros_like(gain_part_ref)

    total_ref[...] += contract(mixed_ref[...], low, 0, 0)

    @pl.when(step <= last // 2)
    def _():
        own_ref[...] = mid[:, :width]
        part = jnp.sum((cot * resid * scale)[:, :width], axis=0, keepdims=True)
        gain_part_ref[...] += jnp.broadcast_to(part, gain_part_ref.shape)

    @pl.when(step == last)
    def _():
        grad_ref[...] = total_ref[...].astype(BF)


def middle(mlp_cot, resid_mid, out_low, gains, w_mine, mixed, width):
    span, full = resid_mid.shape
    heads_width = mixed.shape[1]
    block = 256
    steps = span // block
    line = pl.BlockSpec((block, full), lambda i: (i, 0))
    thin = pl.BlockSpec((block, heads_width), lambda i: (i, 0))
    return pl.pallas_call(
        middle_kernel,
        grid=(steps,),
        in_specs=[
            line, line, line,
            pl.BlockSpec(gains.shape, lambda i: (0, 0)),
            pl.BlockSpec(w_mine.shape, lambda i: (0, 0)),
            thin,
        ],
        out_specs=[
            thin,
            pl.BlockSpec((block, width), lambda i: (jnp.minimum(i, steps // 2 - 1), 0)),
            pl.BlockSpec((heads_width, full), lambda i: (0, 0)),
            pl.BlockSpec((8, width), lambda i: (0, 0)),
        ],
        out_shape=[
            jax.ShapeDtypeStruct((span, heads_width), BF),
            jax.ShapeDtypeStruct((span // 2, width), F32),
            jax.ShapeDtypeStruct((heads_width, full), BF),
            jax.ShapeDtypeStruct((8, width), F32),
        ],
        scratch_shapes=[pltpu.VMEM((heads_width, full), F32)],
        compiler_params=pltpu.CompilerParams(vmem_limit_bytes=48 * MIB),
        cost_estimate=pl.CostEstimate(
            flops=4 * span * full * heads_width, transcendentals=0, bytes_accessed=8 * span * full
        ),
        name="middle",
    )(mlp_cot, resid_mid, out_low, gains, w_mine, mixed)


def head_back_kernel(
    info_ref, qc_ref, kc_ref, vc_ref, wq_ref, wkv_ref, normed_ref, x_ref, gain_ref,
    part_ref, dot_ref, grad_ref, total_ref,
):
    step = pl.program_id(0)
    wide = qc_ref.shape[1]
    keyval = jnp.concatenate([kc_ref[...], vc_ref[...]], axis=1)
    counted = keyval * info_ref[2].astype(BF)
    part = contract(qc_ref[...], wq_ref[...], 1, 1) + contract(counted, wkv_ref[...], 1, 1)
    part_ref[...] = part.astype(BF)
    inner = jnp.sum(part * gain_ref[0:1, :] * x_ref[...].astype(F32), axis=1, keepdims=True)
    dot_ref[0] = jnp.broadcast_to(inner, (inner.shape[0], LANES)).T[0:1, :]

    @pl.when(step == 0)
    def _():
        total_ref[...] = jnp.zeros_like(total_ref)

    total_ref[:, :wide] += contract(normed_ref[...], qc_ref[...], 0, 0)
    total_ref[:, wide:] += contract(normed_ref[...], keyval, 0, 0)

    @pl.when(step == pl.num_programs(0) - 1)
    def _():
        used = wide + 2 * HD
        grad_ref[:, :used] = total_ref[...].astype(BF)
        grad_ref[:, used:] = jnp.zeros((grad_ref.shape[0], grad_ref.shape[1] - used), BF)


def head_back(info, query_cot, key_cot, value_cot, wq, wkv, normed, tokens_full, gains):
    span, full = normed.shape
    wide = query_cot.shape[1]
    block = 512
    steps = span // block
    line = lambda n: pl.BlockSpec((block, n), lambda i, info_ref: (i, 0))
    whole = lambda shape: pl.BlockSpec(shape, lambda i, info_ref: (0, 0))
    grad_width = max(CC, wide + 2 * HD)
    return pl.pallas_call(
        head_back_kernel,
        grid_spec=pltpu.PrefetchScalarGridSpec(
            num_scalar_prefetch=1,
            grid=(steps,),
            in_specs=[
                line(wide), line(HD), line(HD), whole(wq.shape), whole(wkv.shape), line(full), line(full),
                whole(gains.shape),
            ],
            out_specs=[
                line(full),
                pl.BlockSpec((1, 1, block), lambda i, info_ref: (i, 0, 0)),
                whole((full, grad_width)),
            ],
            scratch_shapes=[pltpu.VMEM((full, wide + 2 * HD), F32)],
        ),
        out_shape=[
            jax.ShapeDtypeStruct((span, full), BF),
            jax.ShapeDtypeStruct((steps, 1, block), F32),
            jax.ShapeDtypeStruct((full, grad_width), BF),
        ],
        compiler_params=pltpu.CompilerParams(vmem_limit_bytes=48 * MIB),
        cost_estimate=pl.CostEstimate(
            flops=4 * span * full * (wide + LANES), transcendentals=0, bytes_accessed=6 * span * full
        ),
        name="head_back",
    )(info, query_cot, key_cot, value_cot, wq, wkv, normed, tokens_full, gains)


def fill_units(out, pieces, part, sem):
    mine = lax.rem(lax.axis_index("dp"), 2)
    rows = out.shape[0] // 8
    copies = []
    for s in range(4):
        for which, piece in ((mine, pieces[0]), (1 - mine, pieces[1])):
            lines = pl.ds(pl.multiple_of(s * 2 * rows + which * rows, rows), rows)
            src = piece.at[pl.ds((2 * s + part) * rows, rows), :]
            copies.append(pltpu.make_async_copy(src, out.at[lines, :], sem.at[len(copies)]))
    return copies


def hidden_kernel(x_ref, *refs):
    pieces = refs[:2]
    gate_ref, up_ref, hidden_ref, w_gate, w_up, gate_sem, up_sem = refs[2:]

    @pl.when(pl.program_id(0) == 0)
    def _():
        copies = fill_units(w_gate, pieces, 0, gate_sem) + fill_units(w_up, pieces, 1, up_sem)
        for c in copies:
            c.start()
        for c in copies:
            c.wait()

    gate = contract(x_ref[...], w_gate[...], 1, 0)
    gate_ref[...] = gate
    up = contract(x_ref[...], w_up[...], 1, 0)
    up_ref[...] = up
    hidden_ref[...] = (gate * jax.nn.sigmoid(gate) * up).astype(BF)


def hidden_units(normed, pieces):
    span, full = normed.shape
    units = pieces[0].shape[1]
    block = 512
    thin = pl.BlockSpec((block, units), lambda i: (i, 0))
    return pl.pallas_call(
        hidden_kernel,
        grid=(span // block,),
        in_specs=[pl.BlockSpec((block, full), lambda i: (i, 0))] + [ANY] * 2,
        out_specs=[thin] * 3,
        out_shape=[
            jax.ShapeDtypeStruct((span, units), F32),
            jax.ShapeDtypeStruct((span, units), F32),
            jax.ShapeDtypeStruct((span, units), BF),
        ],
        scratch_shapes=[
            pltpu.VMEM((full, units), BF),
            pltpu.VMEM((full, units), BF),
            pltpu.SemaphoreType.DMA((8,)),
            pltpu.SemaphoreType.DMA((8,)),
        ],
        compiler_params=pltpu.CompilerParams(vmem_limit_bytes=48 * MIB),
        cost_estimate=pl.CostEstimate(
            flops=4 * span * full * units, transcendentals=span * units, bytes_accessed=6 * span * full
        ),
        name="hidden_units",
    )(normed, *pieces)


def hidden_back_kernel(low_ref, gate_ref, up_ref, hidden_ref, own_ref, *refs):
    pieces, down_pieces = refs[:2], refs[2:5]
    gate_cot_ref, up_cot_ref, part_ref, low_part_ref, w_gate, w_up, w_down, gate_sem, up_sem, down_sem = refs[5:]
    units = w_down.shape[0]
    width = w_down.shape[1] // 4

    @pl.when(pl.program_id(0) == 0)
    def _():
        mine = own_ref.at[pl.ds(pl.multiple_of(lax.axis_index("col") * units, units), units), :]
        copies = [
            pltpu.make_async_copy(p, w_down.at[:, pl.ds(s * width, width)], down_sem.at[s])
            for s, p in enumerate((mine, *down_pieces))
        ]
        copies += fill_units(w_gate, pieces, 0, gate_sem) + fill_units(w_up, pieces, 1, up_sem)
        for c in copies:
            c.start()
        for c in copies:
            c.wait()

    hidden_cot = contract(low_ref[...], w_down[...], 1, 1)
    gate = gate_ref[...]
    sig = jax.nn.sigmoid(gate)
    gate_cot = (hidden_cot * up_ref[...] * sig * (1.0 + gate * (1.0 - sig))).astype(BF)
    up_cot = (hidden_cot * gate * sig).astype(BF)
    gate_cot_ref[...] = gate_cot
    up_cot_ref[...] = up_cot
    part = contract(gate_cot, w_gate[...], 1, 1) + contract(up_cot, w_up[...], 1, 1)
    part_ref[...] = part.astype(BF)
    low_part_ref[...] = contract(hidden_ref[...], w_down[...], 1, 0).astype(BF)


def hidden_back(low, gate, up, hidden, w_down, pieces, down_pieces):
    span, full = low.shape
    units = gate.shape[1]
    block = 512
    thin = pl.BlockSpec((block, units), lambda i: (i, 0))
    line = pl.BlockSpec((block, full), lambda i: (i, 0))
    return pl.pallas_call(
        hidden_back_kernel,
        grid=(span // block,),
        in_specs=[line, thin, thin, thin] + [ANY] * 6,
        out_specs=[thin, thin, line, line],
        out_shape=[jax.ShapeDtypeStruct((span, units), BF)] * 2 + [jax.ShapeDtypeStruct((span, full), BF)] * 2,
        scratch_shapes=[
            pltpu.VMEM((full, units), BF),
            pltpu.VMEM((full, units), BF),
            pltpu.VMEM((units, full), BF),
            pltpu.SemaphoreType.DMA((8,)),
            pltpu.SemaphoreType.DMA((8,)),
            pltpu.SemaphoreType.DMA((4,)),
        ],
        compiler_params=pltpu.CompilerParams(vmem_limit_bytes=VMEM_ALL),
        cost_estimate=pl.CostEstimate(
            flops=8 * span * full * units, transcendentals=span * units, bytes_accessed=12 * span * full
        ),
        name="hidden_back",
    )(low, gate, up, hidden, w_down, *pieces, *down_pieces)


def on_device(
    tokens, lengths, attn_gain, w_query, w_key, w_value, w_out, mlp_gain, w_gate, w_up, w_down, cotangent
):
    row_devices = lax.axis_size("row")
    col_devices = lax.axis_size("col")
    row = lax.axis_index("row")
    col = lax.axis_index("col")
    fit = kernels_fit()
    tok, width = tokens.shape
    span = tok * row_devices
    group = HQ // KV
    heads_row = HQ // row_devices
    heads = heads_row // col_devices
    head_width = heads * HD
    keyval_row = KV // row_devices
    units = w_gate.shape[1] // col_devices
    length = lengths[0]
    shared_key = heads < group
    sharers = max(1, group // heads)
    leader = (col % sharers == 0).astype(jnp.int32)
    info = jnp.stack([length, row, leader]).astype(jnp.int32)

    keyval = []
    for owner in range(col_devices):
        first = owner * heads // group * HD
        keyval += [w_key[:, first : first + HD], w_value[:, first : first + HD]]
    keyval = jnp.concatenate(keyval, axis=1)
    gains = jnp.concatenate([attn_gain[None], mlp_gain[None], jnp.zeros((6, width), F32)], axis=0)

    if fit:
        tokens_full, wq, wkv, gains = first_gather(tokens, w_query, keyval, gains, 1)
    else:
        tokens_full = plain_gather(tokens)
        def slices(weight, size):
            return [lax.dynamic_slice_in_dim(weight, (col ^ s) * size, size, 1) for s in range(col_devices)]

        wq = jnp.concatenate(exchange(slices(w_query, head_width)), axis=0)
        wkv = jnp.concatenate(exchange(slices(keyval, LANES)), axis=0)
        gains = by_distance(lax.all_gather(gains, "col"), 1)
    w_gate, w_up, tokens_full = lax.optimization_barrier((w_gate, w_up, tokens_full))
    place = lax.rem(jnp.arange(span, dtype=jnp.int32) + row * tok, span)
    frequency = ROPE_BASE ** (-jnp.arange(HD // 2, dtype=F32) * (2.0 / HD))
    angle = place.astype(F32)[:, None] * frequency[None, :]
    cos = jnp.tile(jnp.cos(angle), (1, 2))
    sin = jnp.tile(jnp.sin(angle), (1, 2))

    normed_attn, query, key, value, scale_a = project_heads(tokens_full, gains, wq, wkv, cos, sin)
    valid = (row * tok + jnp.arange(tok, dtype=jnp.int32) < length).astype(BF)
    cot_low = cotangent * valid[:, None]
    def unit_pieces():
        rows = width // 2
        start = lax.rem(lax.axis_index("dp"), 2) * rows
        near = [
            jnp.concatenate(
                [lax.dynamic_slice(w, (start, (col ^ s) * units), (rows, units)) for w in (w_gate, w_up)], axis=0
            )
            for s in range(col_devices)
        ]
        return jnp.concatenate(exchange(near), axis=0)

    def unit_slices(weight, dim):
        return [lax.dynamic_slice_in_dim(weight, (col ^ s) * units, units, dim) for s in range(col_devices)]

    if fit:
        near_units = unit_pieces()
        mixed, mixed_wide, log_total, peak, w_out_full = attn_forward(info, query, key, value, w_out, 7)
        mixed, near_units = lax.optimization_barrier((mixed, near_units))
        pieces = [near_units, swap(near_units, "dp", 1)]
        mixed_full = gather_heads(mixed, 2)
        resid_mid, normed_mlp, out_low = project_out(mixed_full, w_out_full, tokens_full, gains, cot_low, 8)
        w_down, normed_mlp = lax.optimization_barrier((w_down, normed_mlp))
        down_pieces = [
            swap(lax.dynamic_slice_in_dim(w_down, (col ^ s) * units, units, 0), "col", s) for s in range(1, col_devices)
        ]
        gate, up, hidden = hidden_units(normed_mlp, pieces)
        hidden, peak = lax.optimization_barrier((hidden, peak))
        moved = [swap(peak, "dp", step) for step in (1, 2, 3)]
        gate_cot, up_cot, mlp_part, down_part = hidden_back(
            out_low, gate, up, hidden, w_down, pieces, down_pieces
        )
        mlp_part, moved = lax.optimization_barrier((mlp_part, moved))
        for other in moved:
            peak = jnp.maximum(peak, other)
    else:
        mixed, mixed_wide, log_total, peak = attn_forward(info, query, key, value)
        mixed_full = plain_gather_heads(mixed)
        w_out_full = plain_gather(w_out)
        resid_mid, normed_mlp = project_out(mixed_full, w_out_full, tokens_full, gains)
        out_low = plain_gather(cot_low)
        w_gate_units = jnp.concatenate(exchange(unit_slices(w_gate, 1)), axis=0)
        w_up_units = jnp.concatenate(exchange(unit_slices(w_up, 1)), axis=0)
        w_down_units = jnp.concatenate(exchange(unit_slices(w_down, 0)), axis=1)
        gate = jnp.dot(normed_mlp, w_gate_units, preferred_element_type=F32)
        up = jnp.dot(normed_mlp, w_up_units, preferred_element_type=F32)
        gate_sigmoid = jax.nn.sigmoid(gate)
        hidden = (gate * gate_sigmoid * up).astype(BF)
        hidden_cot = contract(out_low, w_down_units, 1, 1)
        gate_cot = (
            hidden_cot * up * gate_sigmoid * (1.0 + gate * (1.0 - gate_sigmoid))
        ).astype(BF)
        up_cot = (hidden_cot * gate * gate_sigmoid).astype(BF)
        mlp_part = (contract(gate_cot, w_gate_units, 1, 1) + contract(up_cot, w_up_units, 1, 1)).astype(BF)
        down_part = jnp.dot(hidden, w_down_units, preferred_element_type=F32).astype(BF)

    if fit:
        *sums, mid_cot, gain_m_part, attn_cot, down_sum, width_dot = backward(
            info, gains, normed_mlp, gate_cot, up_cot, hidden, mlp_part, down_part, resid_mid, out_low, w_out_full,
            mixed, query, key, value, mixed_wide, log_total, cos, sin, wq, wkv, normed_attn, tokens_full, 3,
        )
        width_dot = width_dot.reshape(tok)
    else:
        mlp_cot = plain_gather(plain_reduce(mlp_part).astype(BF))
        down_sum = plain_reduce(down_part)
        w_mine = lax.dynamic_slice_in_dim(w_out_full, col * head_width, head_width, 0)
        mixed_cot, mid_cot, grad_out, gain_m_part = middle(
            mlp_cot, resid_mid, out_low, gains, w_mine, mixed, width
        )
        query_cot, key_cot, value_cot = attn_backward(
            info, query, key, value, mixed_cot, mixed_wide, log_total, cos, sin, F32 if shared_key else BF
        )
        if shared_key:
            for bit in range(sharers.bit_length() - 1):
                key_cot = key_cot + swap(key_cot, "col", 1 << bit)
                value_cot = value_cot + swap(value_cot, "col", 1 << bit)
            key_cot, value_cot = key_cot.astype(BF), value_cot.astype(BF)
        attn_part, dot_part, grad_heads = head_back(
            info, query_cot, key_cot, value_cot, wq, wkv, normed_attn, tokens_full, gains
        )
        dot_part = dot_part.reshape(span)
        width_dot = lax.psum(dot_part[:tok] + swap(dot_part[tok:], "row", 1), "col")
        attn_cot = plain_reduce(attn_part)
        grad_gate = contract(normed_mlp, gate_cot, 0, 0).astype(BF)
        grad_up = contract(normed_mlp, up_cot, 0, 0).astype(BF)
        grad_down = contract(hidden, out_low, 0, 0).astype(BF)
        sums = plain_group_sum(
            [grad_gate, grad_up, grad_down, grad_out, grad_heads], ["columns", "columns", "rows", "rows", "stack"]
        )
    output = (resid_mid[:tok, :width] + down_sum).astype(BF)
    own_in = tokens.astype(F32)
    scale_own = scale_a[:tok, :1]
    input_grad = (
        mid_cot
        + attn_cot * attn_gain * scale_own
        - own_in * (scale_own * scale_own * scale_own * width_dot[:, None] / D)
    )
    gain_a_part = jnp.sum(attn_cot * own_in * scale_own, axis=0)

    out_gate, out_up, out_down, out_out, out_heads = [g.astype(F32) for g in sums]
    out_heads = out_heads.reshape(col_devices, width, out_heads.shape[1])
    out_query = jnp.concatenate([out_heads[i, :, :head_width] for i in range(col_devices)], axis=1)
    leaders = range(0, col_devices, sharers)
    out_key = jnp.concatenate([out_heads[i, :, head_width : head_width + HD] for i in leaders], axis=1)
    out_value = jnp.concatenate(
        [out_heads[i, :, head_width + HD : head_width + 2 * HD] for i in leaders], axis=1
    )

    gain_sums = jnp.stack([gain_a_part, gain_m_part[0]])
    if fit:
        grown, hops = [out_gate, out_up, out_down], [("row", 1), ("dp", 1), ("dp", 2)]
        for n, (axis, step) in enumerate(hops):
            other = swap(gain_sums, axis, step)
            other, grown[n] = lax.optimization_barrier((other, grown[n]))
            gain_sums = gain_sums + other
        out_gate, out_up, out_down = grown
        own_peaks = peak[:, 0]
        row_peaks = jnp.where(jnp.arange(col_devices)[:, None] == col, own_peaks[None, :], NEG_FILL)
        row_peaks = jnp.maximum(row_peaks, swap(row_peaks, "col", 1))
        row_peaks = jnp.maximum(row_peaks, swap(row_peaks, "col", 2))
    else:
        gain_sums = lax.psum(gain_sums, ("dp", "row"))
        own_peaks = lax.pmax(peak, "dp")[:, 0]
        row_peaks = lax.all_gather(own_peaks, "col")
    row_peaks = row_peaks.reshape(heads_row)
    clip_factor = CLIP_LEVEL / jnp.maximum(row_peaks, CLIP_LEVEL)
    query_scale = jnp.repeat(jnp.sqrt(clip_factor), HD)
    key_scale = jnp.repeat(jnp.sqrt(jnp.min(clip_factor.reshape(keyval_row, group), axis=1)), HD)
    clipped_query = (w_query.astype(F32) * query_scale[None, :]).astype(BF)
    clipped_key = (w_key.astype(F32) * key_scale[None, :]).astype(BF)
    return (
        output,
        input_grad,
        gain_sums[0],
        out_query,
        out_key,
        out_value,
        out_out,
        gain_sums[1],
        out_gate,
        out_up,
        out_down,
        own_peaks,
        clipped_query,
        clipped_key,
    )


def solution(mesh):
    in_specs = (
        P(("dp", "row"), "col"),
        P("dp"),
        P("col"),
        P("col", "row"),
        P("col", "row"),
        P("col", "row"),
        P("row", "col"),
        P("col"),
        P("col", "row"),
        P("col", "row"),
        P("row", "col"),
        P(("dp", "row"), "col"),
    )
    out_specs = (
        P(("dp", "row"), "col"),
        P(("dp", "row"), "col"),
        P("col"),
        P("col", "row"),
        P("col", "row"),
        P("col", "row"),
        P("row", "col"),
        P("col"),
        P("col", "row"),
        P("col", "row"),
        P("row", "col"),
        P(("row", "col")),
        P("col", "row"),
        P("col", "row"),
    )
    return jax.shard_map(
        on_device, mesh=mesh, in_specs=in_specs, out_specs=out_specs, check_vma=False
    )
```

```python
import functools

import jax
import jax.numpy as jnp
from jax import lax
from jax.experimental import pallas as pl
from jax.experimental.pallas import tpu as pltpu
from jax.sharding import PartitionSpec as P

D = 2048
HQ = 32
KV = 8
HD = 64
SEQ_LEN = 2048

EPSILON = 1e-05
NEG_FILL = -1e30
CLIP_LEVEL = 5.0
ROPE_BASE = 500000.0

BF = jnp.bfloat16
F32 = jnp.float32
LANES = 128
QB = 512
FWD_KB = 512
BWD_KB = 512
MESH = pl.DeviceIdType.MESH
ANY = pl.BlockSpec(memory_space=pl.ANY)
NCH = 4
CR, CC = 256, 512
HR = CR // 2
OFFS = (0, 2, 4, 8)
RING = 13
MIB = 2**20
VMEM_ALL = 63 * MIB


def contract(left, right, left_dim, right_dim):
    return lax.dot_general(
        left, right, (((left_dim,), (right_dim,)), ((), ())), preferred_element_type=F32
    )


def swap(values, axis, step):
    count = lax.axis_size(axis)
    return lax.ppermute(values, axis, [(i, i ^ step) for i in range(count)])


def flip(index, bit):
    return index + bit - 2 * bit * lax.rem(index // bit, 2)


def xor(index, step):
    return lax.rem(lax.rem(index, 2) + step % 2, 2) + 2 * lax.rem(index // 2 + step // 2, 2)


def remote(src, dst, send, recv, **where):
    return pltpu.make_async_remote_copy(
        src_ref=src, dst_ref=dst, send_sem=send, recv_sem=recv, device_id=where, device_id_type=MESH
    )


def done(ref, sem):
    pltpu.make_async_copy(ref, ref, sem).wait()


def greet(targets):
    barrier = pltpu.get_barrier_semaphore()
    for target in targets:
        pl.semaphore_signal(barrier, inc=1, device_id=target, device_id_type=MESH)
    pl.semaphore_wait(barrier, len(targets))


def plane_peers():
    row = lax.axis_index("row")
    col = lax.axis_index("col")
    return {"col": flip(col, 1)}, {"col": flip(col, 2)}, {"row": 1 - row}


def token_place(tok, width):
    rows = tok // NCH

    def place(ref, half, s, j, who):
        return ref.at[pl.ds(half * tok + j * rows, rows), pl.ds(s * width, width)]

    return place


def head_place(span, width):
    rows = span // NCH

    def place(ref, half, s, j, who):
        start = j * rows if half == 0 else ((j + NCH // 2) % NCH) * rows
        return ref.at[pl.ds(start, rows), pl.ds(pl.multiple_of((half * 4 + xor(who, s)) * width, LANES), width)]

    return place


class Gather:
    SEMS = 6

    def __init__(self, src, out, place, stage, sems):
        self.src, self.out, self.place, self.stage = src, out, place, stage
        self.own_send, self.relay_send, self.mate_send, self.recv, self.mate_recv, self.local = sems
        self.col = lax.axis_index("col")
        self.near = plane_peers()

    @staticmethod
    def sems():
        shapes = [(2, NCH), (NCH,), (4, NCH), (3, NCH), (4, NCH), (2,)]
        return [pltpu.SemaphoreType.DMA(s) for s in shapes]

    def chunk(self, j):
        rows = self.src.shape[0] // NCH
        return self.src.at[pl.ds(j * rows, rows), :]

    def here(self, half, s, j):
        return self.place(self.out, half, s, j, self.col)

    def own(self, axis, j):
        peer = self.near[axis]
        dst = self.place(self.out, 0, axis + 1, j, peer["col"])
        return remote(self.chunk(j), dst, self.own_send.at[axis, j], self.recv.at[axis, j], **peer)

    def relay(self, axis, j):
        peer = self.near[1 - axis]
        dst = self.place(self.out, 0, 3, j, peer["col"])
        return remote(self.here(0, axis + 1, j), dst, self.relay_send.at[j], self.recv.at[2, j], **peer)

    def mate(self, s, j):
        src = self.chunk(j) if s == 0 else self.here(0, s, j)
        dst = self.place(self.out, 1, s, j, self.col)
        return remote(src, dst, self.mate_send.at[s, j], self.mate_recv.at[s, j], **self.near[2])

    def load(self):
        return pltpu.make_async_copy(self.src, self.stage, self.local.at[0])

    def keep(self, j):
        rows = self.src.shape[0] // NCH
        whole = self.stage if self.stage is not None else self.src
        return pltpu.make_async_copy(whole.at[pl.ds(j * rows, rows), :], self.here(0, 0, j), self.local.at[1])

    def begin(self):
        half = NCH // 2
        if self.stage is not None:
            self.load().start()
        for i in range(NCH):
            self.own(0, i).start()
            self.own(1, (i + half) % NCH).start()
        for j in range(NCH):
            self.mate(0, j).start()

    def arrived(self, s, j):
        done(self.here(0, s, j), self.recv.at[s - 1, j])

    def first(self):
        half = NCH // 2
        for i in range(half):
            self.arrived(1, i)
            self.relay(0, i).start()
            self.mate(1, i).start()
            self.arrived(2, half + i)
            self.relay(1, half + i).start()
            self.mate(2, half + i).start()

    def second(self):
        half = NCH // 2
        if self.stage is not None:
            self.load().wait()
        for j in range(NCH):
            self.keep(j).start()
        for i in range(half):
            self.arrived(1, half + i)
            self.mate(1, half + i).start()
            self.arrived(2, i)
            self.mate(2, i).start()
        for i in range(half):
            for j in (i, half + i):
                self.arrived(3, j)
                self.mate(3, j).start()

    def finish(self):
        half = NCH // 2
        for s in range(4):
            for j in range(NCH):
                done(self.here(1, s, j), self.mate_recv.at[s, j])
                self.mate(s, j).wait_send()
        for j in range(NCH):
            self.own(0, j).wait_send()
            self.own(1, j).wait_send()
            self.relay(0 if j < half else 1, j).wait_send()
        whole = self.stage if self.stage is not None else self.src
        done(whole, self.local.at[1])


def gather_kernel(place_of, x_ref, out_ref, stage, *sems):
    near_x, near_y, mate = plane_peers()
    greet([near_x, near_y, mate])
    gather = Gather(x_ref, out_ref, place_of(*x_ref.shape), stage, sems)
    gather.begin()
    gather.first()
    gather.second()
    gather.finish()


def gather_call(x, shape, place_of, cid, name):
    return pl.pallas_call(
        functools.partial(gather_kernel, place_of),
        in_specs=[ANY],
        out_specs=ANY,
        out_shape=jax.ShapeDtypeStruct(shape, x.dtype),
        scratch_shapes=[pltpu.VMEM(x.shape, x.dtype)] + Gather.sems(),
        compiler_params=pltpu.CompilerParams(collective_id=cid, has_side_effects=True),
        name=name,
    )(x)


def gather_tokens(x, cid):
    tok, width = x.shape
    return gather_call(x, (2 * tok, 4 * width), token_place, cid, "gather_tokens")


def gather_heads(x, cid):
    span, width = x.shape
    return gather_call(x, (span, 8 * width), head_place, cid, "gather_heads")


class Reduce:
    def __init__(self, part, scratch, sems):
        self.part = part
        self.own, self.given, self.sent, self.got_one, self.got_two = scratch
        self.loads, self.mate_send, self.mate_recv, self.one_send, self.one_recv, self.two_send, self.two_recv = sems
        self.near = plane_peers()
        self.h = self.own.shape[0] // 2
        self.width = self.own.shape[1] // 4

    @staticmethod
    def scratch(tok, full):
        h, w = tok // 2, full // 4
        shapes = [(tok, full), (tok, full), (2, 3, h, w), (2, 2, h, w), (2, h, w)]
        return [pltpu.VMEM(s, BF) for s in shapes]

    @staticmethod
    def sems():
        return [pltpu.SemaphoreType.DMA((2,))] * 7

    def lines(self, a):
        return pl.ds(a * self.h, self.h)

    def give(self, a):
        src = self.part.at[pl.ds((2 + a) * self.h, self.h), :]
        return remote(src, self.given.at[self.lines(a), :], self.mate_send.at[a], self.mate_recv.at[a], **self.near[2])

    def load(self, a):
        return pltpu.make_async_copy(self.part.at[self.lines(a), :], self.own.at[self.lines(a), :], self.loads.at[a])

    def one(self, a):
        src = self.sent.at[a, pl.ds(0, 2)]
        return remote(src, self.got_one.at[a], self.one_send.at[a], self.one_recv.at[a], **self.near[a])

    def two(self, a):
        return remote(self.sent.at[a, 2], self.got_two.at[a], self.two_send.at[a], self.two_recv.at[a], **self.near[1 - a])

    def pair(self, a, s):
        cols = pl.ds(s * self.width, self.width)
        rows = self.lines(a)
        return self.own[rows, cols].astype(F32) + self.given[rows, cols].astype(F32)

    def begin(self):
        for a in range(2):
            self.give(a).start()
            self.load(a).start()

    def first(self, a):
        self.load(a).wait()
        done(self.given.at[self.lines(a), :], self.mate_recv.at[a])
        for i, s in enumerate((a + 1, 3)):
            self.sent[a, i] = self.pair(a, s).astype(BF)
        self.one(a).start()

    def second(self, a):
        done(self.got_one.at[a], self.one_recv.at[a])
        self.sent[a, 2] = (self.pair(a, 2 - a) + self.got_one[a, 1].astype(F32)).astype(BF)
        self.two(a).start()

    def total(self, a):
        done(self.got_two.at[a], self.two_recv.at[a])
        return self.pair(a, 0) + self.got_one[a, 0].astype(F32) + self.got_two[a].astype(F32)

    def finish(self):
        for a in range(2):
            self.give(a).wait_send()
            self.one(a).wait_send()
            self.two(a).wait_send()


def first_gather_kernel(
    x_ref, wq_ref, wkv_ref, gain_ref, out_ref, wq_out, wkv_out, gain_out,
    stage, wq_stage, wkv_stage, gain_stage, stage_sem, small_send, small_recv, *sems,
):
    near_x, near_y, mate = plane_peers()
    col = lax.axis_index("col")
    tok, width = x_ref.shape
    wide = wq_ref.shape[1] // 4
    thin = wkv_ref.shape[1] // 4

    def share(ref, owner, size):
        return ref.at[:, pl.ds(pl.multiple_of(owner * size, LANES), size)]

    loads = [
        pltpu.make_async_copy(share(wq_ref, col, wide), wq_stage, stage_sem.at[0]),
        pltpu.make_async_copy(share(wkv_ref, col, thin), wkv_stage, stage_sem.at[1]),
        pltpu.make_async_copy(gain_ref, gain_stage, stage_sem.at[2]),
    ]
    for c in loads:
        c.start()
    greet([near_x, near_y, {"col": 3 - col}, mate])
    smalls = []
    for s, peer in ((1, near_x), (2, near_y), (3, {"col": 3 - col})):
        owner = peer["col"]
        lines = pl.ds(s * width, width)
        smalls += [
            remote(share(wq_ref, owner, wide), wq_out.at[lines, :], small_send.at[0, s], small_recv.at[0, s], **peer),
            remote(share(wkv_ref, owner, thin), wkv_out.at[lines, :], small_send.at[1, s], small_recv.at[1, s], **peer),
            remote(gain_ref, gain_out.at[:, lines], small_send.at[2, s], small_recv.at[2, s], **peer),
        ]
    gather = Gather(x_ref, out_ref, token_place(tok, width), stage, sems)
    gather.begin()
    for c in smalls:
        c.start()
    lines = pl.ds(0, width)
    keeps = [
        pltpu.make_async_copy(wq_stage, wq_out.at[lines, :], stage_sem.at[3]),
        pltpu.make_async_copy(wkv_stage, wkv_out.at[lines, :], stage_sem.at[4]),
        pltpu.make_async_copy(gain_stage, gain_out.at[:, lines], stage_sem.at[5]),
    ]
    for load, keep in zip(loads, keeps):
        load.wait()
        keep.start()
    gather.first()
    gather.second()
    gather.finish()
    for c in smalls:
        c.wait()
    for c in keeps:
        c.wait()


def first_gather(x, wq, wkv, gains, cid):
    tok, width = x.shape
    wide, thin = wq.shape[1] // 4, wkv.shape[1] // 4
    return pl.pallas_call(
        first_gather_kernel,
        in_specs=[ANY] * 4,
        out_specs=[ANY] * 4,
        out_shape=[
            jax.ShapeDtypeStruct((2 * tok, 4 * width), BF),
            jax.ShapeDtypeStruct((4 * width, wide), BF),
            jax.ShapeDtypeStruct((4 * width, thin), BF),
            jax.ShapeDtypeStruct((8, 4 * width), F32),
        ],
        scratch_shapes=[
            pltpu.VMEM((tok, width), BF),
            pltpu.VMEM((width, wide), BF),
            pltpu.VMEM((width, thin), BF),
            pltpu.VMEM((8, width), F32),
            pltpu.SemaphoreType.DMA((6,)),
            pltpu.SemaphoreType.DMA((3, 4)),
            pltpu.SemaphoreType.DMA((3, 4)),
        ]
        + Gather.sems(),
        compiler_params=pltpu.CompilerParams(collective_id=cid, has_side_effects=True),
        name="first_gather",
    )(x, wq, wkv, gains)


def grad_plan(kind, shape):
    rows, cols = shape
    if kind == "columns":
        w = rows // 4
        high, n = rows // CR, w // CR
        return (
            high * (cols // CC), high,
            lambda i: lax.rem(i, high) // n, lambda i: lax.rem(i, high), lambda i: i // high,
            (w, 4 * cols), lambda c, i: (lax.rem(i, n) * CR, c * cols + i // high * CC),
        )
    high = rows // CR
    if kind == "rows":
        return (
            4 * high, high,
            lambda i: i // high, lambda i: lax.rem(i, high), lambda i: i // high,
            (4 * rows, cols // 4), lambda c, i: (c * rows + lax.rem(i, high) * CR, 0),
        )
    if kind == "query":
        return 4, 1, lambda i: i, lambda i: 0, lambda i: i, (4 * CR, CC), lambda c, i: (c * CR, 0)
    return 2, 1, lambda i: 2 * i, lambda i: 0, lambda i: 2 * i, (4 * HR, CC), lambda c, i: (c * HR, 0)


class GroupSum:
    def __init__(self, kinds, lefts, rights, outs, refs):
        (self.left, self.right, self.left_sem, self.right_sem, self.own, self.land, self.mids, self.tops, self.in_send, self.in_recv, self.mid_send,
         self.mid_recv, self.top_send, self.top_recv, self.out_send, self.out_recv, self.far_send, self.far_recv) = refs
        self.lefts, self.rights, self.outs = lefts, rights, outs
        self.kinds = kinds
        self.plans = [grad_plan(k, (a.shape[1], b.shape[1])) for k, a, b in zip(kinds, lefts, rights)]
        self.counts = [p[0] for p in self.plans]
        self.begins = [sum(self.counts[:i]) for i in range(len(lefts))]
        groups = [p[0] // p[1] for p in self.plans]
        self.groups = [sum(groups[:i]) for i in range(len(lefts))]
        self.total = sum(self.counts)
        z = lax.axis_index("dp")
        self.col = lax.axis_index("col")
        self.is_mid = (z == 1) | (z == 2)
        self.is_end = jnp.logical_not(self.is_mid)
        left = z < 2
        self.inward = {"dp": jnp.where(left, z + 1, z - 1)}
        self.outward = {"dp": jnp.where(left, z - 1, z + 1)}
        self.kept = jnp.where(left, 0, 1)

    @staticmethod
    def scratch(kinds, span):
        dma = pltpu.SemaphoreType.DMA
        return (
            [pltpu.VMEM((2, span, CR), BF), pltpu.VMEM((2, span, CC), BF), dma((2,)), dma((2,))]
            + [pltpu.VMEM((RING, CR, CC), BF)] * 2
            + [pltpu.VMEM((RING, HR, CC), BF)] * 2
            + [dma((RING,))] * 6
            + [dma((RING, 2))] * 3
            + [dma((len(kinds),))]
        )

    def greet(self, others):
        barrier = pltpu.get_barrier_semaphore()
        targets = [self.inward] + others
        for target in targets:
            pl.semaphore_signal(barrier, inc=1, device_id=target, device_id_type=MESH)

        @pl.when(self.is_mid)
        def _():
            pl.semaphore_signal(barrier, inc=1, device_id=self.outward, device_id_type=MESH)
            pl.semaphore_wait(barrier, len(targets) + 1)

        @pl.when(self.is_end)
        def _():
            pl.semaphore_wait(barrier, len(targets))

    def rows(self, half):
        return pl.ds(pl.multiple_of(half * HR, HR), HR)

    def each(self, j, action):
        for m, count in enumerate(self.counts):

            @pl.when((j >= self.begins[m]) & (j < self.begins[m] + count))
            def _(m=m):
                action(m, j - self.begins[m])

    def left_load(self, m, i, j):
        lines = pl.ds(pl.multiple_of(self.plans[m][3](i) * CR, CR), CR)
        slot = lax.rem(j, 2)
        return pltpu.make_async_copy(self.lefts[m].at[:, lines], self.left.at[slot], self.left_sem.at[slot])

    def right_slot(self, m, i):
        return lax.rem(self.groups[m] + i // self.plans[m][1], 2)

    def right_loads(self, m, i):
        first, slot = self.plans[m][4](i), self.right_slot(m, i)
        count = 2 if self.kinds[m] == "keyval" else 1
        copies = []
        for n in range(count):
            lines = pl.ds(pl.multiple_of((first + n) * CC, CC), CC)
            where = slot if count == 1 else n
            copies.append(
                pltpu.make_async_copy(self.rights[m].at[:, lines], self.right.at[where], self.right_sem.at[where])
            )
        return copies

    def fetch(self, j, early=True):
        def action(m, i):
            late = self.kinds[m] == "keyval"
            if not late and self.kinds[m] != "query" and early:
                self.left_load(m, i, j).start()
            if late != early:

                @pl.when(lax.rem(i, self.plans[m][1]) == 0)
                def _():
                    for c in self.right_loads(m, i):
                        c.start()

        self.each(j, action)

    def produce(self, j):
        slot = lax.rem(j, RING)

        def action(m, i):
            @pl.when(lax.rem(i, self.plans[m][1]) == 0)
            def _():
                for c in self.right_loads(m, i):
                    c.wait()

            if self.kinds[m] == "query":
                n = CC // 2
                for h in range(2):
                    block = self.right[self.right_slot(m, i), :, h * n : (h + 1) * n]
                    self.own[slot, :, h * n : (h + 1) * n] = contract(block, self.lefts[m][:, :n], 0, 0).astype(BF)
            elif self.kinds[m] == "keyval":
                n = CC // 4
                start = CC // 2
                for h in range(2):
                    for g in range(4):
                        block = self.right[h, :, g * n : (g + 1) * n]
                        part = contract(block, self.lefts[m][:, start : start + n], 0, 0)
                        self.own[slot, h * HR : (h + 1) * HR, g * n : (g + 1) * n] = part.astype(BF)
            else:
                self.left_load(m, i, j).wait()
                right = self.right[self.right_slot(m, i)]
                self.own[slot] = contract(self.left[lax.rem(j, 2)], right, 0, 0).astype(BF)

        self.each(j, action)

    def spread(self, j, half, src):
        slot = lax.rem(j, RING)

        def action(m, i):
            s = self.plans[m][2](i)
            r, q = self.plans[m][6](self.col, i)
            if self.kinds[m] == "keyval":
                s = s + half
            else:
                r = r + half * HR
            dst = self.outs[m].at[pl.ds(pl.multiple_of(r, HR), HR), pl.ds(pl.multiple_of(q, CC), CC)]

            @pl.when(s == 0)
            def _():
                pltpu.make_async_copy(src, dst, self.far_send.at[slot, half]).start()

            @pl.when(s > 0)
            def _():
                owner = lax.rem(lax.rem(self.col, 2) + lax.rem(s, 2), 2) + 2 * lax.rem(self.col // 2 + s // 2, 2)
                remote(src, dst, self.far_send.at[slot, half], self.far_recv.at[m], col=owner).start()

        self.each(j, action)

    def reclaim(self, j):
        slot = lax.rem(j, RING)
        for half in range(2):
            done(self.mids.at[slot], self.far_send.at[slot, half])

        @pl.when(self.is_mid)
        def _():
            done(self.mids.at[slot], self.mid_send.at[slot])
            done(self.mids.at[slot], self.top_send.at[slot])
            for half in range(2):
                done(self.mids.at[slot], self.out_send.at[slot, half])

        @pl.when(self.is_end)
        def _():
            done(self.own.at[slot], self.in_send.at[slot])

    def inbound(self, j):
        slot = lax.rem(j, RING)

        @pl.when(self.is_mid)
        def _():
            done(self.land.at[slot], self.in_recv.at[slot])
            self.own[slot] = (self.own[slot].astype(F32) + self.land[slot].astype(F32)).astype(BF)
            src = self.own.at[slot, self.rows(1 - self.kept)]
            remote(src, self.mids.at[slot], self.mid_send.at[slot], self.mid_recv.at[slot], **self.inward).start()

        @pl.when(self.is_end)
        def _():
            remote(
                self.own.at[slot], self.land.at[slot], self.in_send.at[slot], self.in_recv.at[slot], **self.inward
            ).start()

    def middle(self, j):
        slot = lax.rem(j, RING)

        @pl.when(self.is_mid)
        def _():
            done(self.mids.at[slot], self.mid_recv.at[slot])
            rows = self.rows(self.kept)
            self.own[slot, rows] = (self.own[slot, rows].astype(F32) + self.mids[slot].astype(F32)).astype(BF)
            src = self.own.at[slot, rows]
            remote(src, self.tops.at[slot], self.top_send.at[slot], self.top_recv.at[slot], **self.inward).start()
            remote(
                src, self.land.at[slot, rows], self.out_send.at[slot, self.kept], self.out_recv.at[slot, self.kept],
                **self.outward,
            ).start()
            self.spread(j, self.kept, src)

    def settle(self, j):
        slot = lax.rem(j, RING)

        @pl.when(self.is_mid)
        def _():
            done(self.tops.at[slot], self.top_recv.at[slot])
            half = 1 - self.kept
            src = self.tops.at[slot]
            remote(
                src, self.land.at[slot, self.rows(half)], self.out_send.at[slot, half], self.out_recv.at[slot, half],
                **self.outward,
            ).start()
            self.spread(j, half, src)

    def outbound(self, j):
        slot = lax.rem(j, RING)

        @pl.when(self.is_end)
        def _():
            for half in range(2):
                src = self.land.at[slot, pl.ds(half * HR, HR)]
                done(src, self.out_recv.at[slot, half])
                self.spread(j, half, src)

    def begin(self):
        self.fetch(jnp.int32(0))
        self.produce(jnp.int32(0))
        self.fetch(jnp.int32(1))

    def tick(self, t):
        for off, stage in zip(OFFS, (self.inbound, self.middle, self.settle, self.outbound)):

            @pl.when((t >= off) & (t < self.total + off))
            def _(off=off, stage=stage):
                stage(t - off)

        ahead = t + 1

        @pl.when(ahead < self.total)
        def _():
            @pl.when(ahead >= RING)
            def _():
                self.reclaim(ahead - RING)

            self.fetch(ahead, False)
            self.produce(ahead)

            @pl.when(ahead + 1 < self.total)
            def _():
                self.fetch(ahead + 1)

    def finish(self):
        def drain(j, carry):
            self.reclaim(j)
            return carry

        lax.fori_loop(self.total - RING, self.total, drain, 0)
        for m, out in enumerate(self.outs):
            done(out.at[pl.ds(0, 3 * out.shape[0] // 4)], self.far_recv.at[m])


MB = 128
AQ, AK = 256, 512


def backward_kernel(
    kinds,
    info_ref, gain_ref, mlp_ref, gate_ref, up_ref, hidden_ref, part_ref, low_part_ref, resid_ref, low_ref, w_ref, mixed_ref,
    wide_ref, normed_ref, x_ref, q_ref, k_ref, v_ref, lse_ref, turn_ref, wq_ref, wkv_ref,
    out_gate, out_up, out_down, out_out, out_query, out_keyval, mid_out, gain_part, attn_out, down_out, dot_out,
    cot_full, attn_part, mid_low,
    *refs,
):
    refs = list(refs)

    def take(count):
        taken = refs[:count]
        del refs[:count]
        return taken

    zsum = GroupSum(
        kinds,
        [hidden_ref, mlp_ref, mlp_ref, mixed_ref, refs[0], refs[0]],
        [low_ref, gate_ref, up_ref, mid_low, normed_ref, normed_ref],
        [out_down, out_gate, out_up, out_out, out_query, out_keyval],
        refs[1:19],
    )
    heads_cot = refs[0]
    del refs[:19]
    scratch = take(5)
    mlp_reduce = Reduce(part_ref, scratch, take(7))
    low_reduce = Reduce(low_part_ref, scratch, take(7))
    attn_reduce = Reduce(attn_part, scratch, take(7))
    mine, = take(1)
    tok, width = mine.shape
    gather = Gather(mine, cot_full, token_place(tok, width), None, take(Gather.SEMS))
    bufs, resid_buf, out_buf, buf_sem, out_sem = take(5)
    mixed_cot, wide_buf, dq_sum, dk_sum, dv_sum, dots, dots_mate, dots_col = take(8)
    dot_send, dot_recv, ready, w_mine, w_sem = take(5)
    span = 2 * tok
    heads_width = q_ref.shape[1]
    heads = heads_width // HD
    half = lax.axis_index("row")
    col = lax.axis_index("col")
    length = info_ref[0]
    near_x, near_y, mate = plane_peers()
    corner = {"col": 3 - col}
    blocks = span // MB

    def mid_loads(i):
        slot = lax.rem(i, 2)
        lines = pl.ds(pl.multiple_of(i * MB, MB), MB)
        return [
            pltpu.make_async_copy(cot_full.at[lines, :], bufs.at[slot, 0], buf_sem.at[slot, 0]),
            pltpu.make_async_copy(low_ref.at[lines, :], bufs.at[slot, 1], buf_sem.at[slot, 1]),
            pltpu.make_async_copy(resid_ref.at[lines, :], resid_buf.at[slot], buf_sem.at[slot, 2]),
        ]

    def row_store(out, i):
        lines = pl.ds(pl.multiple_of(i * MB, MB), MB)
        return pltpu.make_async_copy(bufs.at[lax.rem(i, 2), 2], out.at[lines, :], out_sem.at[1])

    def mid_store(i):
        lines = pl.ds(pl.multiple_of(i * MB, MB), MB)
        return pltpu.make_async_copy(out_buf.at[:, pl.ds(0, width)], mid_out.at[lines, :], out_sem.at[0])

    def mid_item(i):
        slot = lax.rem(i, 2)

        @pl.when(i + 1 < blocks)
        def _():
            for c in mid_loads(i + 1):
                c.start()

        for c in mid_loads(i):
            c.wait()
        cot = bufs[slot, 0].astype(F32)
        resid = resid_buf[slot]
        scale = lax.rsqrt(jnp.mean(resid * resid, axis=1, keepdims=True) + EPSILON)
        weighed = cot * gain_ref[1:2, :]
        inner = jnp.sum(weighed * resid, axis=1, keepdims=True)
        mid = bufs[slot, 1].astype(F32) + weighed * scale - resid * (scale * scale * scale * inner / D)
        low = mid.astype(BF)
        lines = pl.ds(pl.multiple_of(i * MB, MB), MB)
        mixed_cot[lines, :] = contract(low, w_mine[...], 1, 1).astype(BF)

        @pl.when(i > 0)
        def _():
            row_store(mid_low, i - 1).wait()

        bufs[slot, 2] = low
        row_store(mid_low, i).start()

        @pl.when(i < blocks // 2)
        def _():
            @pl.when(i > 0)
            def _():
                mid_store(i - 1).wait()

            out_buf[:, pl.ds(0, width)] = mid[:, :width]
            mid_store(i).start()
            part = jnp.sum((cot * resid * scale)[:, :width], axis=0, keepdims=True)
            gain_part[...] += jnp.broadcast_to(part, gain_part.shape)

        @pl.when(i == blocks // 2)
        def _():
            mid_store(i - 1).wait()

    q_steps = span // AQ
    rows = heads * AQ
    pieces = [slice(h * HD, (h + 1) * HD) for h in range(heads)]

    def attn_item(q_step, tile, diagonal):
        stored = lax.rem(q_step + half * (q_steps // 2), q_steps)
        lines = pl.ds(pl.multiple_of(stored * AQ, AQ), AQ)
        key_tiles = span // AK
        keys = pl.ds(pl.multiple_of(lax.rem(tile + half * (key_tiles // 2), key_tiles) * AK, AK), AK)
        first = q_step * AQ
        q = jnp.concatenate([q_ref[lines, s] for s in pieces], axis=0)
        cot = jnp.concatenate([mixed_cot[lines, s] for s in pieces], axis=0)
        wide = jnp.concatenate([wide_buf[:, s] for s in pieces], axis=0)
        place = first + lax.rem(lax.broadcasted_iota(jnp.int32, (1, rows), 1), AQ)
        log_total = jnp.where(place < length, lse_ref[q_step], -NEG_FILL)
        inner = jnp.sum(wide * cot.astype(F32), axis=1, keepdims=True)
        inner = jnp.broadcast_to(inner, (rows, LANES)).T[0:1, :]
        k_tile = k_ref[keys, :]
        v_tile = v_ref[keys, :]
        scores = contract(k_tile, q, 1, 1) * HD**-0.5 - log_total
        if diagonal:
            key_place = tile * AK + lax.broadcasted_iota(jnp.int32, (AK, rows), 0)
            scores = jnp.where(key_place <= place, scores, NEG_FILL)
        weights = jnp.exp(scores)
        prob_cot = contract(v_tile, cot, 1, 1)
        score_cot = (weights * (prob_cot - inner)).astype(BF)
        dv_sum[keys, :] += contract(weights.astype(BF), cot, 1, 0)
        dk_sum[keys, :] += contract(score_cot, q, 1, 0) * HD**-0.5
        dq = contract(score_cot, k_tile, 0, 0) * HD**-0.5

        @pl.when(tile == 0)
        def _():
            dq_sum[...] = dq

        @pl.when(tile > 0)
        def _():
            dq_sum[...] += dq

        if diagonal:
            cos, sin = turn_ref[lines, :HD], turn_ref[lines, HD:]
            for h in range(heads):
                part = dq_sum[h * AQ : (h + 1) * AQ, :]
                swapped = jnp.concatenate([part[:, HD // 2 :], -part[:, : HD // 2]], axis=1)
                heads_cot[lines, h * HD : (h + 1) * HD] = (part * cos + swapped * sin).astype(BF)

    starts = [0]
    for n in range(q_steps):
        starts.append(starts[-1] + n * AQ // AK + 1)
    attn_items = starts.pop()

    def wide_load(q_step):
        stored = lax.rem(q_step + half * (q_steps // 2), q_steps)
        lines = pl.ds(pl.multiple_of(stored * AQ, AQ), AQ)
        return pltpu.make_async_copy(wide_ref.at[lines, :], wide_buf, w_sem.at[1])

    def attn_one(n):
        q_step = sum([jnp.where(n >= start, 1, 0) for start in starts[1:]], jnp.int32(0))
        tile = n - sum([jnp.where(n >= b, b - a, 0) for a, b in zip(starts, starts[1:])], jnp.int32(0))
        last = q_step * AQ // AK

        @pl.when(tile == 0)
        def _():
            wide_load(q_step).wait()

        @pl.when(tile < last)
        def _():
            attn_item(q_step, tile, False)

        @pl.when(tile == last)
        def _():
            attn_item(q_step, tile, True)

            @pl.when(q_step + 1 < q_steps)
            def _():
                wide_load(q_step + 1).start()

    def attn_finish():
        part = dk_sum[...]
        swapped = jnp.concatenate([part[:, HD // 2 :], -part[:, : HD // 2]], axis=1)
        heads_cot[:, heads_width : heads_width + HD] = (part * turn_ref[:, :HD] + swapped * turn_ref[:, HD:]).astype(BF)
        heads_cot[:, heads_width + HD : heads_width + 2 * HD] = dv_sum[...].astype(BF)

    def head_load(i):
        slot = lax.rem(i, 2)
        lines = pl.ds(pl.multiple_of(i * MB, MB), MB)
        return pltpu.make_async_copy(x_ref.at[lines, :], bufs.at[slot, 1], buf_sem.at[slot, 1])

    def head_item(i):
        slot = lax.rem(i, 2)

        @pl.when(i + 1 < blocks)
        def _():
            head_load(i + 1).start()

        head_load(i).wait()
        lines = pl.ds(pl.multiple_of(i * MB, MB), MB)
        part = contract(heads_cot[lines, :heads_width], wq_ref[...], 1, 1)
        part += contract(heads_cot[lines, heads_width : heads_width + 2 * HD], wkv_ref[...], 1, 1)

        @pl.when(i > 0)
        def _():
            row_store(attn_part, i - 1).wait()

        bufs[slot, 2] = part.astype(BF)
        row_store(attn_part, i).start()
        inner = jnp.sum(part * gain_ref[0:1, :] * bufs[slot, 1].astype(F32), axis=1, keepdims=True)
        dots[pl.ds(i, 1), :] = jnp.broadcast_to(inner, (MB, LANES)).T[0:1, :]

    def dot_give():
        n = blocks // 2
        return remote(dots.at[pl.ds(n, n), :], dots_mate, dot_send.at[0], dot_recv.at[0], **mate)

    def dot_share():
        n = blocks // 2
        return [
            remote(dots.at[pl.ds(0, n), :], dots_col.at[s], dot_send.at[1 + s], dot_recv.at[1 + s], **peer)
            for s, peer in enumerate((near_x, near_y, corner))
        ]

    def emit(work, out, sem):
        for a in range(2):
            sum_total = work.total(a)
            h = tok // 4
            for b in range(2):
                lines = pl.ds(a * 2 * h + b * h, h)
                resid_sum = sum_total[b * h : (b + 1) * h]
                emit_buf[...] = resid_sum
                c = pltpu.make_async_copy(emit_buf, out.at[lines, :], sem)
                c.start()
                c.wait()

    emit_buf, = take(1)

    pltpu.make_async_copy(w_ref.at[pl.ds(pl.multiple_of(col * heads_width, heads_width), heads_width), :], w_mine, w_sem.at[0]).start()
    gain_part[...] = jnp.zeros_like(gain_part)
    zsum.begin()
    dk_sum[...] = jnp.zeros_like(dk_sum)
    dv_sum[...] = jnp.zeros_like(dv_sum)
    zsum.greet([near_x, near_y, corner, mate])

    at = {}

    def plan(tick, action):
        at.setdefault(tick, []).append(action)

    def start_all(copies):
        for c in copies:
            c.start()

    plan(0, mlp_reduce.begin)
    plan(T_ONE, lambda: [mlp_reduce.first(a) for a in range(2)])
    plan(T_TWO, lambda: [mlp_reduce.second(a) for a in range(2)])

    def own_block():
        for a in range(2):
            mine[mlp_reduce.lines(a), :] = mlp_reduce.total(a).astype(BF)
        gather.begin()

    plan(T_SUM, own_block)
    plan(T_GATHER, gather.first)
    plan(T_GATHER + 3, gather.second)

    def start_mid():
        gather.finish()
        mlp_reduce.finish()
        pltpu.make_async_copy(w_ref.at[pl.ds(0, heads_width), :], w_mine, w_sem.at[0]).wait()
        start_all(mid_loads(jnp.int32(0)))
        low_reduce.begin()

    plan(T_MID, start_mid)
    plan(T_MID + 4, lambda: [low_reduce.first(a) for a in range(2)])
    plan(T_MID + 9, lambda: [low_reduce.second(a) for a in range(2)])

    def low_done():
        emit(low_reduce, down_out, out_sem.at[2])
        low_reduce.finish()
        for i, peer in enumerate((near_x, near_y, mate)):
            pl.semaphore_signal(ready.at[i], inc=1, device_id=peer, device_id_type=MESH)

    plan(T_MID + 13, low_done)
    t_attn = T_MID + 1 + blocks // N_MID
    plan(t_attn, lambda: (row_store(mid_low, blocks - 1).wait(), wide_load(jnp.int32(0)).start()))
    t_head = t_attn + 1 + attn_items // N_ATTN
    plan(t_head, lambda: (attn_finish(), head_load(jnp.int32(0)).start()))
    t_last = t_head + 1 + blocks // N_HEAD

    def start_last():
        row_store(attn_part, blocks - 1).wait()
        dot_give().start()
        for i in range(3):
            pl.semaphore_wait(ready.at[i], 1)
        attn_reduce.begin()

    plan(t_last, start_last)

    def last_first():
        n = blocks // 2
        done(dots_mate, dot_recv.at[0])
        dot_give().wait_send()
        dots[pl.ds(0, n), :] = dots[pl.ds(0, n), :] + dots_mate[...]
        start_all(dot_share())
        for a in range(2):
            attn_reduce.first(a)

    plan(t_last + 3, last_first)
    plan(t_last + 7, lambda: [attn_reduce.second(a) for a in range(2)])

    def last_done():
        n = blocks // 2
        shares = dot_share()
        for c in shares:
            c.wait()
        terms = [dots[pl.ds(0, n), :], dots_col[0], dots_col[1], dots_col[2]]
        dot_out[...] = (terms[0] + terms[1]) + (terms[2] + terms[3])
        emit(attn_reduce, attn_out, out_sem.at[2])
        attn_reduce.finish()

    plan(t_last + 10, last_done)
    final = max(zsum.total + OFFS[3], t_last + 11)

    def tick(t, carry):
        zsum.tick(t)
        for when in sorted(at):

            @pl.when(t == when)
            def _(when=when):
                for action in at[when]:
                    action()

        @pl.when((t > T_MID) & (t < t_attn))
        def _():
            for e in range(N_MID):
                mid_item((t - T_MID - 1) * N_MID + e)

        @pl.when((t > t_attn) & (t < t_head))
        def _():
            def body(e, carry):
                attn_one((t - t_attn - 1) * N_ATTN + e)
                return carry

            lax.fori_loop(0, N_ATTN, body, 0)

        @pl.when((t > t_head) & (t < t_last))
        def _():
            for e in range(N_HEAD):
                head_item((t - t_head - 1) * N_HEAD + e)

        return carry

    lax.fori_loop(0, final, tick, 0)
    zsum.finish()


T_ONE, T_TWO, T_SUM, T_GATHER, T_MID = 2, 7, 10, 12, 19
N_MID, N_ATTN, N_HEAD = 2, 2, 4


def backward(info, gains, normed_mlp, gate_cot, up_cot, hidden, mlp_part, low_part, resid, low, w_out_full, mixed, q, k, v, wide, lse, cos, sin,
             wq, wkv, normed, tokens_full, cid):
    span, full = normed.shape
    tok, width = span // 2, full // 4
    heads_width = mixed.shape[1]
    heads = heads_width // HD
    units = hidden.shape[1]
    kinds = ["rows", "columns", "columns", "rows", "query", "keyval"]
    sources = [(units, full), (full, units), (full, units), (heads_width, full), (CC, full), (CC, full)]
    outs = [jax.ShapeDtypeStruct(grad_plan(kd, s)[5], BF) for kd, s in zip(kinds, sources)]
    outs = [outs[i] for i in (1, 2, 0, 3, 4, 5)]
    vmem = pl.BlockSpec(memory_space=pltpu.VMEM)
    dma = pltpu.SemaphoreType.DMA
    blocks = span // MB
    turn = jnp.concatenate([cos, sin], axis=1)
    lse = lse.reshape(span // QB, heads, QB // AQ, AQ).transpose(0, 2, 1, 3).reshape(span // AQ, 1, heads * AQ)
    shapes = outs + [
        jax.ShapeDtypeStruct((tok, width), F32),
        jax.ShapeDtypeStruct((8, width), F32),
        jax.ShapeDtypeStruct((tok, width), F32),
        jax.ShapeDtypeStruct((tok, width), F32),
        jax.ShapeDtypeStruct((blocks // 2, LANES), F32),
        jax.ShapeDtypeStruct((span, full), BF),
        jax.ShapeDtypeStruct((span, full), BF),
        jax.ShapeDtypeStruct((span, full), BF),
    ]
    out_specs = [ANY] * 6 + [ANY, vmem, ANY, ANY, vmem, ANY, ANY, ANY]
    scratch = (
        [pltpu.VMEM((span, heads_width + 2 * HD), BF)]
        + GroupSum.scratch(kinds, span)
        + Reduce.scratch(tok, full)
        + Reduce.sems() * 3
        + [pltpu.VMEM((tok, width), BF)]
        + Gather.sems()
        + [
            pltpu.VMEM((2, 3, MB, full), BF),
            pltpu.VMEM((2, MB, full), F32),
            pltpu.VMEM((MB, width), F32),
            dma((2, 3)),
            dma((3,)),
            pltpu.VMEM((span, heads_width), BF),
            pltpu.VMEM((AQ, heads_width), F32),
            pltpu.VMEM((heads * AQ, HD), F32),
            pltpu.VMEM((span, HD), F32),
            pltpu.VMEM((span, HD), F32),
            pltpu.VMEM((blocks, LANES), F32),
            pltpu.VMEM((blocks // 2, LANES), F32),
            pltpu.VMEM((3, blocks // 2, LANES), F32),
            dma((4,)),
            dma((4,)),
            pltpu.SemaphoreType.REGULAR((3,)),
            pltpu.VMEM((heads_width, full), BF),
            dma((2,)),
            pltpu.VMEM((tok // 4, width), F32),
        ]
    )
    results = pl.pallas_call(
        functools.partial(backward_kernel, kinds),
        in_specs=[pl.BlockSpec(memory_space=pltpu.SMEM), vmem] + [ANY] * 13 + [vmem] * 7,
        out_specs=out_specs,
        out_shape=shapes,
        scratch_shapes=scratch,
        compiler_params=pltpu.CompilerParams(
            collective_id=cid, has_side_effects=True, vmem_limit_bytes=VMEM_ALL
        ),
        name="backward",
    )(info, gains, normed_mlp, gate_cot, up_cot, hidden, mlp_part, low_part, resid, low, w_out_full, mixed, wide, normed,
      tokens_full, q, k, v, lse, turn, wq, wkv)
    return results[:11]


def by_distance(stacked, dim):
    count = lax.axis_size("col")
    order = lax.axis_index("col") ^ jnp.arange(count)
    blocks = jnp.take(stacked, order, axis=0)
    return jnp.concatenate([blocks[i] for i in range(count)], axis=dim)


def plain_gather(x):
    cols = by_distance(lax.all_gather(x, "col"), 1)
    return jnp.concatenate([cols, swap(cols, "row", 1)], axis=0)


def plain_gather_heads(x):
    mine = lax.all_gather(x, "col", axis=1, tiled=True)
    half = x.shape[0] // 2
    other = swap(mine, "row", 1)
    other = jnp.concatenate([other[half:], other[:half]], axis=0)
    return jnp.concatenate([mine, other], axis=1)


def plain_reduce(part):
    span, full = part.shape
    count = lax.axis_size("col")
    width = full // count
    half = part[: span // 2].astype(F32) + swap(part[span // 2 :], "row", 1).astype(F32)
    order = lax.axis_index("col") ^ jnp.arange(count)
    blocks = jnp.stack([half[:, s * width : (s + 1) * width] for s in range(count)])
    return lax.psum_scatter(jnp.take(blocks, order, axis=0), "col", tiled=False)


def exchange(packs):
    if kernels_fit():
        return [p if s == 0 else swap(p, "col", s) for s, p in enumerate(packs)]
    count = len(packs)
    order = lax.axis_index("col") ^ jnp.arange(count)
    sent = jnp.take(jnp.stack(packs), order, axis=0)
    blocks = jnp.take(lax.all_to_all(sent, "col", 0, 0, tiled=True), order, axis=0)
    return [blocks[i] for i in range(count)]


def plain_group_sum(grads, kinds):
    outs = []
    count = lax.axis_size("col")
    order = lax.axis_index("col") ^ jnp.arange(count)
    for grad, kind in zip(grads, kinds):
        grad = lax.psum(grad.astype(F32), "dp").astype(BF)
        dim = 1 if kind == "rows" else 0
        blocks = jnp.stack(jnp.split(grad, count, axis=dim))
        blocks = lax.all_to_all(jnp.take(blocks, order, axis=0), "col", 0, 0, tiled=True)
        out_dim = 1 if kind == "columns" else 0
        outs.append(jnp.concatenate([blocks[i] for i in range(count)], axis=out_dim))
    return outs


def kernels_fit():
    return lax.axis_size("col") == 4 and lax.axis_size("dp") == 4 and lax.axis_size("row") == 2


def attn_forward_kernel(info_ref, q_ref, k_ref, v_ref, *refs):
    linked = len(refs) > 6
    if linked:
        side_ref, mixed_ref, wide_ref, lse_ref, peak_ref, side_out, score_ref, sum_ref, stage = refs[:9]
        gather = Gather(side_ref, side_out, token_place(*side_ref.shape), stage, refs[9:])
    else:
        mixed_ref, wide_ref, lse_ref, peak_ref, score_ref, sum_ref = refs
    heads = q_ref.shape[1] // HD
    span = k_ref.shape[0]
    rows = heads * QB
    length = info_ref[0]
    half = lax.axis_index("row")
    step = pl.program_id(0)
    first = step * QB
    key_tiles = span // FWD_KB
    steps = span // QB
    lines = pl.ds(pl.multiple_of(lax.rem(step + half * (steps // 2), steps) * QB, QB), QB)

    if linked:

        @pl.when(step == 0)
        def _():
            greet(list(gather.near))
            gather.begin()

        @pl.when(step == steps - 1)
        def _():
            gather.first()

    q = jnp.concatenate([q_ref[lines, h * HD : (h + 1) * HD] for h in range(heads)], axis=0)
    tiles = (first + QB) // FWD_KB
    plain = first // FWD_KB

    def tile_of(ref, tile):
        stored = lax.rem(tile + half * (key_tiles // 2), key_tiles)
        return ref[pl.ds(pl.multiple_of(stored * FWD_KB, FWD_KB), FWD_KB), :]

    def fold(values, running, op):
        for t in range(FWD_KB // LANES):
            running = op(running, values[:, t * LANES : (t + 1) * LANES])
        return running

    def scores_of(tile, top, diagonal):
        scores = contract(q, tile_of(k_ref, tile), 1, 1) * HD**-0.5
        if diagonal:
            place = first + lax.broadcasted_iota(jnp.int32, (QB, FWD_KB), 0)
            key_place = tile * FWD_KB + lax.broadcasted_iota(jnp.int32, (QB, FWD_KB), 1)
            allowed = (key_place <= place) & (key_place < length)
            scores = jnp.where(allowed[None], scores.reshape(heads, QB, FWD_KB), NEG_FILL)
            scores = scores.reshape(rows, FWD_KB)
        else:
            key_place = tile * FWD_KB + lax.broadcasted_iota(jnp.int32, (1, FWD_KB), 1)
            scores = jnp.where(key_place < length, scores, NEG_FILL)
        score_ref[tile] = scores
        return fold(scores, top, jnp.maximum)

    top = jnp.full((rows, LANES), NEG_FILL, F32)
    top = lax.fori_loop(0, plain, lambda tile, top: scores_of(tile, top, False), top)
    top = lax.fori_loop(plain, tiles, lambda tile, top: scores_of(tile, top, True), top)
    top = jnp.max(top, axis=1, keepdims=True)
    live = first + lax.broadcasted_iota(jnp.int32, (QB, 1), 0) < length
    peak = jnp.max(jnp.where(live[None], top.reshape(heads, QB, 1), NEG_FILL), axis=1)

    @pl.when(step == 0)
    def _():
        peak_ref[...] = jnp.full_like(peak_ref, NEG_FILL)

    peak_ref[...] = jnp.maximum(peak_ref[...], jnp.broadcast_to(peak, peak_ref.shape))
    sum_ref[...] = jnp.zeros_like(sum_ref)

    def weigh(tile, total):
        weights = jnp.exp(score_ref[tile] - top)
        sum_ref[...] += contract(weights.astype(BF), tile_of(v_ref, tile), 1, 0)
        return fold(weights, total, jnp.add)

    total = lax.fori_loop(0, tiles, weigh, jnp.zeros((rows, LANES), F32))
    total = jnp.sum(total, axis=1, keepdims=True)
    mixed = sum_ref[...] / total
    log_total = jnp.broadcast_to(top + jnp.log(total), (rows, LANES))
    lse_ref[step] = log_total.T[0:1, :]
    for h in range(heads):
        part = mixed[h * QB : (h + 1) * QB]
        mixed_ref[lines, h * HD : (h + 1) * HD] = part.astype(BF)
        wide_ref[lines, h * HD : (h + 1) * HD] = part

    if linked:

        @pl.when(step == steps - 1)
        def _():
            gather.second()
            gather.finish()


def attn_forward(info, q, k, v, side=None, cid=None):
    span, width = q.shape
    heads = width // HD
    steps = span // QB
    whole = lambda shape: pl.BlockSpec(shape, lambda i: (0,) * len(shape))
    pairs = heads * span * span // 2
    shapes = [
        jax.ShapeDtypeStruct((span, width), BF),
        jax.ShapeDtypeStruct((span, width), F32),
        jax.ShapeDtypeStruct((steps, 1, heads * QB), F32),
        jax.ShapeDtypeStruct((heads, LANES), F32),
    ]
    in_specs = [pl.BlockSpec(memory_space=pltpu.SMEM)] + [whole(a.shape) for a in (q, k, v)]
    out_specs = [whole(s.shape) for s in shapes]
    scratch = [
        pltpu.VMEM((span // FWD_KB, heads * QB, FWD_KB), F32),
        pltpu.VMEM((heads * QB, HD), F32),
    ]
    operands = [info, q, k, v]
    params = dict(vmem_limit_bytes=48 * MIB)
    if side is not None:
        tok, wide = side.shape
        operands.append(side)
        in_specs.append(ANY)
        out_specs.append(ANY)
        shapes.append(jax.ShapeDtypeStruct((2 * tok, 4 * wide), side.dtype))
        scratch += [pltpu.VMEM(side.shape, side.dtype)] + Gather.sems()
        params.update(collective_id=cid, has_side_effects=True)
    return pl.pallas_call(
        attn_forward_kernel,
        grid=(steps,),
        in_specs=in_specs,
        out_specs=out_specs,
        scratch_shapes=scratch,
        out_shape=shapes,
        compiler_params=pltpu.CompilerParams(**params),
        cost_estimate=pl.CostEstimate(
            flops=40 * pairs * HD // 4, transcendentals=pairs, bytes_accessed=8 * span * width
        ),
        name="attn_forward",
    )(*operands)


def turn_back(values, cos_ref, sin_ref):
    half = HD // 2
    swapped = jnp.concatenate([values[:, half:], -values[:, :half]], axis=1)
    return values * cos_ref[...] + swapped * sin_ref[...]


def attn_backward_kernel(
    info_ref, q_ref, k_ref, v_ref, cot_ref, wide_ref, lse_ref, cosq_ref, sinq_ref, cosk_ref, sink_ref,
    dq_ref, dk_ref, dv_ref, dq_sum, dk_sum, dv_sum,
):
    heads = q_ref.shape[1] // HD
    span = k_ref.shape[0]
    rows = heads * QB
    length = info_ref[0]
    half = info_ref[1]
    step = pl.program_id(0)
    first = step * QB
    key_tiles = span // BWD_KB

    @pl.when(step == 0)
    def _():
        dk_sum[...] = jnp.zeros_like(dk_sum)
        dv_sum[...] = jnp.zeros_like(dv_sum)

    dq_sum[...] = jnp.zeros_like(dq_sum)

    @pl.when(first < length)
    def _():
        pieces = [slice(h * HD, (h + 1) * HD) for h in range(heads)]
        q = jnp.concatenate([q_ref[:, s] for s in pieces], axis=0)
        cot = jnp.concatenate([cot_ref[:, s] for s in pieces], axis=0)
        wide = jnp.concatenate([wide_ref[:, s] for s in pieces], axis=0)
        log_total = lse_ref[0]
        inner = jnp.sum(wide * cot.astype(F32), axis=1, keepdims=True)
        inner = jnp.broadcast_to(inner, (rows, LANES)).T[0:1, :]

        def tile_step(tile, masked):
            stored = lax.rem(tile + half * (key_tiles // 2), key_tiles)
            keys = pl.ds(pl.multiple_of(stored * BWD_KB, BWD_KB), BWD_KB)
            k_tile = k_ref[keys, :]
            v_tile = v_ref[keys, :]
            scores = contract(k_tile, q, 1, 1) * HD**-0.5 - log_total
            if masked:
                key_place = tile * BWD_KB + lax.broadcasted_iota(jnp.int32, (BWD_KB, rows), 0)
                place = first + lax.rem(lax.broadcasted_iota(jnp.int32, (BWD_KB, rows), 1), QB)
                scores = jnp.where((key_place <= place) & (key_place < length), scores, NEG_FILL)
            weights = jnp.exp(scores)
            prob_cot = contract(v_tile, cot, 1, 1)
            score_cot = (weights * (prob_cot - inner)).astype(BF)
            dv_sum[keys, :] += contract(weights.astype(BF), cot, 1, 0)
            dk_sum[keys, :] += contract(score_cot, q, 1, 0) * HD**-0.5
            dq_sum[...] += contract(score_cot, k_tile, 0, 0) * HD**-0.5

        @pl.loop(0, first // BWD_KB)
        def _(tile):
            tile_step(tile, False)

        @pl.loop(first // BWD_KB, pl.cdiv(first + QB, BWD_KB))
        def _(tile):
            tile_step(tile, True)

    for h in range(heads):
        part = turn_back(dq_sum[h * QB : (h + 1) * QB, :], cosq_ref, sinq_ref)
        dq_ref[:, h * HD : (h + 1) * HD] = part.astype(dq_ref.dtype)

    @pl.when(step == pl.num_programs(0) - 1)
    def _():
        dk_ref[...] = turn_back(dk_sum[...], cosk_ref, sink_ref).astype(dk_ref.dtype)
        dv_ref[...] = dv_sum[...].astype(dv_ref.dtype)


def attn_backward(info, q, k, v, cot, wide, lse, cos, sin, kv_type):
    span, width = q.shape
    heads = width // HD
    steps = span // QB

    def stored(i, info_ref):
        return (lax.rem(i + info_ref[1] * (steps // 2), steps), 0)

    whole = pl.BlockSpec((span, HD), lambda i, info_ref: (0, 0))
    mine = pl.BlockSpec((QB, width), stored)
    turn = pl.BlockSpec((QB, HD), stored)
    pairs = heads * span * span // 2
    return pl.pallas_call(
        attn_backward_kernel,
        grid_spec=pltpu.PrefetchScalarGridSpec(
            num_scalar_prefetch=1,
            grid=(steps,),
            in_specs=[
                mine, whole, whole, mine, mine,
                pl.BlockSpec((1, 1, heads * QB), lambda i, info_ref: (i, 0, 0)),
                turn, turn, whole, whole,
            ],
            out_specs=[mine, whole, whole],
            scratch_shapes=[
                pltpu.VMEM((heads * QB, HD), F32),
                pltpu.VMEM((span, HD), F32),
                pltpu.VMEM((span, HD), F32),
            ],
        ),
        out_shape=[
            jax.ShapeDtypeStruct((span, width), BF),
            jax.ShapeDtypeStruct((span, HD), kv_type),
            jax.ShapeDtypeStruct((span, HD), kv_type),
        ],
        compiler_params=pltpu.CompilerParams(vmem_limit_bytes=40 * 2**20),
        cost_estimate=pl.CostEstimate(
            flops=60 * pairs * HD // 4, transcendentals=pairs, bytes_accessed=12 * span * width
        ),
        name="attn_backward",
    )(info, q, k, v, cot, wide, lse, cos, sin, cos, sin)


def head_kernel(x_ref, gain_ref, wq_ref, wkv_ref, cos_ref, sin_ref, normed_ref, q_ref, k_ref, v_ref, scale_ref):
    x = x_ref[...].astype(F32)
    scale = lax.rsqrt(jnp.mean(x * x, axis=1, keepdims=True) + EPSILON)
    scale_ref[...] = jnp.broadcast_to(scale, scale_ref.shape)
    normed = (x * scale * gain_ref[0:1, :]).astype(BF)
    normed_ref[...] = normed

    def turned(raw):
        pieces = []
        half = HD // 2
        for h in range(raw.shape[1] // HD):
            pieces += [-raw[:, h * HD + half : (h + 1) * HD], raw[:, h * HD : h * HD + half]]
        pieces = jnp.concatenate(pieces, axis=1)
        count = raw.shape[1] // HD
        cos = jnp.concatenate([cos_ref[...]] * count, axis=1)
        sin = jnp.concatenate([sin_ref[...]] * count, axis=1)
        return (raw * cos + pieces * sin).astype(BF)

    q_ref[...] = turned(contract(normed, wq_ref[...], 1, 0))
    keyval = contract(normed, wkv_ref[...], 1, 0)
    k_ref[...] = turned(keyval[:, :HD])
    v_ref[...] = keyval[:, HD:].astype(BF)


def project_heads(tokens_full, gains, wq, wkv, cos, sin):
    span, full = tokens_full.shape
    width = wq.shape[1]
    block = 512
    line = lambda n: pl.BlockSpec((block, n), lambda i: (i, 0))
    whole = lambda a: pl.BlockSpec(a.shape, lambda i: (0, 0))
    return pl.pallas_call(
        head_kernel,
        grid=(span // block,),
        in_specs=[line(full), whole(gains), whole(wq), whole(wkv), line(HD), line(HD)],
        out_specs=[line(full), line(width), line(HD), line(HD), line(LANES)],
        out_shape=[
            jax.ShapeDtypeStruct((span, full), BF),
            jax.ShapeDtypeStruct((span, width), BF),
            jax.ShapeDtypeStruct((span, HD), BF),
            jax.ShapeDtypeStruct((span, HD), BF),
            jax.ShapeDtypeStruct((span, LANES), F32),
        ],
        compiler_params=pltpu.CompilerParams(vmem_limit_bytes=48 * MIB),
        cost_estimate=pl.CostEstimate(
            flops=2 * span * full * (width + LANES), transcendentals=0, bytes_accessed=5 * span * full
        ),
        name="project_heads",
    )(tokens_full, gains, wq, wkv, cos, sin)


def project_out_kernel(mixed_ref, w_ref, x_ref, gain_ref, *refs):
    linked = len(refs) > 2
    step = pl.program_id(0)
    if linked:
        side_ref, resid_ref, normed_ref, side_out, stage = refs[:5]
        gather = Gather(side_ref, side_out, token_place(*side_ref.shape), stage, refs[5:])

        @pl.when(step == 0)
        def _():
            greet(list(gather.near))
            gather.begin()

        @pl.when(step == pl.num_programs(0) // 2)
        def _():
            gather.first()

    else:
        resid_ref, normed_ref = refs
    resid = x_ref[...].astype(F32) + contract(mixed_ref[...], w_ref[...], 1, 0)
    resid_ref[...] = resid
    scale = lax.rsqrt(jnp.mean(resid * resid, axis=1, keepdims=True) + EPSILON)
    normed_ref[...] = (resid * scale * gain_ref[1:2, :]).astype(BF)

    if linked:

        @pl.when(step == pl.num_programs(0) - 1)
        def _():
            gather.second()
            gather.finish()


def project_out(mixed_full, w_out_full, tokens_full, gains, side=None, cid=None):
    span, full = tokens_full.shape
    block = 256
    line = pl.BlockSpec((block, full), lambda i: (i, 0))
    operands = [mixed_full, w_out_full, tokens_full, gains]
    in_specs = [
        pl.BlockSpec((block, mixed_full.shape[1]), lambda i: (i, 0)),
        pl.BlockSpec(w_out_full.shape, lambda i: (0, 0), pipeline_mode=pl.Buffered(1)),
        line,
        pl.BlockSpec(gains.shape, lambda i: (0, 0)),
    ]
    out_specs = [line, line]
    shapes = [jax.ShapeDtypeStruct((span, full), F32), jax.ShapeDtypeStruct((span, full), BF)]
    scratch = []
    params = dict(vmem_limit_bytes=48 * MIB)
    if side is not None:
        tok, wide = side.shape
        operands.append(side)
        in_specs.append(ANY)
        out_specs.append(ANY)
        shapes.append(jax.ShapeDtypeStruct((2 * tok, 4 * wide), side.dtype))
        scratch += [pltpu.VMEM(side.shape, side.dtype)] + Gather.sems()
        params.update(collective_id=cid, has_side_effects=True)
    return pl.pallas_call(
        project_out_kernel,
        grid=(span // block,),
        in_specs=in_specs,
        out_specs=out_specs,
        out_shape=shapes,
        scratch_shapes=scratch,
        compiler_params=pltpu.CompilerParams(**params),
        cost_estimate=pl.CostEstimate(
            flops=2 * span * full * full, transcendentals=0, bytes_accessed=12 * span * full
        ),
        name="project_out",
    )(*operands)


def middle_kernel(
    cot_ref, resid_ref, low_ref, gain_ref, w_ref, mixed_ref,
    mixed_cot_ref, own_ref, grad_ref, gain_part_ref, total_ref,
):
    step = pl.program_id(0)
    last = pl.num_programs(0) - 1
    width = own_ref.shape[1]
    cot = cot_ref[...].astype(F32)
    resid = resid_ref[...]
    scale = lax.rsqrt(jnp.mean(resid * resid, axis=1, keepdims=True) + EPSILON)
    weighed = cot * gain_ref[1:2, :]
    inner = jnp.sum(weighed * resid, axis=1, keepdims=True)
    mid = low_ref[...].astype(F32) + weighed * scale - resid * (scale * scale * scale * inner / D)
    low = mid.astype(BF)
    mixed_cot_ref[...] = contract(low, w_ref[...], 1, 1).astype(BF)

    @pl.when(step == 0)
    def _():
        total_ref[...] = jnp.zeros_like(total_ref)
        gain_part_ref[...] = jnp.zeros_like(gain_part_ref)

    total_ref[...] += contract(mixed_ref[...], low, 0, 0)

    @pl.when(step <= last // 2)
    def _():
        own_ref[...] = mid[:, :width]
        part = jnp.sum((cot * resid * scale)[:, :width], axis=0, keepdims=True)
        gain_part_ref[...] += jnp.broadcast_to(part, gain_part_ref.shape)

    @pl.when(step == last)
    def _():
        grad_ref[...] = total_ref[...].astype(BF)


def middle(mlp_cot, resid_mid, out_low, gains, w_mine, mixed, width):
    span, full = resid_mid.shape
    heads_width = mixed.shape[1]
    block = 256
    steps = span // block
    line = pl.BlockSpec((block, full), lambda i: (i, 0))
    thin = pl.BlockSpec((block, heads_width), lambda i: (i, 0))
    return pl.pallas_call(
        middle_kernel,
        grid=(steps,),
        in_specs=[
            line, line, line,
            pl.BlockSpec(gains.shape, lambda i: (0, 0)),
            pl.BlockSpec(w_mine.shape, lambda i: (0, 0)),
            thin,
        ],
        out_specs=[
            thin,
            pl.BlockSpec((block, width), lambda i: (jnp.minimum(i, steps // 2 - 1), 0)),
            pl.BlockSpec((heads_width, full), lambda i: (0, 0)),
            pl.BlockSpec((8, width), lambda i: (0, 0)),
        ],
        out_shape=[
            jax.ShapeDtypeStruct((span, heads_width), BF),
            jax.ShapeDtypeStruct((span // 2, width), F32),
            jax.ShapeDtypeStruct((heads_width, full), BF),
            jax.ShapeDtypeStruct((8, width), F32),
        ],
        scratch_shapes=[pltpu.VMEM((heads_width, full), F32)],
        compiler_params=pltpu.CompilerParams(vmem_limit_bytes=48 * MIB),
        cost_estimate=pl.CostEstimate(
            flops=4 * span * full * heads_width, transcendentals=0, bytes_accessed=8 * span * full
        ),
        name="middle",
    )(mlp_cot, resid_mid, out_low, gains, w_mine, mixed)


def head_back_kernel(
    info_ref, qc_ref, kc_ref, vc_ref, wq_ref, wkv_ref, normed_ref, x_ref, gain_ref,
    part_ref, dot_ref, grad_ref, total_ref,
):
    step = pl.program_id(0)
    wide = qc_ref.shape[1]
    keyval = jnp.concatenate([kc_ref[...], vc_ref[...]], axis=1)
    counted = keyval * info_ref[2].astype(BF)
    part = contract(qc_ref[...], wq_ref[...], 1, 1) + contract(counted, wkv_ref[...], 1, 1)
    part_ref[...] = part.astype(BF)
    inner = jnp.sum(part * gain_ref[0:1, :] * x_ref[...].astype(F32), axis=1, keepdims=True)
    dot_ref[0] = jnp.broadcast_to(inner, (inner.shape[0], LANES)).T[0:1, :]

    @pl.when(step == 0)
    def _():
        total_ref[...] = jnp.zeros_like(total_ref)

    total_ref[:, :wide] += contract(normed_ref[...], qc_ref[...], 0, 0)
    total_ref[:, wide:] += contract(normed_ref[...], keyval, 0, 0)

    @pl.when(step == pl.num_programs(0) - 1)
    def _():
        used = wide + 2 * HD
        grad_ref[:, :used] = total_ref[...].astype(BF)
        grad_ref[:, used:] = jnp.zeros((grad_ref.shape[0], grad_ref.shape[1] - used), BF)


def head_back(info, query_cot, key_cot, value_cot, wq, wkv, normed, tokens_full, gains):
    span, full = normed.shape
    wide = query_cot.shape[1]
    block = 512
    steps = span // block
    line = lambda n: pl.BlockSpec((block, n), lambda i, info_ref: (i, 0))
    whole = lambda shape: pl.BlockSpec(shape, lambda i, info_ref: (0, 0))
    grad_width = max(CC, wide + 2 * HD)
    return pl.pallas_call(
        head_back_kernel,
        grid_spec=pltpu.PrefetchScalarGridSpec(
            num_scalar_prefetch=1,
            grid=(steps,),
            in_specs=[
                line(wide), line(HD), line(HD), whole(wq.shape), whole(wkv.shape), line(full), line(full),
                whole(gains.shape),
            ],
            out_specs=[
                line(full),
                pl.BlockSpec((1, 1, block), lambda i, info_ref: (i, 0, 0)),
                whole((full, grad_width)),
            ],
            scratch_shapes=[pltpu.VMEM((full, wide + 2 * HD), F32)],
        ),
        out_shape=[
            jax.ShapeDtypeStruct((span, full), BF),
            jax.ShapeDtypeStruct((steps, 1, block), F32),
            jax.ShapeDtypeStruct((full, grad_width), BF),
        ],
        compiler_params=pltpu.CompilerParams(vmem_limit_bytes=48 * MIB),
        cost_estimate=pl.CostEstimate(
            flops=4 * span * full * (wide + LANES), transcendentals=0, bytes_accessed=6 * span * full
        ),
        name="head_back",
    )(info, query_cot, key_cot, value_cot, wq, wkv, normed, tokens_full, gains)


def fill_units(out, pieces, part, sem):
    mine = lax.rem(lax.axis_index("dp"), 2)
    rows = out.shape[0] // 8
    copies = []
    for s in range(4):
        for which, piece in ((mine, pieces[0]), (1 - mine, pieces[1])):
            lines = pl.ds(pl.multiple_of(s * 2 * rows + which * rows, rows), rows)
            src = piece.at[pl.ds((2 * s + part) * rows, rows), :]
            copies.append(pltpu.make_async_copy(src, out.at[lines, :], sem.at[len(copies)]))
    return copies


def hidden_kernel(x_ref, *refs):
    pieces = refs[:2]
    gate_ref, up_ref, hidden_ref, w_gate, w_up, gate_sem, up_sem = refs[2:]

    @pl.when(pl.program_id(0) == 0)
    def _():
        copies = fill_units(w_gate, pieces, 0, gate_sem) + fill_units(w_up, pieces, 1, up_sem)
        for c in copies:
            c.start()
        for c in copies:
            c.wait()

    gate = contract(x_ref[...], w_gate[...], 1, 0)
    gate_ref[...] = gate
    up = contract(x_ref[...], w_up[...], 1, 0)
    up_ref[...] = up
    hidden_ref[...] = (gate * jax.nn.sigmoid(gate) * up).astype(BF)


def hidden_units(normed, pieces):
    span, full = normed.shape
    units = pieces[0].shape[1]
    block = 256
    thin = pl.BlockSpec((block, units), lambda i: (i, 0))
    return pl.pallas_call(
        hidden_kernel,
        grid=(span // block,),
        in_specs=[pl.BlockSpec((block, full), lambda i: (i, 0))] + [ANY] * 2,
        out_specs=[thin] * 3,
        out_shape=[
            jax.ShapeDtypeStruct((span, units), F32),
            jax.ShapeDtypeStruct((span, units), F32),
            jax.ShapeDtypeStruct((span, units), BF),
        ],
        scratch_shapes=[
            pltpu.VMEM((full, units), BF),
            pltpu.VMEM((full, units), BF),
            pltpu.SemaphoreType.DMA((8,)),
            pltpu.SemaphoreType.DMA((8,)),
        ],
        compiler_params=pltpu.CompilerParams(vmem_limit_bytes=48 * MIB),
        cost_estimate=pl.CostEstimate(
            flops=4 * span * full * units, transcendentals=span * units, bytes_accessed=6 * span * full
        ),
        name="hidden_units",
    )(normed, *pieces)


def hidden_back_kernel(low_ref, gate_ref, up_ref, hidden_ref, own_ref, *refs):
    pieces, down_pieces = refs[:2], refs[2:5]
    gate_cot_ref, up_cot_ref, part_ref, low_part_ref, w_gate, w_up, w_down, gate_sem, up_sem, down_sem = refs[5:]
    units = w_down.shape[0]
    width = w_down.shape[1] // 4

    @pl.when(pl.program_id(0) == 0)
    def _():
        mine = own_ref.at[pl.ds(pl.multiple_of(lax.axis_index("col") * units, units), units), :]
        copies = [
            pltpu.make_async_copy(p, w_down.at[:, pl.ds(s * width, width)], down_sem.at[s])
            for s, p in enumerate((mine, *down_pieces))
        ]
        copies += fill_units(w_gate, pieces, 0, gate_sem) + fill_units(w_up, pieces, 1, up_sem)
        for c in copies:
            c.start()
        for c in copies:
            c.wait()

    hidden_cot = contract(low_ref[...], w_down[...], 1, 1)
    gate = gate_ref[...]
    sig = jax.nn.sigmoid(gate)
    gate_cot = (hidden_cot * up_ref[...] * sig * (1.0 + gate * (1.0 - sig))).astype(BF)
    up_cot = (hidden_cot * gate * sig).astype(BF)
    gate_cot_ref[...] = gate_cot
    up_cot_ref[...] = up_cot
    part = contract(gate_cot, w_gate[...], 1, 1) + contract(up_cot, w_up[...], 1, 1)
    part_ref[...] = part.astype(BF)
    low_part_ref[...] = contract(hidden_ref[...], w_down[...], 1, 0).astype(BF)


def hidden_back(low, gate, up, hidden, w_down, pieces, down_pieces):
    span, full = low.shape
    units = gate.shape[1]
    block = 256
    thin = pl.BlockSpec((block, units), lambda i: (i, 0))
    line = pl.BlockSpec((block, full), lambda i: (i, 0))
    return pl.pallas_call(
        hidden_back_kernel,
        grid=(span // block,),
        in_specs=[line, thin, thin, thin] + [ANY] * 6,
        out_specs=[thin, thin, line, line],
        out_shape=[jax.ShapeDtypeStruct((span, units), BF)] * 2 + [jax.ShapeDtypeStruct((span, full), BF)] * 2,
        scratch_shapes=[
            pltpu.VMEM((full, units), BF),
            pltpu.VMEM((full, units), BF),
            pltpu.VMEM((units, full), BF),
            pltpu.SemaphoreType.DMA((8,)),
            pltpu.SemaphoreType.DMA((8,)),
            pltpu.SemaphoreType.DMA((4,)),
        ],
        compiler_params=pltpu.CompilerParams(vmem_limit_bytes=VMEM_ALL),
        cost_estimate=pl.CostEstimate(
            flops=8 * span * full * units, transcendentals=span * units, bytes_accessed=12 * span * full
        ),
        name="hidden_back",
    )(low, gate, up, hidden, w_down, *pieces, *down_pieces)


def on_device(
    tokens, lengths, attn_gain, w_query, w_key, w_value, w_out, mlp_gain, w_gate, w_up, w_down, cotangent
):
    row_devices = lax.axis_size("row")
    col_devices = lax.axis_size("col")
    row = lax.axis_index("row")
    col = lax.axis_index("col")
    fit = kernels_fit()
    tok, width = tokens.shape
    span = tok * row_devices
    group = HQ // KV
    heads_row = HQ // row_devices
    heads = heads_row // col_devices
    head_width = heads * HD
    keyval_row = KV // row_devices
    units = w_gate.shape[1] // col_devices
    length = lengths[0]
    shared_key = heads < group
    sharers = max(1, group // heads)
    leader = (col % sharers == 0).astype(jnp.int32)
    info = jnp.stack([length, row, leader]).astype(jnp.int32)

    keyval = []
    for owner in range(col_devices):
        first = owner * heads // group * HD
        keyval += [w_key[:, first : first + HD], w_value[:, first : first + HD]]
    keyval = jnp.concatenate(keyval, axis=1)
    gains = jnp.concatenate([attn_gain[None], mlp_gain[None], jnp.zeros((6, width), F32)], axis=0)

    if fit:
        tokens_full, wq, wkv, gains = first_gather(tokens, w_query, keyval, gains, 1)
    else:
        tokens_full = plain_gather(tokens)
        def slices(weight, size):
            return [lax.dynamic_slice_in_dim(weight, (col ^ s) * size, size, 1) for s in range(col_devices)]

        wq = jnp.concatenate(exchange(slices(w_query, head_width)), axis=0)
        wkv = jnp.concatenate(exchange(slices(keyval, LANES)), axis=0)
        gains = by_distance(lax.all_gather(gains, "col"), 1)
    w_gate, w_up, tokens_full = lax.optimization_barrier((w_gate, w_up, tokens_full))
    place = lax.rem(jnp.arange(span, dtype=jnp.int32) + row * tok, span)
    frequency = ROPE_BASE ** (-jnp.arange(HD // 2, dtype=F32) * (2.0 / HD))
    angle = place.astype(F32)[:, None] * frequency[None, :]
    cos = jnp.tile(jnp.cos(angle), (1, 2))
    sin = jnp.tile(jnp.sin(angle), (1, 2))

    normed_attn, query, key, value, scale_a = project_heads(tokens_full, gains, wq, wkv, cos, sin)
    valid = (row * tok + jnp.arange(tok, dtype=jnp.int32) < length).astype(BF)
    cot_low = cotangent * valid[:, None]
    def unit_pieces():
        rows = width // 2
        start = lax.rem(lax.axis_index("dp"), 2) * rows
        near = [
            jnp.concatenate(
                [lax.dynamic_slice(w, (start, (col ^ s) * units), (rows, units)) for w in (w_gate, w_up)], axis=0
            )
            for s in range(col_devices)
        ]
        return jnp.concatenate(exchange(near), axis=0)

    def unit_slices(weight, dim):
        return [lax.dynamic_slice_in_dim(weight, (col ^ s) * units, units, dim) for s in range(col_devices)]

    if fit:
        near_units = unit_pieces()
        mixed, mixed_wide, log_total, peak, w_out_full = attn_forward(info, query, key, value, w_out, 7)
        mixed, near_units = lax.optimization_barrier((mixed, near_units))
        pieces = [near_units, swap(near_units, "dp", 1)]
        mixed_full = gather_heads(mixed, 2)
        resid_mid, normed_mlp, out_low = project_out(mixed_full, w_out_full, tokens_full, gains, cot_low, 8)
        w_down, normed_mlp = lax.optimization_barrier((w_down, normed_mlp))
        down_pieces = [
            swap(lax.dynamic_slice_in_dim(w_down, (col ^ s) * units, units, 0), "col", s) for s in range(1, col_devices)
        ]
        gate, up, hidden = hidden_units(normed_mlp, pieces)
        hidden, peak = lax.optimization_barrier((hidden, peak))
        moved = [swap(peak, "dp", step) for step in (1, 2, 3)]
        down_pieces, moved = lax.optimization_barrier((down_pieces, moved))
        for other in moved:
            peak = jnp.maximum(peak, other)
        own_peaks = peak[:, 0]
        others = [swap(own_peaks[None, :], "col", step) for step in (1, 2, 3)]
        gate_cot, up_cot, mlp_part, down_part = hidden_back(
            out_low, gate, up, hidden, w_down, pieces, down_pieces
        )
        mlp_part, others = lax.optimization_barrier((mlp_part, others))
        row_peaks = jnp.where(jnp.arange(4)[:, None] == col, own_peaks[None, :], NEG_FILL)
        for step, other in zip((1, 2, 3), others):
            row_peaks = jnp.where(jnp.arange(4)[:, None] == col ^ step, other, row_peaks)
    else:
        mixed, mixed_wide, log_total, peak = attn_forward(info, query, key, value)
        mixed_full = plain_gather_heads(mixed)
        w_out_full = plain_gather(w_out)
        resid_mid, normed_mlp = project_out(mixed_full, w_out_full, tokens_full, gains)
        out_low = plain_gather(cot_low)
        w_gate_units = jnp.concatenate(exchange(unit_slices(w_gate, 1)), axis=0)
        w_up_units = jnp.concatenate(exchange(unit_slices(w_up, 1)), axis=0)
        w_down_units = jnp.concatenate(exchange(unit_slices(w_down, 0)), axis=1)
        gate = jnp.dot(normed_mlp, w_gate_units, preferred_element_type=F32)
        up = jnp.dot(normed_mlp, w_up_units, preferred_element_type=F32)
        gate_sigmoid = jax.nn.sigmoid(gate)
        hidden = (gate * gate_sigmoid * up).astype(BF)
        hidden_cot = contract(out_low, w_down_units, 1, 1)
        gate_cot = (
            hidden_cot * up * gate_sigmoid * (1.0 + gate * (1.0 - gate_sigmoid))
        ).astype(BF)
        up_cot = (hidden_cot * gate * gate_sigmoid).astype(BF)
        mlp_part = (contract(gate_cot, w_gate_units, 1, 1) + contract(up_cot, w_up_units, 1, 1)).astype(BF)
        down_part = jnp.dot(hidden, w_down_units, preferred_element_type=F32).astype(BF)

    if fit:
        *sums, mid_cot, gain_m_part, attn_cot, down_sum, width_dot = backward(
            info, gains, normed_mlp, gate_cot, up_cot, hidden, mlp_part, down_part, resid_mid, out_low, w_out_full,
            mixed, query, key, value, mixed_wide, log_total, cos, sin, wq, wkv, normed_attn, tokens_full, 3,
        )
        width_dot = width_dot.reshape(tok)
    else:
        mlp_cot = plain_gather(plain_reduce(mlp_part).astype(BF))
        down_sum = plain_reduce(down_part)
        w_mine = lax.dynamic_slice_in_dim(w_out_full, col * head_width, head_width, 0)
        mixed_cot, mid_cot, grad_out, gain_m_part = middle(
            mlp_cot, resid_mid, out_low, gains, w_mine, mixed, width
        )
        query_cot, key_cot, value_cot = attn_backward(
            info, query, key, value, mixed_cot, mixed_wide, log_total, cos, sin, F32 if shared_key else BF
        )
        if shared_key:
            for bit in range(sharers.bit_length() - 1):
                key_cot = key_cot + swap(key_cot, "col", 1 << bit)
                value_cot = value_cot + swap(value_cot, "col", 1 << bit)
            key_cot, value_cot = key_cot.astype(BF), value_cot.astype(BF)
        attn_part, dot_part, grad_heads = head_back(
            info, query_cot, key_cot, value_cot, wq, wkv, normed_attn, tokens_full, gains
        )
        dot_part = dot_part.reshape(span)
        width_dot = lax.psum(dot_part[:tok] + swap(dot_part[tok:], "row", 1), "col")
        attn_cot = plain_reduce(attn_part)
        grad_gate = contract(normed_mlp, gate_cot, 0, 0).astype(BF)
        grad_up = contract(normed_mlp, up_cot, 0, 0).astype(BF)
        grad_down = contract(hidden, out_low, 0, 0).astype(BF)
        sums = plain_group_sum(
            [grad_gate, grad_up, grad_down, grad_out, grad_heads], ["columns", "columns", "rows", "rows", "stack"]
        )
    output = (resid_mid[:tok, :width] + down_sum).astype(BF)
    own_in = tokens.astype(F32)
    scale_own = scale_a[:tok, :1]
    input_grad = (
        mid_cot
        + attn_cot * attn_gain * scale_own
        - own_in * (scale_own * scale_own * scale_own * width_dot[:, None] / D)
    )
    gain_a_part = jnp.sum(attn_cot * own_in * scale_own, axis=0)

    out_gate, out_up, out_down, out_out = [g.astype(F32) for g in sums[:4]]
    if fit:
        blocks = sums[4].reshape(4, CR, 2, CR).transpose(2, 1, 0, 3)
        out_query = blocks.reshape(width, 4 * head_width).astype(F32)
        blocks = sums[5].reshape(4, HR, 4, LANES).transpose(2, 1, 0, 3).reshape(width, 4, 2, HD).astype(F32)
        out_key = blocks[:, :, 0].reshape(w_key.shape)
        out_value = blocks[:, :, 1].reshape(w_value.shape)
    else:
        out_heads = sums[4].astype(F32).reshape(col_devices, width, sums[4].shape[1])
        out_query = jnp.concatenate([out_heads[i, :, :head_width] for i in range(col_devices)], axis=1)
        leaders = range(0, col_devices, sharers)
        out_key = jnp.concatenate([out_heads[i, :, head_width : head_width + HD] for i in leaders], axis=1)
        out_value = jnp.concatenate(
            [out_heads[i, :, head_width + HD : head_width + 2 * HD] for i in leaders], axis=1
        )

    gain_sums = jnp.stack([gain_a_part, gain_m_part[0]])
    if fit:
        grown, hops = [out_gate, out_up, out_down], [("row", 1), ("dp", 1), ("dp", 2)]
        for n, (axis, step) in enumerate(hops):
            other = swap(gain_sums, axis, step)
            other, grown[n] = lax.optimization_barrier((other, grown[n]))
            gain_sums = gain_sums + other
        out_gate, out_up, out_down = grown
    else:
        gain_sums = lax.psum(gain_sums, ("dp", "row"))
        own_peaks = lax.pmax(peak, "dp")[:, 0]
        row_peaks = lax.all_gather(own_peaks, "col")
    row_peaks = row_peaks.reshape(heads_row)
    clip_factor = CLIP_LEVEL / jnp.maximum(row_peaks, CLIP_LEVEL)
    query_scale = jnp.repeat(jnp.sqrt(clip_factor), HD)
    key_scale = jnp.repeat(jnp.sqrt(jnp.min(clip_factor.reshape(keyval_row, group), axis=1)), HD)
    clipped_query = (w_query.astype(F32) * query_scale[None, :]).astype(BF)
    clipped_key = (w_key.astype(F32) * key_scale[None, :]).astype(BF)
    return (
        output,
        input_grad,
        gain_sums[0],
        out_query,
        out_key,
        out_value,
        out_out,
        gain_sums[1],
        out_gate,
        out_up,
        out_down,
        own_peaks,
        clipped_query,
        clipped_key,
    )


def solution(mesh):
    in_specs = (
        P(("dp", "row"), "col"),
        P("dp"),
        P("col"),
        P("col", "row"),
        P("col", "row"),
        P("col", "row"),
        P("row", "col"),
        P("col"),
        P("col", "row"),
        P("col", "row"),
        P("row", "col"),
        P(("dp", "row"), "col"),
    )
    out_specs = (
        P(("dp", "row"), "col"),
        P(("dp", "row"), "col"),
        P("col"),
        P("col", "row"),
        P("col", "row"),
        P("col", "row"),
        P("row", "col"),
        P("col"),
        P("col", "row"),
        P("col", "row"),
        P("row", "col"),
        P(("row", "col")),
        P("col", "row"),
        P("col", "row"),
    )
    return jax.shard_map(
        on_device, mesh=mesh, in_specs=in_specs, out_specs=out_specs, check_vma=False
    )
```

```python
import functools

import jax
import jax.numpy as jnp
from jax import lax
from jax.experimental import pallas as pl
from jax.experimental.pallas import tpu as pltpu
from jax.sharding import PartitionSpec as P

D = 2048
HQ = 32
KV = 8
HD = 64
SEQ_LEN = 2048

EPSILON = 1e-05
NEG_FILL = -1e30
CLIP_LEVEL = 5.0
ROPE_BASE = 500000.0

BF = jnp.bfloat16
F32 = jnp.float32
LANES = 128
QB = 512
FWD_KB = 512
BWD_KB = 512
MESH = pl.DeviceIdType.MESH
ANY = pl.BlockSpec(memory_space=pl.ANY)
NCH = 4
CR, CC = 256, 512
HR = CR // 2
OFFS = (0, 2, 4, 7)
RING = 12
MIB = 2**20
VMEM_ALL = 63 * MIB


def contract(left, right, left_dim, right_dim):
    return lax.dot_general(
        left, right, (((left_dim,), (right_dim,)), ((), ())), preferred_element_type=F32
    )


def swap(values, axis, step):
    count = lax.axis_size(axis)
    return lax.ppermute(values, axis, [(i, i ^ step) for i in range(count)])


def flip(index, bit):
    return index + bit - 2 * bit * lax.rem(index // bit, 2)


def xor(index, step):
    return lax.rem(lax.rem(index, 2) + step % 2, 2) + 2 * lax.rem(index // 2 + step // 2, 2)


def remote(src, dst, send, recv, **where):
    return pltpu.make_async_remote_copy(
        src_ref=src, dst_ref=dst, send_sem=send, recv_sem=recv, device_id=where, device_id_type=MESH
    )


def done(ref, sem):
    pltpu.make_async_copy(ref, ref, sem).wait()


def greet(targets):
    barrier = pltpu.get_barrier_semaphore()
    for target in targets:
        pl.semaphore_signal(barrier, inc=1, device_id=target, device_id_type=MESH)
    pl.semaphore_wait(barrier, len(targets))


def plane_peers():
    row = lax.axis_index("row")
    col = lax.axis_index("col")
    return {"col": flip(col, 1)}, {"col": flip(col, 2)}, {"row": 1 - row}


def token_place(tok, width):
    rows = tok // NCH

    def place(ref, half, s, j, who):
        return ref.at[pl.ds(half * tok + j * rows, rows), pl.ds(s * width, width)]

    return place


def head_place(span, width):
    rows = span // NCH

    def place(ref, half, s, j, who):
        start = j * rows if half == 0 else ((j + NCH // 2) % NCH) * rows
        return ref.at[pl.ds(start, rows), pl.ds(pl.multiple_of((half * 4 + xor(who, s)) * width, LANES), width)]

    return place


class Gather:
    SEMS = 6

    def __init__(self, src, out, place, stage, sems):
        self.src, self.out, self.place, self.stage = src, out, place, stage
        self.own_send, self.relay_send, self.mate_send, self.recv, self.mate_recv, self.local = sems
        self.col = lax.axis_index("col")
        self.near = plane_peers()

    @staticmethod
    def sems():
        shapes = [(2, NCH), (NCH,), (4, NCH), (3, NCH), (4, NCH), (2,)]
        return [pltpu.SemaphoreType.DMA(s) for s in shapes]

    def chunk(self, j):
        rows = self.src.shape[0] // NCH
        return self.src.at[pl.ds(j * rows, rows), :]

    def here(self, half, s, j):
        return self.place(self.out, half, s, j, self.col)

    def own(self, axis, j):
        peer = self.near[axis]
        dst = self.place(self.out, 0, axis + 1, j, peer["col"])
        return remote(self.chunk(j), dst, self.own_send.at[axis, j], self.recv.at[axis, j], **peer)

    def relay(self, axis, j):
        peer = self.near[1 - axis]
        dst = self.place(self.out, 0, 3, j, peer["col"])
        return remote(self.here(0, axis + 1, j), dst, self.relay_send.at[j], self.recv.at[2, j], **peer)

    def mate(self, s, j):
        src = self.chunk(j) if s == 0 else self.here(0, s, j)
        dst = self.place(self.out, 1, s, j, self.col)
        return remote(src, dst, self.mate_send.at[s, j], self.mate_recv.at[s, j], **self.near[2])

    def load(self):
        return pltpu.make_async_copy(self.src, self.stage, self.local.at[0])

    def keep(self, j):
        rows = self.src.shape[0] // NCH
        whole = self.stage if self.stage is not None else self.src
        return pltpu.make_async_copy(whole.at[pl.ds(j * rows, rows), :], self.here(0, 0, j), self.local.at[1])

    def begin(self):
        half = NCH // 2
        if self.stage is not None:
            self.load().start()
        for i in range(NCH):
            self.own(0, i).start()
            self.own(1, (i + half) % NCH).start()
        for j in range(NCH):
            self.mate(0, j).start()

    def arrived(self, s, j):
        done(self.here(0, s, j), self.recv.at[s - 1, j])

    def first(self):
        half = NCH // 2
        for i in range(half):
            self.arrived(1, i)
            self.relay(0, i).start()
            self.mate(1, i).start()
            self.arrived(2, half + i)
            self.relay(1, half + i).start()
            self.mate(2, half + i).start()

    def second(self):
        half = NCH // 2
        if self.stage is not None:
            self.load().wait()
        for j in range(NCH):
            self.keep(j).start()
        for i in range(half):
            self.arrived(1, half + i)
            self.mate(1, half + i).start()
            self.arrived(2, i)
            self.mate(2, i).start()
        for i in range(half):
            for j in (i, half + i):
                self.arrived(3, j)
                self.mate(3, j).start()

    def finish(self):
        half = NCH // 2
        for s in range(4):
            for j in range(NCH):
                done(self.here(1, s, j), self.mate_recv.at[s, j])
                self.mate(s, j).wait_send()
        for j in range(NCH):
            self.own(0, j).wait_send()
            self.own(1, j).wait_send()
            self.relay(0 if j < half else 1, j).wait_send()
        whole = self.stage if self.stage is not None else self.src
        done(whole, self.local.at[1])


def gather_kernel(place_of, x_ref, out_ref, stage, *sems):
    near_x, near_y, mate = plane_peers()
    greet([near_x, near_y, mate])
    gather = Gather(x_ref, out_ref, place_of(*x_ref.shape), stage, sems)
    gather.begin()
    gather.first()
    gather.second()
    gather.finish()


def gather_call(x, shape, place_of, cid, name):
    return pl.pallas_call(
        functools.partial(gather_kernel, place_of),
        in_specs=[ANY],
        out_specs=ANY,
        out_shape=jax.ShapeDtypeStruct(shape, x.dtype),
        scratch_shapes=[pltpu.VMEM(x.shape, x.dtype)] + Gather.sems(),
        compiler_params=pltpu.CompilerParams(collective_id=cid, has_side_effects=True),
        name=name,
    )(x)


def gather_tokens(x, cid):
    tok, width = x.shape
    return gather_call(x, (2 * tok, 4 * width), token_place, cid, "gather_tokens")


def gather_heads(x, cid):
    span, width = x.shape
    return gather_call(x, (span, 8 * width), head_place, cid, "gather_heads")


class Reduce:
    def __init__(self, part, scratch, sems):
        self.part = part
        self.own, self.given, self.sent, self.got_one, self.got_two = scratch
        self.loads, self.mate_send, self.mate_recv, self.one_send, self.one_recv, self.two_send, self.two_recv = sems
        self.near = plane_peers()
        self.h = self.own.shape[0] // 2
        self.width = self.own.shape[1] // 4

    @staticmethod
    def scratch(tok, full):
        h, w = tok // 2, full // 4
        shapes = [(tok, full), (tok, full), (2, 3, h, w), (2, 2, h, w), (2, h, w)]
        return [pltpu.VMEM(s, BF) for s in shapes]

    @staticmethod
    def sems():
        return [pltpu.SemaphoreType.DMA((2,))] * 7

    def lines(self, a):
        return pl.ds(a * self.h, self.h)

    def give(self, a):
        src = self.part.at[pl.ds((2 + a) * self.h, self.h), :]
        return remote(src, self.given.at[self.lines(a), :], self.mate_send.at[a], self.mate_recv.at[a], **self.near[2])

    def load(self, a):
        return pltpu.make_async_copy(self.part.at[self.lines(a), :], self.own.at[self.lines(a), :], self.loads.at[a])

    def one(self, a):
        src = self.sent.at[a, pl.ds(0, 2)]
        return remote(src, self.got_one.at[a], self.one_send.at[a], self.one_recv.at[a], **self.near[a])

    def two(self, a):
        return remote(self.sent.at[a, 2], self.got_two.at[a], self.two_send.at[a], self.two_recv.at[a], **self.near[1 - a])

    def pair(self, a, s):
        cols = pl.ds(s * self.width, self.width)
        rows = self.lines(a)
        return self.own[rows, cols].astype(F32) + self.given[rows, cols].astype(F32)

    def begin(self):
        for a in range(2):
            self.give(a).start()
            self.load(a).start()

    def first(self, a):
        self.load(a).wait()
        done(self.given.at[self.lines(a), :], self.mate_recv.at[a])
        for i, s in enumerate((a + 1, 3)):
            self.sent[a, i] = self.pair(a, s).astype(BF)
        self.one(a).start()

    def second(self, a):
        done(self.got_one.at[a], self.one_recv.at[a])
        self.sent[a, 2] = (self.pair(a, 2 - a) + self.got_one[a, 1].astype(F32)).astype(BF)
        self.two(a).start()

    def total(self, a):
        done(self.got_two.at[a], self.two_recv.at[a])
        return self.pair(a, 0) + self.got_one[a, 0].astype(F32) + self.got_two[a].astype(F32)

    def finish(self):
        for a in range(2):
            self.give(a).wait_send()
            self.one(a).wait_send()
            self.two(a).wait_send()


def first_gather_kernel(
    x_ref, wq_ref, wkv_ref, gain_ref, out_ref, wq_out, wkv_out, gain_out,
    stage, wq_stage, wkv_stage, gain_stage, stage_sem, small_send, small_recv, *sems,
):
    near_x, near_y, mate = plane_peers()
    col = lax.axis_index("col")
    tok, width = x_ref.shape
    wide = wq_ref.shape[1] // 4
    thin = wkv_ref.shape[1] // 4

    def share(ref, owner, size):
        return ref.at[:, pl.ds(pl.multiple_of(owner * size, LANES), size)]

    loads = [
        pltpu.make_async_copy(share(wq_ref, col, wide), wq_stage, stage_sem.at[0]),
        pltpu.make_async_copy(share(wkv_ref, col, thin), wkv_stage, stage_sem.at[1]),
        pltpu.make_async_copy(gain_ref, gain_stage, stage_sem.at[2]),
    ]
    for c in loads:
        c.start()
    greet([near_x, near_y, {"col": 3 - col}, mate])
    smalls = []
    for s, peer in ((1, near_x), (2, near_y), (3, {"col": 3 - col})):
        owner = peer["col"]
        lines = pl.ds(s * width, width)
        smalls += [
            remote(share(wq_ref, owner, wide), wq_out.at[lines, :], small_send.at[0, s], small_recv.at[0, s], **peer),
            remote(share(wkv_ref, owner, thin), wkv_out.at[lines, :], small_send.at[1, s], small_recv.at[1, s], **peer),
            remote(gain_ref, gain_out.at[:, lines], small_send.at[2, s], small_recv.at[2, s], **peer),
        ]
    gather = Gather(x_ref, out_ref, token_place(tok, width), stage, sems)
    gather.begin()
    for c in smalls:
        c.start()
    lines = pl.ds(0, width)
    keeps = [
        pltpu.make_async_copy(wq_stage, wq_out.at[lines, :], stage_sem.at[3]),
        pltpu.make_async_copy(wkv_stage, wkv_out.at[lines, :], stage_sem.at[4]),
        pltpu.make_async_copy(gain_stage, gain_out.at[:, lines], stage_sem.at[5]),
    ]
    for load, keep in zip(loads, keeps):
        load.wait()
        keep.start()
    gather.first()
    gather.second()
    gather.finish()
    for c in smalls:
        c.wait()
    for c in keeps:
        c.wait()


def first_gather(x, wq, wkv, gains, cid):
    tok, width = x.shape
    wide, thin = wq.shape[1] // 4, wkv.shape[1] // 4
    return pl.pallas_call(
        first_gather_kernel,
        in_specs=[ANY] * 4,
        out_specs=[ANY] * 4,
        out_shape=[
            jax.ShapeDtypeStruct((2 * tok, 4 * width), BF),
            jax.ShapeDtypeStruct((4 * width, wide), BF),
            jax.ShapeDtypeStruct((4 * width, thin), BF),
            jax.ShapeDtypeStruct((8, 4 * width), F32),
        ],
        scratch_shapes=[
            pltpu.VMEM((tok, width), BF),
            pltpu.VMEM((width, wide), BF),
            pltpu.VMEM((width, thin), BF),
            pltpu.VMEM((8, width), F32),
            pltpu.SemaphoreType.DMA((6,)),
            pltpu.SemaphoreType.DMA((3, 4)),
            pltpu.SemaphoreType.DMA((3, 4)),
        ]
        + Gather.sems(),
        compiler_params=pltpu.CompilerParams(collective_id=cid, has_side_effects=True),
        name="first_gather",
    )(x, wq, wkv, gains)


def grad_plan(kind, shape):
    rows, cols = shape
    if kind == "columns":
        w = rows // 4
        high, n = rows // CR, w // CR
        return (
            high * (cols // CC), high,
            lambda i: lax.rem(i, high) // n, lambda i: lax.rem(i, high), lambda i: i // high,
            (w, 4 * cols), lambda c, i: (lax.rem(i, n) * CR, c * cols + i // high * CC),
        )
    high = rows // CR
    if kind == "rows":
        return (
            4 * high, high,
            lambda i: i // high, lambda i: lax.rem(i, high), lambda i: i // high,
            (4 * rows, cols // 4), lambda c, i: (c * rows + lax.rem(i, high) * CR, 0),
        )
    n = high // 4
    return (
        high, high,
        lambda i: i // n, lambda i: i, lambda i: 0,
        (rows, cols), lambda c, i: ((c * n + lax.rem(i, n)) * CR, 0),
    )


class GroupSum:
    def __init__(self, kinds, lefts, rights, outs, refs):
        (self.left, self.right, self.left_sem, self.right_sem, self.own, self.land, self.mids, self.tops, self.in_send, self.in_recv, self.mid_send,
         self.mid_recv, self.top_send, self.top_recv, self.out_send, self.out_recv, self.far_send, self.far_recv) = refs
        self.lefts, self.rights, self.outs = lefts, rights, outs
        self.plans = [grad_plan(k, (a.shape[1], b.shape[1])) for k, a, b in zip(kinds, lefts, rights)]
        self.counts = [p[0] for p in self.plans]
        self.begins = [sum(self.counts[:i]) for i in range(len(lefts))]
        groups = [p[0] // p[1] for p in self.plans]
        self.groups = [sum(groups[:i]) for i in range(len(lefts))]
        self.total = sum(self.counts)
        z = lax.axis_index("dp")
        self.col = lax.axis_index("col")
        self.is_mid = (z == 1) | (z == 2)
        self.is_end = jnp.logical_not(self.is_mid)
        left = z < 2
        self.inward = {"dp": jnp.where(left, z + 1, z - 1)}
        self.outward = {"dp": jnp.where(left, z - 1, z + 1)}
        self.kept = jnp.where(left, 0, 1)

    @staticmethod
    def scratch(kinds, span):
        dma = pltpu.SemaphoreType.DMA
        return (
            [pltpu.VMEM((2, span, CR), BF), pltpu.VMEM((2, span, CC), BF), dma((2,)), dma((2,))]
            + [pltpu.VMEM((RING, CR, CC), BF)] * 2
            + [pltpu.VMEM((RING, HR, CC), BF)] * 2
            + [dma((RING,))] * 6
            + [dma((RING, 2))] * 3
            + [dma((len(kinds),))]
        )

    def greet(self, others):
        barrier = pltpu.get_barrier_semaphore()
        targets = [self.inward] + others
        for target in targets:
            pl.semaphore_signal(barrier, inc=1, device_id=target, device_id_type=MESH)

        @pl.when(self.is_mid)
        def _():
            pl.semaphore_signal(barrier, inc=1, device_id=self.outward, device_id_type=MESH)
            pl.semaphore_wait(barrier, len(targets) + 1)

        @pl.when(self.is_end)
        def _():
            pl.semaphore_wait(barrier, len(targets))

    def rows(self, half):
        return pl.ds(pl.multiple_of(half * HR, HR), HR)

    def each(self, j, action):
        for m, count in enumerate(self.counts):

            @pl.when((j >= self.begins[m]) & (j < self.begins[m] + count))
            def _(m=m):
                action(m, j - self.begins[m])

    def left_load(self, m, i, j):
        lines = pl.ds(pl.multiple_of(self.plans[m][3](i) * CR, CR), CR)
        slot = lax.rem(j, 2)
        return pltpu.make_async_copy(self.lefts[m].at[:, lines], self.left.at[slot], self.left_sem.at[slot])

    def right_slot(self, m, i):
        return lax.rem(self.groups[m] + i // self.plans[m][1], 2)

    def right_load(self, m, i):
        lines = pl.ds(pl.multiple_of(self.plans[m][4](i) * CC, CC), CC)
        slot = self.right_slot(m, i)
        return pltpu.make_async_copy(self.rights[m].at[:, lines], self.right.at[slot], self.right_sem.at[slot])

    def fetch(self, j):
        def action(m, i):
            self.left_load(m, i, j).start()
            if self.resident[m] is None:

                @pl.when(lax.rem(i, self.plans[m][1]) == 0)
                def _():
                    self.right_load(m, i).start()

        self.each(j, action)

    def produce(self, j):
        slot = lax.rem(j, RING)

        def action(m, i):
            self.left_load(m, i, j).wait()
            if self.resident[m] is None:

                @pl.when(lax.rem(i, self.plans[m][1]) == 0)
                def _():
                    self.right_load(m, i).wait()

                right = self.right[self.right_slot(m, i)]
            else:
                right = self.resident[m][...]
            self.own[slot] = contract(self.left[lax.rem(j, 2)], right, 0, 0).astype(BF)

        self.each(j, action)

    def spread(self, j, half, src):
        slot = lax.rem(j, RING)

        def action(m, i):
            s = self.plans[m][2](i)
            r, q = self.plans[m][6](self.col, i)
            dst = self.outs[m].at[
                pl.ds(pl.multiple_of(r + half * HR, HR), HR), pl.ds(pl.multiple_of(q, CC), CC)
            ]

            @pl.when(s == 0)
            def _():
                pltpu.make_async_copy(src, dst, self.far_send.at[slot, half]).start()

            @pl.when(s > 0)
            def _():
                owner = lax.rem(lax.rem(self.col, 2) + lax.rem(s, 2), 2) + 2 * lax.rem(self.col // 2 + s // 2, 2)
                remote(src, dst, self.far_send.at[slot, half], self.far_recv.at[m], col=owner).start()

        self.each(j, action)

    def reclaim(self, j):
        slot = lax.rem(j, RING)
        for half in range(2):
            done(self.mids.at[slot], self.far_send.at[slot, half])

        @pl.when(self.is_mid)
        def _():
            done(self.mids.at[slot], self.mid_send.at[slot])
            done(self.mids.at[slot], self.top_send.at[slot])
            for half in range(2):
                done(self.mids.at[slot], self.out_send.at[slot, half])

        @pl.when(self.is_end)
        def _():
            done(self.own.at[slot], self.in_send.at[slot])

    def inbound(self, j):
        slot = lax.rem(j, RING)

        @pl.when(self.is_mid)
        def _():
            done(self.land.at[slot], self.in_recv.at[slot])
            self.own[slot] = (self.own[slot].astype(F32) + self.land[slot].astype(F32)).astype(BF)
            src = self.own.at[slot, self.rows(1 - self.kept)]
            remote(src, self.mids.at[slot], self.mid_send.at[slot], self.mid_recv.at[slot], **self.inward).start()

        @pl.when(self.is_end)
        def _():
            remote(
                self.own.at[slot], self.land.at[slot], self.in_send.at[slot], self.in_recv.at[slot], **self.inward
            ).start()

    def middle(self, j):
        slot = lax.rem(j, RING)

        @pl.when(self.is_mid)
        def _():
            done(self.mids.at[slot], self.mid_recv.at[slot])
            rows = self.rows(self.kept)
            self.own[slot, rows] = (self.own[slot, rows].astype(F32) + self.mids[slot].astype(F32)).astype(BF)
            src = self.own.at[slot, rows]
            remote(src, self.tops.at[slot], self.top_send.at[slot], self.top_recv.at[slot], **self.inward).start()
            remote(
                src, self.land.at[slot, rows], self.out_send.at[slot, self.kept], self.out_recv.at[slot, self.kept],
                **self.outward,
            ).start()
            self.spread(j, self.kept, src)

    def settle(self, j):
        slot = lax.rem(j, RING)

        @pl.when(self.is_mid)
        def _():
            done(self.tops.at[slot], self.top_recv.at[slot])
            half = 1 - self.kept
            src = self.tops.at[slot]
            remote(
                src, self.land.at[slot, self.rows(half)], self.out_send.at[slot, half], self.out_recv.at[slot, half],
                **self.outward,
            ).start()
            self.spread(j, half, src)

    def outbound(self, j):
        slot = lax.rem(j, RING)

        @pl.when(self.is_end)
        def _():
            for half in range(2):
                src = self.land.at[slot, pl.ds(half * HR, HR)]
                done(src, self.out_recv.at[slot, half])
                self.spread(j, half, src)

    def begin(self):
        self.fetch(jnp.int32(0))
        self.produce(jnp.int32(0))
        self.fetch(jnp.int32(1))

    def tick(self, t):
        for off, stage in zip(OFFS, (self.inbound, self.middle, self.settle, self.outbound)):

            @pl.when((t >= off) & (t < self.total + off))
            def _(off=off, stage=stage):
                stage(t - off)

        ahead = t + 1

        @pl.when(ahead < self.total)
        def _():
            @pl.when(ahead >= RING)
            def _():
                self.reclaim(ahead - RING)

            self.produce(ahead)

            @pl.when(ahead + 1 < self.total)
            def _():
                self.fetch(ahead + 1)

    def finish(self):
        def drain(j, carry):
            self.reclaim(j)
            return carry

        lax.fori_loop(self.total - RING, self.total, drain, 0)
        for m, out in enumerate(self.outs):
            done(out.at[pl.ds(0, 3 * out.shape[0] // 4)], self.far_recv.at[m])


MB = 128
AQ, AK = 256, 512


def backward_kernel(
    kinds,
    info_ref, gain_ref, mlp_ref, gate_ref, up_ref, hidden_ref, part_ref, low_part_ref, resid_ref, low_ref, w_ref, mixed_ref,
    wide_ref, normed_ref, x_ref, q_ref, k_ref, v_ref, lse_ref, turn_ref, wq_ref, wkv_ref,
    out_gate, out_up, out_down, out_out, out_heads, mid_out, gain_part, attn_out, down_out, dot_out,
    cot_full, attn_part, mid_low,
    *refs,
):
    refs = list(refs)

    def take(count):
        taken = refs[:count]
        del refs[:count]
        return taken

    zsum = GroupSum(
        kinds,
        [hidden_ref, mlp_ref, mlp_ref, mixed_ref, normed_ref],
        [low_ref, gate_ref, up_ref, mid_low, refs[0]],
        [out_down, out_gate, out_up, out_out, out_heads],
        refs[1:19],
    )
    heads_cot = refs[0]
    zsum.resident = [None, None, None, None, heads_cot]
    del refs[:19]
    scratch = take(5)
    mlp_reduce = Reduce(part_ref, scratch, take(7))
    low_reduce = Reduce(low_part_ref, scratch, take(7))
    attn_reduce = Reduce(attn_part, scratch, take(7))
    mine, = take(1)
    tok, width = mine.shape
    gather = Gather(mine, cot_full, token_place(tok, width), None, take(Gather.SEMS))
    bufs, resid_buf, out_buf, buf_sem, out_sem = take(5)
    mixed_cot, wide_buf, dq_sum, dk_sum, dv_sum, dots, dots_mate, dots_col = take(8)
    dot_send, dot_recv, ready, w_mine, w_sem = take(5)
    span = 2 * tok
    heads_width = q_ref.shape[1]
    heads = heads_width // HD
    half = lax.axis_index("row")
    col = lax.axis_index("col")
    length = info_ref[0]
    near_x, near_y, mate = plane_peers()
    corner = {"col": 3 - col}
    blocks = span // MB

    def mid_loads(i):
        slot = lax.rem(i, 2)
        lines = pl.ds(pl.multiple_of(i * MB, MB), MB)
        return [
            pltpu.make_async_copy(cot_full.at[lines, :], bufs.at[slot, 0], buf_sem.at[slot, 0]),
            pltpu.make_async_copy(low_ref.at[lines, :], bufs.at[slot, 1], buf_sem.at[slot, 1]),
            pltpu.make_async_copy(resid_ref.at[lines, :], resid_buf.at[slot], buf_sem.at[slot, 2]),
        ]

    def row_store(out, i):
        lines = pl.ds(pl.multiple_of(i * MB, MB), MB)
        return pltpu.make_async_copy(bufs.at[lax.rem(i, 2), 2], out.at[lines, :], out_sem.at[1])

    def mid_store(i):
        lines = pl.ds(pl.multiple_of(i * MB, MB), MB)
        return pltpu.make_async_copy(out_buf.at[:, pl.ds(0, width)], mid_out.at[lines, :], out_sem.at[0])

    def mid_item(i):
        slot = lax.rem(i, 2)

        @pl.when(i + 1 < blocks)
        def _():
            for c in mid_loads(i + 1):
                c.start()

        for c in mid_loads(i):
            c.wait()
        cot = bufs[slot, 0].astype(F32)
        resid = resid_buf[slot]
        scale = lax.rsqrt(jnp.mean(resid * resid, axis=1, keepdims=True) + EPSILON)
        weighed = cot * gain_ref[1:2, :]
        inner = jnp.sum(weighed * resid, axis=1, keepdims=True)
        mid = bufs[slot, 1].astype(F32) + weighed * scale - resid * (scale * scale * scale * inner / D)
        low = mid.astype(BF)
        lines = pl.ds(pl.multiple_of(i * MB, MB), MB)
        mixed_cot[lines, :] = contract(low, w_mine[...], 1, 1).astype(BF)

        @pl.when(i > 0)
        def _():
            row_store(mid_low, i - 1).wait()

        bufs[slot, 2] = low
        row_store(mid_low, i).start()

        @pl.when(i < blocks // 2)
        def _():
            @pl.when(i > 0)
            def _():
                mid_store(i - 1).wait()

            out_buf[:, pl.ds(0, width)] = mid[:, :width]
            mid_store(i).start()
            part = jnp.sum((cot * resid * scale)[:, :width], axis=0, keepdims=True)
            gain_part[...] += jnp.broadcast_to(part, gain_part.shape)

        @pl.when(i == blocks // 2)
        def _():
            mid_store(i - 1).wait()

    q_steps = span // AQ
    rows = heads * AQ
    pieces = [slice(h * HD, (h + 1) * HD) for h in range(heads)]

    def attn_item(q_step, tile, diagonal):
        stored = lax.rem(q_step + half * (q_steps // 2), q_steps)
        lines = pl.ds(pl.multiple_of(stored * AQ, AQ), AQ)
        key_tiles = span // AK
        keys = pl.ds(pl.multiple_of(lax.rem(tile + half * (key_tiles // 2), key_tiles) * AK, AK), AK)
        first = q_step * AQ
        q = jnp.concatenate([q_ref[lines, s] for s in pieces], axis=0)
        cot = jnp.concatenate([mixed_cot[lines, s] for s in pieces], axis=0)
        wide = jnp.concatenate([wide_buf[:, s] for s in pieces], axis=0)
        place = first + lax.rem(lax.broadcasted_iota(jnp.int32, (1, rows), 1), AQ)
        log_total = jnp.where(place < length, lse_ref[q_step], -NEG_FILL)
        inner = jnp.sum(wide * cot.astype(F32), axis=1, keepdims=True)
        inner = jnp.broadcast_to(inner, (rows, LANES)).T[0:1, :]
        k_tile = k_ref[keys, :]
        v_tile = v_ref[keys, :]
        scores = contract(k_tile, q, 1, 1) * HD**-0.5 - log_total
        if diagonal:
            key_place = tile * AK + lax.broadcasted_iota(jnp.int32, (AK, rows), 0)
            scores = jnp.where(key_place <= place, scores, NEG_FILL)
        weights = jnp.exp(scores)
        prob_cot = contract(v_tile, cot, 1, 1)
        score_cot = (weights * (prob_cot - inner)).astype(BF)
        dv_sum[keys, :] += contract(weights.astype(BF), cot, 1, 0)
        dk_sum[keys, :] += contract(score_cot, q, 1, 0) * HD**-0.5
        dq = contract(score_cot, k_tile, 0, 0) * HD**-0.5

        @pl.when(tile == 0)
        def _():
            dq_sum[...] = dq

        @pl.when(tile > 0)
        def _():
            dq_sum[...] += dq

        if diagonal:
            cos, sin = turn_ref[lines, :HD], turn_ref[lines, HD:]
            for h in range(heads):
                part = dq_sum[h * AQ : (h + 1) * AQ, :]
                swapped = jnp.concatenate([part[:, HD // 2 :], -part[:, : HD // 2]], axis=1)
                heads_cot[lines, h * HD : (h + 1) * HD] = (part * cos + swapped * sin).astype(BF)

    starts = [0]
    for n in range(q_steps):
        starts.append(starts[-1] + n * AQ // AK + 1)
    attn_items = starts.pop()

    def wide_load(q_step):
        stored = lax.rem(q_step + half * (q_steps // 2), q_steps)
        lines = pl.ds(pl.multiple_of(stored * AQ, AQ), AQ)
        return pltpu.make_async_copy(wide_ref.at[lines, :], wide_buf, w_sem.at[1])

    def attn_one(n):
        q_step = sum([jnp.where(n >= start, 1, 0) for start in starts[1:]], jnp.int32(0))
        tile = n - sum([jnp.where(n >= b, b - a, 0) for a, b in zip(starts, starts[1:])], jnp.int32(0))
        last = q_step * AQ // AK

        @pl.when(tile == 0)
        def _():
            wide_load(q_step).wait()

        @pl.when(tile < last)
        def _():
            attn_item(q_step, tile, False)

        @pl.when(tile == last)
        def _():
            attn_item(q_step, tile, True)

            @pl.when(q_step + 1 < q_steps)
            def _():
                wide_load(q_step + 1).start()

    def attn_finish():
        part = dk_sum[...]
        swapped = jnp.concatenate([part[:, HD // 2 :], -part[:, : HD // 2]], axis=1)
        heads_cot[:, heads_width : heads_width + HD] = (part * turn_ref[:, :HD] + swapped * turn_ref[:, HD:]).astype(BF)
        heads_cot[:, heads_width + HD : heads_width + 2 * HD] = dv_sum[...].astype(BF)

    def head_load(i):
        slot = lax.rem(i, 2)
        lines = pl.ds(pl.multiple_of(i * MB, MB), MB)
        return pltpu.make_async_copy(x_ref.at[lines, :], bufs.at[slot, 1], buf_sem.at[slot, 1])

    def head_item(i):
        slot = lax.rem(i, 2)

        @pl.when(i + 1 < blocks)
        def _():
            head_load(i + 1).start()

        head_load(i).wait()
        lines = pl.ds(pl.multiple_of(i * MB, MB), MB)
        part = contract(heads_cot[lines, :heads_width], wq_ref[...], 1, 1)
        part += contract(heads_cot[lines, heads_width : heads_width + 2 * HD], wkv_ref[...], 1, 1)

        @pl.when(i > 0)
        def _():
            row_store(attn_part, i - 1).wait()

        bufs[slot, 2] = part.astype(BF)
        row_store(attn_part, i).start()
        inner = jnp.sum(part * gain_ref[0:1, :] * bufs[slot, 1].astype(F32), axis=1, keepdims=True)
        dots[pl.ds(i, 1), :] = jnp.broadcast_to(inner, (MB, LANES)).T[0:1, :]

    def dot_give():
        n = blocks // 2
        return remote(dots.at[pl.ds(n, n), :], dots_mate, dot_send.at[0], dot_recv.at[0], **mate)

    def dot_share():
        n = blocks // 2
        return [
            remote(dots.at[pl.ds(0, n), :], dots_col.at[s], dot_send.at[1 + s], dot_recv.at[1 + s], **peer)
            for s, peer in enumerate((near_x, near_y, corner))
        ]

    def emit(work, out, sem):
        for a in range(2):
            sum_total = work.total(a)
            h = tok // 4
            for b in range(2):
                lines = pl.ds(a * 2 * h + b * h, h)
                resid_sum = sum_total[b * h : (b + 1) * h]
                emit_buf[...] = resid_sum
                c = pltpu.make_async_copy(emit_buf, out.at[lines, :], sem)
                c.start()
                c.wait()

    emit_buf, = take(1)

    pltpu.make_async_copy(w_ref.at[pl.ds(pl.multiple_of(col * heads_width, heads_width), heads_width), :], w_mine, w_sem.at[0]).start()
    gain_part[...] = jnp.zeros_like(gain_part)
    heads_cot[:, heads_width + 2 * HD :] = jnp.zeros((span, CC - heads_width - 2 * HD), BF)
    zsum.begin()
    dk_sum[...] = jnp.zeros_like(dk_sum)
    dv_sum[...] = jnp.zeros_like(dv_sum)
    zsum.greet([near_x, near_y, corner, mate])

    at = {}

    def plan(tick, action):
        at.setdefault(tick, []).append(action)

    def start_all(copies):
        for c in copies:
            c.start()

    plan(0, mlp_reduce.begin)
    plan(T_ONE, lambda: [mlp_reduce.first(a) for a in range(2)])
    plan(T_TWO, lambda: [mlp_reduce.second(a) for a in range(2)])

    def own_block():
        for a in range(2):
            mine[mlp_reduce.lines(a), :] = mlp_reduce.total(a).astype(BF)
        gather.begin()

    plan(T_SUM, own_block)
    plan(T_GATHER, gather.first)
    plan(T_GATHER + 3, gather.second)

    def start_mid():
        gather.finish()
        mlp_reduce.finish()
        pltpu.make_async_copy(w_ref.at[pl.ds(0, heads_width), :], w_mine, w_sem.at[0]).wait()
        start_all(mid_loads(jnp.int32(0)))
        low_reduce.begin()

    plan(T_MID, start_mid)
    plan(T_MID + 4, lambda: [low_reduce.first(a) for a in range(2)])
    plan(T_MID + 9, lambda: [low_reduce.second(a) for a in range(2)])

    def low_done():
        emit(low_reduce, down_out, out_sem.at[2])
        low_reduce.finish()
        for i, peer in enumerate((near_x, near_y, mate)):
            pl.semaphore_signal(ready.at[i], inc=1, device_id=peer, device_id_type=MESH)

    plan(T_MID + 13, low_done)
    t_attn = T_MID + 1 + blocks // N_MID
    plan(t_attn, lambda: (row_store(mid_low, blocks - 1).wait(), wide_load(jnp.int32(0)).start()))
    t_head = t_attn + 1 + attn_items // N_ATTN
    plan(t_head, lambda: (attn_finish(), head_load(jnp.int32(0)).start()))
    t_last = t_head + 1 + blocks // N_HEAD

    def start_last():
        row_store(attn_part, blocks - 1).wait()
        dot_give().start()
        for i in range(3):
            pl.semaphore_wait(ready.at[i], 1)
        attn_reduce.begin()

    plan(t_last, start_last)

    def last_first():
        n = blocks // 2
        done(dots_mate, dot_recv.at[0])
        dot_give().wait_send()
        dots[pl.ds(0, n), :] = dots[pl.ds(0, n), :] + dots_mate[...]
        start_all(dot_share())
        for a in range(2):
            attn_reduce.first(a)

    plan(t_last + 3, last_first)
    plan(t_last + 7, lambda: [attn_reduce.second(a) for a in range(2)])

    def last_done():
        n = blocks // 2
        shares = dot_share()
        for c in shares:
            c.wait()
        terms = [dots[pl.ds(0, n), :], dots_col[0], dots_col[1], dots_col[2]]
        dot_out[...] = (terms[0] + terms[1]) + (terms[2] + terms[3])
        emit(attn_reduce, attn_out, out_sem.at[2])
        attn_reduce.finish()

    plan(t_last + 10, last_done)
    final = max(zsum.total + OFFS[3], t_last + 11)

    def tick(t, carry):
        zsum.tick(t)
        for when in sorted(at):

            @pl.when(t == when)
            def _(when=when):
                for action in at[when]:
                    action()

        @pl.when((t > T_MID) & (t < t_attn))
        def _():
            for e in range(N_MID):
                mid_item((t - T_MID - 1) * N_MID + e)

        @pl.when((t > t_attn) & (t < t_head))
        def _():
            def body(e, carry):
                attn_one((t - t_attn - 1) * N_ATTN + e)
                return carry

            lax.fori_loop(0, N_ATTN, body, 0)

        @pl.when((t > t_head) & (t < t_last))
        def _():
            for e in range(N_HEAD):
                head_item((t - t_head - 1) * N_HEAD + e)

        return carry

    lax.fori_loop(0, final, tick, 0)
    zsum.finish()


T_ONE, T_TWO, T_SUM, T_GATHER, T_MID = 2, 7, 10, 12, 19
N_MID, N_ATTN, N_HEAD = 2, 2, 4


def backward(info, gains, normed_mlp, gate_cot, up_cot, hidden, mlp_part, low_part, resid, low, w_out_full, mixed, q, k, v, wide, lse, cos, sin,
             wq, wkv, normed, tokens_full, cid):
    span, full = normed.shape
    tok, width = span // 2, full // 4
    heads_width = mixed.shape[1]
    heads = heads_width // HD
    units = hidden.shape[1]
    kinds = ["rows", "columns", "columns", "rows", "stack"]
    sources = [(units, full), (full, units), (full, units), (heads_width, full), (full, CC)]
    outs = [jax.ShapeDtypeStruct(grad_plan(kd, s)[5], BF) for kd, s in zip(kinds, sources)]
    outs = [outs[i] for i in (1, 2, 0, 3, 4)]
    vmem = pl.BlockSpec(memory_space=pltpu.VMEM)
    dma = pltpu.SemaphoreType.DMA
    blocks = span // MB
    turn = jnp.concatenate([cos, sin], axis=1)
    lse = lse.reshape(span // QB, heads, QB // AQ, AQ).transpose(0, 2, 1, 3).reshape(span // AQ, 1, heads * AQ)
    shapes = outs + [
        jax.ShapeDtypeStruct((tok, width), F32),
        jax.ShapeDtypeStruct((8, width), F32),
        jax.ShapeDtypeStruct((tok, width), F32),
        jax.ShapeDtypeStruct((tok, width), F32),
        jax.ShapeDtypeStruct((blocks // 2, LANES), F32),
        jax.ShapeDtypeStruct((span, full), BF),
        jax.ShapeDtypeStruct((span, full), BF),
        jax.ShapeDtypeStruct((span, full), BF),
    ]
    out_specs = [ANY] * 5 + [ANY, vmem, ANY, ANY, vmem, ANY, ANY, ANY]
    scratch = (
        [pltpu.VMEM((span, CC), BF)]
        + GroupSum.scratch(kinds, span)
        + Reduce.scratch(tok, full)
        + Reduce.sems() * 3
        + [pltpu.VMEM((tok, width), BF)]
        + Gather.sems()
        + [
            pltpu.VMEM((2, 3, MB, full), BF),
            pltpu.VMEM((2, MB, full), F32),
            pltpu.VMEM((MB, width), F32),
            dma((2, 3)),
            dma((3,)),
            pltpu.VMEM((span, heads_width), BF),
            pltpu.VMEM((AQ, heads_width), F32),
            pltpu.VMEM((heads * AQ, HD), F32),
            pltpu.VMEM((span, HD), F32),
            pltpu.VMEM((span, HD), F32),
            pltpu.VMEM((blocks, LANES), F32),
            pltpu.VMEM((blocks // 2, LANES), F32),
            pltpu.VMEM((3, blocks // 2, LANES), F32),
            dma((4,)),
            dma((4,)),
            pltpu.SemaphoreType.REGULAR((3,)),
            pltpu.VMEM((heads_width, full), BF),
            dma((2,)),
            pltpu.VMEM((tok // 4, width), F32),
        ]
    )
    results = pl.pallas_call(
        functools.partial(backward_kernel, kinds),
        in_specs=[pl.BlockSpec(memory_space=pltpu.SMEM), vmem] + [ANY] * 13 + [vmem] * 7,
        out_specs=out_specs,
        out_shape=shapes,
        scratch_shapes=scratch,
        compiler_params=pltpu.CompilerParams(
            collective_id=cid, has_side_effects=True, vmem_limit_bytes=VMEM_ALL
        ),
        name="backward",
    )(info, gains, normed_mlp, gate_cot, up_cot, hidden, mlp_part, low_part, resid, low, w_out_full, mixed, wide, normed,
      tokens_full, q, k, v, lse, turn, wq, wkv)
    return results[:10]


def by_distance(stacked, dim):
    count = lax.axis_size("col")
    order = lax.axis_index("col") ^ jnp.arange(count)
    blocks = jnp.take(stacked, order, axis=0)
    return jnp.concatenate([blocks[i] for i in range(count)], axis=dim)


def plain_gather(x):
    cols = by_distance(lax.all_gather(x, "col"), 1)
    return jnp.concatenate([cols, swap(cols, "row", 1)], axis=0)


def plain_gather_heads(x):
    mine = lax.all_gather(x, "col", axis=1, tiled=True)
    half = x.shape[0] // 2
    other = swap(mine, "row", 1)
    other = jnp.concatenate([other[half:], other[:half]], axis=0)
    return jnp.concatenate([mine, other], axis=1)


def plain_reduce(part):
    span, full = part.shape
    count = lax.axis_size("col")
    width = full // count
    half = part[: span // 2].astype(F32) + swap(part[span // 2 :], "row", 1).astype(F32)
    order = lax.axis_index("col") ^ jnp.arange(count)
    blocks = jnp.stack([half[:, s * width : (s + 1) * width] for s in range(count)])
    return lax.psum_scatter(jnp.take(blocks, order, axis=0), "col", tiled=False)


def exchange(packs):
    if kernels_fit():
        return [p if s == 0 else swap(p, "col", s) for s, p in enumerate(packs)]
    count = len(packs)
    order = lax.axis_index("col") ^ jnp.arange(count)
    sent = jnp.take(jnp.stack(packs), order, axis=0)
    blocks = jnp.take(lax.all_to_all(sent, "col", 0, 0, tiled=True), order, axis=0)
    return [blocks[i] for i in range(count)]


def plain_group_sum(grads, kinds):
    outs = []
    count = lax.axis_size("col")
    order = lax.axis_index("col") ^ jnp.arange(count)
    for grad, kind in zip(grads, kinds):
        grad = lax.psum(grad.astype(F32), "dp").astype(BF)
        dim = 1 if kind == "rows" else 0
        blocks = jnp.stack(jnp.split(grad, count, axis=dim))
        blocks = lax.all_to_all(jnp.take(blocks, order, axis=0), "col", 0, 0, tiled=True)
        out_dim = 1 if kind == "columns" else 0
        outs.append(jnp.concatenate([blocks[i] for i in range(count)], axis=out_dim))
    return outs


def kernels_fit():
    return lax.axis_size("col") == 4 and lax.axis_size("dp") == 4 and lax.axis_size("row") == 2


def attn_forward_kernel(info_ref, q_ref, k_ref, v_ref, *refs):
    linked = len(refs) > 6
    if linked:
        side_ref, mixed_ref, wide_ref, lse_ref, peak_ref, side_out, score_ref, sum_ref, stage = refs[:9]
        gather = Gather(side_ref, side_out, token_place(*side_ref.shape), stage, refs[9:])
    else:
        mixed_ref, wide_ref, lse_ref, peak_ref, score_ref, sum_ref = refs
    heads = q_ref.shape[1] // HD
    span = k_ref.shape[0]
    rows = heads * QB
    length = info_ref[0]
    half = lax.axis_index("row")
    step = pl.program_id(0)
    first = step * QB
    key_tiles = span // FWD_KB
    steps = span // QB
    lines = pl.ds(pl.multiple_of(lax.rem(step + half * (steps // 2), steps) * QB, QB), QB)

    if linked:

        @pl.when(step == 0)
        def _():
            greet(list(gather.near))
            gather.begin()

        @pl.when(step == steps - 1)
        def _():
            gather.first()

    q = jnp.concatenate([q_ref[lines, h * HD : (h + 1) * HD] for h in range(heads)], axis=0)
    tiles = (first + QB) // FWD_KB
    plain = first // FWD_KB

    def tile_of(ref, tile):
        stored = lax.rem(tile + half * (key_tiles // 2), key_tiles)
        return ref[pl.ds(pl.multiple_of(stored * FWD_KB, FWD_KB), FWD_KB), :]

    def fold(values, running, op):
        for t in range(FWD_KB // LANES):
            running = op(running, values[:, t * LANES : (t + 1) * LANES])
        return running

    def scores_of(tile, top, diagonal):
        scores = contract(q, tile_of(k_ref, tile), 1, 1) * HD**-0.5
        if diagonal:
            place = first + lax.broadcasted_iota(jnp.int32, (QB, FWD_KB), 0)
            key_place = tile * FWD_KB + lax.broadcasted_iota(jnp.int32, (QB, FWD_KB), 1)
            allowed = (key_place <= place) & (key_place < length)
            scores = jnp.where(allowed[None], scores.reshape(heads, QB, FWD_KB), NEG_FILL)
            scores = scores.reshape(rows, FWD_KB)
        else:
            key_place = tile * FWD_KB + lax.broadcasted_iota(jnp.int32, (1, FWD_KB), 1)
            scores = jnp.where(key_place < length, scores, NEG_FILL)
        score_ref[tile] = scores
        return fold(scores, top, jnp.maximum)

    top = jnp.full((rows, LANES), NEG_FILL, F32)
    top = lax.fori_loop(0, plain, lambda tile, top: scores_of(tile, top, False), top)
    top = lax.fori_loop(plain, tiles, lambda tile, top: scores_of(tile, top, True), top)
    top = jnp.max(top, axis=1, keepdims=True)
    live = first + lax.broadcasted_iota(jnp.int32, (QB, 1), 0) < length
    peak = jnp.max(jnp.where(live[None], top.reshape(heads, QB, 1), NEG_FILL), axis=1)

    @pl.when(step == 0)
    def _():
        peak_ref[...] = jnp.full_like(peak_ref, NEG_FILL)

    peak_ref[...] = jnp.maximum(peak_ref[...], jnp.broadcast_to(peak, peak_ref.shape))
    sum_ref[...] = jnp.zeros_like(sum_ref)

    def weigh(tile, total):
        weights = jnp.exp(score_ref[tile] - top)
        sum_ref[...] += contract(weights.astype(BF), tile_of(v_ref, tile), 1, 0)
        return fold(weights, total, jnp.add)

    total = lax.fori_loop(0, tiles, weigh, jnp.zeros((rows, LANES), F32))
    total = jnp.sum(total, axis=1, keepdims=True)
    mixed = sum_ref[...] / total
    log_total = jnp.broadcast_to(top + jnp.log(total), (rows, LANES))
    lse_ref[step] = log_total.T[0:1, :]
    for h in range(heads):
        part = mixed[h * QB : (h + 1) * QB]
        mixed_ref[lines, h * HD : (h + 1) * HD] = part.astype(BF)
        wide_ref[lines, h * HD : (h + 1) * HD] = part

    if linked:

        @pl.when(step == steps - 1)
        def _():
            gather.second()
            gather.finish()


def attn_forward(info, q, k, v, side=None, cid=None):
    span, width = q.shape
    heads = width // HD
    steps = span // QB
    whole = lambda shape: pl.BlockSpec(shape, lambda i: (0,) * len(shape))
    pairs = heads * span * span // 2
    shapes = [
        jax.ShapeDtypeStruct((span, width), BF),
        jax.ShapeDtypeStruct((span, width), F32),
        jax.ShapeDtypeStruct((steps, 1, heads * QB), F32),
        jax.ShapeDtypeStruct((heads, LANES), F32),
    ]
    in_specs = [pl.BlockSpec(memory_space=pltpu.SMEM)] + [whole(a.shape) for a in (q, k, v)]
    out_specs = [whole(s.shape) for s in shapes]
    scratch = [
        pltpu.VMEM((span // FWD_KB, heads * QB, FWD_KB), F32),
        pltpu.VMEM((heads * QB, HD), F32),
    ]
    operands = [info, q, k, v]
    params = dict(vmem_limit_bytes=48 * MIB)
    if side is not None:
        tok, wide = side.shape
        operands.append(side)
        in_specs.append(ANY)
        out_specs.append(ANY)
        shapes.append(jax.ShapeDtypeStruct((2 * tok, 4 * wide), side.dtype))
        scratch += [pltpu.VMEM(side.shape, side.dtype)] + Gather.sems()
        params.update(collective_id=cid, has_side_effects=True)
    return pl.pallas_call(
        attn_forward_kernel,
        grid=(steps,),
        in_specs=in_specs,
        out_specs=out_specs,
        scratch_shapes=scratch,
        out_shape=shapes,
        compiler_params=pltpu.CompilerParams(**params),
        cost_estimate=pl.CostEstimate(
            flops=40 * pairs * HD // 4, transcendentals=pairs, bytes_accessed=8 * span * width
        ),
        name="attn_forward",
    )(*operands)


def turn_back(values, cos_ref, sin_ref):
    half = HD // 2
    swapped = jnp.concatenate([values[:, half:], -values[:, :half]], axis=1)
    return values * cos_ref[...] + swapped * sin_ref[...]


def attn_backward_kernel(
    info_ref, q_ref, k_ref, v_ref, cot_ref, wide_ref, lse_ref, cosq_ref, sinq_ref, cosk_ref, sink_ref,
    dq_ref, dk_ref, dv_ref, dq_sum, dk_sum, dv_sum,
):
    heads = q_ref.shape[1] // HD
    span = k_ref.shape[0]
    rows = heads * QB
    length = info_ref[0]
    half = info_ref[1]
    step = pl.program_id(0)
    first = step * QB
    key_tiles = span // BWD_KB

    @pl.when(step == 0)
    def _():
        dk_sum[...] = jnp.zeros_like(dk_sum)
        dv_sum[...] = jnp.zeros_like(dv_sum)

    dq_sum[...] = jnp.zeros_like(dq_sum)

    @pl.when(first < length)
    def _():
        pieces = [slice(h * HD, (h + 1) * HD) for h in range(heads)]
        q = jnp.concatenate([q_ref[:, s] for s in pieces], axis=0)
        cot = jnp.concatenate([cot_ref[:, s] for s in pieces], axis=0)
        wide = jnp.concatenate([wide_ref[:, s] for s in pieces], axis=0)
        log_total = lse_ref[0]
        inner = jnp.sum(wide * cot.astype(F32), axis=1, keepdims=True)
        inner = jnp.broadcast_to(inner, (rows, LANES)).T[0:1, :]

        def tile_step(tile, masked):
            stored = lax.rem(tile + half * (key_tiles // 2), key_tiles)
            keys = pl.ds(pl.multiple_of(stored * BWD_KB, BWD_KB), BWD_KB)
            k_tile = k_ref[keys, :]
            v_tile = v_ref[keys, :]
            scores = contract(k_tile, q, 1, 1) * HD**-0.5 - log_total
            if masked:
                key_place = tile * BWD_KB + lax.broadcasted_iota(jnp.int32, (BWD_KB, rows), 0)
                place = first + lax.rem(lax.broadcasted_iota(jnp.int32, (BWD_KB, rows), 1), QB)
                scores = jnp.where((key_place <= place) & (key_place < length), scores, NEG_FILL)
            weights = jnp.exp(scores)
            prob_cot = contract(v_tile, cot, 1, 1)
            score_cot = (weights * (prob_cot - inner)).astype(BF)
            dv_sum[keys, :] += contract(weights.astype(BF), cot, 1, 0)
            dk_sum[keys, :] += contract(score_cot, q, 1, 0) * HD**-0.5
            dq_sum[...] += contract(score_cot, k_tile, 0, 0) * HD**-0.5

        @pl.loop(0, first // BWD_KB)
        def _(tile):
            tile_step(tile, False)

        @pl.loop(first // BWD_KB, pl.cdiv(first + QB, BWD_KB))
        def _(tile):
            tile_step(tile, True)

    for h in range(heads):
        part = turn_back(dq_sum[h * QB : (h + 1) * QB, :], cosq_ref, sinq_ref)
        dq_ref[:, h * HD : (h + 1) * HD] = part.astype(dq_ref.dtype)

    @pl.when(step == pl.num_programs(0) - 1)
    def _():
        dk_ref[...] = turn_back(dk_sum[...], cosk_ref, sink_ref).astype(dk_ref.dtype)
        dv_ref[...] = dv_sum[...].astype(dv_ref.dtype)


def attn_backward(info, q, k, v, cot, wide, lse, cos, sin, kv_type):
    span, width = q.shape
    heads = width // HD
    steps = span // QB

    def stored(i, info_ref):
        return (lax.rem(i + info_ref[1] * (steps // 2), steps), 0)

    whole = pl.BlockSpec((span, HD), lambda i, info_ref: (0, 0))
    mine = pl.BlockSpec((QB, width), stored)
    turn = pl.BlockSpec((QB, HD), stored)
    pairs = heads * span * span // 2
    return pl.pallas_call(
        attn_backward_kernel,
        grid_spec=pltpu.PrefetchScalarGridSpec(
            num_scalar_prefetch=1,
            grid=(steps,),
            in_specs=[
                mine, whole, whole, mine, mine,
                pl.BlockSpec((1, 1, heads * QB), lambda i, info_ref: (i, 0, 0)),
                turn, turn, whole, whole,
            ],
            out_specs=[mine, whole, whole],
            scratch_shapes=[
                pltpu.VMEM((heads * QB, HD), F32),
                pltpu.VMEM((span, HD), F32),
                pltpu.VMEM((span, HD), F32),
            ],
        ),
        out_shape=[
            jax.ShapeDtypeStruct((span, width), BF),
            jax.ShapeDtypeStruct((span, HD), kv_type),
            jax.ShapeDtypeStruct((span, HD), kv_type),
        ],
        compiler_params=pltpu.CompilerParams(vmem_limit_bytes=40 * 2**20),
        cost_estimate=pl.CostEstimate(
            flops=60 * pairs * HD // 4, transcendentals=pairs, bytes_accessed=12 * span * width
        ),
        name="attn_backward",
    )(info, q, k, v, cot, wide, lse, cos, sin, cos, sin)


def head_kernel(x_ref, gain_ref, wq_ref, wkv_ref, cos_ref, sin_ref, normed_ref, q_ref, k_ref, v_ref, scale_ref):
    x = x_ref[...].astype(F32)
    scale = lax.rsqrt(jnp.mean(x * x, axis=1, keepdims=True) + EPSILON)
    scale_ref[...] = jnp.broadcast_to(scale, scale_ref.shape)
    normed = (x * scale * gain_ref[0:1, :]).astype(BF)
    normed_ref[...] = normed

    def turned(raw):
        pieces = []
        half = HD // 2
        for h in range(raw.shape[1] // HD):
            pieces += [-raw[:, h * HD + half : (h + 1) * HD], raw[:, h * HD : h * HD + half]]
        pieces = jnp.concatenate(pieces, axis=1)
        count = raw.shape[1] // HD
        cos = jnp.concatenate([cos_ref[...]] * count, axis=1)
        sin = jnp.concatenate([sin_ref[...]] * count, axis=1)
        return (raw * cos + pieces * sin).astype(BF)

    q_ref[...] = turned(contract(normed, wq_ref[...], 1, 0))
    keyval = contract(normed, wkv_ref[...], 1, 0)
    k_ref[...] = turned(keyval[:, :HD])
    v_ref[...] = keyval[:, HD:].astype(BF)


def project_heads(tokens_full, gains, wq, wkv, cos, sin):
    span, full = tokens_full.shape
    width = wq.shape[1]
    block = 512
    line = lambda n: pl.BlockSpec((block, n), lambda i: (i, 0))
    whole = lambda a: pl.BlockSpec(a.shape, lambda i: (0, 0))
    return pl.pallas_call(
        head_kernel,
        grid=(span // block,),
        in_specs=[line(full), whole(gains), whole(wq), whole(wkv), line(HD), line(HD)],
        out_specs=[line(full), line(width), line(HD), line(HD), line(LANES)],
        out_shape=[
            jax.ShapeDtypeStruct((span, full), BF),
            jax.ShapeDtypeStruct((span, width), BF),
            jax.ShapeDtypeStruct((span, HD), BF),
            jax.ShapeDtypeStruct((span, HD), BF),
            jax.ShapeDtypeStruct((span, LANES), F32),
        ],
        compiler_params=pltpu.CompilerParams(vmem_limit_bytes=48 * MIB),
        cost_estimate=pl.CostEstimate(
            flops=2 * span * full * (width + LANES), transcendentals=0, bytes_accessed=5 * span * full
        ),
        name="project_heads",
    )(tokens_full, gains, wq, wkv, cos, sin)


def project_out_kernel(mixed_ref, w_ref, x_ref, gain_ref, *refs):
    linked = len(refs) > 2
    step = pl.program_id(0)
    if linked:
        side_ref, resid_ref, normed_ref, side_out, stage = refs[:5]
        gather = Gather(side_ref, side_out, token_place(*side_ref.shape), stage, refs[5:])

        @pl.when(step == 0)
        def _():
            greet(list(gather.near))
            gather.begin()

        @pl.when(step == pl.num_programs(0) // 2)
        def _():
            gather.first()

    else:
        resid_ref, normed_ref = refs
    resid = x_ref[...].astype(F32) + contract(mixed_ref[...], w_ref[...], 1, 0)
    resid_ref[...] = resid
    scale = lax.rsqrt(jnp.mean(resid * resid, axis=1, keepdims=True) + EPSILON)
    normed_ref[...] = (resid * scale * gain_ref[1:2, :]).astype(BF)

    if linked:

        @pl.when(step == pl.num_programs(0) - 1)
        def _():
            gather.second()
            gather.finish()


def project_out(mixed_full, w_out_full, tokens_full, gains, side=None, cid=None):
    span, full = tokens_full.shape
    block = 256
    line = pl.BlockSpec((block, full), lambda i: (i, 0))
    operands = [mixed_full, w_out_full, tokens_full, gains]
    in_specs = [
        pl.BlockSpec((block, mixed_full.shape[1]), lambda i: (i, 0)),
        pl.BlockSpec(w_out_full.shape, lambda i: (0, 0), pipeline_mode=pl.Buffered(1)),
        line,
        pl.BlockSpec(gains.shape, lambda i: (0, 0)),
    ]
    out_specs = [line, line]
    shapes = [jax.ShapeDtypeStruct((span, full), F32), jax.ShapeDtypeStruct((span, full), BF)]
    scratch = []
    params = dict(vmem_limit_bytes=48 * MIB)
    if side is not None:
        tok, wide = side.shape
        operands.append(side)
        in_specs.append(ANY)
        out_specs.append(ANY)
        shapes.append(jax.ShapeDtypeStruct((2 * tok, 4 * wide), side.dtype))
        scratch += [pltpu.VMEM(side.shape, side.dtype)] + Gather.sems()
        params.update(collective_id=cid, has_side_effects=True)
    return pl.pallas_call(
        project_out_kernel,
        grid=(span // block,),
        in_specs=in_specs,
        out_specs=out_specs,
        out_shape=shapes,
        scratch_shapes=scratch,
        compiler_params=pltpu.CompilerParams(**params),
        cost_estimate=pl.CostEstimate(
            flops=2 * span * full * full, transcendentals=0, bytes_accessed=12 * span * full
        ),
        name="project_out",
    )(*operands)


def middle_kernel(
    cot_ref, resid_ref, low_ref, gain_ref, w_ref, mixed_ref,
    mixed_cot_ref, own_ref, grad_ref, gain_part_ref, total_ref,
):
    step = pl.program_id(0)
    last = pl.num_programs(0) - 1
    width = own_ref.shape[1]
    cot = cot_ref[...].astype(F32)
    resid = resid_ref[...]
    scale = lax.rsqrt(jnp.mean(resid * resid, axis=1, keepdims=True) + EPSILON)
    weighed = cot * gain_ref[1:2, :]
    inner = jnp.sum(weighed * resid, axis=1, keepdims=True)
    mid = low_ref[...].astype(F32) + weighed * scale - resid * (scale * scale * scale * inner / D)
    low = mid.astype(BF)
    mixed_cot_ref[...] = contract(low, w_ref[...], 1, 1).astype(BF)

    @pl.when(step == 0)
    def _():
        total_ref[...] = jnp.zeros_like(total_ref)
        gain_part_ref[...] = jnp.zeros_like(gain_part_ref)

    total_ref[...] += contract(mixed_ref[...], low, 0, 0)

    @pl.when(step <= last // 2)
    def _():
        own_ref[...] = mid[:, :width]
        part = jnp.sum((cot * resid * scale)[:, :width], axis=0, keepdims=True)
        gain_part_ref[...] += jnp.broadcast_to(part, gain_part_ref.shape)

    @pl.when(step == last)
    def _():
        grad_ref[...] = total_ref[...].astype(BF)


def middle(mlp_cot, resid_mid, out_low, gains, w_mine, mixed, width):
    span, full = resid_mid.shape
    heads_width = mixed.shape[1]
    block = 256
    steps = span // block
    line = pl.BlockSpec((block, full), lambda i: (i, 0))
    thin = pl.BlockSpec((block, heads_width), lambda i: (i, 0))
    return pl.pallas_call(
        middle_kernel,
        grid=(steps,),
        in_specs=[
            line, line, line,
            pl.BlockSpec(gains.shape, lambda i: (0, 0)),
            pl.BlockSpec(w_mine.shape, lambda i: (0, 0)),
            thin,
        ],
        out_specs=[
            thin,
            pl.BlockSpec((block, width), lambda i: (jnp.minimum(i, steps // 2 - 1), 0)),
            pl.BlockSpec((heads_width, full), lambda i: (0, 0)),
            pl.BlockSpec((8, width), lambda i: (0, 0)),
        ],
        out_shape=[
            jax.ShapeDtypeStruct((span, heads_width), BF),
            jax.ShapeDtypeStruct((span // 2, width), F32),
            jax.ShapeDtypeStruct((heads_width, full), BF),
            jax.ShapeDtypeStruct((8, width), F32),
        ],
        scratch_shapes=[pltpu.VMEM((heads_width, full), F32)],
        compiler_params=pltpu.CompilerParams(vmem_limit_bytes=48 * MIB),
        cost_estimate=pl.CostEstimate(
            flops=4 * span * full * heads_width, transcendentals=0, bytes_accessed=8 * span * full
        ),
        name="middle",
    )(mlp_cot, resid_mid, out_low, gains, w_mine, mixed)


def head_back_kernel(
    info_ref, qc_ref, kc_ref, vc_ref, wq_ref, wkv_ref, normed_ref, x_ref, gain_ref,
    part_ref, dot_ref, grad_ref, total_ref,
):
    step = pl.program_id(0)
    wide = qc_ref.shape[1]
    keyval = jnp.concatenate([kc_ref[...], vc_ref[...]], axis=1)
    counted = keyval * info_ref[2].astype(BF)
    part = contract(qc_ref[...], wq_ref[...], 1, 1) + contract(counted, wkv_ref[...], 1, 1)
    part_ref[...] = part.astype(BF)
    inner = jnp.sum(part * gain_ref[0:1, :] * x_ref[...].astype(F32), axis=1, keepdims=True)
    dot_ref[0] = jnp.broadcast_to(inner, (inner.shape[0], LANES)).T[0:1, :]

    @pl.when(step == 0)
    def _():
        total_ref[...] = jnp.zeros_like(total_ref)

    total_ref[:, :wide] += contract(normed_ref[...], qc_ref[...], 0, 0)
    total_ref[:, wide:] += contract(normed_ref[...], keyval, 0, 0)

    @pl.when(step == pl.num_programs(0) - 1)
    def _():
        used = wide + 2 * HD
        grad_ref[:, :used] = total_ref[...].astype(BF)
        grad_ref[:, used:] = jnp.zeros((grad_ref.shape[0], grad_ref.shape[1] - used), BF)


def head_back(info, query_cot, key_cot, value_cot, wq, wkv, normed, tokens_full, gains):
    span, full = normed.shape
    wide = query_cot.shape[1]
    block = 512
    steps = span // block
    line = lambda n: pl.BlockSpec((block, n), lambda i, info_ref: (i, 0))
    whole = lambda shape: pl.BlockSpec(shape, lambda i, info_ref: (0, 0))
    grad_width = max(CC, wide + 2 * HD)
    return pl.pallas_call(
        head_back_kernel,
        grid_spec=pltpu.PrefetchScalarGridSpec(
            num_scalar_prefetch=1,
            grid=(steps,),
            in_specs=[
                line(wide), line(HD), line(HD), whole(wq.shape), whole(wkv.shape), line(full), line(full),
                whole(gains.shape),
            ],
            out_specs=[
                line(full),
                pl.BlockSpec((1, 1, block), lambda i, info_ref: (i, 0, 0)),
                whole((full, grad_width)),
            ],
            scratch_shapes=[pltpu.VMEM((full, wide + 2 * HD), F32)],
        ),
        out_shape=[
            jax.ShapeDtypeStruct((span, full), BF),
            jax.ShapeDtypeStruct((steps, 1, block), F32),
            jax.ShapeDtypeStruct((full, grad_width), BF),
        ],
        compiler_params=pltpu.CompilerParams(vmem_limit_bytes=48 * MIB),
        cost_estimate=pl.CostEstimate(
            flops=4 * span * full * (wide + LANES), transcendentals=0, bytes_accessed=6 * span * full
        ),
        name="head_back",
    )(info, query_cot, key_cot, value_cot, wq, wkv, normed, tokens_full, gains)


def fill_units(out, pieces, part, sem):
    mine = lax.rem(lax.axis_index("dp"), 2)
    rows = out.shape[0] // 8
    copies = []
    for s in range(4):
        for which, piece in ((mine, pieces[0]), (1 - mine, pieces[1])):
            lines = pl.ds(pl.multiple_of(s * 2 * rows + which * rows, rows), rows)
            src = piece.at[pl.ds((2 * s + part) * rows, rows), :]
            copies.append(pltpu.make_async_copy(src, out.at[lines, :], sem.at[len(copies)]))
    return copies


def hidden_kernel(x_ref, *refs):
    pieces = refs[:2]
    gate_ref, up_ref, hidden_ref, w_gate, w_up, gate_sem, up_sem = refs[2:]

    @pl.when(pl.program_id(0) == 0)
    def _():
        copies = fill_units(w_gate, pieces, 0, gate_sem) + fill_units(w_up, pieces, 1, up_sem)
        for c in copies:
            c.start()
        for c in copies:
            c.wait()

    gate = contract(x_ref[...], w_gate[...], 1, 0)
    gate_ref[...] = gate
    up = contract(x_ref[...], w_up[...], 1, 0)
    up_ref[...] = up
    hidden_ref[...] = (gate * jax.nn.sigmoid(gate) * up).astype(BF)


def hidden_units(normed, pieces):
    span, full = normed.shape
    units = pieces[0].shape[1]
    block = 256
    thin = pl.BlockSpec((block, units), lambda i: (i, 0))
    return pl.pallas_call(
        hidden_kernel,
        grid=(span // block,),
        in_specs=[pl.BlockSpec((block, full), lambda i: (i, 0))] + [ANY] * 2,
        out_specs=[thin] * 3,
        out_shape=[
            jax.ShapeDtypeStruct((span, units), F32),
            jax.ShapeDtypeStruct((span, units), F32),
            jax.ShapeDtypeStruct((span, units), BF),
        ],
        scratch_shapes=[
            pltpu.VMEM((full, units), BF),
            pltpu.VMEM((full, units), BF),
            pltpu.SemaphoreType.DMA((8,)),
            pltpu.SemaphoreType.DMA((8,)),
        ],
        compiler_params=pltpu.CompilerParams(vmem_limit_bytes=48 * MIB),
        cost_estimate=pl.CostEstimate(
            flops=4 * span * full * units, transcendentals=span * units, bytes_accessed=6 * span * full
        ),
        name="hidden_units",
    )(normed, *pieces)


def hidden_back_kernel(low_ref, gate_ref, up_ref, hidden_ref, own_ref, *refs):
    pieces, down_pieces = refs[:2], refs[2:5]
    gate_cot_ref, up_cot_ref, part_ref, low_part_ref, w_gate, w_up, w_down, gate_sem, up_sem, down_sem = refs[5:]
    units = w_down.shape[0]
    width = w_down.shape[1] // 4

    @pl.when(pl.program_id(0) == 0)
    def _():
        mine = own_ref.at[pl.ds(pl.multiple_of(lax.axis_index("col") * units, units), units), :]
        copies = [
            pltpu.make_async_copy(p, w_down.at[:, pl.ds(s * width, width)], down_sem.at[s])
            for s, p in enumerate((mine, *down_pieces))
        ]
        copies += fill_units(w_gate, pieces, 0, gate_sem) + fill_units(w_up, pieces, 1, up_sem)
        for c in copies:
            c.start()
        for c in copies:
            c.wait()

    hidden_cot = contract(low_ref[...], w_down[...], 1, 1)
    gate = gate_ref[...]
    sig = jax.nn.sigmoid(gate)
    gate_cot = (hidden_cot * up_ref[...] * sig * (1.0 + gate * (1.0 - sig))).astype(BF)
    up_cot = (hidden_cot * gate * sig).astype(BF)
    gate_cot_ref[...] = gate_cot
    up_cot_ref[...] = up_cot
    part = contract(gate_cot, w_gate[...], 1, 1) + contract(up_cot, w_up[...], 1, 1)
    part_ref[...] = part.astype(BF)
    low_part_ref[...] = contract(hidden_ref[...], w_down[...], 1, 0).astype(BF)


def hidden_back(low, gate, up, hidden, w_down, pieces, down_pieces):
    span, full = low.shape
    units = gate.shape[1]
    block = 256
    thin = pl.BlockSpec((block, units), lambda i: (i, 0))
    line = pl.BlockSpec((block, full), lambda i: (i, 0))
    return pl.pallas_call(
        hidden_back_kernel,
        grid=(span // block,),
        in_specs=[line, thin, thin, thin] + [ANY] * 6,
        out_specs=[thin, thin, line, line],
        out_shape=[jax.ShapeDtypeStruct((span, units), BF)] * 2 + [jax.ShapeDtypeStruct((span, full), BF)] * 2,
        scratch_shapes=[
            pltpu.VMEM((full, units), BF),
            pltpu.VMEM((full, units), BF),
            pltpu.VMEM((units, full), BF),
            pltpu.SemaphoreType.DMA((8,)),
            pltpu.SemaphoreType.DMA((8,)),
            pltpu.SemaphoreType.DMA((4,)),
        ],
        compiler_params=pltpu.CompilerParams(vmem_limit_bytes=52 * MIB),
        cost_estimate=pl.CostEstimate(
            flops=8 * span * full * units, transcendentals=span * units, bytes_accessed=12 * span * full
        ),
        name="hidden_back",
    )(low, gate, up, hidden, w_down, *pieces, *down_pieces)


def on_device(
    tokens, lengths, attn_gain, w_query, w_key, w_value, w_out, mlp_gain, w_gate, w_up, w_down, cotangent
):
    row_devices = lax.axis_size("row")
    col_devices = lax.axis_size("col")
    row = lax.axis_index("row")
    col = lax.axis_index("col")
    fit = kernels_fit()
    tok, width = tokens.shape
    span = tok * row_devices
    group = HQ // KV
    heads_row = HQ // row_devices
    heads = heads_row // col_devices
    head_width = heads * HD
    keyval_row = KV // row_devices
    units = w_gate.shape[1] // col_devices
    length = lengths[0]
    shared_key = heads < group
    sharers = max(1, group // heads)
    leader = (col % sharers == 0).astype(jnp.int32)
    info = jnp.stack([length, row, leader]).astype(jnp.int32)

    keyval = []
    for owner in range(col_devices):
        first = owner * heads // group * HD
        keyval += [w_key[:, first : first + HD], w_value[:, first : first + HD]]
    keyval = jnp.concatenate(keyval, axis=1)
    gains = jnp.concatenate([attn_gain[None], mlp_gain[None], jnp.zeros((6, width), F32)], axis=0)

    if fit:
        tokens_full, wq, wkv, gains = first_gather(tokens, w_query, keyval, gains, 1)
    else:
        tokens_full = plain_gather(tokens)
        def slices(weight, size):
            return [lax.dynamic_slice_in_dim(weight, (col ^ s) * size, size, 1) for s in range(col_devices)]

        wq = jnp.concatenate(exchange(slices(w_query, head_width)), axis=0)
        wkv = jnp.concatenate(exchange(slices(keyval, LANES)), axis=0)
        gains = by_distance(lax.all_gather(gains, "col"), 1)
    w_gate, w_up, tokens_full = lax.optimization_barrier((w_gate, w_up, tokens_full))
    place = lax.rem(jnp.arange(span, dtype=jnp.int32) + row * tok, span)
    frequency = ROPE_BASE ** (-jnp.arange(HD // 2, dtype=F32) * (2.0 / HD))
    angle = place.astype(F32)[:, None] * frequency[None, :]
    cos = jnp.tile(jnp.cos(angle), (1, 2))
    sin = jnp.tile(jnp.sin(angle), (1, 2))

    normed_attn, query, key, value, scale_a = project_heads(tokens_full, gains, wq, wkv, cos, sin)
    valid = (row * tok + jnp.arange(tok, dtype=jnp.int32) < length).astype(BF)
    cot_low = cotangent * valid[:, None]
    def unit_pieces():
        rows = width // 2
        start = lax.rem(lax.axis_index("dp"), 2) * rows
        near = [
            jnp.concatenate(
                [lax.dynamic_slice(w, (start, (col ^ s) * units), (rows, units)) for w in (w_gate, w_up)], axis=0
            )
            for s in range(col_devices)
        ]
        return jnp.concatenate(exchange(near), axis=0)

    def unit_slices(weight, dim):
        return [lax.dynamic_slice_in_dim(weight, (col ^ s) * units, units, dim) for s in range(col_devices)]

    if fit:
        near_units = unit_pieces()
        mixed, mixed_wide, log_total, peak, w_out_full = attn_forward(info, query, key, value, w_out, 7)
        mixed, near_units = lax.optimization_barrier((mixed, near_units))
        pieces = [near_units, swap(near_units, "dp", 1)]
        mixed_full = gather_heads(mixed, 2)
        resid_mid, normed_mlp, out_low = project_out(mixed_full, w_out_full, tokens_full, gains, cot_low, 8)
        w_down, normed_mlp = lax.optimization_barrier((w_down, normed_mlp))
        down_pieces = [
            swap(lax.dynamic_slice_in_dim(w_down, (col ^ s) * units, units, 0), "col", s) for s in range(1, col_devices)
        ]
        gate, up, hidden = hidden_units(normed_mlp, pieces)
        hidden, peak = lax.optimization_barrier((hidden, peak))
        moved = [swap(peak, "dp", step) for step in (1, 2, 3)]
        down_pieces, moved = lax.optimization_barrier((down_pieces, moved))
        for other in moved:
            peak = jnp.maximum(peak, other)
        own_peaks = peak[:, 0]
        others = [swap(own_peaks[None, :], "col", step) for step in (1, 2, 3)]
        gate_cot, up_cot, mlp_part, down_part = hidden_back(
            out_low, gate, up, hidden, w_down, pieces, down_pieces
        )
        mlp_part, others = lax.optimization_barrier((mlp_part, others))
        row_peaks = jnp.where(jnp.arange(4)[:, None] == col, own_peaks[None, :], NEG_FILL)
        for step, other in zip((1, 2, 3), others):
            row_peaks = jnp.where(jnp.arange(4)[:, None] == col ^ step, other, row_peaks)
    else:
        mixed, mixed_wide, log_total, peak = attn_forward(info, query, key, value)
        mixed_full = plain_gather_heads(mixed)
        w_out_full = plain_gather(w_out)
        resid_mid, normed_mlp = project_out(mixed_full, w_out_full, tokens_full, gains)
        out_low = plain_gather(cot_low)
        w_gate_units = jnp.concatenate(exchange(unit_slices(w_gate, 1)), axis=0)
        w_up_units = jnp.concatenate(exchange(unit_slices(w_up, 1)), axis=0)
        w_down_units = jnp.concatenate(exchange(unit_slices(w_down, 0)), axis=1)
        gate = jnp.dot(normed_mlp, w_gate_units, preferred_element_type=F32)
        up = jnp.dot(normed_mlp, w_up_units, preferred_element_type=F32)
        gate_sigmoid = jax.nn.sigmoid(gate)
        hidden = (gate * gate_sigmoid * up).astype(BF)
        hidden_cot = contract(out_low, w_down_units, 1, 1)
        gate_cot = (
            hidden_cot * up * gate_sigmoid * (1.0 + gate * (1.0 - gate_sigmoid))
        ).astype(BF)
        up_cot = (hidden_cot * gate * gate_sigmoid).astype(BF)
        mlp_part = (contract(gate_cot, w_gate_units, 1, 1) + contract(up_cot, w_up_units, 1, 1)).astype(BF)
        down_part = jnp.dot(hidden, w_down_units, preferred_element_type=F32).astype(BF)

    if fit:
        *sums, mid_cot, gain_m_part, attn_cot, down_sum, width_dot = backward(
            info, gains, normed_mlp, gate_cot, up_cot, hidden, mlp_part, down_part, resid_mid, out_low, w_out_full,
            mixed, query, key, value, mixed_wide, log_total, cos, sin, wq, wkv, normed_attn, tokens_full, 3,
        )
        width_dot = width_dot.reshape(tok)
    else:
        mlp_cot = plain_gather(plain_reduce(mlp_part).astype(BF))
        down_sum = plain_reduce(down_part)
        w_mine = lax.dynamic_slice_in_dim(w_out_full, col * head_width, head_width, 0)
        mixed_cot, mid_cot, grad_out, gain_m_part = middle(
            mlp_cot, resid_mid, out_low, gains, w_mine, mixed, width
        )
        query_cot, key_cot, value_cot = attn_backward(
            info, query, key, value, mixed_cot, mixed_wide, log_total, cos, sin, F32 if shared_key else BF
        )
        if shared_key:
            for bit in range(sharers.bit_length() - 1):
                key_cot = key_cot + swap(key_cot, "col", 1 << bit)
                value_cot = value_cot + swap(value_cot, "col", 1 << bit)
            key_cot, value_cot = key_cot.astype(BF), value_cot.astype(BF)
        attn_part, dot_part, grad_heads = head_back(
            info, query_cot, key_cot, value_cot, wq, wkv, normed_attn, tokens_full, gains
        )
        dot_part = dot_part.reshape(span)
        width_dot = lax.psum(dot_part[:tok] + swap(dot_part[tok:], "row", 1), "col")
        attn_cot = plain_reduce(attn_part)
        grad_gate = contract(normed_mlp, gate_cot, 0, 0).astype(BF)
        grad_up = contract(normed_mlp, up_cot, 0, 0).astype(BF)
        grad_down = contract(hidden, out_low, 0, 0).astype(BF)
        sums = plain_group_sum(
            [grad_gate, grad_up, grad_down, grad_out, grad_heads], ["columns", "columns", "rows", "rows", "stack"]
        )
    output = (resid_mid[:tok, :width] + down_sum).astype(BF)
    own_in = tokens.astype(F32)
    scale_own = scale_a[:tok, :1]
    input_grad = (
        mid_cot
        + attn_cot * attn_gain * scale_own
        - own_in * (scale_own * scale_own * scale_own * width_dot[:, None] / D)
    )
    gain_a_part = jnp.sum(attn_cot * own_in * scale_own, axis=0)

    out_gate, out_up, out_down, out_out, out_heads = [g.astype(F32) for g in sums]
    out_heads = out_heads.reshape(col_devices, width, out_heads.shape[1])
    out_query = jnp.concatenate([out_heads[i, :, :head_width] for i in range(col_devices)], axis=1)
    leaders = range(0, col_devices, sharers)
    out_key = jnp.concatenate([out_heads[i, :, head_width : head_width + HD] for i in leaders], axis=1)
    out_value = jnp.concatenate(
        [out_heads[i, :, head_width + HD : head_width + 2 * HD] for i in leaders], axis=1
    )

    gain_sums = jnp.stack([gain_a_part, gain_m_part[0]])
    if fit:
        grown, hops = [out_gate, out_up, out_down], [("row", 1), ("dp", 1), ("dp", 2)]
        for n, (axis, step) in enumerate(hops):
            other = swap(gain_sums, axis, step)
            other, grown[n] = lax.optimization_barrier((other, grown[n]))
            gain_sums = gain_sums + other
        out_gate, out_up, out_down = grown
    else:
        gain_sums = lax.psum(gain_sums, ("dp", "row"))
        own_peaks = lax.pmax(peak, "dp")[:, 0]
        row_peaks = lax.all_gather(own_peaks, "col")
    row_peaks = row_peaks.reshape(heads_row)
    clip_factor = CLIP_LEVEL / jnp.maximum(row_peaks, CLIP_LEVEL)
    query_scale = jnp.repeat(jnp.sqrt(clip_factor), HD)
    key_scale = jnp.repeat(jnp.sqrt(jnp.min(clip_factor.reshape(keyval_row, group), axis=1)), HD)
    clipped_query = (w_query.astype(F32) * query_scale[None, :]).astype(BF)
    clipped_key = (w_key.astype(F32) * key_scale[None, :]).astype(BF)
    return (
        output,
        input_grad,
        gain_sums[0],
        out_query,
        out_key,
        out_value,
        out_out,
        gain_sums[1],
        out_gate,
        out_up,
        out_down,
        own_peaks,
        clipped_query,
        clipped_key,
    )


def solution(mesh):
    in_specs = (
        P(("dp", "row"), "col"),
        P("dp"),
        P("col"),
        P("col", "row"),
        P("col", "row"),
        P("col", "row"),
        P("row", "col"),
        P("col"),
        P("col", "row"),
        P("col", "row"),
        P("row", "col"),
        P(("dp", "row"), "col"),
    )
    out_specs = (
        P(("dp", "row"), "col"),
        P(("dp", "row"), "col"),
        P("col"),
        P("col", "row"),
        P("col", "row"),
        P("col", "row"),
        P("row", "col"),
        P("col"),
        P("col", "row"),
        P("col", "row"),
        P("row", "col"),
        P(("row", "col")),
        P("col", "row"),
        P("col", "row"),
    )
    return jax.shard_map(
        on_device, mesh=mesh, in_specs=in_specs, out_specs=out_specs, check_vma=False
    )
```
